32 devices in a mesh: utt: 4 (over x, core), seq: 8 (over z, y).
Axes of the slice: x: 2, y: 2, z: 4, core: 2. Of those that a mesh axis runs over, the one named last changes fastest.
Arguments:
- frames_in: bfloat16 [4, 1024, 1024], P('utt', 'seq'), may hold values from -6 to 6
- skip_in: bfloat16 [4, 1024, 1024], P('utt', 'seq'), may hold values from -6 to 6
- flow_times: float32 [4, 3], P('utt'), may hold values from 0 to 1
- frame_lengths: int32 [4, 3], P('utt'), may hold values from 1 to 512, 1024 in all within a row
- char_lengths: int32 [4, 3], P('utt'), may hold values from 64 to 255
- drop_mask: int32 [4, 1024], P('utt', 'seq'), may hold values from 0 to 1, as said below
- out_grad: bfloat16 [4, 1024, 1024], P('utt', 'seq'), may hold values from -6 to 6
- w_skip: bfloat16 [2048, 1024], replicated, may hold values from -0.125 to 0.125
- b_skip: float32 [1024], replicated, may hold values from -2 to 2
- w_mod: bfloat16 [1024, 6144], replicated, as said below
- b_mod: float32 [6144], replicated, may hold values from -1.6 to 1.6
- w_qkv: bfloat16 [1024, 3072], replicated, as said below
- b_qkv: float32 [3072], replicated, may hold values from -2 to 2
- w_out: bfloat16 [1024, 1024], replicated, may hold values from -3.5 to 3.5
- b_out: float32 [1024], replicated, may hold values from -2 to 2
- w_up: bfloat16 [1024, 4096], replicated, may hold values from -0.1875 to 0.1875
- b_up: float32 [4096], replicated, may hold values from -2 to 2
- w_down: bfloat16 [4096, 1024], replicated, may hold values from -0.09375 to 0.09375
- b_down: float32 [1024], replicated, may hold values from -2 to 2
Outputs:
- mixed_out: bfloat16 [4, 1024, 1024], P('utt', 'seq')
- grad_frames: bfloat16 [4, 1024, 1024], P('utt', 'seq')
- grad_skip: bfloat16 [4, 1024, 1024], P('utt', 'seq')
- grad_w_skip: float32 [2048, 1024], P('seq')
- grad_b_skip: float32 [1024], P('seq')
- grad_w_mod: float32 [1024, 6144], P('seq')
- grad_b_mod: float32 [6144], P('seq')
- grad_w_qkv: float32 [1024, 3072], P('seq')
- grad_b_qkv: float32 [3072], P('seq')
- grad_w_out: float32 [1024, 1024], P('seq')
- grad_b_out: float32 [1024], P('seq')
- grad_w_up: float32 [1024, 4096], P('seq')
- grad_b_up: float32 [4096], P('seq')
- grad_w_down: float32 [4096, 1024], P('seq')
- grad_b_down: float32 [1024], P('seq')
The draws below stay inside these ranges and needn't reach their ends.
Inputs may be any that keep to these rules, and one draw needn't show every extreme that they name: `frame_lengths`: frames of each utterance of a group in frame order; they sum to 1024 and the longest has exactly 512. `drop_mask`: 1 where a frame's text condition is dropped. `w_qkv`: entries of magnitude at most 4 / sqrt(1024). `w_mod`: entries of magnitude at most 4 / sqrt(1024).
All inputs are finite; a program needn't handle non-finite values.
Results may differ from the reference program's by a relative error of at most 0.02.
Values may be sent and summed in bfloat16 or wider, within the bound.
A program may use at most 256 MiB of HBM per device.

```python
import math
import jax
import jax.numpy as jnp
import numpy as np
from jax import lax

D = 1024
HEADS = 16
HEAD_DIM = 64
FF = 4096
AVG = 1024
FRAMES = 1024
GROUPS = 4
LONGEST = 512
UTTS = 3


def draw_drop_mask(key, part):
    random_vals = jax.random.randint(jax.random.fold_in(key, 13), (GROUPS, FRAMES), 0, 1000)
    frame_index = jnp.arange(FRAMES, dtype=jnp.int32)
    thresholds = 100 + 650 * frame_index // max(FRAMES - 1, 1)
    return (random_vals < thresholds[None, :]).astype(jnp.int32)


def draw_w_qkv(key, part):
    entries = jnp.clip(jax.random.normal(jax.random.fold_in(key, 11), (D, 3 * D), dtype=jnp.float32), -4.0, 4.0)
    return (entries * (1.0 / math.sqrt(D))).astype(jnp.bfloat16)


def draw_w_mod(key, part):
    entries = jnp.clip(jax.random.normal(jax.random.fold_in(key, 17), (D, 6 * D), dtype=jnp.float32), -4.0, 4.0)
    return (entries * (1.0 / math.sqrt(D))).astype(jnp.bfloat16)


def touch_ends(drawn, stream_key, smallest, top_value):
    longest = drawn.shape.index(max(drawn.shape))
    spots = []
    for shift in (0, 1):
        where = [jax.random.randint(jax.random.fold_in(stream_key, axis), (), 0, length) for axis, length in enumerate(drawn.shape)]
        where[longest] = (where[longest] + shift) % drawn.shape[longest]
        spots.append(tuple(where))
    return drawn.at[spots[0]].set(smallest).at[spots[1]].set(top_value)


def block_scale(key, shape, cuts, least, largest):
    loudness = 1.0
    for dim, shards_of in cuts:
        heights = jax.random.uniform(jax.random.fold_in(jax.random.fold_in(key, 6), dim), (shards_of,), jnp.float32, least / len(cuts), largest / len(cuts))
        loudness = loudness * jnp.repeat(jnp.exp(heights), shape[dim] // shards_of).reshape((-1,) + (1,) * (len(shape) - 1 - dim))
    return loudness


def profile(amount, total, limit, lean):
    portions = [(1 << 20) // math.isqrt(rank ** lean) + 1 for rank in range(2, amount + 1)]
    spare, holding = total - limit - (amount - 1), [1] * (amount - 1)
    while spare > 0:
        free = [i for i in range(amount - 1) if holding[i] < limit]
        mass, left = sum([portions[i] for i in free]), spare
        for i in free:
            addition = min(limit - holding[i], max(1, left * portions[i] // mass), spare)
            holding[i] = holding[i] + addition
            spare = spare - addition
    return np.array([limit] + holding)


def uneven_parts(rng, amount, total, reach, skew):
    if amount == 2:
        one = jax.random.randint(rng, (), max(1, total - reach), min(reach, total - 1) + 1)
        return jnp.stack([one, total - one])
    tallies = jnp.asarray(profile(amount, total, reach, skew), jnp.int32)
    couples = (amount - 1) // 2
    giver, sink = tallies[1:1 + 2 * couples:2], tallies[2:2 + 2 * couples:2]
    slack = jnp.minimum(giver - 1, reach - sink)
    shifted = jax.random.randint(jax.random.fold_in(rng, 1), (couples,), 0, 1 << 20) % (slack + 1)
    tallies = tallies.at[1:1 + 2 * couples:2].set(giver - shifted).at[2:2 + 2 * couples:2].set(sink + shifted)
    return tallies[jax.random.permutation(jax.random.fold_in(rng, 2), amount)]


def bell_draw(key, dims, scale, bound, cuts=(), kind=jnp.bfloat16):
    values = scale * jax.random.normal(key, dims, jnp.float32)
    if cuts:
        values = values * block_scale(key, dims, cuts, -0.22, 0.18)
    return jnp.clip(values, -bound, bound).astype(kind)


def setup_inputs(seed: int = 0) -> dict:
    streams_of = jax.random.split(jax.random.key(seed), 20)
    return {
        "frames_in": bell_draw(streams_of[0], (GROUPS, FRAMES, D), 1.0, 6.0, ((0, 4), (1, 8))),
        "skip_in": bell_draw(streams_of[1], (GROUPS, FRAMES, D), 1.0, 6.0, ((0, 4), (1, 8))),
        "flow_times": jnp.clip(1.0 * jax.random.uniform(streams_of[2], (GROUPS, UTTS), jnp.float32) ** block_scale(streams_of[2], (GROUPS, UTTS), ((0, 4),), -0.2, 0.2), 0.0, 1.0),
        "frame_lengths": jax.vmap(lambda own: uneven_parts(own, UTTS, FRAMES, LONGEST, 1))(jax.random.split(streams_of[3], GROUPS)).reshape((GROUPS, UTTS)).astype(jnp.int32),
        "char_lengths": touch_ends(jax.random.randint(streams_of[4], (GROUPS, UTTS), AVG // 16, AVG // 4), jax.random.fold_in(streams_of[4], 1), AVG // 16, (AVG // 4) - 1).astype(jnp.int32),
        "drop_mask": draw_drop_mask(jax.random.fold_in(streams_of[19], 71), 0),
        "out_grad": bell_draw(streams_of[6], (GROUPS, FRAMES, D), 1.0, 6.0, ((0, 4), (1, 8))),
        "w_skip": bell_draw(streams_of[7], (2 * D, D), (2 * D) ** -0.5, 0.125),
        "b_skip": bell_draw(streams_of[8], (D,), 0.5, 2.0, (), jnp.float32),
        "w_mod": draw_w_mod(jax.random.fold_in(streams_of[19], 71), 0),
        "b_mod": bell_draw(streams_of[10], (6 * D,), 0.4, 1.6, (), jnp.float32),
        "w_qkv": draw_w_qkv(jax.random.fold_in(streams_of[19], 71), 0),
        "b_qkv": bell_draw(streams_of[12], (3 * D,), 0.5, 2.0, (), jnp.float32),
        "w_out": bell_draw(streams_of[13], (D, D), (max(1, 3 * D // AVG)) ** -0.5, 3.5),
        "b_out": bell_draw(streams_of[14], (D,), 0.5, 2.0, (), jnp.float32),
        "w_up": bell_draw(streams_of[15], (D, FF), D ** -0.5, 0.1875),
        "b_up": bell_draw(streams_of[16], (FF,), 0.5, 2.0, (), jnp.float32),
        "w_down": bell_draw(streams_of[17], (FF, D), FF ** -0.5, 0.09375),
        "b_down": bell_draw(streams_of[18], (D,), 0.5, 2.0, (), jnp.float32),
    }


HIGHEST_PRECISION = lax.Precision.HIGHEST
EPSILON = 1e-06

@jax.custom_vjp
def low(v):
    return lax.optimization_barrier(v.astype(jnp.bfloat16)).astype(jnp.float32)

@jax.custom_vjp
def low_back(v):
    return v

def low_keep(v):
    return (low(v), None)

def low_pass(kept, grad):
    return (grad,)

def back_keep(v):
    return (v, None)

def back_low(kept, grad):
    return (low(grad),)
low.defvjp(low_keep, low_pass)
low_back.defvjp(back_keep, back_low)

def layer_norm(values):
    average = lax.optimization_barrier(jnp.mean(values, axis=-1, keepdims=True))
    centred = values - average
    spread = lax.optimization_barrier(jnp.mean(centred * centred, axis=-1, keepdims=True))
    return centred * lax.rsqrt(spread + EPSILON)

def modulate(values, scale_part, shift_part):
    return layer_norm(values) * (1.0 + scale_part) + shift_part

def time_embed(flow_vals, model_width):
    half_dim = model_width // 2
    inverse = jnp.exp(-math.log(10000.0) * jnp.arange(half_dim, dtype=jnp.float32) / half_dim)
    angles = 1000.0 * flow_vals[:, None] * inverse[None, :]
    return jnp.concatenate([jnp.sin(angles), jnp.cos(angles)], axis=1)

def rotary_tables(position, head_size):
    half_dim = head_size // 2
    inverse = jnp.exp(-math.log(10000.0) * 2.0 * jnp.arange(half_dim, dtype=jnp.float32) / head_size)
    angles = position.astype(jnp.float32)[:, None] * inverse[None, :]
    return (jnp.cos(angles)[:, None, :], jnp.sin(angles)[:, None, :])

def rotate(tensor, angle_cos, angle_sin):
    half_dim = tensor.shape[-1] // 2
    leading = tensor[..., :half_dim]
    trailing = tensor[..., half_dim:]
    return jnp.concatenate([leading * angle_cos - trailing * angle_sin, trailing * angle_cos + leading * angle_sin], axis=-1)

def frame_tables(lengths, char_counts, first_frame, frame_count):
    utt_ends = jnp.cumsum(lengths).astype(jnp.int32)
    utt_starts = utt_ends - lengths
    frame_index = first_frame + jnp.arange(frame_count, dtype=jnp.int32)
    segment = lax.optimization_barrier(jnp.sum((frame_index[:, None] >= utt_ends[None, :]).astype(jnp.int32), axis=1))
    member = segment[:, None] == jnp.arange(lengths.shape[0], dtype=jnp.int32)[None, :]
    position = frame_index - lax.optimization_barrier(jnp.sum(jnp.where(member, utt_starts[None, :], 0), axis=1))
    prompt = lax.optimization_barrier(jnp.sum(jnp.where(member, char_counts[None, :], 0), axis=1))
    return (segment, position, position >= prompt, member)

def attend_rows(query_block, query_segment, key_rot, values, key_segment):
    scores = low_back(jnp.einsum('qhd,khd->hqk', query_block, key_rot, precision=HIGHEST_PRECISION) * 0.125)
    allowed = query_segment[:, None] == key_segment[None, :]
    weights = jnp.where(allowed[None], jnp.exp(scores), 0.0)
    totals = lax.optimization_barrier(jnp.sum(weights, axis=2))
    weighted = low_back(jnp.einsum('hqk,khd->qhd', low(weights), values, precision=HIGHEST_PRECISION))
    return (weighted / jnp.transpose(totals)[:, :, None]).reshape(query_block.shape[0], -1)

def attention(queries, key_rot, values, segment):
    frame_count = queries.shape[0]
    block_rows = min(512, frame_count)
    query_blocks = queries.reshape(frame_count // block_rows, block_rows, HEADS, HEAD_DIM)
    segment_blocks = segment.reshape(frame_count // block_rows, block_rows)
    block_fn = jax.checkpoint(lambda block_item: attend_rows(block_item[0], block_item[1], key_rot, values, segment))
    return lax.map(block_fn, (query_blocks, segment_blocks)).reshape(frame_count, -1)

def group_forward(params, group_item):
    w_skip, b_skip, w_mod, b_mod, w_qkv, b_qkv, w_out, b_out, w_up, b_up, w_down, b_down = params
    frames_g, skip_g, segment, position, member_f, flow_vals = group_item
    frame_count = frames_g.shape[0]
    time_act = low(jax.nn.silu(time_embed(flow_vals, D)))
    mod_u = jnp.dot(time_act, w_mod, precision=HIGHEST_PRECISION) + b_mod
    mod_f = jnp.dot(member_f, mod_u, precision=HIGHEST_PRECISION)
    shift_a, scale_a, gate_a, shift_f, scale_f, gate_f = jnp.split(mod_f, 6, axis=1)
    joined = jnp.concatenate([frames_g, skip_g], axis=1)
    residual = low_back(jnp.dot(joined, w_skip, precision=HIGHEST_PRECISION) + b_skip)
    norm_a = low(modulate(residual, scale_a, shift_a))
    qkv_full = low_back(jnp.dot(norm_a, w_qkv, precision=HIGHEST_PRECISION) + b_qkv)
    angle_cos, angle_sin = rotary_tables(position, HEAD_DIM)
    queries = low(rotate(qkv_full[:, :D].reshape(frame_count, HEADS, HEAD_DIM), angle_cos, angle_sin))
    key_rot = low(rotate(qkv_full[:, D:2 * D].reshape(frame_count, HEADS, HEAD_DIM), angle_cos, angle_sin))
    values = low(qkv_full[:, 2 * D:].reshape(frame_count, HEADS, HEAD_DIM))
    attended = attention(queries, key_rot, values, segment)
    branch = low_back(jnp.dot(low(attended), w_out, precision=HIGHEST_PRECISION) + b_out)
    mid_state = residual + gate_a * branch
    norm_f = low(modulate(mid_state, scale_f, shift_f))
    ff_inner = low_back(jnp.dot(norm_f, w_up, precision=HIGHEST_PRECISION) + b_up)
    ff_act = low(jax.nn.gelu(ff_inner, approximate=True))
    ff_out = low_back(jnp.dot(ff_act, w_down, precision=HIGHEST_PRECISION) + b_down)
    return mid_state + gate_f * ff_out

def reference(frames_in, skip_in, flow_times, frame_lengths, char_lengths, drop_mask, out_grad, w_skip, b_skip, w_mod, b_mod, w_qkv, b_qkv, w_out, b_out, w_up, b_up, w_down, b_down):
    segment, position, in_loss, member = jax.vmap(lambda lengths, char_counts: frame_tables(lengths, char_counts, 0, FRAMES))(frame_lengths, char_lengths)
    loss_mask = in_loss.astype(jnp.float32)
    dropped = drop_mask.astype(jnp.float32)
    n_drop = jnp.sum(loss_mask * dropped)
    n_keep = jnp.sum(loss_mask * (1.0 - dropped))
    loss_weight = loss_mask * (n_drop + n_keep) * 0.5 * (dropped / (n_drop + 1.0) + (1.0 - dropped) / (n_keep + 1.0))
    params = tuple((source_array.astype(jnp.float32) for source_array in (w_skip, b_skip, w_mod, b_mod, w_qkv, b_qkv, w_out, b_out, w_up, b_up, w_down, b_down)))
    member_f = member.astype(jnp.float32)

    def forward(weights_all, frames_f, skip_f):
        return lax.map(lambda group_item: group_forward(weights_all, group_item), (frames_f, skip_f, segment, position, member_f, flow_times))
    out_f, pull = jax.vjp(forward, params, frames_in.astype(jnp.float32), skip_in.astype(jnp.float32))
    grads, grad_frames, grad_skip = pull(out_grad.astype(jnp.float32) * loss_weight[:, :, None])
    return (out_f.astype(jnp.bfloat16), grad_frames.astype(jnp.bfloat16), grad_skip.astype(jnp.bfloat16), grads[0], grads[1], grads[2], grads[3], grads[4], grads[5], grads[6], grads[7], grads[8], grads[9], grads[10], grads[11])
```

```python
from functools import partial
import math

import jax
import jax.numpy as jnp
from jax import lax
from jax.experimental import pallas as pl
from jax.experimental.pallas import tpu as pltpu
from jax.sharding import PartitionSpec as P

HEADS = 16
HEAD_DIM = 64


HIGHEST_PRECISION = lax.Precision.HIGHEST
EPSILON = 1e-06


def layer_norm(values):
    average = jnp.mean(values, axis=-1, keepdims=True)
    centred = values - average
    spread = jnp.mean(centred * centred, axis=-1, keepdims=True)
    return centred * lax.rsqrt(spread + EPSILON)


def modulate(values, scale_part, shift_part):
    return layer_norm(values) * (1.0 + scale_part) + shift_part


def time_embed(flow_vals, model_width):
    half_dim = model_width // 2
    inverse = jnp.exp(-math.log(10000.0) * jnp.arange(half_dim, dtype=jnp.float32) / half_dim)
    angles = 1000.0 * flow_vals[:, None] * inverse[None, :]
    return jnp.concatenate([jnp.sin(angles), jnp.cos(angles)], axis=1)


def rotary_tables(position, head_size):
    half_dim = head_size // 2
    inverse = jnp.exp(
        -math.log(10000.0) * 2.0 * jnp.arange(half_dim, dtype=jnp.float32) / head_size
    )
    angles = position.astype(jnp.float32)[:, None] * inverse[None, :]
    return (jnp.cos(angles)[:, None, :], jnp.sin(angles)[:, None, :])


def rotate(tensor, angle_cos, angle_sin):
    half_dim = tensor.shape[-1] // 2
    leading = tensor[..., :half_dim]
    trailing = tensor[..., half_dim:]
    return jnp.concatenate(
        [leading * angle_cos - trailing * angle_sin, trailing * angle_cos + leading * angle_sin],
        axis=-1,
    )


def unrotate(gradient, angle_cos, angle_sin):
    half_dim = gradient.shape[-1] // 2
    leading = gradient[..., :half_dim]
    trailing = gradient[..., half_dim:]
    return jnp.concatenate(
        [leading * angle_cos + trailing * angle_sin, trailing * angle_cos - leading * angle_sin],
        axis=-1,
    )


def frame_tables(lengths, char_counts, first_frame, frame_count):
    utt_ends = jnp.cumsum(lengths)
    utt_starts = utt_ends - lengths
    frame_index = first_frame + jnp.arange(frame_count, dtype=jnp.int32)
    segment = jnp.sum((frame_index[:, None] >= utt_ends[None, :]).astype(jnp.int32), axis=1)
    member = segment[:, None] == jnp.arange(lengths.shape[0], dtype=jnp.int32)[None, :]
    position = frame_index - jnp.sum(jnp.where(member, utt_starts[None, :], 0), axis=1)
    prompt = jnp.sum(jnp.where(member, char_counts[None, :], 0), axis=1)
    return (segment, position, position >= prompt, member)


def key_segments(key_start, key_count, utt_ends):
    frame_index = key_start + jnp.arange(key_count, dtype=jnp.int32)
    return jnp.sum((frame_index[:, None] >= utt_ends[None, :]).astype(jnp.int32), axis=1)


def block_scores(queries, key_piece, query_segment, key_segment, usable):
    key_rows = key_piece.reshape(key_piece.shape[0], queries.shape[1], queries.shape[2])
    scores = (
        jnp.einsum("qhd,khd->hqk", queries, key_rows, preferred_element_type=jnp.float32) * 0.125
    )
    allowed = jnp.logical_and(query_segment[:, None] == key_segment[None, :], usable)
    return (jnp.where(allowed[None], jnp.exp(scores), 0.0), key_rows)


def over_blocks(block_fn, running, piece, key_start, shard_rows):
    key_count = piece.shape[1]
    shard_total = key_count // shard_rows
    group_size = max(1, min(shard_total, 1024 // shard_rows))
    while shard_total % group_size != 0:
        group_size = group_size - 1
    block_rows = group_size * shard_rows
    if block_rows == key_count:
        return block_fn(running, piece, key_start)

    def one_block(block_index, inner_state):
        portion = lax.dynamic_slice_in_dim(piece, block_index * block_rows, block_rows, 1)
        return block_fn(inner_state, portion, key_start + block_index * block_rows)

    return lax.fori_loop(0, key_count // block_rows, one_block, running)


def forward_piece(running, piece, key_start, usable, queries, query_segment, utt_ends):
    weighted, totals = running
    key_segment = key_segments(key_start, piece.shape[1], utt_ends)
    weights, key_rows = block_scores(queries, piece[0], query_segment, key_segment, usable)
    value_rows = piece[1].reshape(key_rows.shape)
    totals = totals + jnp.sum(weights, axis=2)
    weighted = weighted + jnp.einsum(
        "hqk,khd->qhd", weights.astype(jnp.bfloat16), value_rows, preferred_element_type=jnp.float32
    )
    return (weighted, totals)


def backward_piece(piece, key_start, usable, queries, query_segment, utt_ends, grad_acc, delta):
    key_count = piece.shape[1]
    key_segment = key_segments(key_start, key_count, utt_ends)
    weights, key_rows = block_scores(queries, piece[0], query_segment, key_segment, usable)
    value_rows = piece[1].reshape(key_rows.shape)
    value_dots = jnp.einsum(
        "qhd,khd->hqk", grad_acc, value_rows, preferred_element_type=jnp.float32
    )
    d_scores = (weights * (value_dots - delta[:, :, None])).astype(jnp.bfloat16)
    d_query = (
        jnp.einsum("hqk,khd->qhd", d_scores, key_rows, preferred_element_type=jnp.float32) * 0.125
    )
    d_key = (
        jnp.einsum("hqk,qhd->khd", d_scores, queries, preferred_element_type=jnp.float32) * 0.125
    )
    d_value = jnp.einsum(
        "hqk,qhd->khd", weights.astype(jnp.bfloat16), grad_acc, preferred_element_type=jnp.float32
    )
    return (
        d_query,
        jnp.stack([d_key.reshape(key_count, -1), d_value.reshape(key_count, -1)], axis=0),
    )


def back_product(gradient_rows, matrix):
    return jnp.einsum("fo,io->fi", gradient_rows, matrix, preferred_element_type=jnp.float32)


def xor_permute(value, axis_name, bit):
    size = lax.axis_size(axis_name)
    return lax.ppermute(value, axis_name, [(i, i ^ bit) for i in range(size)])


def bits_of(axis_name):
    size, bits, bit = lax.axis_size(axis_name), [], 1
    while bit < size:
        bits.append(bit)
        bit *= 2
    return bits


def xor_sum(value, axis_name):
    for bit in bits_of(axis_name):
        value = value + xor_permute(value, axis_name, bit)
    return value


def gather_left(rows):
    for bit in reversed(bits_of("utt")):
        rows = jnp.concatenate([rows, xor_permute(rows, "utt", bit)], axis=0)
    return rows


def gather_right(rows):
    place = lax.axis_index("utt")
    for bit in reversed(bits_of("utt")):
        mine = (place & bit) // bit
        width = rows.shape[1] // 2
        kept = lax.dynamic_slice_in_dim(rows, mine * width, width, 1)
        given = lax.dynamic_slice_in_dim(rows, (1 - mine) * width, width, 1)
        rows = jnp.concatenate([kept, xor_permute(given, "utt", bit)], axis=0)
    return rows


def gather_ordered(value, axis):
    place = lax.axis_index("utt")
    for bit in bits_of("utt"):
        other = xor_permute(value, "utt", bit)
        low = (place & bit) == 0
        value = jnp.concatenate(
            [jnp.where(low, value, other), jnp.where(low, other, value)], axis=axis
        )
    return value


def scatter_rows(tile):
    place = lax.axis_index("seq")
    for bit in bits_of("seq"):
        mine = (place & bit) // bit
        rest = lax.axis_size("seq") // (2 * bit)
        pieces = tile.reshape(rest, 2, -1, tile.shape[-1])
        kept = lax.dynamic_index_in_dim(pieces, mine, 1, keepdims=False)
        given = lax.dynamic_index_in_dim(pieces, 1 - mine, 1, keepdims=False)
        given = xor_permute(given, "seq", bit)
        tile = (kept.astype(jnp.float32) + given.astype(jnp.float32)).astype(jnp.bfloat16)
    return tile.reshape(-1, tile.shape[-1])


def weight_grad(left_all, right_rows):
    right_all = gather_right(right_rows)
    tile = jnp.einsum(
        "fi,fo->io", left_all, right_all, preferred_element_type=jnp.float32
    ).astype(jnp.bfloat16)
    tile = tile.reshape(-1, tile.shape[-1])
    piece = scatter_rows(tile)
    return gather_ordered(piece, 1).astype(jnp.float32)


def swap_halves(values, lower):
    return jnp.where(lower, pltpu.roll(values, 96, 1), pltpu.roll(values, 32, 1))


def lower_half(shape):
    return lax.broadcasted_iota(jnp.int32, shape, 1) % HEAD_DIM < HEAD_DIM // 2


def rotate_pack_kernel(q_ref, k_ref, v_ref, cos_ref, sin_ref, out_ref):
    lower = lower_half(q_ref.shape)
    cos, sin = cos_ref[...], sin_ref[...]
    q, k = q_ref[...], k_ref[...]
    out_ref[0, :, 0:128] = (q * cos + swap_halves(q, lower) * sin).astype(jnp.bfloat16)
    out_ref[0, :, 128:256] = (k * cos + swap_halves(k, lower) * sin).astype(jnp.bfloat16)
    out_ref[0, :, 256:384] = v_ref[...].astype(jnp.bfloat16)


def rotate_pack(qkv_full, cos, sin):
    rows = qkv_full.shape[0]
    blocks = qkv_full.shape[1] // 384
    table = pl.BlockSpec((rows, 128), lambda i: (0, 0))
    return pl.pallas_call(
        rotate_pack_kernel,
        grid=(blocks,),
        in_specs=[
            pl.BlockSpec((rows, 128), lambda i: (0, i)),
            pl.BlockSpec((rows, 128), lambda i: (0, blocks + i)),
            pl.BlockSpec((rows, 128), lambda i: (0, 2 * blocks + i)),
            table,
            table,
        ],
        out_specs=pl.BlockSpec((1, rows, 384), lambda i: (i, 0, 0)),
        out_shape=jax.ShapeDtypeStruct((blocks, rows, 384), jnp.bfloat16),
    )(qkv_full, qkv_full, qkv_full, cos, sin)


def head_scores(q, k, seg_q, seg_k):
    scores = lax.dot_general(q, k, (((1,), (1,)), ((), ())), preferred_element_type=jnp.float32)
    return jnp.where(seg_q == seg_k, jnp.exp(scores * 0.125), 0.0)


def attend_kernel(q_ref, k_ref, v_ref, segq_ref, segk_ref, out_ref, exact_ref, total_ref):
    q, k, v = q_ref[...], k_ref[...], v_ref[...]
    lane = lax.broadcasted_iota(jnp.int32, q.shape, 1)
    first = lane < HEAD_DIM
    zero = jnp.zeros_like(q)
    seg_q, seg_k = segq_ref[...], segk_ref[...]
    results = []
    for own in (first, jnp.logical_not(first)):
        weights = head_scores(jnp.where(own, q, zero), k, seg_q, seg_k)
        total = jnp.sum(weights, axis=1, keepdims=True)
        summed = jnp.dot(weights.astype(jnp.bfloat16), v, preferred_element_type=jnp.float32)
        results.append((summed, total))
    total = jnp.where(first, results[0][1], results[1][1])
    attended = jnp.where(first, results[0][0], results[1][0]) / total
    out_ref[...] = attended.astype(jnp.bfloat16)
    exact_ref[...] = attended
    total_ref[...] = total


def attend(qkv_heads, seg_col, seg_row):
    frames = qkv_heads.shape[0]
    step = 256
    column = lambda c: pl.BlockSpec((frames, 128), lambda i: (0, c))
    tile = pl.BlockSpec((step, 128), lambda i: (i, 0))
    return pl.pallas_call(
        attend_kernel,
        grid=(frames // step,),
        in_specs=[
            tile,
            column(1),
            column(2),
            pl.BlockSpec((step, 1), lambda i: (i, 0)),
            pl.BlockSpec((1, frames), lambda i: (0, 0)),
        ],
        out_specs=[tile, tile, tile],
        out_shape=[
            jax.ShapeDtypeStruct((frames, 128), jnp.bfloat16),
            jax.ShapeDtypeStruct((frames, 128), jnp.float32),
            jax.ShapeDtypeStruct((frames, 128), jnp.float32),
        ],
    )(qkv_heads, qkv_heads, qkv_heads, seg_col, seg_row)


def attend_back_kernel(
    q_ref, k_ref, v_ref, segq_ref, segk_ref, exact_ref, total_ref, grad_ref, cos_ref, sin_ref,
    out_ref, dk_ref, dv_ref,
):
    step = pl.program_id(0)
    rows = q_ref.shape[0]

    @pl.when(step == 0)
    def _():
        dk_ref[...] = jnp.zeros_like(dk_ref)
        dv_ref[...] = jnp.zeros_like(dv_ref)

    q, k, v = q_ref[...], k_ref[...], v_ref[...]
    first = lax.broadcasted_iota(jnp.int32, q.shape, 1) < HEAD_DIM
    zero = jnp.zeros_like(q)
    seg_q, seg_k = segq_ref[...], segk_ref[...]
    scaled = grad_ref[...].astype(jnp.float32) / total_ref[...]
    grad_acc = scaled.astype(jnp.bfloat16)
    product = scaled * exact_ref[...]
    along = (((1,), (1,)), ((), ()))
    down = (((0,), (0,)), ((), ()))
    d_query = []
    for own in (first, jnp.logical_not(first)):
        q_own = jnp.where(own, q, zero)
        g_own = jnp.where(own, grad_acc, zero)
        delta = jnp.sum(jnp.where(own, product, 0.0), axis=1, keepdims=True)
        weights = head_scores(q_own, k, seg_q, seg_k)
        dots = lax.dot_general(g_own, v, along, preferred_element_type=jnp.float32)
        d_scores = (weights * (dots - delta)).astype(jnp.bfloat16)
        d_query.append(jnp.dot(d_scores, k, preferred_element_type=jnp.float32))
        dk_ref[...] += lax.dot_general(d_scores, q_own, down, preferred_element_type=jnp.float32)
        dv_ref[...] += lax.dot_general(
            weights.astype(jnp.bfloat16), g_own, down, preferred_element_type=jnp.float32
        )
    d_q = jnp.where(first, d_query[0], d_query[1]) * 0.125
    here = pl.ds(pl.multiple_of(step * rows, rows), rows)
    lower = lower_half(d_q.shape)
    turned = d_q * cos_ref[here, :] - swap_halves(d_q, lower) * sin_ref[here, :]
    out_ref[here, 0:128] = turned.astype(jnp.bfloat16)

    @pl.when(step == pl.num_programs(0) - 1)
    def _():
        for part in range(out_ref.shape[0] // rows):
            now = pl.ds(part * rows, rows)
            d_k = dk_ref[now, :] * 0.125
            turned_k = d_k * cos_ref[now, :] - swap_halves(d_k, lower) * sin_ref[now, :]
            out_ref[now, 128:256] = turned_k.astype(jnp.bfloat16)
            out_ref[now, 256:384] = dv_ref[now, :].astype(jnp.bfloat16)


def attend_back(qkv_heads, seg_col, seg_row, exact, total, grad_heads, cos, sin):
    frames = qkv_heads.shape[0]
    step = 256
    column = lambda c: pl.BlockSpec((frames, 128), lambda i: (0, c))
    tile = pl.BlockSpec((step, 128), lambda i: (i, 0))
    return pl.pallas_call(
        attend_back_kernel,
        grid=(frames // step,),
        in_specs=[
            tile,
            column(1),
            column(2),
            pl.BlockSpec((step, 1), lambda i: (i, 0)),
            pl.BlockSpec((1, frames), lambda i: (0, 0)),
            tile,
            tile,
            tile,
            column(0),
            column(0),
        ],
        out_specs=pl.BlockSpec((frames, 384), lambda i: (0, 0)),
        out_shape=jax.ShapeDtypeStruct((frames, 384), jnp.bfloat16),
        scratch_shapes=[pltpu.VMEM((frames, 128), jnp.float32)] * 2,
    )(
        qkv_heads, qkv_heads, qkv_heads, seg_col, seg_row, exact, total, grad_heads, cos, sin
    )


def wide_tables(position):
    half_dim = HEAD_DIM // 2
    lane = jnp.arange(128, dtype=jnp.int32) % HEAD_DIM
    inverse = jnp.exp(
        -math.log(10000.0) * 2.0 * (lane % half_dim).astype(jnp.float32) / HEAD_DIM
    )
    angles = position.astype(jnp.float32)[:, None] * inverse[None, :]
    sign = jnp.where(lane < half_dim, -1.0, 1.0)
    return jnp.cos(angles), jnp.sin(angles) * sign[None, :]


def local(
    frames_in,
    skip_in,
    flow_times,
    frame_lengths,
    char_lengths,
    drop_mask,
    out_grad,
    w_skip,
    b_skip,
    w_mod,
    b_mod,
    w_qkv,
    b_qkv,
    w_out,
    b_out,
    w_up,
    b_up,
    w_down,
    b_down,
):
    local_rows = frames_in.shape[1]
    model_width = frames_in.shape[2]
    shards = lax.axis_size("seq")
    seq_place = lax.axis_index("seq")
    lengths = frame_lengths[0]
    utt_ends = jnp.cumsum(lengths)
    segment, position, in_loss, member = frame_tables(
        lengths, char_lengths[0], seq_place * local_rows, local_rows
    )
    member_f = member.astype(jnp.float32)
    loss_mask = in_loss.astype(jnp.float32)
    dropped = drop_mask[0].astype(jnp.float32)
    counts = jnp.stack([jnp.sum(loss_mask * dropped), jnp.sum(loss_mask * (1.0 - dropped))])
    counts = jnp.pad(counts[None, :], ((0, 7), (0, 126)))
    counts = xor_sum(xor_sum(counts, "utt"), "seq")
    n_drop, n_keep = counts[0, 0], counts[0, 1]
    loss_weight = (
        loss_mask
        * (n_drop + n_keep)
        * 0.5
        * (dropped / (n_drop + 1.0) + (1.0 - dropped) / (n_keep + 1.0))
    )
    time_act = jax.nn.silu(time_embed(flow_times[0], model_width)).astype(jnp.bfloat16)
    mod_u = jnp.dot(time_act, w_mod, preferred_element_type=jnp.float32) + b_mod
    mod_f = jnp.dot(member_f, mod_u, precision=HIGHEST_PRECISION)
    shift_a, scale_a, gate_a, shift_f, scale_f, gate_f = jnp.split(mod_f, 6, axis=1)
    joined = jnp.concatenate([frames_in[0], skip_in[0]], axis=1)
    residual = jnp.dot(joined, w_skip, preferred_element_type=jnp.float32) + b_skip
    norm_a = modulate(residual, scale_a, shift_a).astype(jnp.bfloat16)
    qkv_full = jnp.dot(norm_a, w_qkv, preferred_element_type=jnp.float32) + b_qkv
    by_heads = HEADS * HEAD_DIM == 128 * shards and local_rows * shards % 256 == 0
    if by_heads:
        all_segment, all_position, _, _ = frame_tables(
            lengths, char_lengths[0], 0, local_rows * shards
        )
        cos_all, sin_all = wide_tables(all_position)
        cos_own, sin_own = wide_tables(position)
        qkv_heads = lax.all_to_all(
            rotate_pack(qkv_full, cos_own, sin_own), "seq", 0, 0, tiled=True
        ).reshape(local_rows * shards, 384)
        seg_col, seg_row = all_segment[:, None], all_segment[None, :]
        attn_heads, exact, total = attend(qkv_heads, seg_col, seg_row)
        attn_b = lax.all_to_all(
            attn_heads.reshape(shards, local_rows, 128), "seq", 0, 0, tiled=True
        )
        attn_b = jnp.transpose(attn_b, (1, 0, 2)).reshape(local_rows, model_width)
    else:
        angle_cos, angle_sin = rotary_tables(position, HEAD_DIM)
        queries = rotate(
            qkv_full[:, :model_width].reshape(local_rows, HEADS, HEAD_DIM), angle_cos, angle_sin
        ).astype(jnp.bfloat16)
        key_rot = rotate(
            qkv_full[:, model_width : 2 * model_width].reshape(local_rows, HEADS, HEAD_DIM),
            angle_cos,
            angle_sin,
        ).astype(jnp.bfloat16)
        key_value = jnp.stack(
            [
                key_rot.reshape(local_rows, model_width),
                qkv_full[:, 2 * model_width :].astype(jnp.bfloat16),
            ],
            axis=0,
        )
        start_state = (
            jnp.zeros((local_rows, HEADS, HEAD_DIM), jnp.float32),
            jnp.zeros((HEADS, local_rows), jnp.float32),
        )
        fwd_piece = partial(forward_piece, queries=queries, query_segment=segment, utt_ends=utt_ends)
        weighted, totals = over_blocks(
            partial(fwd_piece, usable=True),
            start_state,
            lax.all_gather(key_value, "seq", axis=1, tiled=True),
            jnp.int32(0),
            local_rows,
        )
        totals_rows = jnp.transpose(totals)
        attended = weighted / totals_rows[:, :, None]
        attn_b = attended.reshape(local_rows, model_width).astype(jnp.bfloat16)
    branch = jnp.dot(attn_b, w_out, preferred_element_type=jnp.float32) + b_out
    mid_state = residual + gate_a * branch
    norm_f = modulate(mid_state, scale_f, shift_f).astype(jnp.bfloat16)
    ff_inner = jnp.dot(norm_f, w_up, preferred_element_type=jnp.float32) + b_up
    ff_act, gelu_pull = jax.vjp(partial(jax.nn.gelu, approximate=True), ff_inner)
    act_b = ff_act.astype(jnp.bfloat16)
    ff_out = jnp.dot(act_b, w_down, preferred_element_type=jnp.float32) + b_down
    out_state = mid_state + gate_f * ff_out
    d_out = out_grad[0].astype(jnp.float32) * loss_weight[:, None]
    d_ff = (gate_f * d_out).astype(jnp.bfloat16)
    d_gate_f = d_out * ff_out
    g_w_down = weight_grad(gather_left(act_b), d_ff)
    g_b_down = jnp.sum(d_ff.astype(jnp.float32), axis=0)
    (d_inner,) = gelu_pull(back_product(d_ff, w_down))
    d_inner_b = d_inner.astype(jnp.bfloat16)
    g_w_up = weight_grad(gather_left(norm_f), d_inner_b)
    g_b_up = jnp.sum(d_inner_b.astype(jnp.float32), axis=0)
    d_norm_f = back_product(d_inner_b, w_up)
    _, norm_f_pull = jax.vjp(modulate, mid_state, scale_f, shift_f)
    d_mid_norm, d_scale_f, d_shift_f = norm_f_pull(d_norm_f)
    d_mid = d_out + d_mid_norm
    d_branch = (gate_a * d_mid).astype(jnp.bfloat16)
    d_gate_a = d_mid * branch
    g_w_out = weight_grad(gather_left(attn_b), d_branch)
    g_b_out = jnp.sum(d_branch.astype(jnp.float32), axis=0)
    d_attn = back_product(d_branch, w_out)
    if by_heads:
        grad_heads = lax.all_to_all(
            jnp.transpose(
                d_attn.astype(jnp.bfloat16).reshape(local_rows, shards, 128), (1, 0, 2)
            ),
            "seq",
            0,
            0,
            tiled=True,
        ).reshape(local_rows * shards, 128)
        d_heads = attend_back(
            qkv_heads, seg_col, seg_row, exact, total, grad_heads, cos_all, sin_all
        )
        d_qkv = lax.all_to_all(
            d_heads.reshape(shards, local_rows, 384), "seq", 0, 0, tiled=True
        ).reshape(shards, local_rows, 3, 128)
        d_qkv = jnp.transpose(d_qkv, (1, 2, 0, 3)).reshape(local_rows, 3 * model_width)
    else:
        d_attn = d_attn.reshape(local_rows, HEADS, HEAD_DIM)
        grad_acc = (d_attn / totals_rows[:, :, None]).astype(jnp.bfloat16)
        delta = jnp.transpose(jnp.sum(d_attn * attended, axis=2) / totals_rows)
        bwd_piece = partial(
            backward_piece,
            queries=queries,
            query_segment=segment,
            utt_ends=utt_ends,
            grad_acc=grad_acc,
            delta=delta,
        )
        zero_query = jnp.zeros((local_rows, HEADS, HEAD_DIM), jnp.float32)
        zero_all = jnp.zeros((2, local_rows * shards, model_width), jnp.float32)

        def block_fn(inner_state, portion, block_start):
            d_query_sum, d_all = inner_state
            d_query_add, d_block = bwd_piece(portion, block_start, True)
            return (
                d_query_sum + d_query_add,
                lax.dynamic_update_slice_in_dim(d_all, d_block, block_start, 1),
            )

        d_query, d_all = over_blocks(
            block_fn,
            (zero_query, zero_all),
            lax.all_gather(key_value, "seq", axis=1, tiled=True),
            jnp.int32(0),
            local_rows,
        )
        d_key_value = lax.psum_scatter(d_all, "seq", scatter_dimension=1, tiled=True)
        d_query_pre = unrotate(d_query, angle_cos, angle_sin).reshape(local_rows, model_width)
        d_key_pre = unrotate(
            d_key_value[0].reshape(local_rows, HEADS, HEAD_DIM), angle_cos, angle_sin
        ).reshape(local_rows, model_width)
        d_qkv = jnp.concatenate([d_query_pre, d_key_pre, d_key_value[1]], axis=1).astype(jnp.bfloat16)
    g_w_qkv = weight_grad(gather_left(norm_a), d_qkv)
    g_b_qkv = jnp.sum(d_qkv.astype(jnp.float32), axis=0)
    d_norm_a = back_product(d_qkv, w_qkv)
    _, norm_a_pull = jax.vjp(modulate, residual, scale_a, shift_a)
    d_resid_norm, d_scale_a, d_shift_a = norm_a_pull(d_norm_a)
    d_resid = (d_mid + d_resid_norm).astype(jnp.bfloat16)
    g_w_skip = weight_grad(gather_left(joined), d_resid)
    g_b_skip = jnp.sum(d_resid.astype(jnp.float32), axis=0)
    d_joined = back_product(d_resid, w_skip)
    d_mod_f = jnp.concatenate(
        [d_shift_a, d_scale_a, d_gate_a, d_shift_f, d_scale_f, d_gate_f], axis=1
    )
    d_mod_u = jnp.dot(jnp.transpose(member_f), d_mod_f, precision=HIGHEST_PRECISION)
    small = jnp.concatenate(
        [g_b_skip, g_b_qkv, g_b_out, g_b_up, g_b_down, d_mod_u.reshape(-1)]
    )
    biases = small.shape[0] - d_mod_u.size
    small = xor_sum(small.reshape(-1, 128), "seq").reshape(-1)
    bias_sum = xor_sum(small[:biases].reshape(-1, 128), "utt").reshape(-1)
    d_mod_all = gather_ordered(small[biases:].reshape(d_mod_u.shape), 0)
    own_width = model_width // shards
    act_all = gather_ordered(time_act, 0).astype(jnp.float32)
    act_own = lax.dynamic_slice_in_dim(act_all, seq_place * own_width, own_width, 1)
    g_w_mod = jnp.dot(jnp.transpose(act_own), d_mod_all, precision=HIGHEST_PRECISION)
    mod_width = d_mod_all.shape[1] // shards
    g_b_mod = jnp.sum(
        lax.dynamic_slice_in_dim(d_mod_all, seq_place * mod_width, mod_width, 1), axis=0
    )
    own_biases, offset = [], 0
    for vector in (g_b_skip, g_b_qkv, g_b_out, g_b_up, g_b_down):
        width = vector.shape[0] // shards
        own_biases.append(
            lax.dynamic_slice_in_dim(bias_sum, offset + seq_place * width, width, 0)
        )
        offset += vector.shape[0]
    return (
        out_state.astype(jnp.bfloat16)[None],
        d_joined[:, :model_width].astype(jnp.bfloat16)[None],
        d_joined[:, model_width:].astype(jnp.bfloat16)[None],
        g_w_skip,
        own_biases[0],
        g_w_mod,
        g_b_mod,
        g_w_qkv,
        own_biases[1],
        g_w_out,
        own_biases[2],
        g_w_up,
        own_biases[3],
        g_w_down,
        own_biases[4],
    )


def solution(mesh):
    return jax.shard_map(
        local,
        mesh=mesh,
        in_specs=(
            P("utt", "seq", None),
            P("utt", "seq", None),
            P("utt", None),
            P("utt", None),
            P("utt", None),
            P("utt", "seq"),
            P("utt", "seq", None),
            P(),
            P(),
            P(),
            P(),
            P(),
            P(),
            P(),
            P(),
            P(),
            P(),
            P(),
            P(),
        ),
        out_specs=(
            P("utt", "seq", None),
            P("utt", "seq", None),
            P("utt", "seq", None),
            P("seq", None),
            P("seq"),
            P("seq", None),
            P("seq"),
            P("seq", None),
            P("seq"),
            P("seq", None),
            P("seq"),
            P("seq", None),
            P("seq"),
            P("seq", None),
            P("seq"),
        ),
        check_vma=False,
    )
```

```python
from functools import partial
import math

import jax
import jax.numpy as jnp
from jax import lax
from jax.experimental import pallas as pl
from jax.experimental.pallas import tpu as pltpu
from jax.sharding import PartitionSpec as P

HEADS = 16
HEAD_DIM = 64


HIGHEST_PRECISION = lax.Precision.HIGHEST
EPSILON = 1e-06


def layer_norm(values):
    average = jnp.mean(values, axis=-1, keepdims=True)
    centred = values - average
    spread = jnp.mean(centred * centred, axis=-1, keepdims=True)
    return centred * lax.rsqrt(spread + EPSILON)


def modulate(values, scale_part, shift_part):
    return layer_norm(values) * (1.0 + scale_part) + shift_part


def time_embed(flow_vals, model_width):
    half_dim = model_width // 2
    inverse = jnp.exp(-math.log(10000.0) * jnp.arange(half_dim, dtype=jnp.float32) / half_dim)
    angles = 1000.0 * flow_vals[:, None] * inverse[None, :]
    return jnp.concatenate([jnp.sin(angles), jnp.cos(angles)], axis=1)


def rotary_tables(position, head_size):
    half_dim = head_size // 2
    inverse = jnp.exp(
        -math.log(10000.0) * 2.0 * jnp.arange(half_dim, dtype=jnp.float32) / head_size
    )
    angles = position.astype(jnp.float32)[:, None] * inverse[None, :]
    return (jnp.cos(angles)[:, None, :], jnp.sin(angles)[:, None, :])


def rotate(tensor, angle_cos, angle_sin):
    half_dim = tensor.shape[-1] // 2
    leading = tensor[..., :half_dim]
    trailing = tensor[..., half_dim:]
    return jnp.concatenate(
        [leading * angle_cos - trailing * angle_sin, trailing * angle_cos + leading * angle_sin],
        axis=-1,
    )


def unrotate(gradient, angle_cos, angle_sin):
    half_dim = gradient.shape[-1] // 2
    leading = gradient[..., :half_dim]
    trailing = gradient[..., half_dim:]
    return jnp.concatenate(
        [leading * angle_cos + trailing * angle_sin, trailing * angle_cos - leading * angle_sin],
        axis=-1,
    )


def frame_tables(lengths, char_counts, first_frame, frame_count):
    utt_ends = jnp.cumsum(lengths)
    utt_starts = utt_ends - lengths
    frame_index = first_frame + jnp.arange(frame_count, dtype=jnp.int32)
    segment = jnp.sum((frame_index[:, None] >= utt_ends[None, :]).astype(jnp.int32), axis=1)
    member = segment[:, None] == jnp.arange(lengths.shape[0], dtype=jnp.int32)[None, :]
    position = frame_index - jnp.sum(jnp.where(member, utt_starts[None, :], 0), axis=1)
    prompt = jnp.sum(jnp.where(member, char_counts[None, :], 0), axis=1)
    return (segment, position, position >= prompt, member)


def key_segments(key_start, key_count, utt_ends):
    frame_index = key_start + jnp.arange(key_count, dtype=jnp.int32)
    return jnp.sum((frame_index[:, None] >= utt_ends[None, :]).astype(jnp.int32), axis=1)


def block_scores(queries, key_piece, query_segment, key_segment, usable):
    key_rows = key_piece.reshape(key_piece.shape[0], queries.shape[1], queries.shape[2])
    scores = (
        jnp.einsum("qhd,khd->hqk", queries, key_rows, preferred_element_type=jnp.float32) * 0.125
    )
    allowed = jnp.logical_and(query_segment[:, None] == key_segment[None, :], usable)
    return (jnp.where(allowed[None], jnp.exp(scores), 0.0), key_rows)


def over_blocks(block_fn, running, piece, key_start, shard_rows):
    key_count = piece.shape[1]
    shard_total = key_count // shard_rows
    group_size = max(1, min(shard_total, 1024 // shard_rows))
    while shard_total % group_size != 0:
        group_size = group_size - 1
    block_rows = group_size * shard_rows
    if block_rows == key_count:
        return block_fn(running, piece, key_start)

    def one_block(block_index, inner_state):
        portion = lax.dynamic_slice_in_dim(piece, block_index * block_rows, block_rows, 1)
        return block_fn(inner_state, portion, key_start + block_index * block_rows)

    return lax.fori_loop(0, key_count // block_rows, one_block, running)


def forward_piece(running, piece, key_start, usable, queries, query_segment, utt_ends):
    weighted, totals = running
    key_segment = key_segments(key_start, piece.shape[1], utt_ends)
    weights, key_rows = block_scores(queries, piece[0], query_segment, key_segment, usable)
    value_rows = piece[1].reshape(key_rows.shape)
    totals = totals + jnp.sum(weights, axis=2)
    weighted = weighted + jnp.einsum(
        "hqk,khd->qhd", weights.astype(jnp.bfloat16), value_rows, preferred_element_type=jnp.float32
    )
    return (weighted, totals)


def backward_piece(piece, key_start, usable, queries, query_segment, utt_ends, grad_acc, delta):
    key_count = piece.shape[1]
    key_segment = key_segments(key_start, key_count, utt_ends)
    weights, key_rows = block_scores(queries, piece[0], query_segment, key_segment, usable)
    value_rows = piece[1].reshape(key_rows.shape)
    value_dots = jnp.einsum(
        "qhd,khd->hqk", grad_acc, value_rows, preferred_element_type=jnp.float32
    )
    d_scores = (weights * (value_dots - delta[:, :, None])).astype(jnp.bfloat16)
    d_query = (
        jnp.einsum("hqk,khd->qhd", d_scores, key_rows, preferred_element_type=jnp.float32) * 0.125
    )
    d_key = (
        jnp.einsum("hqk,qhd->khd", d_scores, queries, preferred_element_type=jnp.float32) * 0.125
    )
    d_value = jnp.einsum(
        "hqk,qhd->khd", weights.astype(jnp.bfloat16), grad_acc, preferred_element_type=jnp.float32
    )
    return (
        d_query,
        jnp.stack([d_key.reshape(key_count, -1), d_value.reshape(key_count, -1)], axis=0),
    )


def back_product(gradient_rows, matrix):
    return jnp.einsum("fo,io->fi", gradient_rows, matrix, preferred_element_type=jnp.float32)


def xor_permute(value, axis_name, bit):
    size = lax.axis_size(axis_name)
    return lax.ppermute(value, axis_name, [(i, i ^ bit) for i in range(size)])


def bits_of(axis_name):
    size, bits, bit = lax.axis_size(axis_name), [], 1
    while bit < size:
        bits.append(bit)
        bit *= 2
    return bits


def xor_sum(value, axis_name):
    for bit in bits_of(axis_name):
        value = value + xor_permute(value, axis_name, bit)
    return value


def gather_left(rows):
    for bit in reversed(bits_of("utt")):
        rows = jnp.concatenate([rows, xor_permute(rows, "utt", bit)], axis=0)
    return rows


def gather_right(rows):
    place = lax.axis_index("utt")
    for bit in reversed(bits_of("utt")):
        mine = (place & bit) // bit
        width = rows.shape[1] // 2
        kept = lax.dynamic_slice_in_dim(rows, mine * width, width, 1)
        given = lax.dynamic_slice_in_dim(rows, (1 - mine) * width, width, 1)
        rows = jnp.concatenate([kept, xor_permute(given, "utt", bit)], axis=0)
    return rows


def gather_ordered(value, axis):
    place = lax.axis_index("utt")
    for bit in bits_of("utt"):
        other = xor_permute(value, "utt", bit)
        low = (place & bit) == 0
        value = jnp.concatenate(
            [jnp.where(low, value, other), jnp.where(low, other, value)], axis=axis
        )
    return value


def scatter_rows(tile):
    place = lax.axis_index("seq")
    for bit in bits_of("seq"):
        mine = (place & bit) // bit
        rest = lax.axis_size("seq") // (2 * bit)
        pieces = tile.reshape(rest, 2, -1, tile.shape[-1])
        kept = lax.dynamic_index_in_dim(pieces, mine, 1, keepdims=False)
        given = lax.dynamic_index_in_dim(pieces, 1 - mine, 1, keepdims=False)
        given = xor_permute(given, "seq", bit)
        tile = (kept.astype(jnp.float32) + given.astype(jnp.float32)).astype(jnp.bfloat16)
    return tile.reshape(-1, tile.shape[-1])


def weight_grad(left_all, right_rows):
    right_all = gather_right(right_rows)
    tile = jnp.einsum(
        "fi,fo->io", left_all, right_all, preferred_element_type=jnp.float32
    ).astype(jnp.bfloat16)
    tile = tile.reshape(-1, tile.shape[-1])
    piece = scatter_rows(tile)
    return gather_ordered(piece, 1).astype(jnp.float32)


def swap_halves(values, lower):
    return jnp.where(lower, pltpu.roll(values, 96, 1), pltpu.roll(values, 32, 1))


def lower_half(shape):
    return lax.broadcasted_iota(jnp.int32, shape, 1) % HEAD_DIM < HEAD_DIM // 2


def rotate_pack_kernel(q_ref, k_ref, v_ref, cos_ref, sin_ref, out_ref):
    lower = lower_half(q_ref.shape)
    cos, sin = cos_ref[...], sin_ref[...]
    q, k = q_ref[...], k_ref[...]
    out_ref[0, :, 0:128] = (q * cos + swap_halves(q, lower) * sin).astype(jnp.bfloat16)
    out_ref[0, :, 128:256] = (k * cos + swap_halves(k, lower) * sin).astype(jnp.bfloat16)
    out_ref[0, :, 256:384] = v_ref[...].astype(jnp.bfloat16)


def rotate_pack(qkv_full, cos, sin):
    rows = qkv_full.shape[0]
    blocks = qkv_full.shape[1] // 384
    table = pl.BlockSpec((rows, 128), lambda i: (0, 0))
    return pl.pallas_call(
        rotate_pack_kernel,
        grid=(blocks,),
        in_specs=[
            pl.BlockSpec((rows, 128), lambda i: (0, i)),
            pl.BlockSpec((rows, 128), lambda i: (0, blocks + i)),
            pl.BlockSpec((rows, 128), lambda i: (0, 2 * blocks + i)),
            table,
            table,
        ],
        out_specs=pl.BlockSpec((1, rows, 384), lambda i: (i, 0, 0)),
        out_shape=jax.ShapeDtypeStruct((blocks, rows, 384), jnp.bfloat16),
    )(qkv_full, qkv_full, qkv_full, cos, sin)


def head_scores(q, k, seg_q, seg_k):
    scores = lax.dot_general(q, k, (((1,), (1,)), ((), ())), preferred_element_type=jnp.float32)
    return jnp.where(seg_q == seg_k, jnp.exp(scores * 0.125), 0.0)


MESH = pl.DeviceIdType.MESH
VMEM_LIMIT = 60 * 1024 * 1024


def flip(index, bit):
    return index + bit - 2 * bit * ((index // bit) % 2)


def everywhere(memory):
    return pl.BlockSpec(memory_space=memory)


class Links:
    def __init__(self, send_sems, recv_sems, local_sems):
        self.send_sems, self.recv_sems, self.local_sems = send_sems, recv_sems, local_sems
        self.sent, self.held = [], 0
        self.utt, self.seq = lax.axis_index("utt"), lax.axis_index("seq")

    def enter(self, utt_peers, seq_peers):
        barrier = pltpu.get_barrier_semaphore()
        targets = [self.mate(r) for r in utt_peers] + [self.peer(r) for r in seq_peers]
        for target in targets:
            pl.semaphore_signal(barrier, inc=1, device_id=target, device_id_type=MESH)
        pl.semaphore_wait(barrier, len(targets))

    def mate(self, offset):
        return (self.utt_of(offset), self.seq)

    def utt_of(self, offset):
        place = self.utt
        for bit in (1, 2):
            if offset & bit:
                place = flip(place, bit)
        return place

    def seq_of(self, offset):
        place = self.seq
        for bit in (1, 2, 4):
            if offset & bit:
                place = flip(place, bit)
        return place

    def peer(self, offset):
        return (self.utt, self.seq_of(offset))

    def send(self, source, target, device):
        index = len(self.sent)
        copy = pltpu.make_async_remote_copy(
            src_ref=source,
            dst_ref=target,
            send_sem=self.send_sems.at[index],
            recv_sem=self.recv_sems.at[index],
            device_id=device,
            device_id_type=MESH,
        )
        copy.start()
        self.sent.append(copy)
        return copy

    def keep(self, source, target):
        copy = pltpu.make_async_copy(source, target, self.local_sems.at[self.held])
        self.held += 1
        copy.start()
        return copy

    def leave(self):
        for copy in self.sent:
            copy.wait_send()


class Gathered:
    def __init__(self, links, source, target, columns=None):
        self.links, self.target = links, target
        self.rows = source.shape[0]
        self.columns = columns
        self.own = links.keep(source, self.slot(0))
        self.across = links.send(source, self.slot(2), links.mate(2))
        self.beside = links.send(source, self.slot(1), links.mate(1))

    def slot(self, offset):
        rows = pl.ds(offset * self.rows, self.rows)
        if self.columns is None:
            return self.target.at[rows, :]
        return self.target.at[rows, self.columns]

    def relay(self):
        self.across.wait_recv()
        self.relayed = self.links.send(self.slot(2), self.slot(3), self.links.mate(1))

    def wait(self):
        self.own.wait()
        self.beside.wait_recv()
        self.relayed.wait_recv()


class Quarter:
    def __init__(self, links, piece_of, target):
        rows = target.shape[0] // 4
        slot = lambda r: target.at[pl.ds(r * rows, rows), :]
        self.own = links.keep(piece_of(links.utt), slot(0))
        self.copies = [
            links.send(piece_of(links.utt_of(r)), slot(r), links.mate(r)) for r in (2, 3, 1)
        ]

    def wait(self):
        self.own.wait()
        for copy in self.copies:
            copy.wait_recv()


class Share:
    def __init__(self, links, left, right, columns, tile, got_y, got_z1, got_z2, result):
        self.links = links
        self.left, self.right, self.columns = left, right, columns
        self.tile, self.got_y, self.got_z1, self.got_z2 = tile, got_y, got_z1, got_z2
        self.result = result
        seq = links.seq
        self.y, self.zl, self.zh = seq % 2, (seq // 2) % 2, seq // 4

    def product(self, y):
        rows = self.tile.shape[3]

        def block(z, _):
            base = pl.multiple_of((2 * z + y) * rows, rows)
            self.tile[z // 2, z % 2, y] = lax.dot_general(
                self.left[:, pl.ds(base, rows)],
                self.right[:, self.columns],
                (((0,), (0,)), ((), ())),
                preferred_element_type=jnp.float32,
            ).astype(jnp.bfloat16)
            return 0

        lax.fori_loop(0, 4, block, 0)

    def start(self):
        self.product(1 - self.y)
        self.sent_y = self.links.send(
            self.tile.at[:, :, 1 - self.y], self.got_y, self.links.peer(1)
        )
        self.product(self.y)

    def add(self, index, got):
        tile = self.tile
        tile[index] = (tile[index].astype(jnp.float32) + got.astype(jnp.float32)).astype(
            jnp.bfloat16
        )

    def after_y(self):
        self.sent_y.wait_recv()

        def block(zh, _):
            self.add((zh, 1 - self.zl, self.y), self.got_y[zh, 1 - self.zl])
            return 0

        lax.fori_loop(0, 2, block, 0)
        self.sent_z1 = self.links.send(
            self.tile.at[:, 1 - self.zl, self.y], self.got_z1, self.links.peer(2)
        )

        def rest(zh, _):
            self.add((zh, self.zl, self.y), self.got_y[zh, self.zl])
            return 0

        lax.fori_loop(0, 2, rest, 0)

    def after_z1(self):
        self.sent_z1.wait_recv()
        self.add((1 - self.zh, self.zl, self.y), self.got_z1[1 - self.zh])
        self.sent_z2 = self.links.send(
            self.tile.at[1 - self.zh, self.zl, self.y], self.got_z2, self.links.peer(4)
        )
        self.add((self.zh, self.zl, self.y), self.got_z1[self.zh])

    def after_z2(self):
        self.sent_z2.wait_recv()
        links = self.links
        mine = self.result(links.utt)
        mine[...] = (
            self.tile[self.zh, self.zl, self.y].astype(jnp.float32)
            + self.got_z2[...].astype(jnp.float32)
        ).astype(jnp.bfloat16)
        self.across = links.send(mine, mine, links.mate(2))
        self.beside = links.send(mine, mine, links.mate(1))

    def relay(self):
        self.across.wait_recv()
        links = self.links
        theirs = self.result(links.utt_of(2))
        self.relayed = links.send(theirs, theirs, links.mate(1))

    def wait(self):
        self.beside.wait_recv()
        self.relayed.wait_recv()


def share_scratch(rows, columns):
    return [
        pltpu.VMEM((2, 2, 2, rows, columns), jnp.bfloat16),
        pltpu.VMEM((2, 2, rows, columns), jnp.bfloat16),
        pltpu.VMEM((2, rows, columns), jnp.bfloat16),
        pltpu.VMEM((rows, columns), jnp.bfloat16),
    ]


def run_shares(shares):
    stages = ("after_y", "after_z1", "after_z2", "relay", "wait")
    for turn in range(len(shares) + len(stages) - 1):
        for place, stage in enumerate(stages):
            if 0 <= turn - place < len(shares):
                getattr(shares[turn - place], stage)()


def semaphores(count):
    return [pltpu.SemaphoreType.DMA((count,))] * 2 + [pltpu.SemaphoreType.DMA((16,))]


def comm_params(collective_id):
    return pltpu.CompilerParams(
        collective_id=collective_id, has_side_effects=True, vmem_limit_bytes=VMEM_LIMIT
    )


def attend_kernel(
    packed_ref, segq_ref, segk_ref, counts_ref, flow_ref, norm_ref, frames_ref, skip_ref,
    attn_ref, heads_ref, exact_ref, total_ref, sums_ref, flows_ref, norm_all, joined_all,
    attn_heads, counts_got, send_sems, recv_sems, local_sems,
):
    links = Links(send_sems, recv_sems, local_sems)
    links.enter((1, 2, 3), range(1, 8))
    rows = packed_ref.shape[1]
    width = frames_ref.shape[1]
    own_rows = pl.ds(pl.multiple_of(links.seq * rows, rows), rows)
    own = links.keep(packed_ref.at[links.seq], heads_ref.at[own_rows, :])
    incoming = [
        links.send(packed_ref.at[links.seq_of(r)], heads_ref.at[own_rows, :], links.peer(r))
        for r in (6, 7, 4, 5, 2, 3, 1)
    ]
    flows_ref[links.utt] = flow_ref[...]
    flow_copies = [
        links.send(flow_ref, flows_ref.at[links.utt], links.mate(r)) for r in (1, 2, 3)
    ]
    gathers = [
        Gathered(links, norm_ref, norm_all),
        Gathered(links, frames_ref, joined_all, pl.ds(0, width)),
        Gathered(links, skip_ref, joined_all, pl.ds(width, width)),
    ]
    sums_ref[...] = counts_ref[...]
    for place, (target, source) in enumerate(
        ((links.mate(1), 0), (links.mate(2), 1), (links.peer(1), 2), (links.peer(2), 3),
         (links.peer(4), 4))
    ):
        counts_got[5 + place] = sums_ref[...]
        copy = links.send(counts_got.at[5 + place], counts_got.at[source], target)
        copy.wait_recv()
        sums_ref[...] = sums_ref[...] + counts_got[source]
    gathers[0].relay()
    own.wait()
    for copy in incoming:
        copy.wait_recv()
    first = lax.broadcasted_iota(jnp.int32, (256, 128), 1) < HEAD_DIM
    zero = jnp.zeros((256, 128), jnp.bfloat16)
    k, v = heads_ref[:, 128:256], heads_ref[:, 256:384]
    seg_k = segk_ref[...]

    def block(step, _):
        here = pl.ds(pl.multiple_of(step * 256, 256), 256)
        q, seg_q = heads_ref[here, 0:128], segq_ref[here, :]
        results = []
        for mine in (first, jnp.logical_not(first)):
            weights = head_scores(jnp.where(mine, q, zero), k, seg_q, seg_k)
            total = jnp.sum(weights, axis=1, keepdims=True)
            summed = jnp.dot(weights.astype(jnp.bfloat16), v, preferred_element_type=jnp.float32)
            results.append((summed, total))
        total = jnp.where(first, results[0][1], results[1][1])
        attended = jnp.where(first, results[0][0], results[1][0]) / total
        attn_heads[here, :] = attended.astype(jnp.bfloat16)
        exact_ref[here, :] = attended
        total_ref[here, :] = total
        return 0

    lax.fori_loop(0, heads_ref.shape[0] // 256, block, 0)
    column = attn_ref.at[:, pl.ds(pl.multiple_of(links.seq * 128, 128), 128)]
    part = lambda place: attn_heads.at[pl.ds(pl.multiple_of(place * rows, rows), rows), :]
    own = links.keep(part(links.seq), column)
    incoming = [
        links.send(part(links.seq_of(r)), column, links.peer(r)) for r in (6, 7, 4, 5, 2, 3, 1)
    ]
    for gather in gathers[1:]:
        gather.relay()
    for copy in flow_copies:
        copy.wait_recv()
    own.wait()
    for copy in incoming:
        copy.wait_recv()
    for gather in gathers:
        gather.wait()
    links.leave()


def attend(packed, seg_col, seg_row, counts, flow, norm_a, frames, skip):
    shards, rows, _ = packed.shape
    total_rows, width = shards * rows, norm_a.shape[1]
    vmem, there = everywhere(pltpu.VMEM), everywhere(pl.ANY)
    shape = jax.ShapeDtypeStruct
    return pl.pallas_call(
        attend_kernel,
        in_specs=[there, vmem, vmem, vmem, vmem, there, there, there],
        out_specs=[vmem] * 8,
        out_shape=[
            shape((rows, width), jnp.bfloat16),
            shape((total_rows, 384), jnp.bfloat16),
            shape((total_rows, 128), jnp.float32),
            shape((total_rows, 128), jnp.float32),
            shape(counts.shape, jnp.float32),
            shape((4,) + flow.shape, jnp.float32),
            shape((4 * rows, width), jnp.bfloat16),
            shape((4 * rows, 2 * width), jnp.bfloat16),
        ],
        scratch_shapes=[
            pltpu.VMEM((total_rows, 128), jnp.bfloat16),
            pltpu.VMEM((10,) + counts.shape, jnp.float32),
        ]
        + semaphores(40),
        compiler_params=comm_params(1),
    )(packed, seg_col, seg_row, counts, flow, norm_a, frames, skip)


def attend_back_kernel(
    d_attn_ref, heads_ref, segq_ref, segk_ref, exact_ref, total_ref, cos_ref, sin_ref,
    d_ff_ref, act_ref, norm_ref, d_inner_ref, attn_ref, d_branch_ref,
    d_qkv_ref, g_down, g_up, g_out,
    grad_heads, d_heads, dk_ref, dv_ref,
    d_ff_all, act_all, norm_all, d_inner_all, attn_all, d_branch_all,
    *rest,
):
    tiles, (send_sems, recv_sems, local_sems) = rest[:-3], rest[-3:]
    links = Links(send_sems, recv_sems, local_sems)
    links.enter((1, 2, 3), range(1, 8))
    rows = d_attn_ref.shape[0]
    far_first = (6, 7, 4, 5, 2, 3, 1)
    own_rows = pl.ds(pl.multiple_of(links.seq * rows, rows), rows)
    strip = lambda ref, place, size: ref.at[
        :, pl.ds(pl.multiple_of(place * size, size), size)
    ]
    own = links.keep(strip(d_attn_ref, links.seq, 128), grad_heads.at[own_rows, :])
    incoming = [
        links.send(
            strip(d_attn_ref, links.seq_of(r), 128), grad_heads.at[own_rows, :], links.peer(r)
        )
        for r in far_first
    ]
    gather_d = Gathered(links, d_ff_ref, d_ff_all)
    quarter_a = Quarter(links, lambda u: act_ref.at[u], act_all)
    gather_n = Gathered(links, norm_ref, norm_all)
    width = d_inner_all.shape[1]
    quarter_i = Quarter(links, lambda u: strip(d_inner_ref, u, width), d_inner_all)
    gather_b = Gathered(links, attn_ref, attn_all)
    narrow = d_branch_all.shape[1]
    quarter_b = Quarter(links, lambda u: strip(d_branch_ref, u, narrow), d_branch_all)
    own.wait()
    for copy in incoming:
        copy.wait_recv()
    dk_ref[...] = jnp.zeros_like(dk_ref)
    dv_ref[...] = jnp.zeros_like(dv_ref)
    first = lax.broadcasted_iota(jnp.int32, (256, 128), 1) < HEAD_DIM
    zero = jnp.zeros((256, 128), jnp.bfloat16)
    lower = lower_half((256, 128))
    k, v = heads_ref[:, 128:256], heads_ref[:, 256:384]
    seg_k = segk_ref[...]
    along = (((1,), (1,)), ((), ()))
    down = (((0,), (0,)), ((), ()))

    def turned(values, here):
        return (
            values * cos_ref[here, :] - swap_halves(values, lower) * sin_ref[here, :]
        ).astype(jnp.bfloat16)

    def block(step, _):
        here = pl.ds(pl.multiple_of(step * 256, 256), 256)
        q, seg_q = heads_ref[here, 0:128], segq_ref[here, :]
        scaled = grad_heads[here, :].astype(jnp.float32) / total_ref[here, :]
        grad_acc = scaled.astype(jnp.bfloat16)
        product = scaled * exact_ref[here, :]
        d_query = []
        for mine in (first, jnp.logical_not(first)):
            q_own = jnp.where(mine, q, zero)
            g_own = jnp.where(mine, grad_acc, zero)
            delta = jnp.sum(jnp.where(mine, product, 0.0), axis=1, keepdims=True)
            weights = head_scores(q_own, k, seg_q, seg_k)
            dots = lax.dot_general(g_own, v, along, preferred_element_type=jnp.float32)
            d_scores = (weights * (dots - delta)).astype(jnp.bfloat16)
            d_query.append(jnp.dot(d_scores, k, preferred_element_type=jnp.float32))
            dk_ref[...] += lax.dot_general(
                d_scores, q_own, down, preferred_element_type=jnp.float32
            )
            dv_ref[...] += lax.dot_general(
                weights.astype(jnp.bfloat16), g_own, down, preferred_element_type=jnp.float32
            )
        d_heads[here, 0:128] = turned(jnp.where(first, d_query[0], d_query[1]) * 0.125, here)
        return 0

    blocks = heads_ref.shape[0] // 256
    lax.fori_loop(0, blocks, block, 0)

    def finish(step, _):
        here = pl.ds(pl.multiple_of(step * 256, 256), 256)
        d_heads[here, 128:256] = turned(dk_ref[here, :] * 0.125, here)
        d_heads[here, 256:384] = dv_ref[here, :].astype(jnp.bfloat16)
        return 0

    lax.fori_loop(0, blocks, finish, 0)
    model = d_attn_ref.shape[1]
    part = lambda place, c: d_heads.at[
        pl.ds(pl.multiple_of(place * rows, rows), rows), pl.ds(c * 128, 128)
    ]
    home = lambda c: d_qkv_ref.at[
        :, pl.ds(pl.multiple_of(c * model + links.seq * 128, 128), 128)
    ]
    owns = [links.keep(part(links.seq, c), home(c)) for c in range(3)]
    incoming = [
        links.send(part(links.seq_of(r), c), home(c), links.peer(r))
        for r in far_first
        for c in range(3)
    ]
    half = width // 2
    shares = []
    for index, (left, right, columns, result) in enumerate(
        (
            (act_all, d_ff_all, 0, lambda u: g_down.at[
                pl.ds(pl.multiple_of(u * 128, 128), 128), pl.ds(0, half)]),
            (act_all, d_ff_all, 1, lambda u: g_down.at[
                pl.ds(pl.multiple_of(u * 128, 128), 128), pl.ds(half, half)]),
            (norm_all, d_inner_all, 0, lambda u: g_up.at[
                :, pl.ds(pl.multiple_of(u * width, width), half)]),
            (norm_all, d_inner_all, 1, lambda u: g_up.at[
                :, pl.ds(pl.multiple_of(u * width + half, half), half)]),
        )
    ):
        shares.append(
            Share(links, left, right, pl.ds(columns * half, half),
                  *tiles[4 * index : 4 * index + 4], result)
        )
    shares.append(
        Share(links, attn_all, d_branch_all, pl.ds(0, narrow), *tiles[16:20],
              lambda u: g_out.at[:, pl.ds(pl.multiple_of(u * narrow, narrow), narrow)])
    )
    gather_d.relay()
    gather_n.relay()
    gather_d.wait()
    quarter_a.wait()
    shares[0].start()
    shares[1].start()
    gather_b.relay()
    gather_n.wait()
    quarter_i.wait()
    shares[2].start()
    shares[3].start()
    gather_b.wait()
    quarter_b.wait()
    shares[4].start()
    run_shares(shares)
    for copy in owns:
        copy.wait()
    for copy in incoming:
        copy.wait_recv()
    links.leave()


def attend_back(
    d_attn, heads, seg_col, seg_row, exact, total, cos, sin,
    d_ff, act_quarters, norm_f, d_inner, attn_b, d_branch,
):
    rows, model = d_attn.shape
    frames = heads.shape[0]
    inner = d_inner.shape[1]
    vmem, there = everywhere(pltpu.VMEM), everywhere(pl.ANY)
    shape = jax.ShapeDtypeStruct
    bf16 = lambda *dims: pltpu.VMEM(dims, jnp.bfloat16)
    half = inner // 8
    return pl.pallas_call(
        attend_back_kernel,
        in_specs=[there] + [vmem] * 7 + [there] * 6,
        out_specs=[vmem] * 4,
        out_shape=[
            shape((rows, 3 * model), jnp.bfloat16),
            shape((inner // 8, model), jnp.bfloat16),
            shape((model // 8, inner), jnp.bfloat16),
            shape((model // 8, model), jnp.bfloat16),
        ],
        scratch_shapes=[
            bf16(frames, 128),
            bf16(frames, 384),
            pltpu.VMEM((frames, 128), jnp.float32),
            pltpu.VMEM((frames, 128), jnp.float32),
            bf16(4 * rows, model),
            bf16(4 * rows, inner // 4),
            bf16(4 * rows, model),
            bf16(4 * rows, inner // 4),
            bf16(4 * rows, model),
            bf16(4 * rows, model // 4),
        ]
        + share_scratch(128, half) * 4
        + share_scratch(model // 8, model // 4)
        + semaphores(80),
        compiler_params=comm_params(2),
    )(
        d_attn, heads, seg_col, seg_row, exact, total, cos, sin,
        d_ff, act_quarters, norm_f, d_inner, attn_b, d_branch,
    )


def last_kernel(
    norm_all, joined_all, d_qkv_ref, d_resid_ref, small_ref,
    g_qkv, g_skip, smalls,
    d_qkv_all, d_resid_all, small_got, small_sum, *rest,
):
    tiles, (send_sems, recv_sems, local_sems) = rest[:-3], rest[-3:]
    links = Links(send_sems, recv_sems, local_sems)
    links.enter((1, 2, 3), (1, 2, 4))
    strip = lambda ref, place, size: ref.at[
        :, pl.ds(pl.multiple_of(place * size, size), size)
    ]
    wide, narrow = d_qkv_all.shape[1], d_resid_all.shape[1]
    quarter_q = Quarter(links, lambda u: strip(d_qkv_ref, u, wide), d_qkv_all)
    quarter_r = Quarter(links, lambda u: strip(d_resid_ref, u, narrow), d_resid_all)
    exchange = [links.send(small_ref, small_got.at[0], links.peer(1))]
    half = wide // 2
    shares = [
        Share(links, norm_all, d_qkv_all, pl.ds(0, half), *tiles[0:4],
              lambda u: g_qkv.at[:, pl.ds(pl.multiple_of(u * wide, 128), half)]),
        Share(links, norm_all, d_qkv_all, pl.ds(half, half), *tiles[4:8],
              lambda u: g_qkv.at[:, pl.ds(pl.multiple_of(u * wide + half, 128), half)]),
        Share(links, joined_all, d_resid_all, pl.ds(0, narrow), *tiles[8:12],
              lambda u: g_skip.at[:, pl.ds(pl.multiple_of(u * narrow, narrow), narrow)]),
    ]
    quarter_q.wait()
    shares[0].start()
    shares[1].start()
    quarter_r.wait()
    shares[2].start()
    exchange[0].wait_recv()
    small_sum[0] = small_ref[...] + small_got[0]
    exchange.append(links.send(small_sum.at[0], small_got.at[1], links.peer(2)))
    shares[0].after_y()
    exchange[1].wait_recv()
    small_sum[1] = small_sum[0] + small_got[1]
    exchange.append(links.send(small_sum.at[1], small_got.at[2], links.peer(4)))
    shares[1].after_y()
    shares[0].after_z1()
    exchange[2].wait_recv()
    mine = smalls.at[links.utt]
    mine[...] = small_sum[1] + small_got[2]
    spread = [links.send(mine, mine, links.mate(r)) for r in (2, 3, 1)]
    shares[2].after_y()
    shares[1].after_z1()
    shares[0].after_z2()
    shares[2].after_z1()
    shares[1].after_z2()
    shares[0].relay()
    shares[2].after_z2()
    shares[1].relay()
    shares[0].wait()
    shares[2].relay()
    shares[1].wait()
    shares[2].wait()
    for copy in spread:
        copy.wait_recv()
    links.leave()


def last(norm_all, joined_all, d_qkv, d_resid, small):
    rows, model = d_resid.shape
    vmem, there = everywhere(pltpu.VMEM), everywhere(pl.ANY)
    shape = jax.ShapeDtypeStruct
    bf16 = lambda *dims: pltpu.VMEM(dims, jnp.bfloat16)
    wide = d_qkv.shape[1] // 4
    return pl.pallas_call(
        last_kernel,
        in_specs=[vmem, vmem, there, there, vmem],
        out_specs=[vmem] * 3,
        out_shape=[
            shape((model // 8, 4 * wide), jnp.bfloat16),
            shape((model // 4, model), jnp.bfloat16),
            shape((4,) + small.shape, jnp.float32),
        ],
        scratch_shapes=[
            bf16(4 * rows, wide),
            bf16(4 * rows, model // 4),
            pltpu.VMEM((3,) + small.shape, jnp.float32),
            pltpu.VMEM((2,) + small.shape, jnp.float32),
        ]
        + share_scratch(model // 8, wide // 2) * 2
        + share_scratch(model // 4, model // 4)
        + semaphores(48),
        compiler_params=comm_params(3),
    )(norm_all, joined_all, d_qkv, d_resid, small)


def wide_tables(position):
    half_dim = HEAD_DIM // 2
    lane = jnp.arange(128, dtype=jnp.int32) % HEAD_DIM
    inverse = jnp.exp(
        -math.log(10000.0) * 2.0 * (lane % half_dim).astype(jnp.float32) / HEAD_DIM
    )
    angles = position.astype(jnp.float32)[:, None] * inverse[None, :]
    sign = jnp.where(lane < half_dim, -1.0, 1.0)
    return jnp.cos(angles), jnp.sin(angles) * sign[None, :]


def local(
    frames_in,
    skip_in,
    flow_times,
    frame_lengths,
    char_lengths,
    drop_mask,
    out_grad,
    w_skip,
    b_skip,
    w_mod,
    b_mod,
    w_qkv,
    b_qkv,
    w_out,
    b_out,
    w_up,
    b_up,
    w_down,
    b_down,
):
    local_rows = frames_in.shape[1]
    model_width = frames_in.shape[2]
    shards = lax.axis_size("seq")
    seq_place = lax.axis_index("seq")
    lengths = frame_lengths[0]
    utt_ends = jnp.cumsum(lengths)
    segment, position, in_loss, member = frame_tables(
        lengths, char_lengths[0], seq_place * local_rows, local_rows
    )
    member_f = member.astype(jnp.float32)
    loss_mask = in_loss.astype(jnp.float32)
    dropped = drop_mask[0].astype(jnp.float32)
    counts = jnp.stack([jnp.sum(loss_mask * dropped), jnp.sum(loss_mask * (1.0 - dropped))])
    counts = jnp.pad(counts[None, :], ((0, 7), (0, 126)))
    whole = model_width * 4
    fused = (
        lax.axis_size("utt") == 4
        and shards == 8
        and HEADS * HEAD_DIM == 1024
        and w_up.shape[1] == whole
        and local_rows == 128
    )
    if not fused:
        counts = xor_sum(xor_sum(counts, "utt"), "seq")
    time_act = jax.nn.silu(time_embed(flow_times[0], model_width)).astype(jnp.bfloat16)
    mod_u = jnp.dot(time_act, w_mod, preferred_element_type=jnp.float32) + b_mod
    mod_f = jnp.dot(member_f, mod_u, precision=HIGHEST_PRECISION)
    shift_a, scale_a, gate_a, shift_f, scale_f, gate_f = jnp.split(mod_f, 6, axis=1)
    joined = jnp.concatenate([frames_in[0], skip_in[0]], axis=1)
    residual = jnp.dot(joined, w_skip, preferred_element_type=jnp.float32) + b_skip
    norm_a = modulate(residual, scale_a, shift_a).astype(jnp.bfloat16)
    qkv_full = jnp.dot(norm_a, w_qkv, preferred_element_type=jnp.float32) + b_qkv
    if fused:
        all_segment, all_position, _, _ = frame_tables(
            lengths, char_lengths[0], 0, local_rows * shards
        )
        cos_all, sin_all = wide_tables(all_position)
        cos_own, sin_own = wide_tables(position)
        seg_col, seg_row = all_segment[:, None], all_segment[None, :]
        flow = jnp.pad(flow_times, ((0, 7), (0, 128 - flow_times.shape[1])))
        attn_b, qkv_heads, exact, total, counts, flows, norm_all, joined_all = attend(
            rotate_pack(qkv_full, cos_own, sin_own),
            seg_col,
            seg_row,
            counts,
            flow,
            norm_a,
            frames_in[0],
            skip_in[0],
        )
    else:
        angle_cos, angle_sin = rotary_tables(position, HEAD_DIM)
        queries = rotate(
            qkv_full[:, :model_width].reshape(local_rows, HEADS, HEAD_DIM), angle_cos, angle_sin
        ).astype(jnp.bfloat16)
        key_rot = rotate(
            qkv_full[:, model_width : 2 * model_width].reshape(local_rows, HEADS, HEAD_DIM),
            angle_cos,
            angle_sin,
        ).astype(jnp.bfloat16)
        key_value = jnp.stack(
            [
                key_rot.reshape(local_rows, model_width),
                qkv_full[:, 2 * model_width :].astype(jnp.bfloat16),
            ],
            axis=0,
        )
        start_state = (
            jnp.zeros((local_rows, HEADS, HEAD_DIM), jnp.float32),
            jnp.zeros((HEADS, local_rows), jnp.float32),
        )
        fwd_piece = partial(forward_piece, queries=queries, query_segment=segment, utt_ends=utt_ends)
        weighted, totals = over_blocks(
            partial(fwd_piece, usable=True),
            start_state,
            lax.all_gather(key_value, "seq", axis=1, tiled=True),
            jnp.int32(0),
            local_rows,
        )
        totals_rows = jnp.transpose(totals)
        attended = weighted / totals_rows[:, :, None]
        attn_b = attended.reshape(local_rows, model_width).astype(jnp.bfloat16)
    n_drop, n_keep = counts[0, 0], counts[0, 1]
    loss_weight = (
        loss_mask
        * (n_drop + n_keep)
        * 0.5
        * (dropped / (n_drop + 1.0) + (1.0 - dropped) / (n_keep + 1.0))
    )
    branch = jnp.dot(attn_b, w_out, preferred_element_type=jnp.float32) + b_out
    mid_state = residual + gate_a * branch
    norm_f = modulate(mid_state, scale_f, shift_f).astype(jnp.bfloat16)
    ff_inner = jnp.dot(norm_f, w_up, preferred_element_type=jnp.float32) + b_up
    ff_act, gelu_pull = jax.vjp(partial(jax.nn.gelu, approximate=True), ff_inner)
    act_b = ff_act.astype(jnp.bfloat16)
    ff_out = jnp.dot(act_b, w_down, preferred_element_type=jnp.float32) + b_down
    out_state = mid_state + gate_f * ff_out
    d_out = out_grad[0].astype(jnp.float32) * loss_weight[:, None]
    d_ff = (gate_f * d_out).astype(jnp.bfloat16)
    d_gate_f = d_out * ff_out
    g_b_down = jnp.sum(d_ff.astype(jnp.float32), axis=0)
    (d_inner,) = gelu_pull(back_product(d_ff, w_down))
    d_inner_b = d_inner.astype(jnp.bfloat16)
    g_b_up = jnp.sum(d_inner_b.astype(jnp.float32), axis=0)
    d_norm_f = back_product(d_inner_b, w_up)
    _, norm_f_pull = jax.vjp(modulate, mid_state, scale_f, shift_f)
    d_mid_norm, d_scale_f, d_shift_f = norm_f_pull(d_norm_f)
    d_mid = d_out + d_mid_norm
    d_branch = (gate_a * d_mid).astype(jnp.bfloat16)
    d_gate_a = d_mid * branch
    g_b_out = jnp.sum(d_branch.astype(jnp.float32), axis=0)
    d_attn = back_product(d_branch, w_out)
    if fused:
        act_quarters = jnp.transpose(act_b.reshape(local_rows, shards, 4, -1), (2, 0, 1, 3))
        d_qkv, g_w_down, g_w_up, g_w_out = attend_back(
            d_attn.astype(jnp.bfloat16),
            qkv_heads,
            seg_col,
            seg_row,
            exact,
            total,
            cos_all,
            sin_all,
            d_ff,
            act_quarters.reshape(4, local_rows, -1),
            norm_f,
            d_inner_b,
            attn_b,
            d_branch,
        )
    else:
        g_w_down = weight_grad(gather_left(act_b), d_ff)
        g_w_up = weight_grad(gather_left(norm_f), d_inner_b)
        g_w_out = weight_grad(gather_left(attn_b), d_branch)
        d_attn = d_attn.reshape(local_rows, HEADS, HEAD_DIM)
        grad_acc = (d_attn / totals_rows[:, :, None]).astype(jnp.bfloat16)
        delta = jnp.transpose(jnp.sum(d_attn * attended, axis=2) / totals_rows)
        bwd_piece = partial(
            backward_piece,
            queries=queries,
            query_segment=segment,
            utt_ends=utt_ends,
            grad_acc=grad_acc,
            delta=delta,
        )
        zero_query = jnp.zeros((local_rows, HEADS, HEAD_DIM), jnp.float32)
        zero_all = jnp.zeros((2, local_rows * shards, model_width), jnp.float32)

        def block_fn(inner_state, portion, block_start):
            d_query_sum, d_all = inner_state
            d_query_add, d_block = bwd_piece(portion, block_start, True)
            return (
                d_query_sum + d_query_add,
                lax.dynamic_update_slice_in_dim(d_all, d_block, block_start, 1),
            )

        d_query, d_all = over_blocks(
            block_fn,
            (zero_query, zero_all),
            lax.all_gather(key_value, "seq", axis=1, tiled=True),
            jnp.int32(0),
            local_rows,
        )
        d_key_value = lax.psum_scatter(d_all, "seq", scatter_dimension=1, tiled=True)
        d_query_pre = unrotate(d_query, angle_cos, angle_sin).reshape(local_rows, model_width)
        d_key_pre = unrotate(
            d_key_value[0].reshape(local_rows, HEADS, HEAD_DIM), angle_cos, angle_sin
        ).reshape(local_rows, model_width)
        d_qkv = jnp.concatenate([d_query_pre, d_key_pre, d_key_value[1]], axis=1).astype(jnp.bfloat16)
    g_b_qkv = jnp.sum(d_qkv.astype(jnp.float32), axis=0)
    d_norm_a = back_product(d_qkv, w_qkv)
    _, norm_a_pull = jax.vjp(modulate, residual, scale_a, shift_a)
    d_resid_norm, d_scale_a, d_shift_a = norm_a_pull(d_norm_a)
    d_resid = (d_mid + d_resid_norm).astype(jnp.bfloat16)
    g_b_skip = jnp.sum(d_resid.astype(jnp.float32), axis=0)
    d_joined = back_product(d_resid, w_skip)
    d_mod_f = jnp.concatenate(
        [d_shift_a, d_scale_a, d_gate_a, d_shift_f, d_scale_f, d_gate_f], axis=1
    )
    d_mod_u = jnp.dot(jnp.transpose(member_f), d_mod_f, precision=HIGHEST_PRECISION)
    small = jnp.concatenate(
        [g_b_skip, g_b_qkv, g_b_out, g_b_up, g_b_down, d_mod_u.reshape(-1)]
    )
    biases = small.shape[0] - d_mod_u.size
    if fused:
        g_w_qkv, g_w_skip, smalls = last(
            norm_all, joined_all, d_qkv, d_resid, small.reshape(-1, 128)
        )
        smalls = smalls.reshape(4, -1)
        bias_sum = jnp.sum(smalls[:, :biases], axis=0)
        d_mod_all = smalls[:, biases:].reshape(-1, d_mod_u.shape[1])
        flow_all = flows[:, 0, : flow_times.shape[1]].reshape(-1)
        act_all = jax.nn.silu(time_embed(flow_all, model_width)).astype(jnp.bfloat16)
        g_w_skip, g_w_qkv, g_w_out, g_w_up, g_w_down = (
            grad.astype(jnp.float32) for grad in (g_w_skip, g_w_qkv, g_w_out, g_w_up, g_w_down)
        )
    else:
        g_w_qkv = weight_grad(gather_left(norm_a), d_qkv)
        g_w_skip = weight_grad(gather_left(joined), d_resid)
        small = xor_sum(small.reshape(-1, 128), "seq").reshape(-1)
        bias_sum = xor_sum(small[:biases].reshape(-1, 128), "utt").reshape(-1)
        d_mod_all = gather_ordered(small[biases:].reshape(d_mod_u.shape), 0)
        act_all = gather_ordered(time_act, 0)
    act_all = act_all.astype(jnp.float32)
    own_width = model_width // shards
    act_own = lax.dynamic_slice_in_dim(act_all, seq_place * own_width, own_width, 1)
    g_w_mod = jnp.dot(jnp.transpose(act_own), d_mod_all, precision=HIGHEST_PRECISION)
    mod_width = d_mod_all.shape[1] // shards
    g_b_mod = jnp.sum(
        lax.dynamic_slice_in_dim(d_mod_all, seq_place * mod_width, mod_width, 1), axis=0
    )
    own_biases, offset = [], 0
    for vector in (g_b_skip, g_b_qkv, g_b_out, g_b_up, g_b_down):
        width = vector.shape[0] // shards
        own_biases.append(
            lax.dynamic_slice_in_dim(bias_sum, offset + seq_place * width, width, 0)
        )
        offset += vector.shape[0]
    return (
        out_state.astype(jnp.bfloat16)[None],
        d_joined[:, :model_width].astype(jnp.bfloat16)[None],
        d_joined[:, model_width:].astype(jnp.bfloat16)[None],
        g_w_skip,
        own_biases[0],
        g_w_mod,
        g_b_mod,
        g_w_qkv,
        own_biases[1],
        g_w_out,
        own_biases[2],
        g_w_up,
        own_biases[3],
        g_w_down,
        own_biases[4],
    )


def solution(mesh):
    return jax.shard_map(
        local,
        mesh=mesh,
        in_specs=(
            P("utt", "seq", None),
            P("utt", "seq", None),
            P("utt", None),
            P("utt", None),
            P("utt", None),
            P("utt", "seq"),
            P("utt", "seq", None),
            P(),
            P(),
            P(),
            P(),
            P(),
            P(),
            P(),
            P(),
            P(),
            P(),
            P(),
            P(),
        ),
        out_specs=(
            P("utt", "seq", None),
            P("utt", "seq", None),
            P("utt", "seq", None),
            P("seq", None),
            P("seq"),
            P("seq", None),
            P("seq"),
            P("seq", None),
            P("seq"),
            P("seq", None),
            P("seq"),
            P("seq", None),
            P("seq"),
            P("seq", None),
            P("seq"),
        ),
        check_vma=False,
    )
```

```python
from functools import partial
import math

import jax
import jax.numpy as jnp
from jax import lax
from jax.experimental import pallas as pl
from jax.experimental.pallas import tpu as pltpu
from jax.sharding import PartitionSpec as P

HEADS = 16
HEAD_DIM = 64


HIGHEST_PRECISION = lax.Precision.HIGHEST
EPSILON = 1e-06


def layer_norm(values):
    average = jnp.mean(values, axis=-1, keepdims=True)
    centred = values - average
    spread = jnp.mean(centred * centred, axis=-1, keepdims=True)
    return centred * lax.rsqrt(spread + EPSILON)


def modulate(values, scale_part, shift_part):
    return layer_norm(values) * (1.0 + scale_part) + shift_part


def time_embed(flow_vals, model_width):
    half_dim = model_width // 2
    inverse = jnp.exp(-math.log(10000.0) * jnp.arange(half_dim, dtype=jnp.float32) / half_dim)
    angles = 1000.0 * flow_vals[:, None] * inverse[None, :]
    return jnp.concatenate([jnp.sin(angles), jnp.cos(angles)], axis=1)


def rotary_tables(position, head_size):
    half_dim = head_size // 2
    inverse = jnp.exp(
        -math.log(10000.0) * 2.0 * jnp.arange(half_dim, dtype=jnp.float32) / head_size
    )
    angles = position.astype(jnp.float32)[:, None] * inverse[None, :]
    return (jnp.cos(angles)[:, None, :], jnp.sin(angles)[:, None, :])


def rotate(tensor, angle_cos, angle_sin):
    half_dim = tensor.shape[-1] // 2
    leading = tensor[..., :half_dim]
    trailing = tensor[..., half_dim:]
    return jnp.concatenate(
        [leading * angle_cos - trailing * angle_sin, trailing * angle_cos + leading * angle_sin],
        axis=-1,
    )


def unrotate(gradient, angle_cos, angle_sin):
    half_dim = gradient.shape[-1] // 2
    leading = gradient[..., :half_dim]
    trailing = gradient[..., half_dim:]
    return jnp.concatenate(
        [leading * angle_cos + trailing * angle_sin, trailing * angle_cos - leading * angle_sin],
        axis=-1,
    )


def frame_tables(lengths, char_counts, first_frame, frame_count):
    utt_ends = jnp.cumsum(lengths)
    utt_starts = utt_ends - lengths
    frame_index = first_frame + jnp.arange(frame_count, dtype=jnp.int32)
    segment = jnp.sum((frame_index[:, None] >= utt_ends[None, :]).astype(jnp.int32), axis=1)
    member = segment[:, None] == jnp.arange(lengths.shape[0], dtype=jnp.int32)[None, :]
    position = frame_index - jnp.sum(jnp.where(member, utt_starts[None, :], 0), axis=1)
    prompt = jnp.sum(jnp.where(member, char_counts[None, :], 0), axis=1)
    return (segment, position, position >= prompt, member)


def key_segments(key_start, key_count, utt_ends):
    frame_index = key_start + jnp.arange(key_count, dtype=jnp.int32)
    return jnp.sum((frame_index[:, None] >= utt_ends[None, :]).astype(jnp.int32), axis=1)


def block_scores(queries, key_piece, query_segment, key_segment, usable):
    key_rows = key_piece.reshape(key_piece.shape[0], queries.shape[1], queries.shape[2])
    scores = (
        jnp.einsum("qhd,khd->hqk", queries, key_rows, preferred_element_type=jnp.float32) * 0.125
    )
    allowed = jnp.logical_and(query_segment[:, None] == key_segment[None, :], usable)
    return (jnp.where(allowed[None], jnp.exp(scores), 0.0), key_rows)


def over_blocks(block_fn, running, piece, key_start, shard_rows):
    key_count = piece.shape[1]
    shard_total = key_count // shard_rows
    group_size = max(1, min(shard_total, 1024 // shard_rows))
    while shard_total % group_size != 0:
        group_size = group_size - 1
    block_rows = group_size * shard_rows
    if block_rows == key_count:
        return block_fn(running, piece, key_start)

    def one_block(block_index, inner_state):
        portion = lax.dynamic_slice_in_dim(piece, block_index * block_rows, block_rows, 1)
        return block_fn(inner_state, portion, key_start + block_index * block_rows)

    return lax.fori_loop(0, key_count // block_rows, one_block, running)


def forward_piece(running, piece, key_start, usable, queries, query_segment, utt_ends):
    weighted, totals = running
    key_segment = key_segments(key_start, piece.shape[1], utt_ends)
    weights, key_rows = block_scores(queries, piece[0], query_segment, key_segment, usable)
    value_rows = piece[1].reshape(key_rows.shape)
    totals = totals + jnp.sum(weights, axis=2)
    weighted = weighted + jnp.einsum(
        "hqk,khd->qhd", weights.astype(jnp.bfloat16), value_rows, preferred_element_type=jnp.float32
    )
    return (weighted, totals)


def backward_piece(piece, key_start, usable, queries, query_segment, utt_ends, grad_acc, delta):
    key_count = piece.shape[1]
    key_segment = key_segments(key_start, key_count, utt_ends)
    weights, key_rows = block_scores(queries, piece[0], query_segment, key_segment, usable)
    value_rows = piece[1].reshape(key_rows.shape)
    value_dots = jnp.einsum(
        "qhd,khd->hqk", grad_acc, value_rows, preferred_element_type=jnp.float32
    )
    d_scores = (weights * (value_dots - delta[:, :, None])).astype(jnp.bfloat16)
    d_query = (
        jnp.einsum("hqk,khd->qhd", d_scores, key_rows, preferred_element_type=jnp.float32) * 0.125
    )
    d_key = (
        jnp.einsum("hqk,qhd->khd", d_scores, queries, preferred_element_type=jnp.float32) * 0.125
    )
    d_value = jnp.einsum(
        "hqk,qhd->khd", weights.astype(jnp.bfloat16), grad_acc, preferred_element_type=jnp.float32
    )
    return (
        d_query,
        jnp.stack([d_key.reshape(key_count, -1), d_value.reshape(key_count, -1)], axis=0),
    )


def back_product(gradient_rows, matrix):
    return jnp.einsum("fo,io->fi", gradient_rows, matrix, preferred_element_type=jnp.float32)


def xor_permute(value, axis_name, bit):
    size = lax.axis_size(axis_name)
    return lax.ppermute(value, axis_name, [(i, i ^ bit) for i in range(size)])


def bits_of(axis_name):
    size, bits, bit = lax.axis_size(axis_name), [], 1
    while bit < size:
        bits.append(bit)
        bit *= 2
    return bits


def xor_sum(value, axis_name):
    for bit in bits_of(axis_name):
        value = value + xor_permute(value, axis_name, bit)
    return value


def gather_left(rows):
    for bit in reversed(bits_of("utt")):
        rows = jnp.concatenate([rows, xor_permute(rows, "utt", bit)], axis=0)
    return rows


def gather_right(rows):
    place = lax.axis_index("utt")
    for bit in reversed(bits_of("utt")):
        mine = (place & bit) // bit
        width = rows.shape[1] // 2
        kept = lax.dynamic_slice_in_dim(rows, mine * width, width, 1)
        given = lax.dynamic_slice_in_dim(rows, (1 - mine) * width, width, 1)
        rows = jnp.concatenate([kept, xor_permute(given, "utt", bit)], axis=0)
    return rows


def gather_ordered(value, axis):
    place = lax.axis_index("utt")
    for bit in bits_of("utt"):
        other = xor_permute(value, "utt", bit)
        low = (place & bit) == 0
        value = jnp.concatenate(
            [jnp.where(low, value, other), jnp.where(low, other, value)], axis=axis
        )
    return value


def scatter_rows(tile):
    place = lax.axis_index("seq")
    for bit in bits_of("seq"):
        mine = (place & bit) // bit
        rest = lax.axis_size("seq") // (2 * bit)
        pieces = tile.reshape(rest, 2, -1, tile.shape[-1])
        kept = lax.dynamic_index_in_dim(pieces, mine, 1, keepdims=False)
        given = lax.dynamic_index_in_dim(pieces, 1 - mine, 1, keepdims=False)
        given = xor_permute(given, "seq", bit)
        tile = (kept.astype(jnp.float32) + given.astype(jnp.float32)).astype(jnp.bfloat16)
    return tile.reshape(-1, tile.shape[-1])


def weight_grad(left_all, right_rows):
    right_all = gather_right(right_rows)
    tile = jnp.einsum(
        "fi,fo->io", left_all, right_all, preferred_element_type=jnp.float32
    ).astype(jnp.bfloat16)
    tile = tile.reshape(-1, tile.shape[-1])
    piece = scatter_rows(tile)
    return gather_ordered(piece, 1).astype(jnp.float32)


def swap_halves(values, lower):
    return jnp.where(lower, pltpu.roll(values, 96, 1), pltpu.roll(values, 32, 1))


def lower_half(shape):
    return lax.broadcasted_iota(jnp.int32, shape, 1) % HEAD_DIM < HEAD_DIM // 2


def rotate_pack_kernel(q_ref, k_ref, v_ref, cos_ref, sin_ref, out_ref):
    lower = lower_half(q_ref.shape)
    cos, sin = cos_ref[...], sin_ref[...]
    q, k = q_ref[...], k_ref[...]
    out_ref[0, :, 0:128] = (q * cos + swap_halves(q, lower) * sin).astype(jnp.bfloat16)
    out_ref[0, :, 128:256] = (k * cos + swap_halves(k, lower) * sin).astype(jnp.bfloat16)
    out_ref[0, :, 256:384] = v_ref[...].astype(jnp.bfloat16)


def rotate_pack(qkv_full, cos, sin):
    rows = qkv_full.shape[0]
    blocks = qkv_full.shape[1] // 384
    table = pl.BlockSpec((rows, 128), lambda i: (0, 0))
    return pl.pallas_call(
        rotate_pack_kernel,
        grid=(blocks,),
        in_specs=[
            pl.BlockSpec((rows, 128), lambda i: (0, i)),
            pl.BlockSpec((rows, 128), lambda i: (0, blocks + i)),
            pl.BlockSpec((rows, 128), lambda i: (0, 2 * blocks + i)),
            table,
            table,
        ],
        out_specs=pl.BlockSpec((1, rows, 384), lambda i: (i, 0, 0)),
        out_shape=jax.ShapeDtypeStruct((blocks, rows, 384), jnp.bfloat16),
    )(qkv_full, qkv_full, qkv_full, cos, sin)


def head_scores(q, k, seg_q, seg_k):
    scores = lax.dot_general(q, k, (((1,), (1,)), ((), ())), preferred_element_type=jnp.float32)
    return jnp.where(seg_q == seg_k, jnp.exp(scores * 0.125), 0.0)


MESH = pl.DeviceIdType.MESH
VMEM_LIMIT = 60 * 1024 * 1024


def flip(index, bit):
    return index + bit - 2 * bit * ((index // bit) % 2)


def everywhere(memory):
    return pl.BlockSpec(memory_space=memory)


class Links:
    def __init__(self, send_sems, recv_sems, local_sems):
        self.send_sems, self.recv_sems, self.local_sems = send_sems, recv_sems, local_sems
        self.sent, self.held = [], 0
        self.utt, self.seq = lax.axis_index("utt"), lax.axis_index("seq")

    def enter(self, utt_peers, seq_peers):
        barrier = pltpu.get_barrier_semaphore()
        targets = [self.mate(r) for r in utt_peers] + [self.peer(r) for r in seq_peers]
        for target in targets:
            pl.semaphore_signal(barrier, inc=1, device_id=target, device_id_type=MESH)
        pl.semaphore_wait(barrier, len(targets))

    def mate(self, offset):
        return (self.utt_of(offset), self.seq)

    def utt_of(self, offset):
        place = self.utt
        for bit in (1, 2):
            if offset & bit:
                place = flip(place, bit)
        return place

    def seq_of(self, offset):
        place = self.seq
        for bit in (1, 2, 4):
            if offset & bit:
                place = flip(place, bit)
        return place

    def peer(self, offset):
        return (self.utt, self.seq_of(offset))

    def send(self, source, target, device):
        index = len(self.sent)
        copy = pltpu.make_async_remote_copy(
            src_ref=source,
            dst_ref=target,
            send_sem=self.send_sems.at[index],
            recv_sem=self.recv_sems.at[index],
            device_id=device,
            device_id_type=MESH,
        )
        copy.start()
        self.sent.append(copy)
        return copy

    def keep(self, source, target):
        copy = pltpu.make_async_copy(source, target, self.local_sems.at[self.held])
        self.held += 1
        copy.start()
        return copy

    def leave(self):
        for copy in self.sent:
            copy.wait_send()


class Gathered:
    def __init__(self, links, source, target, columns=None):
        self.links, self.target = links, target
        self.rows = source.shape[0]
        self.columns = columns
        self.own = links.keep(source, self.slot(0))
        self.across = links.send(source, self.slot(2), links.mate(2))
        self.beside = links.send(source, self.slot(1), links.mate(1))

    def slot(self, offset):
        rows = pl.ds(offset * self.rows, self.rows)
        if self.columns is None:
            return self.target.at[rows, :]
        return self.target.at[rows, self.columns]

    def relay(self):
        self.across.wait_recv()
        self.relayed = self.links.send(self.slot(2), self.slot(3), self.links.mate(1))

    def wait(self):
        self.own.wait()
        self.beside.wait_recv()
        self.relayed.wait_recv()


class Quarter:
    def __init__(self, links, piece_of, target):
        rows = target.shape[0] // 4
        slot = lambda r: target.at[pl.ds(r * rows, rows), :]
        self.own = links.keep(piece_of(links.utt), slot(0))
        self.copies = [
            links.send(piece_of(links.utt_of(r)), slot(r), links.mate(r)) for r in (2, 3, 1)
        ]

    def wait(self):
        self.own.wait()
        for copy in self.copies:
            copy.wait_recv()


class Share:
    def __init__(self, links, left, right, columns, tile, got_y, got_z1, got_z2, result):
        self.links = links
        self.left, self.right, self.columns = left, right, columns
        self.tile, self.got_y, self.got_z1, self.got_z2 = tile, got_y, got_z1, got_z2
        self.result = result
        seq = links.seq
        self.y, self.zl, self.zh = seq % 2, (seq // 2) % 2, seq // 4

    def product(self, y):
        rows = self.tile.shape[3]

        def block(z, _):
            base = pl.multiple_of((2 * z + y) * rows, rows)
            self.tile[z // 2, z % 2, y] = lax.dot_general(
                self.left[:, pl.ds(base, rows)],
                self.right[:, self.columns],
                (((0,), (0,)), ((), ())),
                preferred_element_type=jnp.float32,
            ).astype(jnp.bfloat16)
            return 0

        lax.fori_loop(0, 4, block, 0)

    def start(self):
        self.product(1 - self.y)
        self.sent_y = self.links.send(
            self.tile.at[:, :, 1 - self.y], self.got_y, self.links.peer(1)
        )
        self.product(self.y)

    def add(self, index, got):
        tile = self.tile
        tile[index] = (tile[index].astype(jnp.float32) + got.astype(jnp.float32)).astype(
            jnp.bfloat16
        )

    def after_y(self):
        self.sent_y.wait_recv()

        def block(zh, _):
            self.add((zh, 1 - self.zl, self.y), self.got_y[zh, 1 - self.zl])
            return 0

        lax.fori_loop(0, 2, block, 0)
        self.sent_z1 = self.links.send(
            self.tile.at[:, 1 - self.zl, self.y], self.got_z1, self.links.peer(2)
        )

        def rest(zh, _):
            self.add((zh, self.zl, self.y), self.got_y[zh, self.zl])
            return 0

        lax.fori_loop(0, 2, rest, 0)

    def after_z1(self):
        self.sent_z1.wait_recv()
        self.add((1 - self.zh, self.zl, self.y), self.got_z1[1 - self.zh])
        self.sent_z2 = self.links.send(
            self.tile.at[1 - self.zh, self.zl, self.y], self.got_z2, self.links.peer(4)
        )
        self.add((self.zh, self.zl, self.y), self.got_z1[self.zh])

    def after_z2(self):
        self.sent_z2.wait_recv()
        links = self.links
        mine = self.result(links.utt)
        mine[...] = (
            self.tile[self.zh, self.zl, self.y].astype(jnp.float32)
            + self.got_z2[...].astype(jnp.float32)
        ).astype(jnp.bfloat16)
        self.across = links.send(mine, mine, links.mate(2))
        self.beside = links.send(mine, mine, links.mate(1))

    def relay(self):
        self.across.wait_recv()
        links = self.links
        theirs = self.result(links.utt_of(2))
        self.relayed = links.send(theirs, theirs, links.mate(1))

    def wait(self):
        self.beside.wait_recv()
        self.relayed.wait_recv()


def share_scratch(rows, columns):
    return [
        pltpu.VMEM((2, 2, 2, rows, columns), jnp.bfloat16),
        pltpu.VMEM((2, 2, rows, columns), jnp.bfloat16),
        pltpu.VMEM((2, rows, columns), jnp.bfloat16),
        pltpu.VMEM((rows, columns), jnp.bfloat16),
    ]


def run_shares(shares, hooks):
    stages = ("after_y", "after_z1", "after_z2", "relay", "wait")
    for turn in range(len(shares) + len(stages) - 1):
        for hook in hooks.get(turn, ()):
            hook()
        for place, stage in enumerate(stages):
            if 0 <= turn - place < len(shares):
                getattr(shares[turn - place], stage)()


def semaphores(count):
    return [pltpu.SemaphoreType.DMA((count,))] * 2 + [pltpu.SemaphoreType.DMA((16,))]


def comm_params(collective_id):
    return pltpu.CompilerParams(
        collective_id=collective_id, has_side_effects=True, vmem_limit_bytes=VMEM_LIMIT
    )


def attend_kernel(
    packed_ref, segq_ref, segk_ref, counts_ref, flow_ref, norm_ref, frames_ref, skip_ref,
    attn_ref, heads_ref, exact_ref, total_ref, sums_ref, flows_ref, norm_all, joined_all,
    attn_heads, counts_got, send_sems, recv_sems, local_sems,
):
    links = Links(send_sems, recv_sems, local_sems)
    links.enter((1, 2, 3), range(1, 8))
    rows = packed_ref.shape[1]
    width = frames_ref.shape[1]
    own_rows = pl.ds(pl.multiple_of(links.seq * rows, rows), rows)
    own = links.keep(packed_ref.at[links.seq], heads_ref.at[own_rows, :])
    incoming = [
        links.send(packed_ref.at[links.seq_of(r)], heads_ref.at[own_rows, :], links.peer(r))
        for r in (6, 7, 4, 5, 2, 3, 1)
    ]
    flows_ref[links.utt] = flow_ref[...]
    flow_copies = [
        links.send(flow_ref, flows_ref.at[links.utt], links.mate(r)) for r in (1, 2, 3)
    ]
    gathers = [
        Gathered(links, norm_ref, norm_all),
        Gathered(links, frames_ref, joined_all, pl.ds(0, width)),
        Gathered(links, skip_ref, joined_all, pl.ds(width, width)),
    ]
    sums_ref[...] = counts_ref[...]
    for place, (target, source) in enumerate(
        ((links.mate(1), 0), (links.mate(2), 1), (links.peer(1), 2), (links.peer(2), 3),
         (links.peer(4), 4))
    ):
        counts_got[5 + place] = sums_ref[...]
        copy = links.send(counts_got.at[5 + place], counts_got.at[source], target)
        copy.wait_recv()
        sums_ref[...] = sums_ref[...] + counts_got[source]
    gathers[0].relay()
    own.wait()
    for copy in incoming:
        copy.wait_recv()
    first = lax.broadcasted_iota(jnp.int32, (256, 128), 1) < HEAD_DIM
    zero = jnp.zeros((256, 128), jnp.bfloat16)
    k, v = heads_ref[:, 128:256], heads_ref[:, 256:384]
    seg_k = segk_ref[...]

    def block(step, _):
        here = pl.ds(pl.multiple_of(step * 256, 256), 256)
        q, seg_q = heads_ref[here, 0:128], segq_ref[here, :]
        results = []
        for mine in (first, jnp.logical_not(first)):
            weights = head_scores(jnp.where(mine, q, zero), k, seg_q, seg_k)
            total = jnp.sum(weights, axis=1, keepdims=True)
            summed = jnp.dot(weights.astype(jnp.bfloat16), v, preferred_element_type=jnp.float32)
            results.append((summed, total))
        total = jnp.where(first, results[0][1], results[1][1])
        attended = jnp.where(first, results[0][0], results[1][0]) / total
        attn_heads[here, :] = attended.astype(jnp.bfloat16)
        exact_ref[here, :] = attended
        total_ref[here, :] = total
        return 0

    lax.fori_loop(0, heads_ref.shape[0] // 256, block, 0)
    column = attn_ref.at[:, pl.ds(pl.multiple_of(links.seq * 128, 128), 128)]
    part = lambda place: attn_heads.at[pl.ds(pl.multiple_of(place * rows, rows), rows), :]
    own = links.keep(part(links.seq), column)
    incoming = [
        links.send(part(links.seq_of(r)), column, links.peer(r)) for r in (6, 7, 4, 5, 2, 3, 1)
    ]
    for gather in gathers[1:]:
        gather.relay()
    for copy in flow_copies:
        copy.wait_recv()
    own.wait()
    for copy in incoming:
        copy.wait_recv()
    for gather in gathers:
        gather.wait()
    links.leave()


def attend(packed, seg_col, seg_row, counts, flow, norm_a, frames, skip):
    shards, rows, _ = packed.shape
    total_rows, width = shards * rows, norm_a.shape[1]
    vmem, there = everywhere(pltpu.VMEM), everywhere(pl.ANY)
    shape = jax.ShapeDtypeStruct
    return pl.pallas_call(
        attend_kernel,
        in_specs=[there, vmem, vmem, vmem, vmem, there, there, there],
        out_specs=[vmem] * 8,
        out_shape=[
            shape((rows, width), jnp.bfloat16),
            shape((total_rows, 384), jnp.bfloat16),
            shape((total_rows, 128), jnp.float32),
            shape((total_rows, 128), jnp.float32),
            shape(counts.shape, jnp.float32),
            shape((4,) + flow.shape, jnp.float32),
            shape((4 * rows, width), jnp.bfloat16),
            shape((4 * rows, 2 * width), jnp.bfloat16),
        ],
        scratch_shapes=[
            pltpu.VMEM((total_rows, 128), jnp.bfloat16),
            pltpu.VMEM((10,) + counts.shape, jnp.float32),
        ]
        + semaphores(40),
        compiler_params=comm_params(1),
    )(packed, seg_col, seg_row, counts, flow, norm_a, frames, skip)


def backward_kernel(
    d_attn_ref, heads_ref, segq_ref, segk_ref, exact_ref, total_ref, cos_ref, sin_ref,
    resid_ref, gain_ref, d_mid_ref, segment_ref, small_ref,
    d_ff_ref, act_ref, norm_ref, d_inner_ref, attn_ref, d_branch_ref,
    norm_a_ref, joined_ref, w_qkv_ref, w_skip_ref,
    g_down, g_up, g_out, g_qkv, g_skip, smalls, g_frames, g_skip_in,
    grad_heads, d_heads, dk_ref, dv_ref,
    d_ff_all, act_all, norm_all, d_inner_all, attn_all, d_branch_all,
    norm_a_all, joined_all, d_qkv, d_qkv_all, d_resid, d_resid_all,
    w_qkv, w_skip, small_own, small_got, small_sum,
    *rest,
):
    tiles, (send_sems, recv_sems, local_sems) = rest[:-3], rest[-3:]
    links = Links(send_sems, recv_sems, local_sems)
    links.enter((1, 2, 3), range(1, 8))
    rows, model = d_mid_ref.shape
    far_first = (6, 7, 4, 5, 2, 3, 1)
    own_rows = pl.ds(pl.multiple_of(links.seq * rows, rows), rows)
    strip = lambda ref, place, size: ref.at[
        :, pl.ds(pl.multiple_of(place * size, size), size)
    ]
    own = links.keep(strip(d_attn_ref, links.seq, 128), grad_heads.at[own_rows, :])
    incoming = [
        links.send(
            strip(d_attn_ref, links.seq_of(r), 128), grad_heads.at[own_rows, :], links.peer(r)
        )
        for r in far_first
    ]
    gather_d = Gathered(links, d_ff_ref, d_ff_all)
    quarter_a = Quarter(links, lambda u: act_ref.at[u], act_all)
    gather_n = Gathered(links, norm_ref, norm_all)
    width, narrow = d_inner_all.shape[1], d_branch_all.shape[1]
    quarter_i = Quarter(links, lambda u: strip(d_inner_ref, u, width), d_inner_all)
    gather_b = Gathered(links, attn_ref, attn_all)
    quarter_b = Quarter(links, lambda u: strip(d_branch_ref, u, narrow), d_branch_all)
    loads = [
        links.keep(w_qkv_ref, w_qkv),
        links.keep(w_skip_ref, w_skip),
        links.keep(norm_a_ref, norm_a_all),
        links.keep(joined_ref, joined_all),
    ]
    small_own[...] = small_ref[...]
    gather_d.relay()
    own.wait()
    for copy in incoming:
        copy.wait_recv()
    dk_ref[...] = jnp.zeros_like(dk_ref)
    dv_ref[...] = jnp.zeros_like(dv_ref)
    first = lax.broadcasted_iota(jnp.int32, (256, 128), 1) < HEAD_DIM
    zero = jnp.zeros((256, 128), jnp.bfloat16)
    lower = lower_half((256, 128))
    k, v = heads_ref[:, 128:256], heads_ref[:, 256:384]
    seg_k = segk_ref[...]
    along = (((1,), (1,)), ((), ()))
    down = (((0,), (0,)), ((), ()))

    def turned(values, here):
        return (
            values * cos_ref[here, :] - swap_halves(values, lower) * sin_ref[here, :]
        ).astype(jnp.bfloat16)

    def block(step, _):
        here = pl.ds(pl.multiple_of(step * 256, 256), 256)
        q, seg_q = heads_ref[here, 0:128], segq_ref[here, :]
        scaled = grad_heads[here, :].astype(jnp.float32) / total_ref[here, :]
        grad_acc = scaled.astype(jnp.bfloat16)
        product = scaled * exact_ref[here, :]
        d_query = []
        for mine in (first, jnp.logical_not(first)):
            q_own = jnp.where(mine, q, zero)
            g_own = jnp.where(mine, grad_acc, zero)
            delta = jnp.sum(jnp.where(mine, product, 0.0), axis=1, keepdims=True)
            weights = head_scores(q_own, k, seg_q, seg_k)
            dots = lax.dot_general(g_own, v, along, preferred_element_type=jnp.float32)
            d_scores = (weights * (dots - delta)).astype(jnp.bfloat16)
            d_query.append(jnp.dot(d_scores, k, preferred_element_type=jnp.float32))
            dk_ref[...] += lax.dot_general(
                d_scores, q_own, down, preferred_element_type=jnp.float32
            )
            dv_ref[...] += lax.dot_general(
                weights.astype(jnp.bfloat16), g_own, down, preferred_element_type=jnp.float32
            )
        d_heads[here, 0:128] = turned(jnp.where(first, d_query[0], d_query[1]) * 0.125, here)
        return 0

    blocks = heads_ref.shape[0] // 256
    lax.fori_loop(0, blocks, block, 0)

    def finish(step, _):
        here = pl.ds(pl.multiple_of(step * 256, 256), 256)
        d_heads[here, 128:256] = turned(dk_ref[here, :] * 0.125, here)
        d_heads[here, 256:384] = dv_ref[here, :].astype(jnp.bfloat16)
        return 0

    lax.fori_loop(0, blocks, finish, 0)
    part = lambda place, c: d_heads.at[
        pl.ds(pl.multiple_of(place * rows, rows), rows), pl.ds(c * 128, 128)
    ]
    home = lambda c: d_qkv.at[
        :, pl.ds(pl.multiple_of(c * model + links.seq * 128, 128), 128)
    ]
    owns = [links.keep(part(links.seq, c), home(c)) for c in range(3)]
    incoming = [
        links.send(part(links.seq_of(r), c), home(c), links.peer(r))
        for r in far_first
        for c in range(3)
    ]
    half = width // 2
    down_at = lambda h: lambda u: g_down.at[
        pl.ds(pl.multiple_of(u * 128, 128), 128), pl.ds(h * half, half)
    ]
    column_at = lambda ref, step, offset, size: lambda u: ref.at[
        :, pl.ds(pl.multiple_of(u * step + offset, 128), size)
    ]
    wide, thin = d_qkv_all.shape[1], d_resid_all.shape[1]
    third = wide // 2
    plans = [
        (act_all, d_ff_all, pl.ds(0, half), down_at(0)),
        (act_all, d_ff_all, pl.ds(half, half), down_at(1)),
        (norm_all, d_inner_all, pl.ds(0, half), column_at(g_up, width, 0, half)),
        (norm_all, d_inner_all, pl.ds(half, half), column_at(g_up, width, half, half)),
        (attn_all, d_branch_all, pl.ds(0, narrow), column_at(g_out, narrow, 0, narrow)),
        (norm_a_all, d_qkv_all, pl.ds(0, third), column_at(g_qkv, wide, 0, third)),
        (norm_a_all, d_qkv_all, pl.ds(third, third), column_at(g_qkv, wide, third, third)),
        (joined_all, d_resid_all, pl.ds(0, thin), column_at(g_skip, thin, 0, thin)),
    ]
    shares = [
        Share(links, left, right, columns, *tiles[4 * i : 4 * i + 4], result)
        for i, (left, right, columns, result) in enumerate(plans)
    ]
    gather_n.relay()
    gather_d.wait()
    quarter_a.wait()
    shares[0].start()
    shares[1].start()
    gather_b.relay()
    gather_n.wait()
    quarter_i.wait()
    shares[2].start()
    shares[3].start()
    gather_b.wait()
    quarter_b.wait()
    shares[4].start()
    state = {}

    def projections():
        for copy in owns:
            copy.wait()
        for copy in incoming:
            copy.wait_recv()
        for copy in loads:
            copy.wait()
        state["qkv"] = Quarter(links, lambda u: strip(d_qkv, u, wide), d_qkv_all)
        d_norm = lax.dot_general(
            d_qkv[...], w_qkv[...], along, preferred_element_type=jnp.float32
        )
        resid = resid_ref[...]
        centred = resid - jnp.mean(resid, axis=1, keepdims=True)
        scale = lax.rsqrt(jnp.mean(centred * centred, axis=1, keepdims=True) + EPSILON)
        unit = centred * scale
        inward = d_norm * gain_ref[...]
        d_resid_f = d_mid_ref[...] + scale * (
            inward
            - jnp.mean(inward, axis=1, keepdims=True)
            - unit * jnp.mean(inward * unit, axis=1, keepdims=True)
        )
        rounded = d_resid_f.astype(jnp.bfloat16)
        d_resid[...] = rounded
        state["resid"] = Quarter(links, lambda u: strip(d_resid, u, thin), d_resid_all)
        small_own[0:1, :] = jnp.sum(rounded.astype(jnp.float32), axis=0, keepdims=True)
        for c in range(3):
            small_own[1 + c : 2 + c, :] = jnp.sum(
                d_qkv[:, c * model : (c + 1) * model].astype(jnp.float32), axis=0, keepdims=True
            )
        d_scale = d_norm * unit
        for u in range((small_own.shape[0] - 10) // 6):
            inside = segment_ref[...] == u
            row = 10 + 6 * u
            small_own[row : row + 1, :] = jnp.sum(
                jnp.where(inside, d_norm, 0.0), axis=0, keepdims=True
            )
            small_own[row + 1 : row + 2, :] = jnp.sum(
                jnp.where(inside, d_scale, 0.0), axis=0, keepdims=True
            )
        state["small"] = links.send(small_own, small_got.at[0], links.peer(1))

    def last_shares():
        state["qkv"].wait()
        shares[5].start()
        shares[6].start()
        state["resid"].wait()
        shares[7].start()

    def inputs():
        for index, out in enumerate((g_frames, g_skip_in)):
            out[...] = lax.dot_general(
                d_resid[...],
                w_skip[pl.ds(index * model, model), :],
                along,
                preferred_element_type=jnp.float32,
            ).astype(jnp.bfloat16)

    def small_y():
        state["small"].wait_recv()
        small_sum[0] = small_own[...] + small_got[0]
        state["small"] = links.send(small_sum.at[0], small_got.at[1], links.peer(2))

    def small_z1():
        state["small"].wait_recv()
        small_sum[1] = small_sum[0] + small_got[1]
        state["small"] = links.send(small_sum.at[1], small_got.at[2], links.peer(4))

    def small_z2():
        state["small"].wait_recv()
        mine = smalls.at[links.utt]
        mine[...] = small_sum[1] + small_got[2]
        state["spread"] = [links.send(mine, mine, links.mate(r)) for r in (2, 3, 1)]

    run_shares(
        shares,
        {
            1: (projections,),
            2: (last_shares,),
            3: (inputs, small_y),
            4: (small_z1,),
            5: (small_z2,),
        },
    )
    for copy in state["spread"]:
        copy.wait_recv()
    links.leave()


def backward(
    d_attn, heads, seg_col, seg_row, exact, total, cos, sin,
    resid, gain, d_mid, segment, small,
    d_ff, act_quarters, norm_f, d_inner, attn_b, d_branch,
    norm_a_all, joined_all, w_qkv, w_skip,
):
    rows, model = d_attn.shape
    frames = heads.shape[0]
    inner = d_inner.shape[1]
    vmem, there = everywhere(pltpu.VMEM), everywhere(pl.ANY)
    shape = jax.ShapeDtypeStruct
    bf16 = lambda *dims: pltpu.VMEM(dims, jnp.bfloat16)
    f32 = lambda *dims: pltpu.VMEM(dims, jnp.float32)
    part = model // 8
    return pl.pallas_call(
        backward_kernel,
        in_specs=[there] + [vmem] * 12 + [there] * 10,
        out_specs=[vmem] * 8,
        out_shape=[
            shape((inner // 8, model), jnp.bfloat16),
            shape((part, inner), jnp.bfloat16),
            shape((part, model), jnp.bfloat16),
            shape((part, 3 * model), jnp.bfloat16),
            shape((2 * part, model), jnp.bfloat16),
            shape((4,) + small.shape, jnp.float32),
            shape((rows, model), jnp.bfloat16),
            shape((rows, model), jnp.bfloat16),
        ],
        scratch_shapes=[
            bf16(frames, 128),
            bf16(frames, 384),
            f32(frames, 128),
            f32(frames, 128),
            bf16(4 * rows, model),
            bf16(4 * rows, inner // 4),
            bf16(4 * rows, model),
            bf16(4 * rows, inner // 4),
            bf16(4 * rows, model),
            bf16(4 * rows, model // 4),
            bf16(4 * rows, model),
            bf16(4 * rows, 2 * model),
            bf16(rows, 3 * model),
            bf16(4 * rows, 3 * model // 4),
            bf16(rows, model),
            bf16(4 * rows, model // 4),
            bf16(*w_qkv.shape),
            bf16(*w_skip.shape),
            f32(*small.shape),
            f32(3, *small.shape),
            f32(2, *small.shape),
        ]
        + share_scratch(part, inner // 8) * 4
        + share_scratch(part, model // 4)
        + share_scratch(part, 3 * model // 8) * 2
        + share_scratch(2 * part, model // 4)
        + semaphores(112),
        compiler_params=comm_params(2),
    )(
        d_attn, heads, seg_col, seg_row, exact, total, cos, sin,
        resid, gain, d_mid, segment, small,
        d_ff, act_quarters, norm_f, d_inner, attn_b, d_branch,
        norm_a_all, joined_all, w_qkv, w_skip,
    )


def wide_tables(position):
    half_dim = HEAD_DIM // 2
    lane = jnp.arange(128, dtype=jnp.int32) % HEAD_DIM
    inverse = jnp.exp(
        -math.log(10000.0) * 2.0 * (lane % half_dim).astype(jnp.float32) / HEAD_DIM
    )
    angles = position.astype(jnp.float32)[:, None] * inverse[None, :]
    sign = jnp.where(lane < half_dim, -1.0, 1.0)
    return jnp.cos(angles), jnp.sin(angles) * sign[None, :]


def local(
    frames_in,
    skip_in,
    flow_times,
    frame_lengths,
    char_lengths,
    drop_mask,
    out_grad,
    w_skip,
    b_skip,
    w_mod,
    b_mod,
    w_qkv,
    b_qkv,
    w_out,
    b_out,
    w_up,
    b_up,
    w_down,
    b_down,
):
    local_rows = frames_in.shape[1]
    model_width = frames_in.shape[2]
    shards = lax.axis_size("seq")
    seq_place = lax.axis_index("seq")
    lengths = frame_lengths[0]
    utt_ends = jnp.cumsum(lengths)
    segment, position, in_loss, member = frame_tables(
        lengths, char_lengths[0], seq_place * local_rows, local_rows
    )
    member_f = member.astype(jnp.float32)
    loss_mask = in_loss.astype(jnp.float32)
    dropped = drop_mask[0].astype(jnp.float32)
    counts = jnp.stack([jnp.sum(loss_mask * dropped), jnp.sum(loss_mask * (1.0 - dropped))])
    counts = jnp.pad(counts[None, :], ((0, 7), (0, 126)))
    whole = model_width * 4
    fused = (
        lax.axis_size("utt") == 4
        and shards == 8
        and HEADS * HEAD_DIM == 1024
        and w_up.shape[1] == whole
        and local_rows == 128
    )
    if not fused:
        counts = xor_sum(xor_sum(counts, "utt"), "seq")
    time_act = jax.nn.silu(time_embed(flow_times[0], model_width)).astype(jnp.bfloat16)
    mod_u = jnp.dot(time_act, w_mod, preferred_element_type=jnp.float32) + b_mod
    mod_f = jnp.dot(member_f, mod_u, precision=HIGHEST_PRECISION)
    shift_a, scale_a, gate_a, shift_f, scale_f, gate_f = jnp.split(mod_f, 6, axis=1)
    joined = jnp.concatenate([frames_in[0], skip_in[0]], axis=1)
    residual = jnp.dot(joined, w_skip, preferred_element_type=jnp.float32) + b_skip
    norm_a = modulate(residual, scale_a, shift_a).astype(jnp.bfloat16)
    qkv_full = jnp.dot(norm_a, w_qkv, preferred_element_type=jnp.float32) + b_qkv
    if fused:
        all_segment, all_position, _, _ = frame_tables(
            lengths, char_lengths[0], 0, local_rows * shards
        )
        cos_all, sin_all = wide_tables(all_position)
        cos_own, sin_own = wide_tables(position)
        seg_col, seg_row = all_segment[:, None], all_segment[None, :]
        flow = jnp.pad(flow_times, ((0, 7), (0, 128 - flow_times.shape[1])))
        attn_b, qkv_heads, exact, total, counts, flows, norm_all, joined_all = attend(
            rotate_pack(qkv_full, cos_own, sin_own),
            seg_col,
            seg_row,
            counts,
            flow,
            norm_a,
            frames_in[0],
            skip_in[0],
        )
    else:
        angle_cos, angle_sin = rotary_tables(position, HEAD_DIM)
        queries = rotate(
            qkv_full[:, :model_width].reshape(local_rows, HEADS, HEAD_DIM), angle_cos, angle_sin
        ).astype(jnp.bfloat16)
        key_rot = rotate(
            qkv_full[:, model_width : 2 * model_width].reshape(local_rows, HEADS, HEAD_DIM),
            angle_cos,
            angle_sin,
        ).astype(jnp.bfloat16)
        key_value = jnp.stack(
            [
                key_rot.reshape(local_rows, model_width),
                qkv_full[:, 2 * model_width :].astype(jnp.bfloat16),
            ],
            axis=0,
        )
        start_state = (
            jnp.zeros((local_rows, HEADS, HEAD_DIM), jnp.float32),
            jnp.zeros((HEADS, local_rows), jnp.float32),
        )
        fwd_piece = partial(forward_piece, queries=queries, query_segment=segment, utt_ends=utt_ends)
        weighted, totals = over_blocks(
            partial(fwd_piece, usable=True),
            start_state,
            lax.all_gather(key_value, "seq", axis=1, tiled=True),
            jnp.int32(0),
            local_rows,
        )
        totals_rows = jnp.transpose(totals)
        attended = weighted / totals_rows[:, :, None]
        attn_b = attended.reshape(local_rows, model_width).astype(jnp.bfloat16)
    n_drop, n_keep = counts[0, 0], counts[0, 1]
    loss_weight = (
        loss_mask
        * (n_drop + n_keep)
        * 0.5
        * (dropped / (n_drop + 1.0) + (1.0 - dropped) / (n_keep + 1.0))
    )
    branch = jnp.dot(attn_b, w_out, preferred_element_type=jnp.float32) + b_out
    mid_state = residual + gate_a * branch
    norm_f = modulate(mid_state, scale_f, shift_f).astype(jnp.bfloat16)
    ff_inner = jnp.dot(norm_f, w_up, preferred_element_type=jnp.float32) + b_up
    ff_act, gelu_pull = jax.vjp(partial(jax.nn.gelu, approximate=True), ff_inner)
    act_b = ff_act.astype(jnp.bfloat16)
    ff_out = jnp.dot(act_b, w_down, preferred_element_type=jnp.float32) + b_down
    out_state = mid_state + gate_f * ff_out
    d_out = out_grad[0].astype(jnp.float32) * loss_weight[:, None]
    d_ff = (gate_f * d_out).astype(jnp.bfloat16)
    d_gate_f = d_out * ff_out
    g_b_down = jnp.sum(d_ff.astype(jnp.float32), axis=0)
    (d_inner,) = gelu_pull(back_product(d_ff, w_down))
    d_inner_b = d_inner.astype(jnp.bfloat16)
    g_b_up = jnp.sum(d_inner_b.astype(jnp.float32), axis=0)
    d_norm_f = back_product(d_inner_b, w_up)
    _, norm_f_pull = jax.vjp(modulate, mid_state, scale_f, shift_f)
    d_mid_norm, d_scale_f, d_shift_f = norm_f_pull(d_norm_f)
    d_mid = d_out + d_mid_norm
    d_branch = (gate_a * d_mid).astype(jnp.bfloat16)
    d_gate_a = d_mid * branch
    g_b_out = jnp.sum(d_branch.astype(jnp.float32), axis=0)
    d_attn = back_product(d_branch, w_out)
    if fused:
        act_quarters = jnp.transpose(act_b.reshape(local_rows, shards, 4, -1), (2, 0, 1, 3))
        pieces = jnp.concatenate([d_gate_a, d_shift_f, d_scale_f, d_gate_f], axis=1)
        sums = jnp.dot(jnp.transpose(member_f), pieces, precision=HIGHEST_PRECISION)
        sums = jnp.pad(sums.reshape(-1, 4, model_width), ((0, 0), (2, 0), (0, 0)))
        row = lambda vector: vector.reshape(-1, model_width)
        small = jnp.concatenate(
            [
                jnp.zeros((4, model_width), jnp.float32),
                row(g_b_out),
                row(g_b_up),
                row(g_b_down),
                row(sums),
            ],
            axis=0,
        )
        used = small.shape[0]
        small = jnp.pad(small, ((0, -used % 8), (0, 0)))
        g_w_down, g_w_up, g_w_out, g_w_qkv, g_w_skip, smalls, g_frames, g_skip_in = backward(
            d_attn.astype(jnp.bfloat16),
            qkv_heads,
            seg_col,
            seg_row,
            exact,
            total,
            cos_all,
            sin_all,
            residual,
            1.0 + scale_a,
            d_mid,
            segment[:, None],
            small,
            d_ff,
            act_quarters.reshape(4, local_rows, -1),
            norm_f,
            d_inner_b,
            attn_b,
            d_branch,
            norm_all,
            joined_all,
            w_qkv,
            w_skip,
        )
        smalls = smalls[:, :used].reshape(4, -1)
        biases = w_up.shape[1] + 6 * model_width
        bias_sum = jnp.sum(smalls[:, :biases], axis=0)
        d_mod_all = smalls[:, biases:].reshape(-1, 6 * model_width)
        flow_all = flows[:, 0, : flow_times.shape[1]].reshape(-1)
        act_all = jax.nn.silu(time_embed(flow_all, model_width)).astype(jnp.bfloat16)
        g_w_skip, g_w_qkv, g_w_out, g_w_up, g_w_down = (
            grad.astype(jnp.float32) for grad in (g_w_skip, g_w_qkv, g_w_out, g_w_up, g_w_down)
        )
    else:
        g_w_down = weight_grad(gather_left(act_b), d_ff)
        g_w_up = weight_grad(gather_left(norm_f), d_inner_b)
        g_w_out = weight_grad(gather_left(attn_b), d_branch)
        d_attn = d_attn.reshape(local_rows, HEADS, HEAD_DIM)
        grad_acc = (d_attn / totals_rows[:, :, None]).astype(jnp.bfloat16)
        delta = jnp.transpose(jnp.sum(d_attn * attended, axis=2) / totals_rows)
        bwd_piece = partial(
            backward_piece,
            queries=queries,
            query_segment=segment,
            utt_ends=utt_ends,
            grad_acc=grad_acc,
            delta=delta,
        )
        zero_query = jnp.zeros((local_rows, HEADS, HEAD_DIM), jnp.float32)
        zero_all = jnp.zeros((2, local_rows * shards, model_width), jnp.float32)

        def block_fn(inner_state, portion, block_start):
            d_query_sum, d_all = inner_state
            d_query_add, d_block = bwd_piece(portion, block_start, True)
            return (
                d_query_sum + d_query_add,
                lax.dynamic_update_slice_in_dim(d_all, d_block, block_start, 1),
            )

        d_query, d_all = over_blocks(
            block_fn,
            (zero_query, zero_all),
            lax.all_gather(key_value, "seq", axis=1, tiled=True),
            jnp.int32(0),
            local_rows,
        )
        d_key_value = lax.psum_scatter(d_all, "seq", scatter_dimension=1, tiled=True)
        d_query_pre = unrotate(d_query, angle_cos, angle_sin).reshape(local_rows, model_width)
        d_key_pre = unrotate(
            d_key_value[0].reshape(local_rows, HEADS, HEAD_DIM), angle_cos, angle_sin
        ).reshape(local_rows, model_width)
        d_qkv = jnp.concatenate([d_query_pre, d_key_pre, d_key_value[1]], axis=1).astype(jnp.bfloat16)
        g_b_qkv = jnp.sum(d_qkv.astype(jnp.float32), axis=0)
        d_norm_a = back_product(d_qkv, w_qkv)
        _, norm_a_pull = jax.vjp(modulate, residual, scale_a, shift_a)
        d_resid_norm, d_scale_a, d_shift_a = norm_a_pull(d_norm_a)
        d_resid = (d_mid + d_resid_norm).astype(jnp.bfloat16)
        g_b_skip = jnp.sum(d_resid.astype(jnp.float32), axis=0)
        d_joined = back_product(d_resid, w_skip)
        d_mod_f = jnp.concatenate(
            [d_shift_a, d_scale_a, d_gate_a, d_shift_f, d_scale_f, d_gate_f], axis=1
        )
        d_mod_u = jnp.dot(jnp.transpose(member_f), d_mod_f, precision=HIGHEST_PRECISION)
        small = jnp.concatenate(
            [g_b_skip, g_b_qkv, g_b_out, g_b_up, g_b_down, d_mod_u.reshape(-1)]
        )
        biases = small.shape[0] - d_mod_u.size
        g_w_qkv = weight_grad(gather_left(norm_a), d_qkv)
        g_w_skip = weight_grad(gather_left(joined), d_resid)
        small = xor_sum(small.reshape(-1, 128), "seq").reshape(-1)
        bias_sum = xor_sum(small[:biases].reshape(-1, 128), "utt").reshape(-1)
        d_mod_all = gather_ordered(small[biases:].reshape(d_mod_u.shape), 0)
        act_all = gather_ordered(time_act, 0)
        g_frames = d_joined[:, :model_width].astype(jnp.bfloat16)
        g_skip_in = d_joined[:, model_width:].astype(jnp.bfloat16)
    act_all = act_all.astype(jnp.float32)
    own_width = model_width // shards
    act_own = lax.dynamic_slice_in_dim(act_all, seq_place * own_width, own_width, 1)
    g_w_mod = jnp.dot(jnp.transpose(act_own), d_mod_all, precision=HIGHEST_PRECISION)
    mod_width = d_mod_all.shape[1] // shards
    g_b_mod = jnp.sum(
        lax.dynamic_slice_in_dim(d_mod_all, seq_place * mod_width, mod_width, 1), axis=0
    )
    own_biases, offset = [], 0
    for size in (b_skip.shape[0], b_qkv.shape[0], b_out.shape[0], b_up.shape[0], b_down.shape[0]):
        width = size // shards
        own_biases.append(
            lax.dynamic_slice_in_dim(bias_sum, offset + seq_place * width, width, 0)
        )
        offset += size
    return (
        out_state.astype(jnp.bfloat16)[None],
        g_frames[None],
        g_skip_in[None],
        g_w_skip,
        own_biases[0],
        g_w_mod,
        g_b_mod,
        g_w_qkv,
        own_biases[1],
        g_w_out,
        own_biases[2],
        g_w_up,
        own_biases[3],
        g_w_down,
        own_biases[4],
    )


def solution(mesh):
    return jax.shard_map(
        local,
        mesh=mesh,
        in_specs=(
            P("utt", "seq", None),
            P("utt", "seq", None),
            P("utt", None),
            P("utt", None),
            P("utt", None),
            P("utt", "seq"),
            P("utt", "seq", None),
            P(),
            P(),
            P(),
            P(),
            P(),
            P(),
            P(),
            P(),
            P(),
            P(),
            P(),
            P(),
        ),
        out_specs=(
            P("utt", "seq", None),
            P("utt", "seq", None),
            P("utt", "seq", None),
            P("seq", None),
            P("seq"),
            P("seq", None),
            P("seq"),
            P("seq", None),
            P("seq"),
            P("seq", None),
            P("seq"),
            P("seq", None),
            P("seq"),
            P("seq", None),
            P("seq"),
        ),
        check_vma=False,
    )
```

```python
from functools import partial
import math

import jax
import jax.numpy as jnp
from jax import lax
from jax.experimental import pallas as pl
from jax.experimental.pallas import tpu as pltpu
from jax.sharding import PartitionSpec as P

HEADS = 16
HEAD_DIM = 64


HIGHEST_PRECISION = lax.Precision.HIGHEST
EPSILON = 1e-06


def layer_norm(values):
    average = jnp.mean(values, axis=-1, keepdims=True)
    centred = values - average
    spread = jnp.mean(centred * centred, axis=-1, keepdims=True)
    return centred * lax.rsqrt(spread + EPSILON)


def modulate(values, scale_part, shift_part):
    return layer_norm(values) * (1.0 + scale_part) + shift_part


def time_embed(flow_vals, model_width):
    half_dim = model_width // 2
    inverse = jnp.exp(-math.log(10000.0) * jnp.arange(half_dim, dtype=jnp.float32) / half_dim)
    angles = 1000.0 * flow_vals[:, None] * inverse[None, :]
    return jnp.concatenate([jnp.sin(angles), jnp.cos(angles)], axis=1)


def rotary_tables(position, head_size):
    half_dim = head_size // 2
    inverse = jnp.exp(
        -math.log(10000.0) * 2.0 * jnp.arange(half_dim, dtype=jnp.float32) / head_size
    )
    angles = position.astype(jnp.float32)[:, None] * inverse[None, :]
    return (jnp.cos(angles)[:, None, :], jnp.sin(angles)[:, None, :])


def rotate(tensor, angle_cos, angle_sin):
    half_dim = tensor.shape[-1] // 2
    leading = tensor[..., :half_dim]
    trailing = tensor[..., half_dim:]
    return jnp.concatenate(
        [leading * angle_cos - trailing * angle_sin, trailing * angle_cos + leading * angle_sin],
        axis=-1,
    )


def unrotate(gradient, angle_cos, angle_sin):
    half_dim = gradient.shape[-1] // 2
    leading = gradient[..., :half_dim]
    trailing = gradient[..., half_dim:]
    return jnp.concatenate(
        [leading * angle_cos + trailing * angle_sin, trailing * angle_cos - leading * angle_sin],
        axis=-1,
    )


def frame_tables(lengths, char_counts, first_frame, frame_count):
    utt_ends = jnp.cumsum(lengths)
    utt_starts = utt_ends - lengths
    frame_index = first_frame + jnp.arange(frame_count, dtype=jnp.int32)
    segment = jnp.sum((frame_index[:, None] >= utt_ends[None, :]).astype(jnp.int32), axis=1)
    member = segment[:, None] == jnp.arange(lengths.shape[0], dtype=jnp.int32)[None, :]
    position = frame_index - jnp.sum(jnp.where(member, utt_starts[None, :], 0), axis=1)
    prompt = jnp.sum(jnp.where(member, char_counts[None, :], 0), axis=1)
    return (segment, position, position >= prompt, member)


def key_segments(key_start, key_count, utt_ends):
    frame_index = key_start + jnp.arange(key_count, dtype=jnp.int32)
    return jnp.sum((frame_index[:, None] >= utt_ends[None, :]).astype(jnp.int32), axis=1)


def block_scores(queries, key_piece, query_segment, key_segment, usable):
    key_rows = key_piece.reshape(key_piece.shape[0], queries.shape[1], queries.shape[2])
    scores = (
        jnp.einsum("qhd,khd->hqk", queries, key_rows, preferred_element_type=jnp.float32) * 0.125
    )
    allowed = jnp.logical_and(query_segment[:, None] == key_segment[None, :], usable)
    return (jnp.where(allowed[None], jnp.exp(scores), 0.0), key_rows)


def over_blocks(block_fn, running, piece, key_start, shard_rows):
    key_count = piece.shape[1]
    shard_total = key_count // shard_rows
    group_size = max(1, min(shard_total, 1024 // shard_rows))
    while shard_total % group_size != 0:
        group_size = group_size - 1
    block_rows = group_size * shard_rows
    if block_rows == key_count:
        return block_fn(running, piece, key_start)

    def one_block(block_index, inner_state):
        portion = lax.dynamic_slice_in_dim(piece, block_index * block_rows, block_rows, 1)
        return block_fn(inner_state, portion, key_start + block_index * block_rows)

    return lax.fori_loop(0, key_count // block_rows, one_block, running)


def forward_piece(running, piece, key_start, usable, queries, query_segment, utt_ends):
    weighted, totals = running
    key_segment = key_segments(key_start, piece.shape[1], utt_ends)
    weights, key_rows = block_scores(queries, piece[0], query_segment, key_segment, usable)
    value_rows = piece[1].reshape(key_rows.shape)
    totals = totals + jnp.sum(weights, axis=2)
    weighted = weighted + jnp.einsum(
        "hqk,khd->qhd", weights.astype(jnp.bfloat16), value_rows, preferred_element_type=jnp.float32
    )
    return (weighted, totals)


def backward_piece(piece, key_start, usable, queries, query_segment, utt_ends, grad_acc, delta):
    key_count = piece.shape[1]
    key_segment = key_segments(key_start, key_count, utt_ends)
    weights, key_rows = block_scores(queries, piece[0], query_segment, key_segment, usable)
    value_rows = piece[1].reshape(key_rows.shape)
    value_dots = jnp.einsum(
        "qhd,khd->hqk", grad_acc, value_rows, preferred_element_type=jnp.float32
    )
    d_scores = (weights * (value_dots - delta[:, :, None])).astype(jnp.bfloat16)
    d_query = (
        jnp.einsum("hqk,khd->qhd", d_scores, key_rows, preferred_element_type=jnp.float32) * 0.125
    )
    d_key = (
        jnp.einsum("hqk,qhd->khd", d_scores, queries, preferred_element_type=jnp.float32) * 0.125
    )
    d_value = jnp.einsum(
        "hqk,qhd->khd", weights.astype(jnp.bfloat16), grad_acc, preferred_element_type=jnp.float32
    )
    return (
        d_query,
        jnp.stack([d_key.reshape(key_count, -1), d_value.reshape(key_count, -1)], axis=0),
    )


def back_product(gradient_rows, matrix):
    return jnp.einsum("fo,io->fi", gradient_rows, matrix, preferred_element_type=jnp.float32)


def xor_permute(value, axis_name, bit):
    size = lax.axis_size(axis_name)
    return lax.ppermute(value, axis_name, [(i, i ^ bit) for i in range(size)])


def bits_of(axis_name):
    size, bits, bit = lax.axis_size(axis_name), [], 1
    while bit < size:
        bits.append(bit)
        bit *= 2
    return bits


def xor_sum(value, axis_name):
    for bit in bits_of(axis_name):
        value = value + xor_permute(value, axis_name, bit)
    return value


def gather_left(rows):
    for bit in reversed(bits_of("utt")):
        rows = jnp.concatenate([rows, xor_permute(rows, "utt", bit)], axis=0)
    return rows


def gather_right(rows):
    place = lax.axis_index("utt")
    for bit in reversed(bits_of("utt")):
        mine = (place & bit) // bit
        width = rows.shape[1] // 2
        kept = lax.dynamic_slice_in_dim(rows, mine * width, width, 1)
        given = lax.dynamic_slice_in_dim(rows, (1 - mine) * width, width, 1)
        rows = jnp.concatenate([kept, xor_permute(given, "utt", bit)], axis=0)
    return rows


def gather_ordered(value, axis):
    place = lax.axis_index("utt")
    for bit in bits_of("utt"):
        other = xor_permute(value, "utt", bit)
        low = (place & bit) == 0
        value = jnp.concatenate(
            [jnp.where(low, value, other), jnp.where(low, other, value)], axis=axis
        )
    return value


def scatter_rows(tile):
    place = lax.axis_index("seq")
    for bit in bits_of("seq"):
        mine = (place & bit) // bit
        rest = lax.axis_size("seq") // (2 * bit)
        pieces = tile.reshape(rest, 2, -1, tile.shape[-1])
        kept = lax.dynamic_index_in_dim(pieces, mine, 1, keepdims=False)
        given = lax.dynamic_index_in_dim(pieces, 1 - mine, 1, keepdims=False)
        given = xor_permute(given, "seq", bit)
        tile = (kept.astype(jnp.float32) + given.astype(jnp.float32)).astype(jnp.bfloat16)
    return tile.reshape(-1, tile.shape[-1])


def weight_grad(left_all, right_rows):
    right_all = gather_right(right_rows)
    tile = jnp.einsum(
        "fi,fo->io", left_all, right_all, preferred_element_type=jnp.float32
    ).astype(jnp.bfloat16)
    tile = tile.reshape(-1, tile.shape[-1])
    piece = scatter_rows(tile)
    return gather_ordered(piece, 1).astype(jnp.float32)


def swap_halves(values, lower):
    return jnp.where(lower, pltpu.roll(values, 96, 1), pltpu.roll(values, 32, 1))


def lower_half(shape):
    return lax.broadcasted_iota(jnp.int32, shape, 1) % HEAD_DIM < HEAD_DIM // 2


def rotate_pack_kernel(q_ref, k_ref, v_ref, cos_ref, sin_ref, out_ref):
    lower = lower_half(q_ref.shape)
    cos, sin = cos_ref[...], sin_ref[...]
    q, k = q_ref[...], k_ref[...]
    out_ref[0, :, 0:128] = (q * cos + swap_halves(q, lower) * sin).astype(jnp.bfloat16)
    out_ref[0, :, 128:256] = (k * cos + swap_halves(k, lower) * sin).astype(jnp.bfloat16)
    out_ref[0, :, 256:384] = v_ref[...].astype(jnp.bfloat16)


def rotate_pack(qkv_full, cos, sin):
    rows = qkv_full.shape[0]
    blocks = qkv_full.shape[1] // 384
    table = pl.BlockSpec((rows, 128), lambda i: (0, 0))
    return pl.pallas_call(
        rotate_pack_kernel,
        grid=(blocks,),
        in_specs=[
            pl.BlockSpec((rows, 128), lambda i: (0, i)),
            pl.BlockSpec((rows, 128), lambda i: (0, blocks + i)),
            pl.BlockSpec((rows, 128), lambda i: (0, 2 * blocks + i)),
            table,
            table,
        ],
        out_specs=pl.BlockSpec((1, rows, 384), lambda i: (i, 0, 0)),
        out_shape=jax.ShapeDtypeStruct((blocks, rows, 384), jnp.bfloat16),
    )(qkv_full, qkv_full, qkv_full, cos, sin)


def head_scores(q, k, seg_q, seg_k):
    scores = lax.dot_general(q, k, (((1,), (1,)), ((), ())), preferred_element_type=jnp.float32)
    return jnp.where(seg_q == seg_k, jnp.exp(scores * 0.125), 0.0)


MESH = pl.DeviceIdType.MESH
VMEM_LIMIT = 62 * 1024 * 1024


def flip(index, bit):
    return index + bit - 2 * bit * ((index // bit) % 2)


def everywhere(memory):
    return pl.BlockSpec(memory_space=memory)


class Links:
    def __init__(self, send_sems, recv_sems, local_sems):
        self.send_sems, self.recv_sems, self.local_sems = send_sems, recv_sems, local_sems
        self.sent, self.held = [], 0
        self.utt, self.seq = lax.axis_index("utt"), lax.axis_index("seq")

    def enter(self, utt_peers, seq_peers):
        barrier = pltpu.get_barrier_semaphore()
        targets = [self.mate(r) for r in utt_peers] + [self.peer(r) for r in seq_peers]
        for target in targets:
            pl.semaphore_signal(barrier, inc=1, device_id=target, device_id_type=MESH)
        pl.semaphore_wait(barrier, len(targets))

    def mate(self, offset):
        return (self.utt_of(offset), self.seq)

    def utt_of(self, offset):
        place = self.utt
        for bit in (1, 2):
            if offset & bit:
                place = flip(place, bit)
        return place

    def seq_of(self, offset):
        place = self.seq
        for bit in (1, 2, 4):
            if offset & bit:
                place = flip(place, bit)
        return place

    def peer(self, offset):
        return (self.utt, self.seq_of(offset))

    def send(self, source, target, device):
        index = len(self.sent)
        copy = pltpu.make_async_remote_copy(
            src_ref=source,
            dst_ref=target,
            send_sem=self.send_sems.at[index],
            recv_sem=self.recv_sems.at[index],
            device_id=device,
            device_id_type=MESH,
        )
        copy.start()
        self.sent.append(copy)
        return copy

    def keep(self, source, target):
        copy = pltpu.make_async_copy(source, target, self.local_sems.at[self.held])
        self.held += 1
        copy.start()
        return copy

    def leave(self):
        assert len(self.sent) <= self.send_sems.shape[0]
        assert self.held <= self.local_sems.shape[0]
        for copy in self.sent:
            copy.wait_send()


class Gathered:
    def __init__(self, links, source, target, columns=None):
        self.links, self.target = links, target
        self.rows = source.shape[0]
        self.columns = columns
        self.own = links.keep(source, self.slot(0))
        self.across = links.send(source, self.slot(2), links.mate(2))
        self.beside = links.send(source, self.slot(1), links.mate(1))

    def slot(self, offset):
        rows = pl.ds(offset * self.rows, self.rows)
        if self.columns is None:
            return self.target.at[rows, :]
        return self.target.at[rows, self.columns]

    def relay(self):
        self.across.wait_recv()
        self.relayed = self.links.send(self.slot(2), self.slot(3), self.links.mate(1))

    def wait(self):
        self.own.wait()
        self.beside.wait_recv()
        self.relayed.wait_recv()


class Quarter:
    def __init__(self, links, piece_of, target):
        rows = target.shape[0] // 4
        slot = lambda r: target.at[pl.ds(r * rows, rows), :]
        self.own = links.keep(piece_of(links.utt), slot(0))
        self.copies = [
            links.send(piece_of(links.utt_of(r)), slot(r), links.mate(r)) for r in (2, 3, 1)
        ]

    def wait(self):
        self.own.wait()
        for copy in self.copies:
            copy.wait_recv()


class Share:
    def __init__(self, links, left, right, columns, tile, got_y, got_z1, got_z2, result):
        self.links = links
        self.left, self.right, self.columns = left, right, columns
        self.tile, self.got_y, self.got_z1, self.got_z2 = tile, got_y, got_z1, got_z2
        self.result = result
        seq = links.seq
        self.y, self.zl, self.zh = seq % 2, (seq // 2) % 2, seq // 4

    def product(self, y):
        rows = self.tile.shape[3]

        def block(z, _):
            base = pl.multiple_of((2 * z + y) * rows, rows)
            self.tile[z // 2, z % 2, y] = lax.dot_general(
                self.left[:, pl.ds(base, rows)],
                self.right[:, self.columns],
                (((0,), (0,)), ((), ())),
                preferred_element_type=jnp.float32,
            ).astype(jnp.bfloat16)
            return 0

        lax.fori_loop(0, 4, block, 0)

    def start(self):
        self.product(1 - self.y)
        self.sent_y = self.links.send(
            self.tile.at[:, :, 1 - self.y], self.got_y, self.links.peer(1)
        )
        self.product(self.y)

    def add(self, index, got):
        tile = self.tile
        tile[index] = (tile[index].astype(jnp.float32) + got.astype(jnp.float32)).astype(
            jnp.bfloat16
        )

    def after_y(self):
        self.sent_y.wait_recv()

        def block(zh, _):
            self.add((zh, 1 - self.zl, self.y), self.got_y[zh, 1 - self.zl])
            return 0

        lax.fori_loop(0, 2, block, 0)
        self.sent_z1 = self.links.send(
            self.tile.at[:, 1 - self.zl, self.y], self.got_z1, self.links.peer(2)
        )

        def rest(zh, _):
            self.add((zh, self.zl, self.y), self.got_y[zh, self.zl])
            return 0

        lax.fori_loop(0, 2, rest, 0)

    def after_z1(self):
        self.sent_z1.wait_recv()
        self.add((1 - self.zh, self.zl, self.y), self.got_z1[1 - self.zh])
        self.sent_z2 = self.links.send(
            self.tile.at[1 - self.zh, self.zl, self.y], self.got_z2, self.links.peer(4)
        )
        self.add((self.zh, self.zl, self.y), self.got_z1[self.zh])

    def after_z2(self):
        self.sent_z2.wait_recv()
        links = self.links
        mine = self.result(links.utt)
        mine[...] = (
            self.tile[self.zh, self.zl, self.y].astype(jnp.float32)
            + self.got_z2[...].astype(jnp.float32)
        ).astype(jnp.bfloat16)
        self.across = links.send(mine, mine, links.mate(2))
        self.beside = links.send(mine, mine, links.mate(1))

    def relay(self):
        self.across.wait_recv()
        links = self.links
        theirs = self.result(links.utt_of(2))
        self.relayed = links.send(theirs, theirs, links.mate(1))

    def wait(self):
        self.beside.wait_recv()
        self.relayed.wait_recv()


def share_scratch(rows, columns):
    return [
        pltpu.VMEM((2, 2, 2, rows, columns), jnp.bfloat16),
        pltpu.VMEM((2, 2, rows, columns), jnp.bfloat16),
        pltpu.VMEM((2, rows, columns), jnp.bfloat16),
        pltpu.VMEM((rows, columns), jnp.bfloat16),
    ]


def run_shares(shares, hooks):
    stages = ("after_y", "after_z1", "after_z2", "relay", "wait")
    for turn in range(len(shares) + len(stages) - 1):
        for hook in hooks.get(turn, ()):
            hook()
        for place, stage in enumerate(stages):
            if 0 <= turn - place < len(shares):
                getattr(shares[turn - place], stage)()


def semaphores(count):
    return [pltpu.SemaphoreType.DMA((count,))] * 2 + [pltpu.SemaphoreType.DMA((32,))]


def comm_params(collective_id):
    return pltpu.CompilerParams(
        collective_id=collective_id, has_side_effects=True, vmem_limit_bytes=VMEM_LIMIT
    )


def attend_kernel(
    packed_ref, segq_ref, segk_ref, counts_ref, flow_ref, norm_ref, frames_ref, skip_ref,
    attn_ref, heads_ref, exact_ref, total_ref, sums_ref, flows_ref, norm_all, joined_all,
    attn_heads, counts_got, send_sems, recv_sems, local_sems,
):
    links = Links(send_sems, recv_sems, local_sems)
    links.enter((1, 2, 3), range(1, 8))
    rows = packed_ref.shape[1]
    width = frames_ref.shape[1]
    own_rows = pl.ds(pl.multiple_of(links.seq * rows, rows), rows)
    own = links.keep(packed_ref.at[links.seq], heads_ref.at[own_rows, :])
    incoming = [
        links.send(packed_ref.at[links.seq_of(r)], heads_ref.at[own_rows, :], links.peer(r))
        for r in (6, 7, 4, 5, 2, 3, 1)
    ]
    flows_ref[links.utt] = flow_ref[...]
    flow_copies = [
        links.send(flow_ref, flows_ref.at[links.utt], links.mate(r)) for r in (1, 2, 3)
    ]
    gathers = [
        Gathered(links, norm_ref, norm_all),
        Gathered(links, frames_ref, joined_all, pl.ds(0, width)),
        Gathered(links, skip_ref, joined_all, pl.ds(width, width)),
    ]
    sums_ref[...] = counts_ref[...]
    for place, (target, source) in enumerate(
        ((links.mate(1), 0), (links.mate(2), 1), (links.peer(1), 2), (links.peer(2), 3),
         (links.peer(4), 4))
    ):
        counts_got[5 + place] = sums_ref[...]
        copy = links.send(counts_got.at[5 + place], counts_got.at[source], target)
        copy.wait_recv()
        sums_ref[...] = sums_ref[...] + counts_got[source]
    gathers[0].relay()
    own.wait()
    for copy in incoming:
        copy.wait_recv()
    first = lax.broadcasted_iota(jnp.int32, (256, 128), 1) < HEAD_DIM
    zero = jnp.zeros((256, 128), jnp.bfloat16)
    k, v = heads_ref[:, 128:256], heads_ref[:, 256:384]
    seg_k = segk_ref[...]

    def block(step, _):
        here = pl.ds(pl.multiple_of(step * 256, 256), 256)
        q, seg_q = heads_ref[here, 0:128], segq_ref[here, :]
        results = []
        for mine in (first, jnp.logical_not(first)):
            weights = head_scores(jnp.where(mine, q, zero), k, seg_q, seg_k)
            total = jnp.sum(weights, axis=1, keepdims=True)
            summed = jnp.dot(weights.astype(jnp.bfloat16), v, preferred_element_type=jnp.float32)
            results.append((summed, total))
        total = jnp.where(first, results[0][1], results[1][1])
        attended = jnp.where(first, results[0][0], results[1][0]) / total
        attn_heads[here, :] = attended.astype(jnp.bfloat16)
        exact_ref[here, :] = attended
        total_ref[here, :] = total
        return 0

    lax.fori_loop(0, heads_ref.shape[0] // 256, block, 0)
    column = attn_ref.at[:, pl.ds(pl.multiple_of(links.seq * 128, 128), 128)]
    part = lambda place: attn_heads.at[pl.ds(pl.multiple_of(place * rows, rows), rows), :]
    own = links.keep(part(links.seq), column)
    incoming = [
        links.send(part(links.seq_of(r)), column, links.peer(r)) for r in (6, 7, 4, 5, 2, 3, 1)
    ]
    for gather in gathers[1:]:
        gather.relay()
    for copy in flow_copies:
        copy.wait_recv()
    own.wait()
    for copy in incoming:
        copy.wait_recv()
    for gather in gathers:
        gather.wait()
    links.leave()


def attend(packed, seg_col, seg_row, counts, flow, norm_a, frames, skip):
    shards, rows, _ = packed.shape
    total_rows, width = shards * rows, norm_a.shape[1]
    vmem, there = everywhere(pltpu.VMEM), everywhere(pl.ANY)
    shape = jax.ShapeDtypeStruct
    return pl.pallas_call(
        attend_kernel,
        in_specs=[there, vmem, vmem, vmem, vmem, there, there, there],
        out_specs=[vmem] * 8,
        out_shape=[
            shape((rows, width), jnp.bfloat16),
            shape((total_rows, 384), jnp.bfloat16),
            shape((total_rows, 128), jnp.float32),
            shape((total_rows, 128), jnp.float32),
            shape(counts.shape, jnp.float32),
            shape((4,) + flow.shape, jnp.float32),
            shape((4 * rows, width), jnp.bfloat16),
            shape((4 * rows, 2 * width), jnp.bfloat16),
        ],
        scratch_shapes=[
            pltpu.VMEM((total_rows, 128), jnp.bfloat16),
            pltpu.VMEM((10,) + counts.shape, jnp.float32),
        ]
        + semaphores(40),
        compiler_params=comm_params(1),
    )(packed, seg_col, seg_row, counts, flow, norm_a, frames, skip)


ALONG = (((1,), (1,)), ((), ()))
DOWN = (((0,), (0,)), ((), ()))


def normal_parts(values):
    centred = values - jnp.mean(values, axis=1, keepdims=True)
    scale = lax.rsqrt(jnp.mean(centred * centred, axis=1, keepdims=True) + EPSILON)
    return centred * scale, scale


def normal_back(inward, unit, scale):
    return scale * (
        inward
        - jnp.mean(inward, axis=1, keepdims=True)
        - unit * jnp.mean(inward * unit, axis=1, keepdims=True)
    )


def column_sum(values):
    return jnp.sum(values.astype(jnp.float32), axis=0, keepdims=True)


def backward_kernel(
    utts, attn_ref, resid_ref, mod_ref, segment_ref, mask_ref, dropped_ref, counts_ref, out_grad_ref,
    b_out_ref, b_up_ref, b_down_ref,
    heads_ref, segq_ref, segk_ref, exact_ref, total_ref, cos_ref, sin_ref,
    norm_a_ref, joined_ref, w_out_ref, w_up_ref, w_down_ref, w_qkv_ref, w_skip_ref,
    mixed, g_down, g_up, g_out, g_qkv, g_skip, smalls, g_frames, g_skip_in,
    d_ff, norm_f, act, d_inner, d_branch, d_attn, pieces, d_mid, ff_sum, d_norm,
    grad_heads, d_heads, dk_ref, dv_ref,
    d_ff_all, act_all, norm_all, d_inner_all, attn_all, d_branch_all,
    norm_a_all, joined_all, d_qkv, d_qkv_all, d_resid, d_resid_all,
    up_ring, down_ring, w_out, w_qkv, w_skip, small_own, small_got, small_sum,
    *rest,
):
    tiles, (send_sems, recv_sems, local_sems, ring_sems) = rest[:-4], rest[-4:]
    links = Links(send_sems, recv_sems, local_sems)
    rows, model = resid_ref.shape
    block_width = up_ring.shape[2]
    steps = w_up_ref.shape[1] // block_width

    def ring(c):
        slot = c % 2
        columns = pl.ds(pl.multiple_of(c * block_width, block_width), block_width)
        return (
            pltpu.make_async_copy(w_up_ref.at[:, columns], up_ring.at[slot], ring_sems.at[slot]),
            pltpu.make_async_copy(
                w_down_ref.at[columns, :], down_ring.at[slot], ring_sems.at[2 + slot]
            ),
        )

    load_out = links.keep(w_out_ref, w_out)
    for c in (0, 1):
        for copy in ring(c):
            copy.start()
    loads = [
        links.keep(w_qkv_ref, w_qkv),
        links.keep(w_skip_ref, w_skip),
        links.keep(norm_a_ref, norm_a_all),
        links.keep(joined_ref, joined_all),
    ]
    links.enter((1, 2, 3), range(1, 8))

    def modulation(piece):
        columns = slice(piece * model, (piece + 1) * model)
        value = jnp.broadcast_to(mod_ref[0:1, columns], (rows, model))
        for u in range(1, utts):
            value = jnp.where(segment_ref[...] == u, mod_ref[u : u + 1, columns], value)
        return value

    n_drop, n_keep = counts_ref[0:1, 0:1], counts_ref[0:1, 1:2]
    dropped = dropped_ref[...]
    loss_weight = (
        mask_ref[...]
        * (n_drop + n_keep)
        * 0.5
        * (dropped / (n_drop + 1.0) + (1.0 - dropped) / (n_keep + 1.0))
    )

    def d_out():
        return out_grad_ref[...].astype(jnp.float32) * loss_weight

    d_ff[...] = (modulation(5) * d_out()).astype(jnp.bfloat16)
    gather_d = Gathered(links, d_ff, d_ff_all)
    load_out.wait()
    branch = (
        jnp.dot(attn_ref[...], w_out[...], preferred_element_type=jnp.float32) + b_out_ref[...]
    )
    pieces[0] = branch
    mid = resid_ref[...] + modulation(2) * branch
    d_mid[...] = mid
    unit, _ = normal_parts(mid)
    norm_f[...] = (unit * (1.0 + modulation(4)) + modulation(3)).astype(jnp.bfloat16)
    gather_n = Gathered(links, norm_f, norm_all)
    ff_sum[...] = jnp.zeros_like(ff_sum)
    d_norm[...] = jnp.zeros_like(d_norm)
    const = math.sqrt(2.0 / math.pi)

    def feed(c, _):
        slot = c % 2
        columns = pl.ds(pl.multiple_of(c * block_width, block_width), block_width)
        for copy in ring(c):
            copy.wait()
        inner = (
            jnp.dot(norm_f[...], up_ring[slot], preferred_element_type=jnp.float32)
            + b_up_ref[:, columns]
        )
        square = inner * inner
        slope = jnp.tanh(const * inner * (1.0 + 0.044715 * square))
        gate = 0.5 * (1.0 + slope)
        act_b = (inner * gate).astype(jnp.bfloat16)
        turn = gate + 0.5 * inner * (1.0 - slope * slope) * (
            const * (1.0 + 3.0 * 0.044715 * square)
        )
        here = pl.ds(pl.multiple_of(c * 128, 128), 128)
        for u in range(4):
            act[u, :, here] = act_b[:, u * 128 : (u + 1) * 128]
        d_act = lax.dot_general(
            d_ff[...], down_ring[slot], ALONG, preferred_element_type=jnp.float32
        )
        d_inner_b = (turn * d_act).astype(jnp.bfloat16)
        d_inner[:, columns] = d_inner_b
        ff_sum[...] += jnp.dot(act_b, down_ring[slot], preferred_element_type=jnp.float32)
        d_norm[...] += lax.dot_general(
            d_inner_b, up_ring[slot], ALONG, preferred_element_type=jnp.float32
        )

        @pl.when(c + 2 < steps)
        def _():
            for copy in ring(c + 2):
                copy.start()

        return 0

    lax.fori_loop(0, steps, feed, 0)
    far_first = (6, 7, 4, 5, 2, 3, 1)
    own_rows = pl.ds(pl.multiple_of(links.seq * rows, rows), rows)
    strip = lambda ref, place, size: ref.at[
        :, pl.ds(pl.multiple_of(place * size, size), size)
    ]
    width, narrow = d_inner_all.shape[1], d_branch_all.shape[1]
    gather_d.relay()
    quarter_a = Quarter(links, lambda u: act.at[u], act_all)
    quarter_i = Quarter(links, lambda u: strip(d_inner, u, width), d_inner_all)
    gather_b = Gathered(links, attn_ref, attn_all)
    mid = d_mid[...]
    unit, scale = normal_parts(mid)
    d_norm_f = d_norm[...]
    pieces[2] = d_norm_f * unit
    d_mid_f = d_out() + normal_back(d_norm_f * (1.0 + modulation(4)), unit, scale)
    gate_a = modulation(2)
    d_branch[...] = (gate_a * d_mid_f).astype(jnp.bfloat16)
    pieces[0] = pieces[0] * d_mid_f
    d_mid[...] = d_mid_f
    d_attn[...] = lax.dot_general(
        d_branch[...], w_out[...], ALONG, preferred_element_type=jnp.float32
    ).astype(jnp.bfloat16)
    own = links.keep(strip(d_attn, links.seq, 128), grad_heads.at[own_rows, :])
    incoming_d = [
        links.send(
            strip(d_attn, links.seq_of(r), 128), grad_heads.at[own_rows, :], links.peer(r)
        )
        for r in far_first
    ]
    quarter_b = Quarter(links, lambda u: strip(d_branch, u, narrow), d_branch_all)
    ff_out = ff_sum[...] + b_down_ref[...]
    mixed[...] = (mid + modulation(5) * ff_out).astype(jnp.bfloat16)
    pieces[1] = d_out() * ff_out
    small_own[...] = jnp.zeros_like(small_own)
    small_own[4:5, :] = column_sum(d_branch[...])
    for c in range(4):
        small_own[5 + c : 6 + c, :] = column_sum(d_inner[:, c * model : (c + 1) * model])
    small_own[9:10, :] = column_sum(d_ff[...])

    def utterance_sums(piece, values):
        for u in range(utts):
            row = 10 + 6 * u + piece
            small_own[row : row + 1, :] = jnp.sum(
                jnp.where(segment_ref[...] == u, values, 0.0), axis=0, keepdims=True
            )

    utterance_sums(2, pieces[0])
    utterance_sums(3, d_norm[...])
    utterance_sums(4, pieces[2])
    utterance_sums(5, pieces[1])
    half = width // 2
    down_at = lambda h: lambda u: g_down.at[
        pl.ds(pl.multiple_of(u * 128, 128), 128), pl.ds(h * half, half)
    ]
    column_at = lambda ref, step, offset, size: lambda u: ref.at[
        :, pl.ds(pl.multiple_of(u * step + offset, 128), size)
    ]
    wide, thin = d_qkv_all.shape[1], d_resid_all.shape[1]
    third = wide // 2
    plans = [
        (act_all, d_ff_all, pl.ds(0, half), down_at(0)),
        (act_all, d_ff_all, pl.ds(half, half), down_at(1)),
        (norm_all, d_inner_all, pl.ds(0, half), column_at(g_up, width, 0, half)),
        (norm_all, d_inner_all, pl.ds(half, half), column_at(g_up, width, half, half)),
        (attn_all, d_branch_all, pl.ds(0, narrow), column_at(g_out, narrow, 0, narrow)),
        (norm_a_all, d_qkv_all, pl.ds(0, third), column_at(g_qkv, wide, 0, third)),
        (norm_a_all, d_qkv_all, pl.ds(third, third), column_at(g_qkv, wide, third, third)),
        (joined_all, d_resid_all, pl.ds(0, thin), column_at(g_skip, thin, 0, thin)),
    ]
    shares = [
        Share(links, left, right, columns, *tiles[4 * i : 4 * i + 4], result)
        for i, (left, right, columns, result) in enumerate(plans)
    ]
    gather_n.relay()
    gather_d.wait()
    quarter_a.wait()
    shares[0].start()
    shares[1].start()
    own.wait()
    for copy in incoming_d:
        copy.wait_recv()
    dk_ref[...] = jnp.zeros_like(dk_ref)
    dv_ref[...] = jnp.zeros_like(dv_ref)
    first = lax.broadcasted_iota(jnp.int32, (256, 128), 1) < HEAD_DIM
    zero = jnp.zeros((256, 128), jnp.bfloat16)
    lower = lower_half((256, 128))
    k, v = heads_ref[:, 128:256], heads_ref[:, 256:384]
    seg_k = segk_ref[...]

    def turned(values, here):
        return (
            values * cos_ref[here, :] - swap_halves(values, lower) * sin_ref[here, :]
        ).astype(jnp.bfloat16)

    def block(step, _):
        here = pl.ds(pl.multiple_of(step * 256, 256), 256)
        q, seg_q = heads_ref[here, 0:128], segq_ref[here, :]
        scaled = grad_heads[here, :].astype(jnp.float32) / total_ref[here, :]
        grad_acc = scaled.astype(jnp.bfloat16)
        product = scaled * exact_ref[here, :]
        d_query = []
        for mine in (first, jnp.logical_not(first)):
            q_own = jnp.where(mine, q, zero)
            g_own = jnp.where(mine, grad_acc, zero)
            delta = jnp.sum(jnp.where(mine, product, 0.0), axis=1, keepdims=True)
            weights = head_scores(q_own, k, seg_q, seg_k)
            dots = lax.dot_general(g_own, v, ALONG, preferred_element_type=jnp.float32)
            d_scores = (weights * (dots - delta)).astype(jnp.bfloat16)
            d_query.append(jnp.dot(d_scores, k, preferred_element_type=jnp.float32))
            dk_ref[...] += lax.dot_general(
                d_scores, q_own, DOWN, preferred_element_type=jnp.float32
            )
            dv_ref[...] += lax.dot_general(
                weights.astype(jnp.bfloat16), g_own, DOWN, preferred_element_type=jnp.float32
            )
        d_heads[here, 0:128] = turned(jnp.where(first, d_query[0], d_query[1]) * 0.125, here)
        return 0

    blocks = heads_ref.shape[0] // 256
    lax.fori_loop(0, blocks, block, 0)

    def finish(step, _):
        here = pl.ds(pl.multiple_of(step * 256, 256), 256)
        d_heads[here, 128:256] = turned(dk_ref[here, :] * 0.125, here)
        d_heads[here, 256:384] = dv_ref[here, :].astype(jnp.bfloat16)
        return 0

    lax.fori_loop(0, blocks, finish, 0)
    part = lambda place, c: d_heads.at[
        pl.ds(pl.multiple_of(place * rows, rows), rows), pl.ds(c * 128, 128)
    ]
    home = lambda c: d_qkv.at[
        :, pl.ds(pl.multiple_of(c * model + links.seq * 128, 128), 128)
    ]
    owns = [links.keep(part(links.seq, c), home(c)) for c in range(3)]
    incoming = [
        links.send(part(links.seq_of(r), c), home(c), links.peer(r))
        for r in far_first
        for c in range(3)
    ]
    gather_n.wait()
    quarter_i.wait()
    shares[2].start()
    shares[3].start()
    gather_b.relay()
    gather_b.wait()
    quarter_b.wait()
    shares[4].start()
    state = {}

    def projections():
        for copy in owns:
            copy.wait()
        for copy in incoming:
            copy.wait_recv()
        for copy in loads:
            copy.wait()
        state["qkv"] = Quarter(links, lambda u: strip(d_qkv, u, wide), d_qkv_all)
        d_norm_a = lax.dot_general(
            d_qkv[...], w_qkv[...], ALONG, preferred_element_type=jnp.float32
        )
        unit, scale = normal_parts(resid_ref[...])
        d_resid_f = d_mid[...] + normal_back(d_norm_a * (1.0 + modulation(1)), unit, scale)
        rounded = d_resid_f.astype(jnp.bfloat16)
        d_resid[...] = rounded
        state["resid"] = Quarter(links, lambda u: strip(d_resid, u, thin), d_resid_all)
        small_own[0:1, :] = column_sum(rounded)
        for c in range(3):
            small_own[1 + c : 2 + c, :] = column_sum(d_qkv[:, c * model : (c + 1) * model])
        utterance_sums(0, d_norm_a)
        utterance_sums(1, d_norm_a * unit)
        state["small"] = links.send(small_own, small_got.at[0], links.peer(1))

    def last_shares():
        state["qkv"].wait()
        shares[5].start()
        shares[6].start()
        state["resid"].wait()
        shares[7].start()

    def inputs():
        for index, out in enumerate((g_frames, g_skip_in)):
            out[...] = lax.dot_general(
                d_resid[...],
                w_skip[pl.ds(index * model, model), :],
                ALONG,
                preferred_element_type=jnp.float32,
            ).astype(jnp.bfloat16)

    def small_y():
        state["small"].wait_recv()
        small_sum[0] = small_own[...] + small_got[0]
        state["small"] = links.send(small_sum.at[0], small_got.at[1], links.peer(2))

    def small_z1():
        state["small"].wait_recv()
        small_sum[1] = small_sum[0] + small_got[1]
        state["small"] = links.send(small_sum.at[1], small_got.at[2], links.peer(4))

    def small_z2():
        state["small"].wait_recv()
        mine = smalls.at[links.utt]
        mine[...] = small_sum[1] + small_got[2]
        state["spread"] = [links.send(mine, mine, links.mate(r)) for r in (2, 3, 1)]

    run_shares(
        shares,
        {
            1: (projections,),
            2: (last_shares,),
            3: (inputs, small_y),
            4: (small_z1,),
            5: (small_z2,),
        },
    )
    for copy in state["spread"]:
        copy.wait_recv()
    links.leave()


def backward(
    attn_b, resid, mod, segment, mask, dropped, counts, out_grad, b_out, b_up, b_down,
    heads, seg_col, seg_row, exact, total, cos, sin,
    norm_a_all, joined_all, w_out, w_up, w_down, w_qkv, w_skip,
):
    rows, model = resid.shape
    frames, inner = heads.shape[0], w_up.shape[1]
    utts = mod.shape[0]
    small = (-(-(10 + 6 * utts) // 8) * 8, model)
    mod = jnp.pad(mod, ((0, -utts % 8), (0, 0)))
    vmem, there = everywhere(pltpu.VMEM), everywhere(pl.ANY)
    shape = jax.ShapeDtypeStruct
    bf16 = lambda *dims: pltpu.VMEM(dims, jnp.bfloat16)
    f32 = lambda *dims: pltpu.VMEM(dims, jnp.float32)
    part, step = model // 8, inner // 8
    return pl.pallas_call(
        partial(backward_kernel, utts),
        in_specs=[vmem] * 18 + [there] * 7,
        out_specs=[vmem] * 9,
        out_shape=[
            shape((rows, model), jnp.bfloat16),
            shape((inner // 8, model), jnp.bfloat16),
            shape((part, inner), jnp.bfloat16),
            shape((part, model), jnp.bfloat16),
            shape((part, 3 * model), jnp.bfloat16),
            shape((2 * part, model), jnp.bfloat16),
            shape((4,) + small, jnp.float32),
            shape((rows, model), jnp.bfloat16),
            shape((rows, model), jnp.bfloat16),
        ],
        scratch_shapes=[
            bf16(rows, model),
            bf16(rows, model),
            bf16(4, rows, inner // 4),
            bf16(rows, inner),
            bf16(rows, model),
            bf16(rows, model),
            f32(3, rows, model),
            f32(rows, model),
            f32(rows, model),
            f32(rows, model),
            bf16(frames, 128),
            bf16(frames, 384),
            f32(frames, 128),
            f32(frames, 128),
            bf16(4 * rows, model),
            bf16(4 * rows, inner // 4),
            bf16(4 * rows, model),
            bf16(4 * rows, inner // 4),
            bf16(4 * rows, model),
            bf16(4 * rows, model // 4),
            bf16(4 * rows, model),
            bf16(4 * rows, 2 * model),
            bf16(rows, 3 * model),
            bf16(4 * rows, 3 * model // 4),
            bf16(rows, model),
            bf16(4 * rows, model // 4),
            bf16(2, model, step),
            bf16(2, step, model),
            bf16(*w_out.shape),
            bf16(*w_qkv.shape),
            bf16(*w_skip.shape),
            f32(*small),
            f32(3, *small),
            f32(2, *small),
        ]
        + share_scratch(part, inner // 8) * 4
        + share_scratch(part, model // 4)
        + share_scratch(part, 3 * model // 8) * 2
        + share_scratch(2 * part, model // 4)
        + semaphores(112)
        + [pltpu.SemaphoreType.DMA((4,))],
        compiler_params=comm_params(2),
    )(
        attn_b, resid, mod, segment, mask, dropped, counts, out_grad,
        b_out[None, :], b_up[None, :], b_down[None, :],
        heads, seg_col, seg_row, exact, total, cos, sin,
        norm_a_all, joined_all, w_out, w_up, w_down, w_qkv, w_skip,
    )


def wide_tables(position):
    half_dim = HEAD_DIM // 2
    lane = jnp.arange(128, dtype=jnp.int32) % HEAD_DIM
    inverse = jnp.exp(
        -math.log(10000.0) * 2.0 * (lane % half_dim).astype(jnp.float32) / HEAD_DIM
    )
    angles = position.astype(jnp.float32)[:, None] * inverse[None, :]
    sign = jnp.where(lane < half_dim, -1.0, 1.0)
    return jnp.cos(angles), jnp.sin(angles) * sign[None, :]


def local(
    frames_in,
    skip_in,
    flow_times,
    frame_lengths,
    char_lengths,
    drop_mask,
    out_grad,
    w_skip,
    b_skip,
    w_mod,
    b_mod,
    w_qkv,
    b_qkv,
    w_out,
    b_out,
    w_up,
    b_up,
    w_down,
    b_down,
):
    local_rows = frames_in.shape[1]
    model_width = frames_in.shape[2]
    shards = lax.axis_size("seq")
    seq_place = lax.axis_index("seq")
    lengths = frame_lengths[0]
    utt_ends = jnp.cumsum(lengths)
    segment, position, in_loss, member = frame_tables(
        lengths, char_lengths[0], seq_place * local_rows, local_rows
    )
    member_f = member.astype(jnp.float32)
    loss_mask = in_loss.astype(jnp.float32)
    dropped = drop_mask[0].astype(jnp.float32)
    counts = jnp.stack([jnp.sum(loss_mask * dropped), jnp.sum(loss_mask * (1.0 - dropped))])
    counts = jnp.pad(counts[None, :], ((0, 7), (0, 126)))
    whole = model_width * 4
    fused = (
        lax.axis_size("utt") == 4
        and shards == 8
        and HEADS * HEAD_DIM == 1024
        and w_up.shape[1] == whole
        and local_rows == 128
    )
    if not fused:
        counts = xor_sum(xor_sum(counts, "utt"), "seq")
    time_act = jax.nn.silu(time_embed(flow_times[0], model_width)).astype(jnp.bfloat16)
    mod_u = jnp.dot(time_act, w_mod, preferred_element_type=jnp.float32) + b_mod
    mod_f = jnp.dot(member_f, mod_u, precision=HIGHEST_PRECISION)
    shift_a, scale_a, gate_a, shift_f, scale_f, gate_f = jnp.split(mod_f, 6, axis=1)
    joined = jnp.concatenate([frames_in[0], skip_in[0]], axis=1)
    residual = jnp.dot(joined, w_skip, preferred_element_type=jnp.float32) + b_skip
    norm_a = modulate(residual, scale_a, shift_a).astype(jnp.bfloat16)
    qkv_full = jnp.dot(norm_a, w_qkv, preferred_element_type=jnp.float32) + b_qkv
    if fused:
        all_segment, all_position, _, _ = frame_tables(
            lengths, char_lengths[0], 0, local_rows * shards
        )
        cos_all, sin_all = wide_tables(all_position)
        cos_own, sin_own = wide_tables(position)
        seg_col, seg_row = all_segment[:, None], all_segment[None, :]
        flow = jnp.pad(flow_times, ((0, 7), (0, 128 - flow_times.shape[1])))
        attn_b, qkv_heads, exact, total, counts, flows, norm_all, joined_all = attend(
            rotate_pack(qkv_full, cos_own, sin_own),
            seg_col,
            seg_row,
            counts,
            flow,
            norm_a,
            frames_in[0],
            skip_in[0],
        )
    else:
        angle_cos, angle_sin = rotary_tables(position, HEAD_DIM)
        queries = rotate(
            qkv_full[:, :model_width].reshape(local_rows, HEADS, HEAD_DIM), angle_cos, angle_sin
        ).astype(jnp.bfloat16)
        key_rot = rotate(
            qkv_full[:, model_width : 2 * model_width].reshape(local_rows, HEADS, HEAD_DIM),
            angle_cos,
            angle_sin,
        ).astype(jnp.bfloat16)
        key_value = jnp.stack(
            [
                key_rot.reshape(local_rows, model_width),
                qkv_full[:, 2 * model_width :].astype(jnp.bfloat16),
            ],
            axis=0,
        )
        start_state = (
            jnp.zeros((local_rows, HEADS, HEAD_DIM), jnp.float32),
            jnp.zeros((HEADS, local_rows), jnp.float32),
        )
        fwd_piece = partial(forward_piece, queries=queries, query_segment=segment, utt_ends=utt_ends)
        weighted, totals = over_blocks(
            partial(fwd_piece, usable=True),
            start_state,
            lax.all_gather(key_value, "seq", axis=1, tiled=True),
            jnp.int32(0),
            local_rows,
        )
        totals_rows = jnp.transpose(totals)
        attended = weighted / totals_rows[:, :, None]
        attn_b = attended.reshape(local_rows, model_width).astype(jnp.bfloat16)
    if fused:
        column = lambda vector: vector[:, None]
        mixed, g_w_down, g_w_up, g_w_out, g_w_qkv, g_w_skip, smalls, g_frames, g_skip_in = backward(
            attn_b,
            residual,
            mod_u,
            column(segment),
            column(loss_mask),
            column(dropped),
            counts,
            out_grad[0],
            b_out,
            b_up,
            b_down,
            qkv_heads,
            seg_col,
            seg_row,
            exact,
            total,
            cos_all,
            sin_all,
            norm_all,
            joined_all,
            w_out,
            w_up,
            w_down,
            w_qkv,
            w_skip,
        )
        used = 10 + 6 * flow_times.shape[1]
        smalls = smalls[:, :used].reshape(4, -1)
        biases = w_up.shape[1] + 6 * model_width
        bias_sum = jnp.sum(smalls[:, :biases], axis=0)
        d_mod_all = smalls[:, biases:].reshape(-1, 6 * model_width)
        flow_all = flows[:, 0, : flow_times.shape[1]].reshape(-1)
        act_all = jax.nn.silu(time_embed(flow_all, model_width)).astype(jnp.bfloat16)
        g_w_skip, g_w_qkv, g_w_out, g_w_up, g_w_down = (
            grad.astype(jnp.float32) for grad in (g_w_skip, g_w_qkv, g_w_out, g_w_up, g_w_down)
        )
    else:
        n_drop, n_keep = counts[0, 0], counts[0, 1]
        loss_weight = (
            loss_mask
            * (n_drop + n_keep)
            * 0.5
            * (dropped / (n_drop + 1.0) + (1.0 - dropped) / (n_keep + 1.0))
        )
        branch = jnp.dot(attn_b, w_out, preferred_element_type=jnp.float32) + b_out
        mid_state = residual + gate_a * branch
        norm_f = modulate(mid_state, scale_f, shift_f).astype(jnp.bfloat16)
        ff_inner = jnp.dot(norm_f, w_up, preferred_element_type=jnp.float32) + b_up
        ff_act, gelu_pull = jax.vjp(partial(jax.nn.gelu, approximate=True), ff_inner)
        act_b = ff_act.astype(jnp.bfloat16)
        ff_out = jnp.dot(act_b, w_down, preferred_element_type=jnp.float32) + b_down
        out_state = mid_state + gate_f * ff_out
        d_out = out_grad[0].astype(jnp.float32) * loss_weight[:, None]
        d_ff = (gate_f * d_out).astype(jnp.bfloat16)
        d_gate_f = d_out * ff_out
        g_b_down = jnp.sum(d_ff.astype(jnp.float32), axis=0)
        (d_inner,) = gelu_pull(back_product(d_ff, w_down))
        d_inner_b = d_inner.astype(jnp.bfloat16)
        g_b_up = jnp.sum(d_inner_b.astype(jnp.float32), axis=0)
        d_norm_f = back_product(d_inner_b, w_up)
        _, norm_f_pull = jax.vjp(modulate, mid_state, scale_f, shift_f)
        d_mid_norm, d_scale_f, d_shift_f = norm_f_pull(d_norm_f)
        d_mid = d_out + d_mid_norm
        d_branch = (gate_a * d_mid).astype(jnp.bfloat16)
        d_gate_a = d_mid * branch
        g_b_out = jnp.sum(d_branch.astype(jnp.float32), axis=0)
        d_attn = back_product(d_branch, w_out)
        mixed = out_state.astype(jnp.bfloat16)
        g_w_down = weight_grad(gather_left(act_b), d_ff)
        g_w_up = weight_grad(gather_left(norm_f), d_inner_b)
        g_w_out = weight_grad(gather_left(attn_b), d_branch)
        d_attn = d_attn.reshape(local_rows, HEADS, HEAD_DIM)
        grad_acc = (d_attn / totals_rows[:, :, None]).astype(jnp.bfloat16)
        delta = jnp.transpose(jnp.sum(d_attn * attended, axis=2) / totals_rows)
        bwd_piece = partial(
            backward_piece,
            queries=queries,
            query_segment=segment,
            utt_ends=utt_ends,
            grad_acc=grad_acc,
            delta=delta,
        )
        zero_query = jnp.zeros((local_rows, HEADS, HEAD_DIM), jnp.float32)
        zero_all = jnp.zeros((2, local_rows * shards, model_width), jnp.float32)

        def block_fn(inner_state, portion, block_start):
            d_query_sum, d_all = inner_state
            d_query_add, d_block = bwd_piece(portion, block_start, True)
            return (
                d_query_sum + d_query_add,
                lax.dynamic_update_slice_in_dim(d_all, d_block, block_start, 1),
            )

        d_query, d_all = over_blocks(
            block_fn,
            (zero_query, zero_all),
            lax.all_gather(key_value, "seq", axis=1, tiled=True),
            jnp.int32(0),
            local_rows,
        )
        d_key_value = lax.psum_scatter(d_all, "seq", scatter_dimension=1, tiled=True)
        d_query_pre = unrotate(d_query, angle_cos, angle_sin).reshape(local_rows, model_width)
        d_key_pre = unrotate(
            d_key_value[0].reshape(local_rows, HEADS, HEAD_DIM), angle_cos, angle_sin
        ).reshape(local_rows, model_width)
        d_qkv = jnp.concatenate([d_query_pre, d_key_pre, d_key_value[1]], axis=1).astype(jnp.bfloat16)
        g_b_qkv = jnp.sum(d_qkv.astype(jnp.float32), axis=0)
        d_norm_a = back_product(d_qkv, w_qkv)
        _, norm_a_pull = jax.vjp(modulate, residual, scale_a, shift_a)
        d_resid_norm, d_scale_a, d_shift_a = norm_a_pull(d_norm_a)
        d_resid = (d_mid + d_resid_norm).astype(jnp.bfloat16)
        g_b_skip = jnp.sum(d_resid.astype(jnp.float32), axis=0)
        d_joined = back_product(d_resid, w_skip)
        d_mod_f = jnp.concatenate(
            [d_shift_a, d_scale_a, d_gate_a, d_shift_f, d_scale_f, d_gate_f], axis=1
        )
        d_mod_u = jnp.dot(jnp.transpose(member_f), d_mod_f, precision=HIGHEST_PRECISION)
        small = jnp.concatenate(
            [g_b_skip, g_b_qkv, g_b_out, g_b_up, g_b_down, d_mod_u.reshape(-1)]
        )
        biases = small.shape[0] - d_mod_u.size
        g_w_qkv = weight_grad(gather_left(norm_a), d_qkv)
        g_w_skip = weight_grad(gather_left(joined), d_resid)
        small = xor_sum(small.reshape(-1, 128), "seq").reshape(-1)
        bias_sum = xor_sum(small[:biases].reshape(-1, 128), "utt").reshape(-1)
        d_mod_all = gather_ordered(small[biases:].reshape(d_mod_u.shape), 0)
        act_all = gather_ordered(time_act, 0)
        g_frames = d_joined[:, :model_width].astype(jnp.bfloat16)
        g_skip_in = d_joined[:, model_width:].astype(jnp.bfloat16)
    act_all = act_all.astype(jnp.float32)
    own_width = model_width // shards
    act_own = lax.dynamic_slice_in_dim(act_all, seq_place * own_width, own_width, 1)
    g_w_mod = jnp.dot(jnp.transpose(act_own), d_mod_all, precision=HIGHEST_PRECISION)
    mod_width = d_mod_all.shape[1] // shards
    g_b_mod = jnp.sum(
        lax.dynamic_slice_in_dim(d_mod_all, seq_place * mod_width, mod_width, 1), axis=0
    )
    own_biases, offset = [], 0
    for size in (b_skip.shape[0], b_qkv.shape[0], b_out.shape[0], b_up.shape[0], b_down.shape[0]):
        width = size // shards
        own_biases.append(
            lax.dynamic_slice_in_dim(bias_sum, offset + seq_place * width, width, 0)
        )
        offset += size
    return (
        mixed[None],
        g_frames[None],
        g_skip_in[None],
        g_w_skip,
        own_biases[0],
        g_w_mod,
        g_b_mod,
        g_w_qkv,
        own_biases[1],
        g_w_out,
        own_biases[2],
        g_w_up,
        own_biases[3],
        g_w_down,
        own_biases[4],
    )


def solution(mesh):
    return jax.shard_map(
        local,
        mesh=mesh,
        in_specs=(
            P("utt", "seq", None),
            P("utt", "seq", None),
            P("utt", None),
            P("utt", None),
            P("utt", None),
            P("utt", "seq"),
            P("utt", "seq", None),
            P(),
            P(),
            P(),
            P(),
            P(),
            P(),
            P(),
            P(),
            P(),
            P(),
            P(),
            P(),
        ),
        out_specs=(
            P("utt", "seq", None),
            P("utt", "seq", None),
            P("utt", "seq", None),
            P("seq", None),
            P("seq"),
            P("seq", None),
            P("seq"),
            P("seq", None),
            P("seq"),
            P("seq", None),
            P("seq"),
            P("seq", None),
            P("seq"),
            P("seq", None),
            P("seq"),
        ),
        check_vma=False,
    )
```

```python
from functools import partial
import math

import jax
import jax.numpy as jnp
from jax import lax
from jax.experimental import pallas as pl
from jax.experimental.pallas import tpu as pltpu
from jax.sharding import PartitionSpec as P

HEADS = 16
HEAD_DIM = 64


HIGHEST_PRECISION = lax.Precision.HIGHEST
EPSILON = 1e-06


def layer_norm(values):
    average = jnp.mean(values, axis=-1, keepdims=True)
    centred = values - average
    spread = jnp.mean(centred * centred, axis=-1, keepdims=True)
    return centred * lax.rsqrt(spread + EPSILON)


def modulate(values, scale_part, shift_part):
    return layer_norm(values) * (1.0 + scale_part) + shift_part


def time_embed(flow_vals, model_width):
    half_dim = model_width // 2
    inverse = jnp.exp(-math.log(10000.0) * jnp.arange(half_dim, dtype=jnp.float32) / half_dim)
    angles = 1000.0 * flow_vals[:, None] * inverse[None, :]
    return jnp.concatenate([jnp.sin(angles), jnp.cos(angles)], axis=1)


def rotary_tables(position, head_size):
    half_dim = head_size // 2
    inverse = jnp.exp(
        -math.log(10000.0) * 2.0 * jnp.arange(half_dim, dtype=jnp.float32) / head_size
    )
    angles = position.astype(jnp.float32)[:, None] * inverse[None, :]
    return (jnp.cos(angles)[:, None, :], jnp.sin(angles)[:, None, :])


def rotate(tensor, angle_cos, angle_sin):
    half_dim = tensor.shape[-1] // 2
    leading = tensor[..., :half_dim]
    trailing = tensor[..., half_dim:]
    return jnp.concatenate(
        [leading * angle_cos - trailing * angle_sin, trailing * angle_cos + leading * angle_sin],
        axis=-1,
    )


def unrotate(gradient, angle_cos, angle_sin):
    half_dim = gradient.shape[-1] // 2
    leading = gradient[..., :half_dim]
    trailing = gradient[..., half_dim:]
    return jnp.concatenate(
        [leading * angle_cos + trailing * angle_sin, trailing * angle_cos - leading * angle_sin],
        axis=-1,
    )


def frame_tables(lengths, char_counts, first_frame, frame_count):
    utt_ends = jnp.cumsum(lengths)
    utt_starts = utt_ends - lengths
    frame_index = first_frame + jnp.arange(frame_count, dtype=jnp.int32)
    segment = jnp.sum((frame_index[:, None] >= utt_ends[None, :]).astype(jnp.int32), axis=1)
    member = segment[:, None] == jnp.arange(lengths.shape[0], dtype=jnp.int32)[None, :]
    position = frame_index - jnp.sum(jnp.where(member, utt_starts[None, :], 0), axis=1)
    prompt = jnp.sum(jnp.where(member, char_counts[None, :], 0), axis=1)
    return (segment, position, position >= prompt, member)


def key_segments(key_start, key_count, utt_ends):
    frame_index = key_start + jnp.arange(key_count, dtype=jnp.int32)
    return jnp.sum((frame_index[:, None] >= utt_ends[None, :]).astype(jnp.int32), axis=1)


def block_scores(queries, key_piece, query_segment, key_segment, usable):
    key_rows = key_piece.reshape(key_piece.shape[0], queries.shape[1], queries.shape[2])
    scores = (
        jnp.einsum("qhd,khd->hqk", queries, key_rows, preferred_element_type=jnp.float32) * 0.125
    )
    allowed = jnp.logical_and(query_segment[:, None] == key_segment[None, :], usable)
    return (jnp.where(allowed[None], jnp.exp(scores), 0.0), key_rows)


def over_blocks(block_fn, running, piece, key_start, shard_rows):
    key_count = piece.shape[1]
    shard_total = key_count // shard_rows
    group_size = max(1, min(shard_total, 1024 // shard_rows))
    while shard_total % group_size != 0:
        group_size = group_size - 1
    block_rows = group_size * shard_rows
    if block_rows == key_count:
        return block_fn(running, piece, key_start)

    def one_block(block_index, inner_state):
        portion = lax.dynamic_slice_in_dim(piece, block_index * block_rows, block_rows, 1)
        return block_fn(inner_state, portion, key_start + block_index * block_rows)

    return lax.fori_loop(0, key_count // block_rows, one_block, running)


def forward_piece(running, piece, key_start, usable, queries, query_segment, utt_ends):
    weighted, totals = running
    key_segment = key_segments(key_start, piece.shape[1], utt_ends)
    weights, key_rows = block_scores(queries, piece[0], query_segment, key_segment, usable)
    value_rows = piece[1].reshape(key_rows.shape)
    totals = totals + jnp.sum(weights, axis=2)
    weighted = weighted + jnp.einsum(
        "hqk,khd->qhd", weights.astype(jnp.bfloat16), value_rows, preferred_element_type=jnp.float32
    )
    return (weighted, totals)


def backward_piece(piece, key_start, usable, queries, query_segment, utt_ends, grad_acc, delta):
    key_count = piece.shape[1]
    key_segment = key_segments(key_start, key_count, utt_ends)
    weights, key_rows = block_scores(queries, piece[0], query_segment, key_segment, usable)
    value_rows = piece[1].reshape(key_rows.shape)
    value_dots = jnp.einsum(
        "qhd,khd->hqk", grad_acc, value_rows, preferred_element_type=jnp.float32
    )
    d_scores = (weights * (value_dots - delta[:, :, None])).astype(jnp.bfloat16)
    d_query = (
        jnp.einsum("hqk,khd->qhd", d_scores, key_rows, preferred_element_type=jnp.float32) * 0.125
    )
    d_key = (
        jnp.einsum("hqk,qhd->khd", d_scores, queries, preferred_element_type=jnp.float32) * 0.125
    )
    d_value = jnp.einsum(
        "hqk,qhd->khd", weights.astype(jnp.bfloat16), grad_acc, preferred_element_type=jnp.float32
    )
    return (
        d_query,
        jnp.stack([d_key.reshape(key_count, -1), d_value.reshape(key_count, -1)], axis=0),
    )


def back_product(gradient_rows, matrix):
    return jnp.einsum("fo,io->fi", gradient_rows, matrix, preferred_element_type=jnp.float32)


def xor_permute(value, axis_name, bit):
    size = lax.axis_size(axis_name)
    return lax.ppermute(value, axis_name, [(i, i ^ bit) for i in range(size)])


def bits_of(axis_name):
    size, bits, bit = lax.axis_size(axis_name), [], 1
    while bit < size:
        bits.append(bit)
        bit *= 2
    return bits


def xor_sum(value, axis_name):
    for bit in bits_of(axis_name):
        value = value + xor_permute(value, axis_name, bit)
    return value


def gather_left(rows):
    for bit in reversed(bits_of("utt")):
        rows = jnp.concatenate([rows, xor_permute(rows, "utt", bit)], axis=0)
    return rows


def gather_right(rows):
    place = lax.axis_index("utt")
    for bit in reversed(bits_of("utt")):
        mine = (place & bit) // bit
        width = rows.shape[1] // 2
        kept = lax.dynamic_slice_in_dim(rows, mine * width, width, 1)
        given = lax.dynamic_slice_in_dim(rows, (1 - mine) * width, width, 1)
        rows = jnp.concatenate([kept, xor_permute(given, "utt", bit)], axis=0)
    return rows


def gather_ordered(value, axis):
    place = lax.axis_index("utt")
    for bit in bits_of("utt"):
        other = xor_permute(value, "utt", bit)
        low = (place & bit) == 0
        value = jnp.concatenate(
            [jnp.where(low, value, other), jnp.where(low, other, value)], axis=axis
        )
    return value


def scatter_rows(tile):
    place = lax.axis_index("seq")
    for bit in bits_of("seq"):
        mine = (place & bit) // bit
        rest = lax.axis_size("seq") // (2 * bit)
        pieces = tile.reshape(rest, 2, -1, tile.shape[-1])
        kept = lax.dynamic_index_in_dim(pieces, mine, 1, keepdims=False)
        given = lax.dynamic_index_in_dim(pieces, 1 - mine, 1, keepdims=False)
        given = xor_permute(given, "seq", bit)
        tile = (kept.astype(jnp.float32) + given.astype(jnp.float32)).astype(jnp.bfloat16)
    return tile.reshape(-1, tile.shape[-1])


def weight_grad(left_all, right_rows):
    right_all = gather_right(right_rows)
    tile = jnp.einsum(
        "fi,fo->io", left_all, right_all, preferred_element_type=jnp.float32
    ).astype(jnp.bfloat16)
    tile = tile.reshape(-1, tile.shape[-1])
    piece = scatter_rows(tile)
    return gather_ordered(piece, 1).astype(jnp.float32)


def swap_halves(values, lower):
    return jnp.where(lower, pltpu.roll(values, 96, 1), pltpu.roll(values, 32, 1))


def lower_half(shape):
    return lax.broadcasted_iota(jnp.int32, shape, 1) % HEAD_DIM < HEAD_DIM // 2


def rotate_pack_kernel(q_ref, k_ref, v_ref, cos_ref, sin_ref, out_ref):
    lower = lower_half(q_ref.shape)
    cos, sin = cos_ref[...], sin_ref[...]
    q, k = q_ref[...], k_ref[...]
    out_ref[0, :, 0:128] = (q * cos + swap_halves(q, lower) * sin).astype(jnp.bfloat16)
    out_ref[0, :, 128:256] = (k * cos + swap_halves(k, lower) * sin).astype(jnp.bfloat16)
    out_ref[0, :, 256:384] = v_ref[...].astype(jnp.bfloat16)


def rotate_pack(qkv_full, cos, sin):
    rows = qkv_full.shape[0]
    blocks = qkv_full.shape[1] // 384
    table = pl.BlockSpec((rows, 128), lambda i: (0, 0))
    return pl.pallas_call(
        rotate_pack_kernel,
        grid=(blocks,),
        in_specs=[
            pl.BlockSpec((rows, 128), lambda i: (0, i)),
            pl.BlockSpec((rows, 128), lambda i: (0, blocks + i)),
            pl.BlockSpec((rows, 128), lambda i: (0, 2 * blocks + i)),
            table,
            table,
        ],
        out_specs=pl.BlockSpec((1, rows, 384), lambda i: (i, 0, 0)),
        out_shape=jax.ShapeDtypeStruct((blocks, rows, 384), jnp.bfloat16),
    )(qkv_full, qkv_full, qkv_full, cos, sin)


def head_scores(q, k, seg_q, seg_k):
    scores = lax.dot_general(q, k, (((1,), (1,)), ((), ())), preferred_element_type=jnp.float32)
    return jnp.where(seg_q == seg_k, jnp.exp(scores * 0.125), 0.0)


MESH = pl.DeviceIdType.MESH
VMEM_LIMIT = 62 * 1024 * 1024


def flip(index, bit):
    return index + bit - 2 * bit * ((index // bit) % 2)


def everywhere(memory):
    return pl.BlockSpec(memory_space=memory)


class Links:
    def __init__(self, send_sems, recv_sems, local_sems):
        self.send_sems, self.recv_sems, self.local_sems = send_sems, recv_sems, local_sems
        self.sent, self.held = [], 0
        self.utt, self.seq = lax.axis_index("utt"), lax.axis_index("seq")

    def enter(self, utt_peers, seq_peers):
        barrier = pltpu.get_barrier_semaphore()
        targets = [self.mate(r) for r in utt_peers] + [self.peer(r) for r in seq_peers]
        for target in targets:
            pl.semaphore_signal(barrier, inc=1, device_id=target, device_id_type=MESH)
        pl.semaphore_wait(barrier, len(targets))

    def mate(self, offset):
        return (self.utt_of(offset), self.seq)

    def utt_of(self, offset):
        place = self.utt
        for bit in (1, 2):
            if offset & bit:
                place = flip(place, bit)
        return place

    def seq_of(self, offset):
        place = self.seq
        for bit in (1, 2, 4):
            if offset & bit:
                place = flip(place, bit)
        return place

    def peer(self, offset):
        return (self.utt, self.seq_of(offset))

    def send(self, source, target, device):
        index = len(self.sent)
        copy = pltpu.make_async_remote_copy(
            src_ref=source,
            dst_ref=target,
            send_sem=self.send_sems.at[index],
            recv_sem=self.recv_sems.at[index],
            device_id=device,
            device_id_type=MESH,
        )
        copy.start()
        self.sent.append(copy)
        return copy

    def keep(self, source, target):
        copy = pltpu.make_async_copy(source, target, self.local_sems.at[self.held])
        self.held += 1
        copy.start()
        return copy

    def leave(self):
        assert len(self.sent) <= self.send_sems.shape[0]
        assert self.held <= self.local_sems.shape[0]
        for copy in self.sent:
            copy.wait_send()


class Gathered:
    def __init__(self, links, source, target, columns=None):
        self.links, self.target = links, target
        self.rows = source.shape[0]
        self.columns = columns
        self.own = links.keep(source, self.slot(0))
        self.across = links.send(source, self.slot(2), links.mate(2))
        self.beside = links.send(source, self.slot(1), links.mate(1))

    def slot(self, offset):
        rows = pl.ds(offset * self.rows, self.rows)
        if self.columns is None:
            return self.target.at[rows, :]
        return self.target.at[rows, self.columns]

    def relay(self):
        self.across.wait_recv()
        self.relayed = self.links.send(self.slot(2), self.slot(3), self.links.mate(1))

    def wait(self):
        self.own.wait()
        self.beside.wait_recv()
        self.relayed.wait_recv()


class Quarter:
    def __init__(self, links, piece_of, target):
        rows = target.shape[0] // 4
        slot = lambda r: target.at[pl.ds(r * rows, rows), :]
        self.own = links.keep(piece_of(links.utt), slot(0))
        self.copies = [
            links.send(piece_of(links.utt_of(r)), slot(r), links.mate(r)) for r in (2, 3, 1)
        ]

    def wait(self):
        self.own.wait()
        for copy in self.copies:
            copy.wait_recv()


class Share:
    def __init__(self, links, y_first, left, right, columns, tile, got_a, got_b, got_z2, result):
        self.links, self.y_first = links, y_first
        self.left, self.right, self.columns = left, right, columns
        self.tile, self.got_a, self.got_b, self.got_z2 = tile, got_a, got_b, got_z2
        self.result = result
        seq = links.seq
        self.y, self.zl, self.zh = seq % 2, (seq // 2) % 2, seq // 4
        if y_first:
            self.a, self.b, self.peers = self.y, self.zl, (1, 2)
        else:
            self.a, self.b, self.peers = self.zl, self.y, (2, 1)

    def place(self, zh, a, b):
        return (zh, b, a) if self.y_first else (zh, a, b)

    def product(self, a):
        rows = self.tile.shape[3]

        def block(step, _):
            zh, b = step // 2, step % 2
            here = self.place(zh, a, b)
            base = pl.multiple_of((4 * zh + 2 * here[1] + here[2]) * rows, rows)
            self.tile[here] = lax.dot_general(
                self.left[:, pl.ds(base, rows)],
                self.right[:, self.columns],
                (((0,), (0,)), ((), ())),
                preferred_element_type=jnp.float32,
            ).astype(jnp.bfloat16)
            return 0

        lax.fori_loop(0, 4, block, 0)

    def start(self):
        self.product(1 - self.a)
        given = (
            self.tile.at[:, :, 1 - self.a] if self.y_first else self.tile.at[:, 1 - self.a]
        )
        self.sent_a = self.links.send(given, self.got_a, self.links.peer(self.peers[0]))
        self.product(self.a)

    def add(self, index, got):
        tile = self.tile
        tile[index] = (tile[index].astype(jnp.float32) + got.astype(jnp.float32)).astype(
            jnp.bfloat16
        )

    def after_a(self):
        self.sent_a.wait_recv()

        def block(zh, _):
            self.add(self.place(zh, self.a, 1 - self.b), self.got_a[zh, 1 - self.b])
            return 0

        lax.fori_loop(0, 2, block, 0)
        _, low, y = self.place(0, self.a, 1 - self.b)
        self.sent_b = self.links.send(
            self.tile.at[:, low, y], self.got_b, self.links.peer(self.peers[1])
        )

        def rest(zh, _):
            self.add(self.place(zh, self.a, self.b), self.got_a[zh, self.b])
            return 0

        lax.fori_loop(0, 2, rest, 0)

    def after_b(self):
        self.sent_b.wait_recv()
        self.add((1 - self.zh, self.zl, self.y), self.got_b[1 - self.zh])
        self.sent_z2 = self.links.send(
            self.tile.at[1 - self.zh, self.zl, self.y], self.got_z2, self.links.peer(4)
        )
        self.add((self.zh, self.zl, self.y), self.got_b[self.zh])

    def after_z2(self):
        self.sent_z2.wait_recv()
        links = self.links
        mine = self.result(links.utt)
        mine[...] = (
            self.tile[self.zh, self.zl, self.y].astype(jnp.float32)
            + self.got_z2[...].astype(jnp.float32)
        ).astype(jnp.bfloat16)
        self.across = links.send(mine, mine, links.mate(2))
        self.beside = links.send(mine, mine, links.mate(1))

    def relay(self):
        self.across.wait_recv()
        links = self.links
        theirs = self.result(links.utt_of(2))
        self.relayed = links.send(theirs, theirs, links.mate(1))

    def wait(self):
        self.beside.wait_recv()
        self.relayed.wait_recv()


def share_scratch(rows, columns):
    return [
        pltpu.VMEM((2, 2, 2, rows, columns), jnp.bfloat16),
        pltpu.VMEM((2, 2, rows, columns), jnp.bfloat16),
        pltpu.VMEM((2, rows, columns), jnp.bfloat16),
        pltpu.VMEM((rows, columns), jnp.bfloat16),
    ]


def run_shares(shares, hooks):
    stages = ("after_a", "after_b", "after_z2", "relay", "wait")
    for turn in range(len(shares) + len(stages) - 1):
        for hook in hooks.get(turn, ()):
            hook()
        for place, stage in enumerate(stages):
            if 0 <= turn - place < len(shares):
                getattr(shares[turn - place], stage)()


def semaphores(count):
    return [pltpu.SemaphoreType.DMA((count,))] * 2 + [pltpu.SemaphoreType.DMA((32,))]


def comm_params(collective_id):
    return pltpu.CompilerParams(
        collective_id=collective_id, has_side_effects=True, vmem_limit_bytes=VMEM_LIMIT
    )


def attend_kernel(
    packed_ref, segq_ref, segk_ref, counts_ref, flow_ref, norm_ref, frames_ref, skip_ref,
    attn_ref, heads_ref, exact_ref, total_ref, sums_ref, flows_ref, norm_all, joined_all,
    attn_heads, counts_got, send_sems, recv_sems, local_sems,
):
    links = Links(send_sems, recv_sems, local_sems)
    links.enter((1, 2, 3), range(1, 8))
    rows = packed_ref.shape[1]
    width = frames_ref.shape[1]
    own_rows = pl.ds(pl.multiple_of(links.seq * rows, rows), rows)
    own = links.keep(packed_ref.at[links.seq], heads_ref.at[own_rows, :])
    incoming = [
        links.send(packed_ref.at[links.seq_of(r)], heads_ref.at[own_rows, :], links.peer(r))
        for r in (6, 7, 4, 5, 2, 3, 1)
    ]
    flows_ref[links.utt] = flow_ref[...]
    flow_copies = [
        links.send(flow_ref, flows_ref.at[links.utt], links.mate(r)) for r in (1, 2, 3)
    ]
    gathers = [
        Gathered(links, norm_ref, norm_all),
        Gathered(links, frames_ref, joined_all, pl.ds(0, width)),
        Gathered(links, skip_ref, joined_all, pl.ds(width, width)),
    ]
    sums_ref[...] = counts_ref[...]
    for place, (target, source) in enumerate(
        ((links.mate(1), 0), (links.mate(2), 1), (links.peer(1), 2), (links.peer(2), 3),
         (links.peer(4), 4))
    ):
        counts_got[5 + place] = sums_ref[...]
        copy = links.send(counts_got.at[5 + place], counts_got.at[source], target)
        copy.wait_recv()
        sums_ref[...] = sums_ref[...] + counts_got[source]
    gathers[0].relay()
    own.wait()
    for copy in incoming:
        copy.wait_recv()
    first = lax.broadcasted_iota(jnp.int32, (256, 128), 1) < HEAD_DIM
    zero = jnp.zeros((256, 128), jnp.bfloat16)
    k, v = heads_ref[:, 128:256], heads_ref[:, 256:384]
    seg_k = segk_ref[...]

    def block(step, _):
        here = pl.ds(pl.multiple_of(step * 256, 256), 256)
        q, seg_q = heads_ref[here, 0:128], segq_ref[here, :]
        results = []
        for mine in (first, jnp.logical_not(first)):
            weights = head_scores(jnp.where(mine, q, zero), k, seg_q, seg_k)
            total = jnp.sum(weights, axis=1, keepdims=True)
            summed = jnp.dot(weights.astype(jnp.bfloat16), v, preferred_element_type=jnp.float32)
            results.append((summed, total))
        total = jnp.where(first, results[0][1], results[1][1])
        attended = jnp.where(first, results[0][0], results[1][0]) / total
        attn_heads[here, :] = attended.astype(jnp.bfloat16)
        exact_ref[here, :] = attended
        total_ref[here, :] = total
        return 0

    lax.fori_loop(0, heads_ref.shape[0] // 256, block, 0)
    column = attn_ref.at[:, pl.ds(pl.multiple_of(links.seq * 128, 128), 128)]
    part = lambda place: attn_heads.at[pl.ds(pl.multiple_of(place * rows, rows), rows), :]
    own = links.keep(part(links.seq), column)
    incoming = [
        links.send(part(links.seq_of(r)), column, links.peer(r)) for r in (6, 7, 4, 5, 2, 3, 1)
    ]
    for gather in gathers[1:]:
        gather.relay()
    for copy in flow_copies:
        copy.wait_recv()
    own.wait()
    for copy in incoming:
        copy.wait_recv()
    for gather in gathers:
        gather.wait()
    links.leave()


def attend(packed, seg_col, seg_row, counts, flow, norm_a, frames, skip):
    shards, rows, _ = packed.shape
    total_rows, width = shards * rows, norm_a.shape[1]
    vmem, there = everywhere(pltpu.VMEM), everywhere(pl.ANY)
    shape = jax.ShapeDtypeStruct
    return pl.pallas_call(
        attend_kernel,
        in_specs=[there, vmem, vmem, vmem, vmem, there, there, there],
        out_specs=[vmem] * 8,
        out_shape=[
            shape((rows, width), jnp.bfloat16),
            shape((total_rows, 384), jnp.bfloat16),
            shape((total_rows, 128), jnp.float32),
            shape((total_rows, 128), jnp.float32),
            shape(counts.shape, jnp.float32),
            shape((4,) + flow.shape, jnp.float32),
            shape((4 * rows, width), jnp.bfloat16),
            shape((4 * rows, 2 * width), jnp.bfloat16),
        ],
        scratch_shapes=[
            pltpu.VMEM((total_rows, 128), jnp.bfloat16),
            pltpu.VMEM((10,) + counts.shape, jnp.float32),
        ]
        + semaphores(40),
        compiler_params=comm_params(1),
    )(packed, seg_col, seg_row, counts, flow, norm_a, frames, skip)


ALONG = (((1,), (1,)), ((), ()))
DOWN = (((0,), (0,)), ((), ()))


def normal_parts(values):
    centred = values - jnp.mean(values, axis=1, keepdims=True)
    scale = lax.rsqrt(jnp.mean(centred * centred, axis=1, keepdims=True) + EPSILON)
    return centred * scale, scale


def normal_back(inward, unit, scale):
    return scale * (
        inward
        - jnp.mean(inward, axis=1, keepdims=True)
        - unit * jnp.mean(inward * unit, axis=1, keepdims=True)
    )


def column_sum(values):
    return jnp.sum(values.astype(jnp.float32), axis=0, keepdims=True)


def backward_kernel(
    utts, attn_ref, resid_ref, mod_ref, segment_ref, mask_ref, dropped_ref, counts_ref, out_grad_ref,
    b_out_ref, b_up_ref, b_down_ref,
    heads_ref, segq_ref, segk_ref, exact_ref, total_ref, cos_ref, sin_ref,
    norm_a_ref, joined_ref, w_out_ref, w_up_ref, w_down_ref, w_qkv_ref, w_skip_ref,
    mixed, g_down, g_up, g_out, g_qkv, g_skip, smalls, g_frames, g_skip_in,
    d_ff, norm_f, act, d_inner, d_branch, d_attn, pieces, d_mid, ff_sum, d_norm,
    grad_heads, d_heads, dk_ref, dv_ref,
    d_ff_all, act_all, norm_all, d_inner_all, attn_all, d_branch_all,
    norm_a_all, joined_all, d_qkv, d_qkv_all, d_resid, d_resid_all,
    up_ring, down_ring, w_out, w_qkv, w_skip, small_own, small_got, small_sum,
    *rest,
):
    tiles, (send_sems, recv_sems, local_sems, ring_sems) = rest[:-4], rest[-4:]
    links = Links(send_sems, recv_sems, local_sems)
    rows, model = resid_ref.shape
    block_width = up_ring.shape[2]
    steps = w_up_ref.shape[1] // block_width

    def ring(c):
        slot = c % 2
        columns = pl.ds(pl.multiple_of(c * block_width, block_width), block_width)
        return (
            pltpu.make_async_copy(w_up_ref.at[:, columns], up_ring.at[slot], ring_sems.at[slot]),
            pltpu.make_async_copy(
                w_down_ref.at[columns, :], down_ring.at[slot], ring_sems.at[2 + slot]
            ),
        )

    load_out = links.keep(w_out_ref, w_out)
    for c in (0, 1):
        for copy in ring(c):
            copy.start()
    loads = [
        links.keep(w_qkv_ref, w_qkv),
        links.keep(w_skip_ref, w_skip),
        links.keep(norm_a_ref, norm_a_all),
        links.keep(joined_ref, joined_all),
    ]
    links.enter((1, 2, 3), range(1, 8))

    def modulation(piece):
        columns = slice(piece * model, (piece + 1) * model)
        value = jnp.broadcast_to(mod_ref[0:1, columns], (rows, model))
        for u in range(1, utts):
            value = jnp.where(segment_ref[...] == u, mod_ref[u : u + 1, columns], value)
        return value

    n_drop, n_keep = counts_ref[0:1, 0:1], counts_ref[0:1, 1:2]
    dropped = dropped_ref[...]
    loss_weight = (
        mask_ref[...]
        * (n_drop + n_keep)
        * 0.5
        * (dropped / (n_drop + 1.0) + (1.0 - dropped) / (n_keep + 1.0))
    )

    def d_out():
        return out_grad_ref[...].astype(jnp.float32) * loss_weight

    d_ff[...] = (modulation(5) * d_out()).astype(jnp.bfloat16)
    gather_d = Gathered(links, d_ff, d_ff_all)
    load_out.wait()
    branch = (
        jnp.dot(attn_ref[...], w_out[...], preferred_element_type=jnp.float32) + b_out_ref[...]
    )
    pieces[0] = branch
    mid = resid_ref[...] + modulation(2) * branch
    d_mid[...] = mid
    unit, _ = normal_parts(mid)
    norm_f[...] = (unit * (1.0 + modulation(4)) + modulation(3)).astype(jnp.bfloat16)
    gather_n = Gathered(links, norm_f, norm_all)
    ff_sum[...] = jnp.zeros_like(ff_sum)
    d_norm[...] = jnp.zeros_like(d_norm)
    const = math.sqrt(2.0 / math.pi)

    def feed(c, _):
        slot = c % 2
        columns = pl.ds(pl.multiple_of(c * block_width, block_width), block_width)
        for copy in ring(c):
            copy.wait()
        inner = (
            jnp.dot(norm_f[...], up_ring[slot], preferred_element_type=jnp.float32)
            + b_up_ref[:, columns]
        )
        square = inner * inner
        slope = jnp.tanh(const * inner * (1.0 + 0.044715 * square))
        gate = 0.5 * (1.0 + slope)
        act_b = (inner * gate).astype(jnp.bfloat16)
        turn = gate + 0.5 * inner * (1.0 - slope * slope) * (
            const * (1.0 + 3.0 * 0.044715 * square)
        )
        here = pl.ds(pl.multiple_of(c * 128, 128), 128)
        for u in range(4):
            act[u, :, here] = act_b[:, u * 128 : (u + 1) * 128]
        d_act = lax.dot_general(
            d_ff[...], down_ring[slot], ALONG, preferred_element_type=jnp.float32
        )
        d_inner_b = (turn * d_act).astype(jnp.bfloat16)
        d_inner[:, columns] = d_inner_b
        ff_sum[...] += jnp.dot(act_b, down_ring[slot], preferred_element_type=jnp.float32)
        d_norm[...] += lax.dot_general(
            d_inner_b, up_ring[slot], ALONG, preferred_element_type=jnp.float32
        )

        @pl.when(c + 2 < steps)
        def _():
            for copy in ring(c + 2):
                copy.start()

        return 0

    lax.fori_loop(0, steps, feed, 0)
    far_first = (6, 7, 4, 5, 2, 3, 1)
    own_rows = pl.ds(pl.multiple_of(links.seq * rows, rows), rows)
    strip = lambda ref, place, size: ref.at[
        :, pl.ds(pl.multiple_of(place * size, size), size)
    ]
    width, narrow = d_inner_all.shape[1], d_branch_all.shape[1]
    gather_d.relay()
    quarter_a = Quarter(links, lambda u: act.at[u], act_all)
    quarter_i = Quarter(links, lambda u: strip(d_inner, u, width), d_inner_all)
    gather_b = Gathered(links, attn_ref, attn_all)
    mid = d_mid[...]
    unit, scale = normal_parts(mid)
    d_norm_f = d_norm[...]
    pieces[2] = d_norm_f * unit
    d_mid_f = d_out() + normal_back(d_norm_f * (1.0 + modulation(4)), unit, scale)
    gate_a = modulation(2)
    d_branch[...] = (gate_a * d_mid_f).astype(jnp.bfloat16)
    pieces[0] = pieces[0] * d_mid_f
    d_mid[...] = d_mid_f
    d_attn[...] = lax.dot_general(
        d_branch[...], w_out[...], ALONG, preferred_element_type=jnp.float32
    ).astype(jnp.bfloat16)
    own = links.keep(strip(d_attn, links.seq, 128), grad_heads.at[own_rows, :])
    incoming_d = [
        links.send(
            strip(d_attn, links.seq_of(r), 128), grad_heads.at[own_rows, :], links.peer(r)
        )
        for r in far_first
    ]
    quarter_b = Quarter(links, lambda u: strip(d_branch, u, narrow), d_branch_all)
    ff_out = ff_sum[...] + b_down_ref[...]
    mixed[...] = (mid + modulation(5) * ff_out).astype(jnp.bfloat16)
    pieces[1] = d_out() * ff_out
    small_own[...] = jnp.zeros_like(small_own)
    small_own[4:5, :] = column_sum(d_branch[...])
    for c in range(4):
        small_own[5 + c : 6 + c, :] = column_sum(d_inner[:, c * model : (c + 1) * model])
    small_own[9:10, :] = column_sum(d_ff[...])

    def utterance_sums(piece, values):
        for u in range(utts):
            row = 10 + 6 * u + piece
            small_own[row : row + 1, :] = jnp.sum(
                jnp.where(segment_ref[...] == u, values, 0.0), axis=0, keepdims=True
            )

    utterance_sums(2, pieces[0])
    utterance_sums(3, d_norm[...])
    utterance_sums(4, pieces[2])
    utterance_sums(5, pieces[1])
    half = width // 2
    down_at = lambda h: lambda u: g_down.at[
        pl.ds(pl.multiple_of(u * 128, 128), 128), pl.ds(h * half, half)
    ]
    column_at = lambda ref, step, offset, size: lambda u: ref.at[
        :, pl.ds(pl.multiple_of(u * step + offset, 128), size)
    ]
    wide, thin = d_qkv_all.shape[1], d_resid_all.shape[1]
    third, slim = wide // 2, thin // 2
    plans = [
        (act_all, d_ff_all, pl.ds(0, half), down_at(0)),
        (act_all, d_ff_all, pl.ds(half, half), down_at(1)),
        (norm_all, d_inner_all, pl.ds(0, half), column_at(g_up, width, 0, half)),
        (norm_all, d_inner_all, pl.ds(half, half), column_at(g_up, width, half, half)),
        (attn_all, d_branch_all, pl.ds(0, narrow), column_at(g_out, narrow, 0, narrow)),
        (norm_a_all, d_qkv_all, pl.ds(0, third), column_at(g_qkv, wide, 0, third)),
        (norm_a_all, d_qkv_all, pl.ds(third, third), column_at(g_qkv, wide, third, third)),
        (joined_all, d_resid_all, pl.ds(0, slim), column_at(g_skip, thin, 0, slim)),
        (joined_all, d_resid_all, pl.ds(slim, slim), column_at(g_skip, thin, slim, slim)),
    ]
    y_first = (True, False, True, False, True, False, True, False, True)
    shares = [
        Share(links, y_first[i], left, right, columns, *tiles[4 * i : 4 * i + 4], result)
        for i, (left, right, columns, result) in enumerate(plans)
    ]
    gather_n.relay()
    gather_d.wait()
    quarter_a.wait()
    shares[0].start()
    shares[1].start()
    own.wait()
    for copy in incoming_d:
        copy.wait_recv()
    dk_ref[...] = jnp.zeros_like(dk_ref)
    dv_ref[...] = jnp.zeros_like(dv_ref)
    first = lax.broadcasted_iota(jnp.int32, (256, 128), 1) < HEAD_DIM
    zero = jnp.zeros((256, 128), jnp.bfloat16)
    lower = lower_half((256, 128))
    k, v = heads_ref[:, 128:256], heads_ref[:, 256:384]
    seg_k = segk_ref[...]

    def turned(values, here):
        return (
            values * cos_ref[here, :] - swap_halves(values, lower) * sin_ref[here, :]
        ).astype(jnp.bfloat16)

    def block(step, _):
        here = pl.ds(pl.multiple_of(step * 256, 256), 256)
        q, seg_q = heads_ref[here, 0:128], segq_ref[here, :]
        scaled = grad_heads[here, :].astype(jnp.float32) / total_ref[here, :]
        grad_acc = scaled.astype(jnp.bfloat16)
        product = scaled * exact_ref[here, :]
        d_query = []
        for mine in (first, jnp.logical_not(first)):
            q_own = jnp.where(mine, q, zero)
            g_own = jnp.where(mine, grad_acc, zero)
            delta = jnp.sum(jnp.where(mine, product, 0.0), axis=1, keepdims=True)
            weights = head_scores(q_own, k, seg_q, seg_k)
            dots = lax.dot_general(g_own, v, ALONG, preferred_element_type=jnp.float32)
            d_scores = (weights * (dots - delta)).astype(jnp.bfloat16)
            d_query.append(jnp.dot(d_scores, k, preferred_element_type=jnp.float32))
            dk_ref[...] += lax.dot_general(
                d_scores, q_own, DOWN, preferred_element_type=jnp.float32
            )
            dv_ref[...] += lax.dot_general(
                weights.astype(jnp.bfloat16), g_own, DOWN, preferred_element_type=jnp.float32
            )
        d_heads[here, 0:128] = turned(jnp.where(first, d_query[0], d_query[1]) * 0.125, here)
        return 0

    blocks = heads_ref.shape[0] // 256
    lax.fori_loop(0, blocks, block, 0)

    def finish(step, _):
        here = pl.ds(pl.multiple_of(step * 256, 256), 256)
        d_heads[here, 128:256] = turned(dk_ref[here, :] * 0.125, here)
        d_heads[here, 256:384] = dv_ref[here, :].astype(jnp.bfloat16)
        return 0

    lax.fori_loop(0, blocks, finish, 0)
    part = lambda place, c: d_heads.at[
        pl.ds(pl.multiple_of(place * rows, rows), rows), pl.ds(c * 128, 128)
    ]
    home = lambda c: d_qkv.at[
        :, pl.ds(pl.multiple_of(c * model + links.seq * 128, 128), 128)
    ]
    owns = [links.keep(part(links.seq, c), home(c)) for c in range(3)]
    incoming = [
        links.send(part(links.seq_of(r), c), home(c), links.peer(r))
        for r in far_first
        for c in range(3)
    ]
    gather_n.wait()
    quarter_i.wait()
    shares[2].start()
    shares[3].start()
    gather_b.relay()
    gather_b.wait()
    quarter_b.wait()
    shares[4].start()
    state = {}

    def projections():
        for copy in owns:
            copy.wait()
        for copy in incoming:
            copy.wait_recv()
        for copy in loads:
            copy.wait()
        state["qkv"] = Quarter(links, lambda u: strip(d_qkv, u, wide), d_qkv_all)
        d_norm_a = lax.dot_general(
            d_qkv[...], w_qkv[...], ALONG, preferred_element_type=jnp.float32
        )
        unit, scale = normal_parts(resid_ref[...])
        d_resid_f = d_mid[...] + normal_back(d_norm_a * (1.0 + modulation(1)), unit, scale)
        rounded = d_resid_f.astype(jnp.bfloat16)
        d_resid[...] = rounded
        state["resid"] = Quarter(links, lambda u: strip(d_resid, u, thin), d_resid_all)
        small_own[0:1, :] = column_sum(rounded)
        for c in range(3):
            small_own[1 + c : 2 + c, :] = column_sum(d_qkv[:, c * model : (c + 1) * model])
        utterance_sums(0, d_norm_a)
        utterance_sums(1, d_norm_a * unit)
        state["small"] = links.send(small_own, small_got.at[0], links.peer(1))

    def last_shares():
        state["qkv"].wait()
        shares[5].start()
        shares[6].start()
        state["resid"].wait()
        shares[7].start()
        shares[8].start()

    def inputs():
        for index, out in enumerate((g_frames, g_skip_in)):
            out[...] = lax.dot_general(
                d_resid[...],
                w_skip[pl.ds(index * model, model), :],
                ALONG,
                preferred_element_type=jnp.float32,
            ).astype(jnp.bfloat16)

    def small_y():
        state["small"].wait_recv()
        small_sum[0] = small_own[...] + small_got[0]
        state["small"] = links.send(small_sum.at[0], small_got.at[1], links.peer(2))

    def small_z1():
        state["small"].wait_recv()
        small_sum[1] = small_sum[0] + small_got[1]
        state["small"] = links.send(small_sum.at[1], small_got.at[2], links.peer(4))

    def small_z2():
        state["small"].wait_recv()
        mine = smalls.at[links.utt]
        mine[...] = small_sum[1] + small_got[2]
        state["spread"] = [links.send(mine, mine, links.mate(r)) for r in (2, 3, 1)]

    run_shares(
        shares,
        {
            1: (projections,),
            2: (last_shares,),
            3: (inputs, small_y),
            4: (small_z1,),
            5: (small_z2,),
        },
    )
    for copy in state["spread"]:
        copy.wait_recv()
    links.leave()


def backward(
    attn_b, resid, mod, segment, mask, dropped, counts, out_grad, b_out, b_up, b_down,
    heads, seg_col, seg_row, exact, total, cos, sin,
    norm_a_all, joined_all, w_out, w_up, w_down, w_qkv, w_skip,
):
    rows, model = resid.shape
    frames, inner = heads.shape[0], w_up.shape[1]
    utts = mod.shape[0]
    small = (-(-(10 + 6 * utts) // 8) * 8, model)
    mod = jnp.pad(mod, ((0, -utts % 8), (0, 0)))
    vmem, there = everywhere(pltpu.VMEM), everywhere(pl.ANY)
    shape = jax.ShapeDtypeStruct
    bf16 = lambda *dims: pltpu.VMEM(dims, jnp.bfloat16)
    f32 = lambda *dims: pltpu.VMEM(dims, jnp.float32)
    part, step = model // 8, inner // 8
    return pl.pallas_call(
        partial(backward_kernel, utts),
        in_specs=[vmem] * 18 + [there] * 7,
        out_specs=[vmem] * 9,
        out_shape=[
            shape((rows, model), jnp.bfloat16),
            shape((inner // 8, model), jnp.bfloat16),
            shape((part, inner), jnp.bfloat16),
            shape((part, model), jnp.bfloat16),
            shape((part, 3 * model), jnp.bfloat16),
            shape((2 * part, model), jnp.bfloat16),
            shape((4,) + small, jnp.float32),
            shape((rows, model), jnp.bfloat16),
            shape((rows, model), jnp.bfloat16),
        ],
        scratch_shapes=[
            bf16(rows, model),
            bf16(rows, model),
            bf16(4, rows, inner // 4),
            bf16(rows, inner),
            bf16(rows, model),
            bf16(rows, model),
            f32(3, rows, model),
            f32(rows, model),
            f32(rows, model),
            f32(rows, model),
            bf16(frames, 128),
            bf16(frames, 384),
            f32(frames, 128),
            f32(frames, 128),
            bf16(4 * rows, model),
            bf16(4 * rows, inner // 4),
            bf16(4 * rows, model),
            bf16(4 * rows, inner // 4),
            bf16(4 * rows, model),
            bf16(4 * rows, model // 4),
            bf16(4 * rows, model),
            bf16(4 * rows, 2 * model),
            bf16(rows, 3 * model),
            bf16(4 * rows, 3 * model // 4),
            bf16(rows, model),
            bf16(4 * rows, model // 4),
            bf16(2, model, step),
            bf16(2, step, model),
            bf16(*w_out.shape),
            bf16(*w_qkv.shape),
            bf16(*w_skip.shape),
            f32(*small),
            f32(3, *small),
            f32(2, *small),
        ]
        + share_scratch(part, inner // 8) * 4
        + share_scratch(part, model // 4)
        + share_scratch(part, 3 * model // 8) * 2
        + share_scratch(2 * part, model // 8) * 2
        + semaphores(128)
        + [pltpu.SemaphoreType.DMA((4,))],
        compiler_params=comm_params(2),
    )(
        attn_b, resid, mod, segment, mask, dropped, counts, out_grad,
        b_out[None, :], b_up[None, :], b_down[None, :],
        heads, seg_col, seg_row, exact, total, cos, sin,
        norm_a_all, joined_all, w_out, w_up, w_down, w_qkv, w_skip,
    )


def wide_tables(position):
    half_dim = HEAD_DIM // 2
    lane = jnp.arange(128, dtype=jnp.int32) % HEAD_DIM
    inverse = jnp.exp(
        -math.log(10000.0) * 2.0 * (lane % half_dim).astype(jnp.float32) / HEAD_DIM
    )
    angles = position.astype(jnp.float32)[:, None] * inverse[None, :]
    sign = jnp.where(lane < half_dim, -1.0, 1.0)
    return jnp.cos(angles), jnp.sin(angles) * sign[None, :]


def local(
    frames_in,
    skip_in,
    flow_times,
    frame_lengths,
    char_lengths,
    drop_mask,
    out_grad,
    w_skip,
    b_skip,
    w_mod,
    b_mod,
    w_qkv,
    b_qkv,
    w_out,
    b_out,
    w_up,
    b_up,
    w_down,
    b_down,
):
    local_rows = frames_in.shape[1]
    model_width = frames_in.shape[2]
    shards = lax.axis_size("seq")
    seq_place = lax.axis_index("seq")
    lengths = frame_lengths[0]
    utt_ends = jnp.cumsum(lengths)
    segment, position, in_loss, member = frame_tables(
        lengths, char_lengths[0], seq_place * local_rows, local_rows
    )
    member_f = member.astype(jnp.float32)
    loss_mask = in_loss.astype(jnp.float32)
    dropped = drop_mask[0].astype(jnp.float32)
    counts = jnp.stack([jnp.sum(loss_mask * dropped), jnp.sum(loss_mask * (1.0 - dropped))])
    counts = jnp.pad(counts[None, :], ((0, 7), (0, 126)))
    whole = model_width * 4
    fused = (
        lax.axis_size("utt") == 4
        and shards == 8
        and HEADS * HEAD_DIM == 1024
        and w_up.shape[1] == whole
        and local_rows == 128
    )
    if not fused:
        counts = xor_sum(xor_sum(counts, "utt"), "seq")
    time_act = jax.nn.silu(time_embed(flow_times[0], model_width)).astype(jnp.bfloat16)
    mod_u = jnp.dot(time_act, w_mod, preferred_element_type=jnp.float32) + b_mod
    mod_f = jnp.dot(member_f, mod_u, precision=HIGHEST_PRECISION)
    shift_a, scale_a, gate_a, shift_f, scale_f, gate_f = jnp.split(mod_f, 6, axis=1)
    joined = jnp.concatenate([frames_in[0], skip_in[0]], axis=1)
    residual = jnp.dot(joined, w_skip, preferred_element_type=jnp.float32) + b_skip
    norm_a = modulate(residual, scale_a, shift_a).astype(jnp.bfloat16)
    qkv_full = jnp.dot(norm_a, w_qkv, preferred_element_type=jnp.float32) + b_qkv
    if fused:
        all_segment, all_position, _, _ = frame_tables(
            lengths, char_lengths[0], 0, local_rows * shards
        )
        cos_all, sin_all = wide_tables(all_position)
        cos_own, sin_own = wide_tables(position)
        seg_col, seg_row = all_segment[:, None], all_segment[None, :]
        flow = jnp.pad(flow_times, ((0, 7), (0, 128 - flow_times.shape[1])))
        attn_b, qkv_heads, exact, total, counts, flows, norm_all, joined_all = attend(
            rotate_pack(qkv_full, cos_own, sin_own),
            seg_col,
            seg_row,
            counts,
            flow,
            norm_a,
            frames_in[0],
            skip_in[0],
        )
    else:
        angle_cos, angle_sin = rotary_tables(position, HEAD_DIM)
        queries = rotate(
            qkv_full[:, :model_width].reshape(local_rows, HEADS, HEAD_DIM), angle_cos, angle_sin
        ).astype(jnp.bfloat16)
        key_rot = rotate(
            qkv_full[:, model_width : 2 * model_width].reshape(local_rows, HEADS, HEAD_DIM),
            angle_cos,
            angle_sin,
        ).astype(jnp.bfloat16)
        key_value = jnp.stack(
            [
                key_rot.reshape(local_rows, model_width),
                qkv_full[:, 2 * model_width :].astype(jnp.bfloat16),
            ],
            axis=0,
        )
        start_state = (
            jnp.zeros((local_rows, HEADS, HEAD_DIM), jnp.float32),
            jnp.zeros((HEADS, local_rows), jnp.float32),
        )
        fwd_piece = partial(forward_piece, queries=queries, query_segment=segment, utt_ends=utt_ends)
        weighted, totals = over_blocks(
            partial(fwd_piece, usable=True),
            start_state,
            lax.all_gather(key_value, "seq", axis=1, tiled=True),
            jnp.int32(0),
            local_rows,
        )
        totals_rows = jnp.transpose(totals)
        attended = weighted / totals_rows[:, :, None]
        attn_b = attended.reshape(local_rows, model_width).astype(jnp.bfloat16)
    if fused:
        column = lambda vector: vector[:, None]
        mixed, g_w_down, g_w_up, g_w_out, g_w_qkv, g_w_skip, smalls, g_frames, g_skip_in = backward(
            attn_b,
            residual,
            mod_u,
            column(segment),
            column(loss_mask),
            column(dropped),
            counts,
            out_grad[0],
            b_out,
            b_up,
            b_down,
            qkv_heads,
            seg_col,
            seg_row,
            exact,
            total,
            cos_all,
            sin_all,
            norm_all,
            joined_all,
            w_out,
            w_up,
            w_down,
            w_qkv,
            w_skip,
        )
        used = 10 + 6 * flow_times.shape[1]
        smalls = smalls[:, :used].reshape(4, -1)
        biases = w_up.shape[1] + 6 * model_width
        bias_sum = jnp.sum(smalls[:, :biases], axis=0)
        d_mod_all = smalls[:, biases:].reshape(-1, 6 * model_width)
        flow_all = flows[:, 0, : flow_times.shape[1]].reshape(-1)
        act_all = jax.nn.silu(time_embed(flow_all, model_width)).astype(jnp.bfloat16)
        g_w_skip, g_w_qkv, g_w_out, g_w_up, g_w_down = (
            grad.astype(jnp.float32) for grad in (g_w_skip, g_w_qkv, g_w_out, g_w_up, g_w_down)
        )
    else:
        n_drop, n_keep = counts[0, 0], counts[0, 1]
        loss_weight = (
            loss_mask
            * (n_drop + n_keep)
            * 0.5
            * (dropped / (n_drop + 1.0) + (1.0 - dropped) / (n_keep + 1.0))
        )
        branch = jnp.dot(attn_b, w_out, preferred_element_type=jnp.float32) + b_out
        mid_state = residual + gate_a * branch
        norm_f = modulate(mid_state, scale_f, shift_f).astype(jnp.bfloat16)
        ff_inner = jnp.dot(norm_f, w_up, preferred_element_type=jnp.float32) + b_up
        ff_act, gelu_pull = jax.vjp(partial(jax.nn.gelu, approximate=True), ff_inner)
        act_b = ff_act.astype(jnp.bfloat16)
        ff_out = jnp.dot(act_b, w_down, preferred_element_type=jnp.float32) + b_down
        out_state = mid_state + gate_f * ff_out
        d_out = out_grad[0].astype(jnp.float32) * loss_weight[:, None]
        d_ff = (gate_f * d_out).astype(jnp.bfloat16)
        d_gate_f = d_out * ff_out
        g_b_down = jnp.sum(d_ff.astype(jnp.float32), axis=0)
        (d_inner,) = gelu_pull(back_product(d_ff, w_down))
        d_inner_b = d_inner.astype(jnp.bfloat16)
        g_b_up = jnp.sum(d_inner_b.astype(jnp.float32), axis=0)
        d_norm_f = back_product(d_inner_b, w_up)
        _, norm_f_pull = jax.vjp(modulate, mid_state, scale_f, shift_f)
        d_mid_norm, d_scale_f, d_shift_f = norm_f_pull(d_norm_f)
        d_mid = d_out + d_mid_norm
        d_branch = (gate_a * d_mid).astype(jnp.bfloat16)
        d_gate_a = d_mid * branch
        g_b_out = jnp.sum(d_branch.astype(jnp.float32), axis=0)
        d_attn = back_product(d_branch, w_out)
        mixed = out_state.astype(jnp.bfloat16)
        g_w_down = weight_grad(gather_left(act_b), d_ff)
        g_w_up = weight_grad(gather_left(norm_f), d_inner_b)
        g_w_out = weight_grad(gather_left(attn_b), d_branch)
        d_attn = d_attn.reshape(local_rows, HEADS, HEAD_DIM)
        grad_acc = (d_attn / totals_rows[:, :, None]).astype(jnp.bfloat16)
        delta = jnp.transpose(jnp.sum(d_attn * attended, axis=2) / totals_rows)
        bwd_piece = partial(
            backward_piece,
            queries=queries,
            query_segment=segment,
            utt_ends=utt_ends,
            grad_acc=grad_acc,
            delta=delta,
        )
        zero_query = jnp.zeros((local_rows, HEADS, HEAD_DIM), jnp.float32)
        zero_all = jnp.zeros((2, local_rows * shards, model_width), jnp.float32)

        def block_fn(inner_state, portion, block_start):
            d_query_sum, d_all = inner_state
            d_query_add, d_block = bwd_piece(portion, block_start, True)
            return (
                d_query_sum + d_query_add,
                lax.dynamic_update_slice_in_dim(d_all, d_block, block_start, 1),
            )

        d_query, d_all = over_blocks(
            block_fn,
            (zero_query, zero_all),
            lax.all_gather(key_value, "seq", axis=1, tiled=True),
            jnp.int32(0),
            local_rows,
        )
        d_key_value = lax.psum_scatter(d_all, "seq", scatter_dimension=1, tiled=True)
        d_query_pre = unrotate(d_query, angle_cos, angle_sin).reshape(local_rows, model_width)
        d_key_pre = unrotate(
            d_key_value[0].reshape(local_rows, HEADS, HEAD_DIM), angle_cos, angle_sin
        ).reshape(local_rows, model_width)
        d_qkv = jnp.concatenate([d_query_pre, d_key_pre, d_key_value[1]], axis=1).astype(jnp.bfloat16)
        g_b_qkv = jnp.sum(d_qkv.astype(jnp.float32), axis=0)
        d_norm_a = back_product(d_qkv, w_qkv)
        _, norm_a_pull = jax.vjp(modulate, residual, scale_a, shift_a)
        d_resid_norm, d_scale_a, d_shift_a = norm_a_pull(d_norm_a)
        d_resid = (d_mid + d_resid_norm).astype(jnp.bfloat16)
        g_b_skip = jnp.sum(d_resid.astype(jnp.float32), axis=0)
        d_joined = back_product(d_resid, w_skip)
        d_mod_f = jnp.concatenate(
            [d_shift_a, d_scale_a, d_gate_a, d_shift_f, d_scale_f, d_gate_f], axis=1
        )
        d_mod_u = jnp.dot(jnp.transpose(member_f), d_mod_f, precision=HIGHEST_PRECISION)
        small = jnp.concatenate(
            [g_b_skip, g_b_qkv, g_b_out, g_b_up, g_b_down, d_mod_u.reshape(-1)]
        )
        biases = small.shape[0] - d_mod_u.size
        g_w_qkv = weight_grad(gather_left(norm_a), d_qkv)
        g_w_skip = weight_grad(gather_left(joined), d_resid)
        small = xor_sum(small.reshape(-1, 128), "seq").reshape(-1)
        bias_sum = xor_sum(small[:biases].reshape(-1, 128), "utt").reshape(-1)
        d_mod_all = gather_ordered(small[biases:].reshape(d_mod_u.shape), 0)
        act_all = gather_ordered(time_act, 0)
        g_frames = d_joined[:, :model_width].astype(jnp.bfloat16)
        g_skip_in = d_joined[:, model_width:].astype(jnp.bfloat16)
    act_all = act_all.astype(jnp.float32)
    own_width = model_width // shards
    act_own = lax.dynamic_slice_in_dim(act_all, seq_place * own_width, own_width, 1)
    g_w_mod = jnp.dot(jnp.transpose(act_own), d_mod_all, precision=HIGHEST_PRECISION)
    mod_width = d_mod_all.shape[1] // shards
    g_b_mod = jnp.sum(
        lax.dynamic_slice_in_dim(d_mod_all, seq_place * mod_width, mod_width, 1), axis=0
    )
    own_biases, offset = [], 0
    for size in (b_skip.shape[0], b_qkv.shape[0], b_out.shape[0], b_up.shape[0], b_down.shape[0]):
        width = size // shards
        own_biases.append(
            lax.dynamic_slice_in_dim(bias_sum, offset + seq_place * width, width, 0)
        )
        offset += size
    return (
        mixed[None],
        g_frames[None],
        g_skip_in[None],
        g_w_skip,
        own_biases[0],
        g_w_mod,
        g_b_mod,
        g_w_qkv,
        own_biases[1],
        g_w_out,
        own_biases[2],
        g_w_up,
        own_biases[3],
        g_w_down,
        own_biases[4],
    )


def solution(mesh):
    return jax.shard_map(
        local,
        mesh=mesh,
        in_specs=(
            P("utt", "seq", None),
            P("utt", "seq", None),
            P("utt", None),
            P("utt", None),
            P("utt", None),
            P("utt", "seq"),
            P("utt", "seq", None),
            P(),
            P(),
            P(),
            P(),
            P(),
            P(),
            P(),
            P(),
            P(),
            P(),
            P(),
            P(),
        ),
        out_specs=(
            P("utt", "seq", None),
            P("utt", "seq", None),
            P("utt", "seq", None),
            P("seq", None),
            P("seq"),
            P("seq", None),
            P("seq"),
            P("seq", None),
            P("seq"),
            P("seq", None),
            P("seq"),
            P("seq", None),
            P("seq"),
            P("seq", None),
            P("seq"),
        ),
        check_vma=False,
    )
```

```python
from functools import partial
import math

import jax
import jax.numpy as jnp
from jax import lax
from jax.experimental import pallas as pl
from jax.experimental.pallas import tpu as pltpu
from jax.sharding import PartitionSpec as P

HEADS = 16
HEAD_DIM = 64


HIGHEST_PRECISION = lax.Precision.HIGHEST
EPSILON = 1e-06


def layer_norm(values):
    average = jnp.mean(values, axis=-1, keepdims=True)
    centred = values - average
    spread = jnp.mean(centred * centred, axis=-1, keepdims=True)
    return centred * lax.rsqrt(spread + EPSILON)


def modulate(values, scale_part, shift_part):
    return layer_norm(values) * (1.0 + scale_part) + shift_part


def time_embed(flow_vals, model_width):
    half_dim = model_width // 2
    inverse = jnp.exp(-math.log(10000.0) * jnp.arange(half_dim, dtype=jnp.float32) / half_dim)
    angles = 1000.0 * flow_vals[:, None] * inverse[None, :]
    return jnp.concatenate([jnp.sin(angles), jnp.cos(angles)], axis=1)


def rotary_tables(position, head_size):
    half_dim = head_size // 2
    inverse = jnp.exp(
        -math.log(10000.0) * 2.0 * jnp.arange(half_dim, dtype=jnp.float32) / head_size
    )
    angles = position.astype(jnp.float32)[:, None] * inverse[None, :]
    return (jnp.cos(angles)[:, None, :], jnp.sin(angles)[:, None, :])


def rotate(tensor, angle_cos, angle_sin):
    half_dim = tensor.shape[-1] // 2
    leading = tensor[..., :half_dim]
    trailing = tensor[..., half_dim:]
    return jnp.concatenate(
        [leading * angle_cos - trailing * angle_sin, trailing * angle_cos + leading * angle_sin],
        axis=-1,
    )


def unrotate(gradient, angle_cos, angle_sin):
    half_dim = gradient.shape[-1] // 2
    leading = gradient[..., :half_dim]
    trailing = gradient[..., half_dim:]
    return jnp.concatenate(
        [leading * angle_cos + trailing * angle_sin, trailing * angle_cos - leading * angle_sin],
        axis=-1,
    )


def frame_tables(lengths, char_counts, first_frame, frame_count):
    utt_ends = jnp.cumsum(lengths)
    utt_starts = utt_ends - lengths
    frame_index = first_frame + jnp.arange(frame_count, dtype=jnp.int32)
    segment = jnp.sum((frame_index[:, None] >= utt_ends[None, :]).astype(jnp.int32), axis=1)
    member = segment[:, None] == jnp.arange(lengths.shape[0], dtype=jnp.int32)[None, :]
    position = frame_index - jnp.sum(jnp.where(member, utt_starts[None, :], 0), axis=1)
    prompt = jnp.sum(jnp.where(member, char_counts[None, :], 0), axis=1)
    return (segment, position, position >= prompt, member)


def key_segments(key_start, key_count, utt_ends):
    frame_index = key_start + jnp.arange(key_count, dtype=jnp.int32)
    return jnp.sum((frame_index[:, None] >= utt_ends[None, :]).astype(jnp.int32), axis=1)


def block_scores(queries, key_piece, query_segment, key_segment, usable):
    key_rows = key_piece.reshape(key_piece.shape[0], queries.shape[1], queries.shape[2])
    scores = (
        jnp.einsum("qhd,khd->hqk", queries, key_rows, preferred_element_type=jnp.float32) * 0.125
    )
    allowed = jnp.logical_and(query_segment[:, None] == key_segment[None, :], usable)
    return (jnp.where(allowed[None], jnp.exp(scores), 0.0), key_rows)


def over_blocks(block_fn, running, piece, key_start, shard_rows):
    key_count = piece.shape[1]
    shard_total = key_count // shard_rows
    group_size = max(1, min(shard_total, 1024 // shard_rows))
    while shard_total % group_size != 0:
        group_size = group_size - 1
    block_rows = group_size * shard_rows
    if block_rows == key_count:
        return block_fn(running, piece, key_start)

    def one_block(block_index, inner_state):
        portion = lax.dynamic_slice_in_dim(piece, block_index * block_rows, block_rows, 1)
        return block_fn(inner_state, portion, key_start + block_index * block_rows)

    return lax.fori_loop(0, key_count // block_rows, one_block, running)


def forward_piece(running, piece, key_start, usable, queries, query_segment, utt_ends):
    weighted, totals = running
    key_segment = key_segments(key_start, piece.shape[1], utt_ends)
    weights, key_rows = block_scores(queries, piece[0], query_segment, key_segment, usable)
    value_rows = piece[1].reshape(key_rows.shape)
    totals = totals + jnp.sum(weights, axis=2)
    weighted = weighted + jnp.einsum(
        "hqk,khd->qhd", weights.astype(jnp.bfloat16), value_rows, preferred_element_type=jnp.float32
    )
    return (weighted, totals)


def backward_piece(piece, key_start, usable, queries, query_segment, utt_ends, grad_acc, delta):
    key_count = piece.shape[1]
    key_segment = key_segments(key_start, key_count, utt_ends)
    weights, key_rows = block_scores(queries, piece[0], query_segment, key_segment, usable)
    value_rows = piece[1].reshape(key_rows.shape)
    value_dots = jnp.einsum(
        "qhd,khd->hqk", grad_acc, value_rows, preferred_element_type=jnp.float32
    )
    d_scores = (weights * (value_dots - delta[:, :, None])).astype(jnp.bfloat16)
    d_query = (
        jnp.einsum("hqk,khd->qhd", d_scores, key_rows, preferred_element_type=jnp.float32) * 0.125
    )
    d_key = (
        jnp.einsum("hqk,qhd->khd", d_scores, queries, preferred_element_type=jnp.float32) * 0.125
    )
    d_value = jnp.einsum(
        "hqk,qhd->khd", weights.astype(jnp.bfloat16), grad_acc, preferred_element_type=jnp.float32
    )
    return (
        d_query,
        jnp.stack([d_key.reshape(key_count, -1), d_value.reshape(key_count, -1)], axis=0),
    )


def back_product(gradient_rows, matrix):
    return jnp.einsum("fo,io->fi", gradient_rows, matrix, preferred_element_type=jnp.float32)


def xor_permute(value, axis_name, bit):
    size = lax.axis_size(axis_name)
    return lax.ppermute(value, axis_name, [(i, i ^ bit) for i in range(size)])


def bits_of(axis_name):
    size, bits, bit = lax.axis_size(axis_name), [], 1
    while bit < size:
        bits.append(bit)
        bit *= 2
    return bits


def xor_sum(value, axis_name):
    for bit in bits_of(axis_name):
        value = value + xor_permute(value, axis_name, bit)
    return value


def gather_left(rows):
    for bit in reversed(bits_of("utt")):
        rows = jnp.concatenate([rows, xor_permute(rows, "utt", bit)], axis=0)
    return rows


def gather_right(rows):
    place = lax.axis_index("utt")
    for bit in reversed(bits_of("utt")):
        mine = (place & bit) // bit
        width = rows.shape[1] // 2
        kept = lax.dynamic_slice_in_dim(rows, mine * width, width, 1)
        given = lax.dynamic_slice_in_dim(rows, (1 - mine) * width, width, 1)
        rows = jnp.concatenate([kept, xor_permute(given, "utt", bit)], axis=0)
    return rows


def gather_ordered(value, axis):
    place = lax.axis_index("utt")
    for bit in bits_of("utt"):
        other = xor_permute(value, "utt", bit)
        low = (place & bit) == 0
        value = jnp.concatenate(
            [jnp.where(low, value, other), jnp.where(low, other, value)], axis=axis
        )
    return value


def scatter_rows(tile):
    place = lax.axis_index("seq")
    for bit in bits_of("seq"):
        mine = (place & bit) // bit
        rest = lax.axis_size("seq") // (2 * bit)
        pieces = tile.reshape(rest, 2, -1, tile.shape[-1])
        kept = lax.dynamic_index_in_dim(pieces, mine, 1, keepdims=False)
        given = lax.dynamic_index_in_dim(pieces, 1 - mine, 1, keepdims=False)
        given = xor_permute(given, "seq", bit)
        tile = (kept.astype(jnp.float32) + given.astype(jnp.float32)).astype(jnp.bfloat16)
    return tile.reshape(-1, tile.shape[-1])


def weight_grad(left_all, right_rows):
    right_all = gather_right(right_rows)
    tile = jnp.einsum(
        "fi,fo->io", left_all, right_all, preferred_element_type=jnp.float32
    ).astype(jnp.bfloat16)
    tile = tile.reshape(-1, tile.shape[-1])
    piece = scatter_rows(tile)
    return gather_ordered(piece, 1).astype(jnp.float32)


def swap_halves(values, lower):
    return jnp.where(lower, pltpu.roll(values, 96, 1), pltpu.roll(values, 32, 1))


def lower_half(shape):
    return lax.broadcasted_iota(jnp.int32, shape, 1) % HEAD_DIM < HEAD_DIM // 2


def rotate_pack_kernel(q_ref, k_ref, v_ref, cos_ref, sin_ref, out_ref):
    lower = lower_half(q_ref.shape)
    cos, sin = cos_ref[...], sin_ref[...]
    q, k = q_ref[...], k_ref[...]
    out_ref[0, :, 0:128] = (q * cos + swap_halves(q, lower) * sin).astype(jnp.bfloat16)
    out_ref[0, :, 128:256] = (k * cos + swap_halves(k, lower) * sin).astype(jnp.bfloat16)
    out_ref[0, :, 256:384] = v_ref[...].astype(jnp.bfloat16)


def rotate_pack(qkv_full, cos, sin):
    rows = qkv_full.shape[0]
    blocks = qkv_full.shape[1] // 384
    table = pl.BlockSpec((rows, 128), lambda i: (0, 0))
    return pl.pallas_call(
        rotate_pack_kernel,
        grid=(blocks,),
        in_specs=[
            pl.BlockSpec((rows, 128), lambda i: (0, i)),
            pl.BlockSpec((rows, 128), lambda i: (0, blocks + i)),
            pl.BlockSpec((rows, 128), lambda i: (0, 2 * blocks + i)),
            table,
            table,
        ],
        out_specs=pl.BlockSpec((1, rows, 384), lambda i: (i, 0, 0)),
        out_shape=jax.ShapeDtypeStruct((blocks, rows, 384), jnp.bfloat16),
    )(qkv_full, qkv_full, qkv_full, cos, sin)


def head_scores(q, k, seg_q, seg_k):
    scores = lax.dot_general(q, k, (((1,), (1,)), ((), ())), preferred_element_type=jnp.float32)
    return jnp.where(seg_q == seg_k, jnp.exp(scores * 0.125), 0.0)


MESH = pl.DeviceIdType.MESH
VMEM_LIMIT = 62 * 1024 * 1024


def flip(index, bit):
    return index + bit - 2 * bit * ((index // bit) % 2)


def everywhere(memory):
    return pl.BlockSpec(memory_space=memory)


class Links:
    def __init__(self, send_sems, recv_sems, local_sems):
        self.send_sems, self.recv_sems, self.local_sems = send_sems, recv_sems, local_sems
        self.sent, self.held = [], 0
        self.utt, self.seq = lax.axis_index("utt"), lax.axis_index("seq")

    def enter(self, utt_peers, seq_peers):
        barrier = pltpu.get_barrier_semaphore()
        targets = [self.mate(r) for r in utt_peers] + [self.peer(r) for r in seq_peers]
        for target in targets:
            pl.semaphore_signal(barrier, inc=1, device_id=target, device_id_type=MESH)
        pl.semaphore_wait(barrier, len(targets))

    def mate(self, offset):
        return (self.utt_of(offset), self.seq)

    def utt_of(self, offset):
        place = self.utt
        for bit in (1, 2):
            if offset & bit:
                place = flip(place, bit)
        return place

    def seq_of(self, offset):
        place = self.seq
        for bit in (1, 2, 4):
            if offset & bit:
                place = flip(place, bit)
        return place

    def peer(self, offset):
        return (self.utt, self.seq_of(offset))

    def send(self, source, target, device):
        index = len(self.sent)
        copy = pltpu.make_async_remote_copy(
            src_ref=source,
            dst_ref=target,
            send_sem=self.send_sems.at[index],
            recv_sem=self.recv_sems.at[index],
            device_id=device,
            device_id_type=MESH,
        )
        copy.start()
        self.sent.append(copy)
        return copy

    def keep(self, source, target):
        copy = pltpu.make_async_copy(source, target, self.local_sems.at[self.held])
        self.held += 1
        copy.start()
        return copy

    def leave(self):
        assert len(self.sent) <= self.send_sems.shape[0]
        assert self.held <= self.local_sems.shape[0]
        for copy in self.sent:
            copy.wait_send()


class Gathered:
    def __init__(self, links, source, target, columns=None):
        self.links, self.target = links, target
        self.rows = source.shape[0]
        self.columns = columns
        self.own = links.keep(source, self.slot(0))
        self.across = links.send(source, self.slot(2), links.mate(2))
        self.beside = links.send(source, self.slot(1), links.mate(1))

    def slot(self, offset):
        rows = pl.ds(offset * self.rows, self.rows)
        if self.columns is None:
            return self.target.at[rows, :]
        return self.target.at[rows, self.columns]

    def relay(self):
        self.across.wait_recv()
        self.relayed = self.links.send(self.slot(2), self.slot(3), self.links.mate(1))

    def wait(self):
        self.own.wait()
        self.beside.wait_recv()
        self.relayed.wait_recv()


class Quarter:
    def __init__(self, links, piece_of, target, columns=None):
        rows = target.shape[0] // 4
        columns = pl.ds(0, target.shape[1]) if columns is None else columns
        slot = lambda r: target.at[pl.ds(r * rows, rows), columns]
        self.own = links.keep(piece_of(links.utt), slot(0))
        self.copies = [
            links.send(piece_of(links.utt_of(r)), slot(r), links.mate(r)) for r in (2, 3, 1)
        ]

    def wait(self):
        self.own.wait()
        for copy in self.copies:
            copy.wait_recv()


class Share:
    def __init__(self, links, y_first, left, right, columns, tile, got_a, got_b, got_z2, result):
        self.links, self.y_first = links, y_first
        self.left, self.right, self.columns = left, right, columns
        self.tile, self.got_a, self.got_b, self.got_z2 = tile, got_a, got_b, got_z2
        self.result = result
        seq = links.seq
        self.y, self.zl, self.zh = seq % 2, (seq // 2) % 2, seq // 4
        if y_first:
            self.a, self.b, self.peers = self.y, self.zl, (1, 2)
        else:
            self.a, self.b, self.peers = self.zl, self.y, (2, 1)

    def place(self, zh, a, b):
        return (zh, b, a) if self.y_first else (zh, a, b)

    def product(self, a):
        rows = self.tile.shape[3]

        def block(step, _):
            zh, b = step // 2, step % 2
            here = self.place(zh, a, b)
            base = pl.multiple_of((4 * zh + 2 * here[1] + here[2]) * rows, rows)
            self.tile[here] = lax.dot_general(
                self.left[:, pl.ds(base, rows)],
                self.right[:, self.columns],
                (((0,), (0,)), ((), ())),
                preferred_element_type=jnp.float32,
            ).astype(jnp.bfloat16)
            return 0

        lax.fori_loop(0, 4, block, 0)

    def start(self):
        self.product(1 - self.a)
        given = (
            self.tile.at[:, :, 1 - self.a] if self.y_first else self.tile.at[:, 1 - self.a]
        )
        self.sent_a = self.links.send(given, self.got_a, self.links.peer(self.peers[0]))
        self.product(self.a)

    def add(self, index, got):
        tile = self.tile
        tile[index] = (tile[index].astype(jnp.float32) + got.astype(jnp.float32)).astype(
            jnp.bfloat16
        )

    def after_a(self):
        self.sent_a.wait_recv()

        def block(zh, _):
            self.add(self.place(zh, self.a, 1 - self.b), self.got_a[zh, 1 - self.b])
            return 0

        lax.fori_loop(0, 2, block, 0)
        _, low, y = self.place(0, self.a, 1 - self.b)
        self.sent_b = self.links.send(
            self.tile.at[:, low, y], self.got_b, self.links.peer(self.peers[1])
        )

        def rest(zh, _):
            self.add(self.place(zh, self.a, self.b), self.got_a[zh, self.b])
            return 0

        lax.fori_loop(0, 2, rest, 0)

    def after_b(self):
        self.sent_b.wait_recv()
        self.add((1 - self.zh, self.zl, self.y), self.got_b[1 - self.zh])
        self.sent_z2 = self.links.send(
            self.tile.at[1 - self.zh, self.zl, self.y], self.got_z2, self.links.peer(4)
        )
        self.add((self.zh, self.zl, self.y), self.got_b[self.zh])

    def after_z2(self):
        self.sent_z2.wait_recv()
        links = self.links
        mine = self.result(links.utt)
        mine[...] = (
            self.tile[self.zh, self.zl, self.y].astype(jnp.float32)
            + self.got_z2[...].astype(jnp.float32)
        ).astype(jnp.bfloat16)
        self.across = links.send(mine, mine, links.mate(2))
        self.beside = links.send(mine, mine, links.mate(1))

    def relay(self):
        self.across.wait_recv()
        links = self.links
        theirs = self.result(links.utt_of(2))
        self.relayed = links.send(theirs, theirs, links.mate(1))

    def wait(self):
        self.beside.wait_recv()
        self.relayed.wait_recv()


def share_scratch(rows, columns):
    return [
        pltpu.VMEM((2, 2, 2, rows, columns), jnp.bfloat16),
        pltpu.VMEM((2, 2, rows, columns), jnp.bfloat16),
        pltpu.VMEM((2, rows, columns), jnp.bfloat16),
        pltpu.VMEM((rows, columns), jnp.bfloat16),
    ]


def run_shares(shares, hooks):
    stages = ("after_a", "after_b", "after_z2", "relay", "wait")
    for turn in range(len(shares) + len(stages) - 1):
        for hook in hooks.get(turn, ()):
            hook()
        for place, stage in enumerate(stages):
            if 0 <= turn - place < len(shares):
                getattr(shares[turn - place], stage)()


def semaphores(count):
    return [pltpu.SemaphoreType.DMA((count,))] * 2 + [pltpu.SemaphoreType.DMA((32,))]


def comm_params(collective_id):
    return pltpu.CompilerParams(
        collective_id=collective_id, has_side_effects=True, vmem_limit_bytes=VMEM_LIMIT
    )


def attend_kernel(
    packed_ref, segq_ref, segk_ref, counts_ref, flow_ref, norm_ref, frames_ref, skip_ref,
    attn_ref, heads_ref, exact_ref, total_ref, sums_ref, flows_ref, norm_all, joined_all,
    attn_heads, counts_got, send_sems, recv_sems, local_sems,
):
    links = Links(send_sems, recv_sems, local_sems)
    links.enter((1, 2, 3), range(1, 8))
    rows = packed_ref.shape[1]
    width = frames_ref.shape[1]
    own_rows = pl.ds(pl.multiple_of(links.seq * rows, rows), rows)
    own = links.keep(packed_ref.at[links.seq], heads_ref.at[own_rows, :])
    incoming = [
        links.send(packed_ref.at[links.seq_of(r)], heads_ref.at[own_rows, :], links.peer(r))
        for r in (6, 7, 4, 5, 2, 3, 1)
    ]
    flows_ref[links.utt] = flow_ref[...]
    flow_copies = [
        links.send(flow_ref, flows_ref.at[links.utt], links.mate(r)) for r in (1, 2, 3)
    ]
    gathers = [
        Gathered(links, norm_ref, norm_all),
        Gathered(links, frames_ref, joined_all, pl.ds(0, width)),
        Gathered(links, skip_ref, joined_all, pl.ds(width, width)),
    ]
    sums_ref[...] = counts_ref[...]
    for place, (target, source) in enumerate(
        ((links.mate(1), 0), (links.mate(2), 1), (links.peer(1), 2), (links.peer(2), 3),
         (links.peer(4), 4))
    ):
        counts_got[5 + place] = sums_ref[...]
        copy = links.send(counts_got.at[5 + place], counts_got.at[source], target)
        copy.wait_recv()
        sums_ref[...] = sums_ref[...] + counts_got[source]
    gathers[0].relay()
    own.wait()
    for copy in incoming:
        copy.wait_recv()
    first = lax.broadcasted_iota(jnp.int32, (256, 128), 1) < HEAD_DIM
    zero = jnp.zeros((256, 128), jnp.bfloat16)
    k, v = heads_ref[:, 128:256], heads_ref[:, 256:384]
    seg_k = segk_ref[...]

    def block(step, _):
        here = pl.ds(pl.multiple_of(step * 256, 256), 256)
        q, seg_q = heads_ref[here, 0:128], segq_ref[here, :]
        results = []
        for mine in (first, jnp.logical_not(first)):
            weights = head_scores(jnp.where(mine, q, zero), k, seg_q, seg_k)
            total = jnp.sum(weights, axis=1, keepdims=True)
            summed = jnp.dot(weights.astype(jnp.bfloat16), v, preferred_element_type=jnp.float32)
            results.append((summed, total))
        total = jnp.where(first, results[0][1], results[1][1])
        attended = jnp.where(first, results[0][0], results[1][0]) / total
        attn_heads[here, :] = attended.astype(jnp.bfloat16)
        exact_ref[here, :] = attended
        total_ref[here, :] = total
        return 0

    lax.fori_loop(0, heads_ref.shape[0] // 256, block, 0)
    column = attn_ref.at[:, pl.ds(pl.multiple_of(links.seq * 128, 128), 128)]
    part = lambda place: attn_heads.at[pl.ds(pl.multiple_of(place * rows, rows), rows), :]
    own = links.keep(part(links.seq), column)
    incoming = [
        links.send(part(links.seq_of(r)), column, links.peer(r)) for r in (6, 7, 4, 5, 2, 3, 1)
    ]
    for gather in gathers[1:]:
        gather.relay()
    for copy in flow_copies:
        copy.wait_recv()
    own.wait()
    for copy in incoming:
        copy.wait_recv()
    for gather in gathers:
        gather.wait()
    links.leave()


def attend(packed, seg_col, seg_row, counts, flow, norm_a, frames, skip):
    shards, rows, _ = packed.shape
    total_rows, width = shards * rows, norm_a.shape[1]
    vmem, there = everywhere(pltpu.VMEM), everywhere(pl.ANY)
    shape = jax.ShapeDtypeStruct
    return pl.pallas_call(
        attend_kernel,
        in_specs=[there, vmem, vmem, vmem, vmem, there, there, there],
        out_specs=[vmem] * 8,
        out_shape=[
            shape((rows, width), jnp.bfloat16),
            shape((total_rows, 384), jnp.bfloat16),
            shape((total_rows, 128), jnp.float32),
            shape((total_rows, 128), jnp.float32),
            shape(counts.shape, jnp.float32),
            shape((4,) + flow.shape, jnp.float32),
            shape((4 * rows, width), jnp.bfloat16),
            shape((4 * rows, 2 * width), jnp.bfloat16),
        ],
        scratch_shapes=[
            pltpu.VMEM((total_rows, 128), jnp.bfloat16),
            pltpu.VMEM((10,) + counts.shape, jnp.float32),
        ]
        + semaphores(40),
        compiler_params=comm_params(1),
    )(packed, seg_col, seg_row, counts, flow, norm_a, frames, skip)


ALONG = (((1,), (1,)), ((), ()))
DOWN = (((0,), (0,)), ((), ()))


def normal_parts(values):
    centred = values - jnp.mean(values, axis=1, keepdims=True)
    scale = lax.rsqrt(jnp.mean(centred * centred, axis=1, keepdims=True) + EPSILON)
    return centred * scale, scale


def normal_back(inward, unit, scale):
    return scale * (
        inward
        - jnp.mean(inward, axis=1, keepdims=True)
        - unit * jnp.mean(inward * unit, axis=1, keepdims=True)
    )


def column_sum(values):
    return jnp.sum(values.astype(jnp.float32), axis=0, keepdims=True)


def backward_kernel(
    utts, attn_ref, resid_ref, mod_ref, segment_ref, mask_ref, dropped_ref, counts_ref, out_grad_ref,
    b_out_ref, b_up_ref, b_down_ref,
    heads_ref, segq_ref, segk_ref, exact_ref, total_ref, cos_ref, sin_ref,
    norm_a_ref, joined_ref, w_out_ref, w_up_ref, w_down_ref, w_qkv_ref, w_skip_ref,
    mixed, g_down, g_up, g_out, g_qkv, g_skip, smalls, g_frames, g_skip_in,
    d_ff, norm_f, act, d_inner, d_branch, d_attn, pieces, d_mid, ff_sum, d_norm,
    grad_heads, d_heads, dk_ref, dv_ref,
    d_ff_all, act_all, norm_all, d_inner_all, attn_all, d_branch_all,
    norm_a_all, joined_all, d_qkv, d_qkv_all, d_resid, d_resid_all,
    up_ring, down_ring, w_out, w_qkv, w_skip, small_own, small_got, small_sum,
    *rest,
):
    tiles, (send_sems, recv_sems, local_sems, ring_sems) = rest[:-4], rest[-4:]
    links = Links(send_sems, recv_sems, local_sems)
    rows, model = resid_ref.shape
    block_width = up_ring.shape[2]
    steps = w_up_ref.shape[1] // block_width

    def ring(c):
        slot = c % 2
        columns = pl.ds(pl.multiple_of(c * block_width, block_width), block_width)
        return (
            pltpu.make_async_copy(w_up_ref.at[:, columns], up_ring.at[slot], ring_sems.at[slot]),
            pltpu.make_async_copy(
                w_down_ref.at[columns, :], down_ring.at[slot], ring_sems.at[2 + slot]
            ),
        )

    load_out = links.keep(w_out_ref, w_out)
    for c in (0, 1):
        for copy in ring(c):
            copy.start()
    loads = [
        links.keep(w_qkv_ref, w_qkv),
        links.keep(w_skip_ref, w_skip),
        links.keep(norm_a_ref, norm_a_all),
        links.keep(joined_ref, joined_all),
    ]
    links.enter((1, 2, 3), range(1, 8))

    def modulation(piece):
        columns = slice(piece * model, (piece + 1) * model)
        value = jnp.broadcast_to(mod_ref[0:1, columns], (rows, model))
        for u in range(1, utts):
            value = jnp.where(segment_ref[...] == u, mod_ref[u : u + 1, columns], value)
        return value

    n_drop, n_keep = counts_ref[0:1, 0:1], counts_ref[0:1, 1:2]
    dropped = dropped_ref[...]
    loss_weight = (
        mask_ref[...]
        * (n_drop + n_keep)
        * 0.5
        * (dropped / (n_drop + 1.0) + (1.0 - dropped) / (n_keep + 1.0))
    )

    def d_out():
        return out_grad_ref[...].astype(jnp.float32) * loss_weight

    d_ff[...] = (modulation(5) * d_out()).astype(jnp.bfloat16)
    gather_d = Gathered(links, d_ff, d_ff_all)
    load_out.wait()
    branch = (
        jnp.dot(attn_ref[...], w_out[...], preferred_element_type=jnp.float32) + b_out_ref[...]
    )
    pieces[0] = branch
    mid = resid_ref[...] + modulation(2) * branch
    d_mid[...] = mid
    unit, _ = normal_parts(mid)
    norm_f[...] = (unit * (1.0 + modulation(4)) + modulation(3)).astype(jnp.bfloat16)
    ff_sum[...] = jnp.zeros_like(ff_sum)
    d_norm[...] = jnp.zeros_like(d_norm)
    const = math.sqrt(2.0 / math.pi)
    width = d_inner_all.shape[1]

    def feed(c, _):
        slot = c % 2
        columns = pl.ds(pl.multiple_of(c * block_width, block_width), block_width)
        for copy in ring(c):
            copy.wait()
        inner = (
            jnp.dot(norm_f[...], up_ring[slot], preferred_element_type=jnp.float32)
            + b_up_ref[:, columns]
        )
        square = inner * inner
        slope = jnp.tanh(const * inner * (1.0 + 0.044715 * square))
        gate = 0.5 * (1.0 + slope)
        act_b = (inner * gate).astype(jnp.bfloat16)
        turn = gate + 0.5 * inner * (1.0 - slope * slope) * (
            const * (1.0 + 3.0 * 0.044715 * square)
        )
        here = pl.ds(pl.multiple_of(c * 128, 128), 128)
        d_act = lax.dot_general(
            d_ff[...], down_ring[slot], ALONG, preferred_element_type=jnp.float32
        )
        d_inner_b = (turn * d_act).astype(jnp.bfloat16)
        for u in range(4):
            act[u, :, here] = act_b[:, u * 128 : (u + 1) * 128]
            d_inner[u, :, here] = d_inner_b[:, u * 128 : (u + 1) * 128]
        ff_sum[...] += jnp.dot(act_b, down_ring[slot], preferred_element_type=jnp.float32)
        d_norm[...] += lax.dot_general(
            d_inner_b, up_ring[slot], ALONG, preferred_element_type=jnp.float32
        )

        @pl.when(c + 2 < steps)
        def _():
            for copy in ring(c + 2):
                copy.start()

        return 0

    middle = width // 2
    left_half, right_half = pl.ds(0, middle), pl.ds(middle, middle)
    lax.fori_loop(0, steps // 2, feed, 0)
    quarters_a = [Quarter(links, lambda u: act.at[u, :, left_half], act_all, left_half)]
    lax.fori_loop(steps // 2, steps, feed, 0)
    gather_d.relay()
    quarters_a.append(Quarter(links, lambda u: act.at[u, :, right_half], act_all, right_half))
    gather_n = Gathered(links, norm_f, norm_all)
    far_first = (6, 7, 4, 5, 2, 3, 1)
    own_rows = pl.ds(pl.multiple_of(links.seq * rows, rows), rows)
    strip = lambda ref, place, size: ref.at[
        :, pl.ds(pl.multiple_of(place * size, size), size)
    ]
    narrow = d_branch_all.shape[1]
    quarter_i = Quarter(links, lambda u: d_inner.at[u], d_inner_all)
    mid = d_mid[...]
    unit, scale = normal_parts(mid)
    d_norm_f = d_norm[...]
    pieces[2] = d_norm_f * unit
    d_mid_f = d_out() + normal_back(d_norm_f * (1.0 + modulation(4)), unit, scale)
    gate_a = modulation(2)
    d_branch[...] = (gate_a * d_mid_f).astype(jnp.bfloat16)
    pieces[0] = pieces[0] * d_mid_f
    d_mid[...] = d_mid_f
    d_attn[...] = lax.dot_general(
        d_branch[...], w_out[...], ALONG, preferred_element_type=jnp.float32
    ).astype(jnp.bfloat16)
    own = links.keep(strip(d_attn, links.seq, 128), grad_heads.at[own_rows, :])
    incoming_d = [
        links.send(
            strip(d_attn, links.seq_of(r), 128), grad_heads.at[own_rows, :], links.peer(r)
        )
        for r in far_first
    ]
    quarter_b = Quarter(links, lambda u: strip(d_branch, u, narrow), d_branch_all)
    gather_b = Gathered(links, attn_ref, attn_all)
    ff_out = ff_sum[...] + b_down_ref[...]
    mixed[...] = (mid + modulation(5) * ff_out).astype(jnp.bfloat16)
    pieces[1] = d_out() * ff_out
    small_own[...] = jnp.zeros_like(small_own)
    small_own[4:5, :] = column_sum(d_branch[...])
    for c in range(4):
        small_own[5 + c : 6 + c, :] = column_sum(d_inner[c])
    small_own[9:10, :] = column_sum(d_ff[...])

    def utterance_sums(piece, values):
        for u in range(utts):
            row = 10 + utts * piece + u
            small_own[row : row + 1, :] = jnp.sum(
                jnp.where(segment_ref[...] == u, values, 0.0), axis=0, keepdims=True
            )

    utterance_sums(2, pieces[0])
    utterance_sums(3, d_norm[...])
    utterance_sums(4, pieces[2])
    utterance_sums(5, pieces[1])
    half = width // 2
    down_at = lambda h: lambda u: g_down.at[
        pl.ds(pl.multiple_of(u * 128, 128), 128), pl.ds(h * half, half)
    ]
    column_at = lambda ref, step, offset, size: lambda u: ref.at[
        :, pl.ds(pl.multiple_of(u * step + offset, 128), size)
    ]
    wide, thin = d_qkv_all.shape[1], d_resid_all.shape[1]
    third, slim = wide // 2, thin // 2
    plans = [
        (act_all, d_ff_all, pl.ds(0, half), down_at(0)),
        (act_all, d_ff_all, pl.ds(half, half), down_at(1)),
        (norm_all, d_inner_all, pl.ds(0, half), column_at(g_up, width, 0, half)),
        (norm_all, d_inner_all, pl.ds(half, half), column_at(g_up, width, half, half)),
        (attn_all, d_branch_all, pl.ds(0, narrow), column_at(g_out, narrow, 0, narrow)),
        (norm_a_all, d_qkv_all, pl.ds(0, third), column_at(g_qkv, wide, 0, third)),
        (norm_a_all, d_qkv_all, pl.ds(third, third), column_at(g_qkv, wide, third, third)),
        (joined_all, d_resid_all, pl.ds(0, slim), column_at(g_skip, thin, 0, slim)),
        (joined_all, d_resid_all, pl.ds(slim, slim), column_at(g_skip, thin, slim, slim)),
    ]
    y_first = (True, False, True, True, True, False, True, True, True)
    shares = [
        Share(links, y_first[i], left, right, columns, *tiles[4 * i : 4 * i + 4], result)
        for i, (left, right, columns, result) in enumerate(plans)
    ]
    gather_n.relay()
    gather_d.wait()
    for quarter in quarters_a:
        quarter.wait()
    shares[0].start()
    shares[1].start()
    own.wait()
    for copy in incoming_d:
        copy.wait_recv()
    dk_ref[...] = jnp.zeros_like(dk_ref)
    dv_ref[...] = jnp.zeros_like(dv_ref)
    first = lax.broadcasted_iota(jnp.int32, (256, 128), 1) < HEAD_DIM
    zero = jnp.zeros((256, 128), jnp.bfloat16)
    lower = lower_half((256, 128))
    k, v = heads_ref[:, 128:256], heads_ref[:, 256:384]
    seg_k = segk_ref[...]

    def turned(values, here):
        return (
            values * cos_ref[here, :] - swap_halves(values, lower) * sin_ref[here, :]
        ).astype(jnp.bfloat16)

    def block(step, _):
        here = pl.ds(pl.multiple_of(step * 256, 256), 256)
        q, seg_q = heads_ref[here, 0:128], segq_ref[here, :]
        scaled = grad_heads[here, :].astype(jnp.float32) / total_ref[here, :]
        grad_acc = scaled.astype(jnp.bfloat16)
        product = scaled * exact_ref[here, :]
        d_query = []
        for mine in (first, jnp.logical_not(first)):
            q_own = jnp.where(mine, q, zero)
            g_own = jnp.where(mine, grad_acc, zero)
            delta = jnp.sum(jnp.where(mine, product, 0.0), axis=1, keepdims=True)
            weights = head_scores(q_own, k, seg_q, seg_k)
            dots = lax.dot_general(g_own, v, ALONG, preferred_element_type=jnp.float32)
            d_scores = (weights * (dots - delta)).astype(jnp.bfloat16)
            d_query.append(jnp.dot(d_scores, k, preferred_element_type=jnp.float32))
            dk_ref[...] += lax.dot_general(
                d_scores, q_own, DOWN, preferred_element_type=jnp.float32
            )
            dv_ref[...] += lax.dot_general(
                weights.astype(jnp.bfloat16), g_own, DOWN, preferred_element_type=jnp.float32
            )
        d_heads[here, 0:128] = turned(jnp.where(first, d_query[0], d_query[1]) * 0.125, here)
        return 0

    blocks = heads_ref.shape[0] // 256
    lax.fori_loop(0, blocks, block, 0)

    def finish(step, _):
        here = pl.ds(pl.multiple_of(step * 256, 256), 256)
        d_heads[here, 128:256] = turned(dk_ref[here, :] * 0.125, here)
        d_heads[here, 256:384] = dv_ref[here, :].astype(jnp.bfloat16)
        return 0

    lax.fori_loop(0, blocks, finish, 0)
    part = lambda place, c: d_heads.at[
        pl.ds(pl.multiple_of(place * rows, rows), rows), pl.ds(c * 128, 128)
    ]
    home = lambda c: d_qkv.at[
        :, pl.ds(pl.multiple_of(c * model + links.seq * 128, 128), 128)
    ]
    owns = [links.keep(part(links.seq, c), home(c)) for c in range(3)]
    incoming = [
        links.send(part(links.seq_of(r), c), home(c), links.peer(r))
        for r in far_first
        for c in range(3)
    ]
    gather_n.wait()
    quarter_i.wait()
    shares[2].start()
    shares[3].start()
    gather_b.relay()
    gather_b.wait()
    quarter_b.wait()
    shares[4].start()
    state = {}

    def projections():
        for copy in owns:
            copy.wait()
        for copy in incoming:
            copy.wait_recv()
        for copy in loads:
            copy.wait()
        state["qkv"] = Quarter(links, lambda u: strip(d_qkv, u, wide), d_qkv_all)
        d_norm_a = lax.dot_general(
            d_qkv[...], w_qkv[...], ALONG, preferred_element_type=jnp.float32
        )
        unit, scale = normal_parts(resid_ref[...])
        d_resid_f = d_mid[...] + normal_back(d_norm_a * (1.0 + modulation(1)), unit, scale)
        rounded = d_resid_f.astype(jnp.bfloat16)
        d_resid[...] = rounded
        state["resid"] = Quarter(links, lambda u: strip(d_resid, u, thin), d_resid_all)
        small_own[0:1, :] = column_sum(rounded)
        for c in range(3):
            small_own[1 + c : 2 + c, :] = column_sum(d_qkv[:, c * model : (c + 1) * model])
        utterance_sums(0, d_norm_a)
        utterance_sums(1, d_norm_a * unit)
        state["small"] = links.send(small_own, small_got.at[0], links.peer(1))

    def last_shares():
        state["qkv"].wait()
        shares[5].start()
        shares[6].start()
        state["resid"].wait()
        shares[7].start()
        shares[8].start()

    def inputs():
        for index, out in enumerate((g_frames, g_skip_in)):
            out[...] = lax.dot_general(
                d_resid[...],
                w_skip[pl.ds(index * model, model), :],
                ALONG,
                preferred_element_type=jnp.float32,
            ).astype(jnp.bfloat16)

    def small_y():
        state["small"].wait_recv()
        small_sum[0] = small_own[...] + small_got[0]
        state["small"] = links.send(small_sum.at[0], small_got.at[1], links.peer(2))

    def small_z1():
        state["small"].wait_recv()
        small_sum[1] = small_sum[0] + small_got[1]
        state["small"] = links.send(small_sum.at[1], small_got.at[2], links.peer(4))

    def small_z2():
        state["small"].wait_recv()
        mine = smalls.at[links.utt]
        mine[...] = small_sum[1] + small_got[2]
        state["spread"] = [links.send(mine, mine, links.mate(r)) for r in (2, 3, 1)]

    run_shares(
        shares,
        {
            1: (projections,),
            2: (last_shares,),
            3: (inputs, small_y),
            4: (small_z1,),
            5: (small_z2,),
        },
    )
    for copy in state["spread"]:
        copy.wait_recv()
    links.leave()


def backward(
    attn_b, resid, mod, segment, mask, dropped, counts, out_grad, b_out, b_up, b_down,
    heads, seg_col, seg_row, exact, total, cos, sin,
    norm_a_all, joined_all, w_out, w_up, w_down, w_qkv, w_skip,
):
    rows, model = resid.shape
    frames, inner = heads.shape[0], w_up.shape[1]
    utts = mod.shape[0]
    small = (-(-(10 + 6 * utts) // 8) * 8, model)
    mod = jnp.pad(mod, ((0, -utts % 8), (0, 0)))
    vmem, there = everywhere(pltpu.VMEM), everywhere(pl.ANY)
    shape = jax.ShapeDtypeStruct
    bf16 = lambda *dims: pltpu.VMEM(dims, jnp.bfloat16)
    f32 = lambda *dims: pltpu.VMEM(dims, jnp.float32)
    part, step = model // 8, inner // 8
    return pl.pallas_call(
        partial(backward_kernel, utts),
        in_specs=[vmem] * 18 + [there] * 7,
        out_specs=[vmem] * 9,
        out_shape=[
            shape((rows, model), jnp.bfloat16),
            shape((inner // 8, model), jnp.bfloat16),
            shape((part, inner), jnp.bfloat16),
            shape((part, model), jnp.bfloat16),
            shape((part, 3 * model), jnp.bfloat16),
            shape((2 * part, model), jnp.bfloat16),
            shape((4,) + small, jnp.float32),
            shape((rows, model), jnp.bfloat16),
            shape((rows, model), jnp.bfloat16),
        ],
        scratch_shapes=[
            bf16(rows, model),
            bf16(rows, model),
            bf16(4, rows, inner // 4),
            bf16(4, rows, inner // 4),
            bf16(rows, model),
            bf16(rows, model),
            f32(3, rows, model),
            f32(rows, model),
            f32(rows, model),
            f32(rows, model),
            bf16(frames, 128),
            bf16(frames, 384),
            f32(frames, 128),
            f32(frames, 128),
            bf16(4 * rows, model),
            bf16(4 * rows, inner // 4),
            bf16(4 * rows, model),
            bf16(4 * rows, inner // 4),
            bf16(4 * rows, model),
            bf16(4 * rows, model // 4),
            bf16(4 * rows, model),
            bf16(4 * rows, 2 * model),
            bf16(rows, 3 * model),
            bf16(4 * rows, 3 * model // 4),
            bf16(rows, model),
            bf16(4 * rows, model // 4),
            bf16(2, model, step),
            bf16(2, step, model),
            bf16(*w_out.shape),
            bf16(*w_qkv.shape),
            bf16(*w_skip.shape),
            f32(*small),
            f32(3, *small),
            f32(2, *small),
        ]
        + share_scratch(part, inner // 8) * 4
        + share_scratch(part, model // 4)
        + share_scratch(part, 3 * model // 8) * 2
        + share_scratch(2 * part, model // 8) * 2
        + semaphores(128)
        + [pltpu.SemaphoreType.DMA((4,))],
        compiler_params=comm_params(2),
    )(
        attn_b, resid, mod, segment, mask, dropped, counts, out_grad,
        b_out[None, :], b_up[None, :], b_down[None, :],
        heads, seg_col, seg_row, exact, total, cos, sin,
        norm_a_all, joined_all, w_out, w_up, w_down, w_qkv, w_skip,
    )


UP = 3


def finish_kernel(utts, shards, act_ref, *rest):
    kept_in, wide_in, smalls_in = rest[:3], rest[3:8], rest[8]
    kept_out, wide_out, mod_out, bias_out = rest[9:12], rest[12:17], rest[17], rest[18:24]
    kept, wide, staged = rest[24:27], rest[27:32], rest[32:37]
    smalls_ref, mod_stage, bias_stage, d_mod, totals, sems, load_sems = rest[37:]
    seq = lax.axis_index("seq")
    loads, copies = [], []
    for source, target in zip((*wide_in, smalls_in, *kept_in), (*wide, smalls_ref, *kept)):
        copy = pltpu.make_async_copy(source, target, load_sems.at[len(loads)])
        copy.start()
        loads.append(copy)

    def put(source, target):
        copy = pltpu.make_async_copy(source, target, sems.at[len(copies)])
        copy.start()
        copies.append(copy)

    model = smalls_ref.shape[2]
    lanes = 128
    for place, (source, stage, target) in enumerate(zip(wide, staged, wide_out)):
        loads[place].wait()
        if place == UP:
            for u in range(4):
                for c in range(shards):
                    stage[:, (4 * c + u) * lanes : (4 * c + u + 1) * lanes] = source[
                        :, u * model + c * lanes : u * model + (c + 1) * lanes
                    ].astype(jnp.float32)
        else:
            stage[...] = source[...].astype(jnp.float32)
        put(stage, target)
    groups = smalls_ref.shape[0]
    loads[5].wait()
    bias_sum = (
        smalls_ref[0, 0:10] + smalls_ref[1, 0:10] + smalls_ref[2, 0:10] + smalls_ref[3, 0:10]
    )
    for row in range(10):
        totals[row, 0:1] = bias_sum[row : row + 1]
    d_mod[...] = jnp.zeros_like(d_mod)
    for piece in range(6):
        first = 10 + utts * piece
        for g in range(groups):
            d_mod[piece, g * utts : (g + 1) * utts, :] = smalls_ref[g, first : first + utts, :]
        rows = d_mod[piece]
        totals[10 + piece, 0:1] = jnp.sum(rows, axis=0, keepdims=True)
        columns = slice(piece * model, (piece + 1) * model)
        mod_stage[:, columns] = jnp.dot(
            act_ref[...], rows, precision=HIGHEST_PRECISION, preferred_element_type=jnp.float32
        )
    put(mod_stage, mod_out)
    for load, source, target in zip(loads[6:], kept, kept_out):
        load.wait()
        put(source, target)
    line = model // lanes
    first = 0
    for place, target in enumerate(bias_out):
        count = target.shape[1] // lanes
        for i in range(count):
            unit = i * line + seq if place == UP else seq * count + i
            column = pl.multiple_of((unit % line) * lanes, lanes)
            bias_stage[place, 0:1, i * lanes : (i + 1) * lanes] = totals[
                first + unit // line, 0:1, pl.ds(column, lanes)
            ]
        first += count * shards // line
        put(bias_stage.at[place, pl.ds(0, 1), pl.ds(0, count * lanes)], target)
    for copy in copies:
        copy.wait()


def finish(shards, utts, act_own, smalls, mixed, frames, skip, grads):
    vmem, there = everywhere(pltpu.VMEM), everywhere(pl.ANY)
    shape = jax.ShapeDtypeStruct
    model = smalls.shape[2]
    own = model // shards
    depth = act_own.shape[1]
    mod_shape = (own, 6 * model)
    widths = [own, 3 * own, own, 4 * own, own, 6 * own]
    kept = (mixed, frames, skip)
    outs = pl.pallas_call(
        partial(finish_kernel, utts, shards),
        in_specs=[vmem] + [there] * 9,
        out_specs=[there] * 15,
        out_shape=[shape(v.shape, v.dtype) for v in kept]
        + [shape(g.shape, jnp.float32) for g in grads]
        + [shape(mod_shape, jnp.float32)]
        + [shape((1, w), jnp.float32) for w in widths],
        scratch_shapes=[pltpu.VMEM(v.shape, v.dtype) for v in (*kept, *grads)]
        + [pltpu.VMEM(g.shape, jnp.float32) for g in grads]
        + [
            pltpu.VMEM(smalls.shape, jnp.float32),
            pltpu.VMEM(mod_shape, jnp.float32),
            pltpu.VMEM((6, 8, max(widths)), jnp.float32),
            pltpu.VMEM((6, depth, model), jnp.float32),
            pltpu.VMEM((16, 8, model), jnp.float32),
            pltpu.SemaphoreType.DMA((15,)),
            pltpu.SemaphoreType.DMA((9,)),
        ],
        compiler_params=pltpu.CompilerParams(vmem_limit_bytes=VMEM_LIMIT),
    )(act_own, *kept, *grads, smalls)
    return outs[:9], [v.reshape(-1) for v in outs[9:]]


def own_time_act(flows, seq_place, shards, model):
    half_dim, own = model // 2, model // shards
    column = seq_place * own + jnp.arange(own, dtype=jnp.int32)
    inverse = jnp.exp(
        -math.log(10000.0) * (column % half_dim).astype(jnp.float32) / half_dim
    )
    angles = 1000.0 * flows[None, :] * inverse[:, None]
    wave = jnp.where((column < half_dim)[:, None], jnp.sin(angles), jnp.cos(angles))
    return jax.nn.silu(wave).astype(jnp.bfloat16).astype(jnp.float32)


def wide_tables(position):
    half_dim = HEAD_DIM // 2
    lane = jnp.arange(128, dtype=jnp.int32) % HEAD_DIM
    inverse = jnp.exp(
        -math.log(10000.0) * 2.0 * (lane % half_dim).astype(jnp.float32) / HEAD_DIM
    )
    angles = position.astype(jnp.float32)[:, None] * inverse[None, :]
    sign = jnp.where(lane < half_dim, -1.0, 1.0)
    return jnp.cos(angles), jnp.sin(angles) * sign[None, :]


def local(
    frames_in,
    skip_in,
    flow_times,
    frame_lengths,
    char_lengths,
    drop_mask,
    out_grad,
    w_skip,
    b_skip,
    w_mod,
    b_mod,
    w_qkv,
    b_qkv,
    w_out,
    b_out,
    w_up,
    b_up,
    w_down,
    b_down,
):
    local_rows = frames_in.shape[1]
    model_width = frames_in.shape[2]
    shards = lax.axis_size("seq")
    seq_place = lax.axis_index("seq")
    lengths = frame_lengths[0]
    utt_ends = jnp.cumsum(lengths)
    segment, position, in_loss, member = frame_tables(
        lengths, char_lengths[0], seq_place * local_rows, local_rows
    )
    member_f = member.astype(jnp.float32)
    loss_mask = in_loss.astype(jnp.float32)
    dropped = drop_mask[0].astype(jnp.float32)
    counts = jnp.stack([jnp.sum(loss_mask * dropped), jnp.sum(loss_mask * (1.0 - dropped))])
    counts = jnp.pad(counts[None, :], ((0, 7), (0, 126)))
    whole = model_width * 4
    fused = (
        lax.axis_size("utt") == 4
        and shards == 8
        and HEADS * HEAD_DIM == 1024
        and w_up.shape[1] == whole
        and local_rows == 128
    )
    if not fused:
        counts = xor_sum(xor_sum(counts, "utt"), "seq")
    time_act = jax.nn.silu(time_embed(flow_times[0], model_width)).astype(jnp.bfloat16)
    mod_u = jnp.dot(time_act, w_mod, preferred_element_type=jnp.float32) + b_mod
    mod_f = jnp.dot(member_f, mod_u, precision=HIGHEST_PRECISION)
    shift_a, scale_a, gate_a, shift_f, scale_f, gate_f = jnp.split(mod_f, 6, axis=1)
    joined = jnp.concatenate([frames_in[0], skip_in[0]], axis=1)
    residual = jnp.dot(joined, w_skip, preferred_element_type=jnp.float32) + b_skip
    norm_a = modulate(residual, scale_a, shift_a).astype(jnp.bfloat16)
    qkv_full = jnp.dot(norm_a, w_qkv, preferred_element_type=jnp.float32) + b_qkv
    if fused:
        all_segment, all_position, _, _ = frame_tables(
            lengths, char_lengths[0], 0, local_rows * shards
        )
        cos_all, sin_all = wide_tables(all_position)
        cos_own, sin_own = wide_tables(position)
        seg_col, seg_row = all_segment[:, None], all_segment[None, :]
        flow = jnp.pad(flow_times, ((0, 7), (0, 128 - flow_times.shape[1])))
        attn_b, qkv_heads, exact, total, counts, flows, norm_all, joined_all = attend(
            rotate_pack(qkv_full, cos_own, sin_own),
            seg_col,
            seg_row,
            counts,
            flow,
            norm_a,
            frames_in[0],
            skip_in[0],
        )
    else:
        angle_cos, angle_sin = rotary_tables(position, HEAD_DIM)
        queries = rotate(
            qkv_full[:, :model_width].reshape(local_rows, HEADS, HEAD_DIM), angle_cos, angle_sin
        ).astype(jnp.bfloat16)
        key_rot = rotate(
            qkv_full[:, model_width : 2 * model_width].reshape(local_rows, HEADS, HEAD_DIM),
            angle_cos,
            angle_sin,
        ).astype(jnp.bfloat16)
        key_value = jnp.stack(
            [
                key_rot.reshape(local_rows, model_width),
                qkv_full[:, 2 * model_width :].astype(jnp.bfloat16),
            ],
            axis=0,
        )
        start_state = (
            jnp.zeros((local_rows, HEADS, HEAD_DIM), jnp.float32),
            jnp.zeros((HEADS, local_rows), jnp.float32),
        )
        fwd_piece = partial(forward_piece, queries=queries, query_segment=segment, utt_ends=utt_ends)
        weighted, totals = over_blocks(
            partial(fwd_piece, usable=True),
            start_state,
            lax.all_gather(key_value, "seq", axis=1, tiled=True),
            jnp.int32(0),
            local_rows,
        )
        totals_rows = jnp.transpose(totals)
        attended = weighted / totals_rows[:, :, None]
        attn_b = attended.reshape(local_rows, model_width).astype(jnp.bfloat16)
    if fused:
        column = lambda vector: vector[:, None]
        mixed, g_w_down, g_w_up, g_w_out, g_w_qkv, g_w_skip, smalls, g_frames, g_skip_in = backward(
            attn_b,
            residual,
            mod_u,
            column(segment),
            column(loss_mask),
            column(dropped),
            counts,
            out_grad[0],
            b_out,
            b_up,
            b_down,
            qkv_heads,
            seg_col,
            seg_row,
            exact,
            total,
            cos_all,
            sin_all,
            norm_all,
            joined_all,
            w_out,
            w_up,
            w_down,
            w_qkv,
            w_skip,
        )
        utts = flow_times.shape[1]
        act_own = own_time_act(flows[:, 0, :utts].reshape(-1), seq_place, shards, model_width)
        act_own = jnp.pad(act_own, ((0, 0), (0, -act_own.shape[1] % 8)))
        wide, biases = finish(
            shards,
            utts,
            act_own,
            smalls,
            mixed,
            g_frames,
            g_skip_in,
            (g_w_skip, g_w_qkv, g_w_out, g_w_up, g_w_down),
        )
        mixed, g_frames, g_skip_in, g_w_skip, g_w_qkv, g_w_out, g_w_up, g_w_down, g_w_mod = wide
        own_biases, g_b_mod = biases[:5], biases[5]
    else:
        n_drop, n_keep = counts[0, 0], counts[0, 1]
        loss_weight = (
            loss_mask
            * (n_drop + n_keep)
            * 0.5
            * (dropped / (n_drop + 1.0) + (1.0 - dropped) / (n_keep + 1.0))
        )
        branch = jnp.dot(attn_b, w_out, preferred_element_type=jnp.float32) + b_out
        mid_state = residual + gate_a * branch
        norm_f = modulate(mid_state, scale_f, shift_f).astype(jnp.bfloat16)
        ff_inner = jnp.dot(norm_f, w_up, preferred_element_type=jnp.float32) + b_up
        ff_act, gelu_pull = jax.vjp(partial(jax.nn.gelu, approximate=True), ff_inner)
        act_b = ff_act.astype(jnp.bfloat16)
        ff_out = jnp.dot(act_b, w_down, preferred_element_type=jnp.float32) + b_down
        out_state = mid_state + gate_f * ff_out
        d_out = out_grad[0].astype(jnp.float32) * loss_weight[:, None]
        d_ff = (gate_f * d_out).astype(jnp.bfloat16)
        d_gate_f = d_out * ff_out
        g_b_down = jnp.sum(d_ff.astype(jnp.float32), axis=0)
        (d_inner,) = gelu_pull(back_product(d_ff, w_down))
        d_inner_b = d_inner.astype(jnp.bfloat16)
        g_b_up = jnp.sum(d_inner_b.astype(jnp.float32), axis=0)
        d_norm_f = back_product(d_inner_b, w_up)
        _, norm_f_pull = jax.vjp(modulate, mid_state, scale_f, shift_f)
        d_mid_norm, d_scale_f, d_shift_f = norm_f_pull(d_norm_f)
        d_mid = d_out + d_mid_norm
        d_branch = (gate_a * d_mid).astype(jnp.bfloat16)
        d_gate_a = d_mid * branch
        g_b_out = jnp.sum(d_branch.astype(jnp.float32), axis=0)
        d_attn = back_product(d_branch, w_out)
        mixed = out_state.astype(jnp.bfloat16)
        g_w_down = weight_grad(gather_left(act_b), d_ff)
        g_w_up = weight_grad(gather_left(norm_f), d_inner_b)
        g_w_out = weight_grad(gather_left(attn_b), d_branch)
        d_attn = d_attn.reshape(local_rows, HEADS, HEAD_DIM)
        grad_acc = (d_attn / totals_rows[:, :, None]).astype(jnp.bfloat16)
        delta = jnp.transpose(jnp.sum(d_attn * attended, axis=2) / totals_rows)
        bwd_piece = partial(
            backward_piece,
            queries=queries,
            query_segment=segment,
            utt_ends=utt_ends,
            grad_acc=grad_acc,
            delta=delta,
        )
        zero_query = jnp.zeros((local_rows, HEADS, HEAD_DIM), jnp.float32)
        zero_all = jnp.zeros((2, local_rows * shards, model_width), jnp.float32)

        def block_fn(inner_state, portion, block_start):
            d_query_sum, d_all = inner_state
            d_query_add, d_block = bwd_piece(portion, block_start, True)
            return (
                d_query_sum + d_query_add,
                lax.dynamic_update_slice_in_dim(d_all, d_block, block_start, 1),
            )

        d_query, d_all = over_blocks(
            block_fn,
            (zero_query, zero_all),
            lax.all_gather(key_value, "seq", axis=1, tiled=True),
            jnp.int32(0),
            local_rows,
        )
        d_key_value = lax.psum_scatter(d_all, "seq", scatter_dimension=1, tiled=True)
        d_query_pre = unrotate(d_query, angle_cos, angle_sin).reshape(local_rows, model_width)
        d_key_pre = unrotate(
            d_key_value[0].reshape(local_rows, HEADS, HEAD_DIM), angle_cos, angle_sin
        ).reshape(local_rows, model_width)
        d_qkv = jnp.concatenate([d_query_pre, d_key_pre, d_key_value[1]], axis=1).astype(jnp.bfloat16)
        g_b_qkv = jnp.sum(d_qkv.astype(jnp.float32), axis=0)
        d_norm_a = back_product(d_qkv, w_qkv)
        _, norm_a_pull = jax.vjp(modulate, residual, scale_a, shift_a)
        d_resid_norm, d_scale_a, d_shift_a = norm_a_pull(d_norm_a)
        d_resid = (d_mid + d_resid_norm).astype(jnp.bfloat16)
        g_b_skip = jnp.sum(d_resid.astype(jnp.float32), axis=0)
        d_joined = back_product(d_resid, w_skip)
        d_mod_f = jnp.concatenate(
            [d_shift_a, d_scale_a, d_gate_a, d_shift_f, d_scale_f, d_gate_f], axis=1
        )
        d_mod_u = jnp.dot(jnp.transpose(member_f), d_mod_f, precision=HIGHEST_PRECISION)
        small = jnp.concatenate(
            [g_b_skip, g_b_qkv, g_b_out, g_b_up, g_b_down, d_mod_u.reshape(-1)]
        )
        biases = small.shape[0] - d_mod_u.size
        g_w_qkv = weight_grad(gather_left(norm_a), d_qkv)
        g_w_skip = weight_grad(gather_left(joined), d_resid)
        small = xor_sum(small.reshape(-1, 128), "seq").reshape(-1)
        bias_sum = xor_sum(small[:biases].reshape(-1, 128), "utt").reshape(-1)
        d_mod_all = gather_ordered(small[biases:].reshape(d_mod_u.shape), 0)
        act_all = gather_ordered(time_act, 0)
        g_frames = d_joined[:, :model_width].astype(jnp.bfloat16)
        g_skip_in = d_joined[:, model_width:].astype(jnp.bfloat16)
        act_all = act_all.astype(jnp.float32)
        own_width = model_width // shards
        act_own = lax.dynamic_slice_in_dim(act_all, seq_place * own_width, own_width, 1)
        g_w_mod = jnp.dot(jnp.transpose(act_own), d_mod_all, precision=HIGHEST_PRECISION)
        mod_width = d_mod_all.shape[1] // shards
        g_b_mod = jnp.sum(
            lax.dynamic_slice_in_dim(d_mod_all, seq_place * mod_width, mod_width, 1), axis=0
        )
        own_biases, offset = [], 0
        for size in (b_skip.shape[0], b_qkv.shape[0], b_out.shape[0], b_up.shape[0], b_down.shape[0]):
            width = size // shards
            own_biases.append(
                lax.dynamic_slice_in_dim(bias_sum, offset + seq_place * width, width, 0)
            )
            offset += size
    return (
        mixed[None],
        g_frames[None],
        g_skip_in[None],
        g_w_skip,
        own_biases[0],
        g_w_mod,
        g_b_mod,
        g_w_qkv,
        own_biases[1],
        g_w_out,
        own_biases[2],
        g_w_up,
        own_biases[3],
        g_w_down,
        own_biases[4],
    )


def solution(mesh):
    return jax.shard_map(
        local,
        mesh=mesh,
        in_specs=(
            P("utt", "seq", None),
            P("utt", "seq", None),
            P("utt", None),
            P("utt", None),
            P("utt", None),
            P("utt", "seq"),
            P("utt", "seq", None),
            P(),
            P(),
            P(),
            P(),
            P(),
            P(),
            P(),
            P(),
            P(),
            P(),
            P(),
            P(),
        ),
        out_specs=(
            P("utt", "seq", None),
            P("utt", "seq", None),
            P("utt", "seq", None),
            P("seq", None),
            P("seq"),
            P("seq", None),
            P("seq"),
            P("seq", None),
            P("seq"),
            P("seq", None),
            P("seq"),
            P("seq", None),
            P("seq"),
            P("seq", None),
            P("seq"),
        ),
        check_vma=False,
    )
```

```python
from functools import partial
import math

import jax
import jax.numpy as jnp
from jax import lax
from jax.experimental import pallas as pl
from jax.experimental.pallas import tpu as pltpu
from jax.sharding import PartitionSpec as P

HEADS = 16
HEAD_DIM = 64


HIGHEST_PRECISION = lax.Precision.HIGHEST
EPSILON = 1e-06


def layer_norm(values):
    average = jnp.mean(values, axis=-1, keepdims=True)
    centred = values - average
    spread = jnp.mean(centred * centred, axis=-1, keepdims=True)
    return centred * lax.rsqrt(spread + EPSILON)


def modulate(values, scale_part, shift_part):
    return layer_norm(values) * (1.0 + scale_part) + shift_part


def time_embed(flow_vals, model_width):
    half_dim = model_width // 2
    inverse = jnp.exp(-math.log(10000.0) * jnp.arange(half_dim, dtype=jnp.float32) / half_dim)
    angles = 1000.0 * flow_vals[:, None] * inverse[None, :]
    return jnp.concatenate([jnp.sin(angles), jnp.cos(angles)], axis=1)


def rotary_tables(position, head_size):
    half_dim = head_size // 2
    inverse = jnp.exp(
        -math.log(10000.0) * 2.0 * jnp.arange(half_dim, dtype=jnp.float32) / head_size
    )
    angles = position.astype(jnp.float32)[:, None] * inverse[None, :]
    return (jnp.cos(angles)[:, None, :], jnp.sin(angles)[:, None, :])


def rotate(tensor, angle_cos, angle_sin):
    half_dim = tensor.shape[-1] // 2
    leading = tensor[..., :half_dim]
    trailing = tensor[..., half_dim:]
    return jnp.concatenate(
        [leading * angle_cos - trailing * angle_sin, trailing * angle_cos + leading * angle_sin],
        axis=-1,
    )


def unrotate(gradient, angle_cos, angle_sin):
    half_dim = gradient.shape[-1] // 2
    leading = gradient[..., :half_dim]
    trailing = gradient[..., half_dim:]
    return jnp.concatenate(
        [leading * angle_cos + trailing * angle_sin, trailing * angle_cos - leading * angle_sin],
        axis=-1,
    )


def frame_tables(lengths, char_counts, first_frame, frame_count):
    utt_ends = jnp.cumsum(lengths)
    utt_starts = utt_ends - lengths
    frame_index = first_frame + jnp.arange(frame_count, dtype=jnp.int32)
    segment = jnp.sum((frame_index[:, None] >= utt_ends[None, :]).astype(jnp.int32), axis=1)
    member = segment[:, None] == jnp.arange(lengths.shape[0], dtype=jnp.int32)[None, :]
    position = frame_index - jnp.sum(jnp.where(member, utt_starts[None, :], 0), axis=1)
    prompt = jnp.sum(jnp.where(member, char_counts[None, :], 0), axis=1)
    return (segment, position, position >= prompt, member)


def key_segments(key_start, key_count, utt_ends):
    frame_index = key_start + jnp.arange(key_count, dtype=jnp.int32)
    return jnp.sum((frame_index[:, None] >= utt_ends[None, :]).astype(jnp.int32), axis=1)


def block_scores(queries, key_piece, query_segment, key_segment, usable):
    key_rows = key_piece.reshape(key_piece.shape[0], queries.shape[1], queries.shape[2])
    scores = (
        jnp.einsum("qhd,khd->hqk", queries, key_rows, preferred_element_type=jnp.float32) * 0.125
    )
    allowed = jnp.logical_and(query_segment[:, None] == key_segment[None, :], usable)
    return (jnp.where(allowed[None], jnp.exp(scores), 0.0), key_rows)


def over_blocks(block_fn, running, piece, key_start, shard_rows):
    key_count = piece.shape[1]
    shard_total = key_count // shard_rows
    group_size = max(1, min(shard_total, 1024 // shard_rows))
    while shard_total % group_size != 0:
        group_size = group_size - 1
    block_rows = group_size * shard_rows
    if block_rows == key_count:
        return block_fn(running, piece, key_start)

    def one_block(block_index, inner_state):
        portion = lax.dynamic_slice_in_dim(piece, block_index * block_rows, block_rows, 1)
        return block_fn(inner_state, portion, key_start + block_index * block_rows)

    return lax.fori_loop(0, key_count // block_rows, one_block, running)


def forward_piece(running, piece, key_start, usable, queries, query_segment, utt_ends):
    weighted, totals = running
    key_segment = key_segments(key_start, piece.shape[1], utt_ends)
    weights, key_rows = block_scores(queries, piece[0], query_segment, key_segment, usable)
    value_rows = piece[1].reshape(key_rows.shape)
    totals = totals + jnp.sum(weights, axis=2)
    weighted = weighted + jnp.einsum(
        "hqk,khd->qhd", weights.astype(jnp.bfloat16), value_rows, preferred_element_type=jnp.float32
    )
    return (weighted, totals)


def backward_piece(piece, key_start, usable, queries, query_segment, utt_ends, grad_acc, delta):
    key_count = piece.shape[1]
    key_segment = key_segments(key_start, key_count, utt_ends)
    weights, key_rows = block_scores(queries, piece[0], query_segment, key_segment, usable)
    value_rows = piece[1].reshape(key_rows.shape)
    value_dots = jnp.einsum(
        "qhd,khd->hqk", grad_acc, value_rows, preferred_element_type=jnp.float32
    )
    d_scores = (weights * (value_dots - delta[:, :, None])).astype(jnp.bfloat16)
    d_query = (
        jnp.einsum("hqk,khd->qhd", d_scores, key_rows, preferred_element_type=jnp.float32) * 0.125
    )
    d_key = (
        jnp.einsum("hqk,qhd->khd", d_scores, queries, preferred_element_type=jnp.float32) * 0.125
    )
    d_value = jnp.einsum(
        "hqk,qhd->khd", weights.astype(jnp.bfloat16), grad_acc, preferred_element_type=jnp.float32
    )
    return (
        d_query,
        jnp.stack([d_key.reshape(key_count, -1), d_value.reshape(key_count, -1)], axis=0),
    )


def back_product(gradient_rows, matrix):
    return jnp.einsum("fo,io->fi", gradient_rows, matrix, preferred_element_type=jnp.float32)


def xor_permute(value, axis_name, bit):
    size = lax.axis_size(axis_name)
    return lax.ppermute(value, axis_name, [(i, i ^ bit) for i in range(size)])


def bits_of(axis_name):
    size, bits, bit = lax.axis_size(axis_name), [], 1
    while bit < size:
        bits.append(bit)
        bit *= 2
    return bits


def xor_sum(value, axis_name):
    for bit in bits_of(axis_name):
        value = value + xor_permute(value, axis_name, bit)
    return value


def gather_left(rows):
    for bit in reversed(bits_of("utt")):
        rows = jnp.concatenate([rows, xor_permute(rows, "utt", bit)], axis=0)
    return rows


def gather_right(rows):
    place = lax.axis_index("utt")
    for bit in reversed(bits_of("utt")):
        mine = (place & bit) // bit
        width = rows.shape[1] // 2
        kept = lax.dynamic_slice_in_dim(rows, mine * width, width, 1)
        given = lax.dynamic_slice_in_dim(rows, (1 - mine) * width, width, 1)
        rows = jnp.concatenate([kept, xor_permute(given, "utt", bit)], axis=0)
    return rows


def gather_ordered(value, axis):
    place = lax.axis_index("utt")
    for bit in bits_of("utt"):
        other = xor_permute(value, "utt", bit)
        low = (place & bit) == 0
        value = jnp.concatenate(
            [jnp.where(low, value, other), jnp.where(low, other, value)], axis=axis
        )
    return value


def scatter_rows(tile):
    place = lax.axis_index("seq")
    for bit in bits_of("seq"):
        mine = (place & bit) // bit
        rest = lax.axis_size("seq") // (2 * bit)
        pieces = tile.reshape(rest, 2, -1, tile.shape[-1])
        kept = lax.dynamic_index_in_dim(pieces, mine, 1, keepdims=False)
        given = lax.dynamic_index_in_dim(pieces, 1 - mine, 1, keepdims=False)
        given = xor_permute(given, "seq", bit)
        tile = (kept.astype(jnp.float32) + given.astype(jnp.float32)).astype(jnp.bfloat16)
    return tile.reshape(-1, tile.shape[-1])


def weight_grad(left_all, right_rows):
    right_all = gather_right(right_rows)
    tile = jnp.einsum(
        "fi,fo->io", left_all, right_all, preferred_element_type=jnp.float32
    ).astype(jnp.bfloat16)
    tile = tile.reshape(-1, tile.shape[-1])
    piece = scatter_rows(tile)
    return gather_ordered(piece, 1).astype(jnp.float32)


def swap_halves(values, lower):
    return jnp.where(lower, pltpu.roll(values, 96, 1), pltpu.roll(values, 32, 1))


def lower_half(shape):
    return lax.broadcasted_iota(jnp.int32, shape, 1) % HEAD_DIM < HEAD_DIM // 2


def head_scores(q, k, seg_q, seg_k):
    scores = lax.dot_general(q, k, (((1,), (1,)), ((), ())), preferred_element_type=jnp.float32)
    return jnp.where(seg_q == seg_k, jnp.exp(scores * 0.125), 0.0)


MESH = pl.DeviceIdType.MESH
VMEM_LIMIT = 62 * 1024 * 1024


def flip(index, bit):
    return index + bit - 2 * bit * ((index // bit) % 2)


def everywhere(memory):
    return pl.BlockSpec(memory_space=memory)


class Links:
    def __init__(self, send_sems, recv_sems, local_sems):
        self.send_sems, self.recv_sems, self.local_sems = send_sems, recv_sems, local_sems
        self.sent, self.held = [], 0
        self.utt, self.seq = lax.axis_index("utt"), lax.axis_index("seq")

    def enter(self, utt_peers, seq_peers):
        barrier = pltpu.get_barrier_semaphore()
        targets = [self.mate(r) for r in utt_peers] + [self.peer(r) for r in seq_peers]
        for target in targets:
            pl.semaphore_signal(barrier, inc=1, device_id=target, device_id_type=MESH)
        pl.semaphore_wait(barrier, len(targets))

    def mate(self, offset):
        return (self.utt_of(offset), self.seq)

    def utt_of(self, offset):
        place = self.utt
        for bit in (1, 2):
            if offset & bit:
                place = flip(place, bit)
        return place

    def seq_of(self, offset):
        place = self.seq
        for bit in (1, 2, 4):
            if offset & bit:
                place = flip(place, bit)
        return place

    def peer(self, offset):
        return (self.utt, self.seq_of(offset))

    def send(self, source, target, device):
        index = len(self.sent)
        copy = pltpu.make_async_remote_copy(
            src_ref=source,
            dst_ref=target,
            send_sem=self.send_sems.at[index],
            recv_sem=self.recv_sems.at[index],
            device_id=device,
            device_id_type=MESH,
        )
        copy.start()
        self.sent.append(copy)
        return copy

    def keep(self, source, target):
        copy = pltpu.make_async_copy(source, target, self.local_sems.at[self.held])
        self.held += 1
        copy.start()
        return copy

    def leave(self):
        assert len(self.sent) <= self.send_sems.shape[0]
        assert self.held <= self.local_sems.shape[0]
        for copy in self.sent:
            copy.wait_send()


class Gathered:
    def __init__(self, links, source, target, columns=None):
        self.links, self.target = links, target
        self.rows = source.shape[0]
        self.columns = columns
        self.own = links.keep(source, self.slot(0))
        self.across = links.send(source, self.slot(2), links.mate(2))
        self.beside = links.send(source, self.slot(1), links.mate(1))

    def slot(self, offset):
        rows = pl.ds(offset * self.rows, self.rows)
        if self.columns is None:
            return self.target.at[rows, :]
        return self.target.at[rows, self.columns]

    def relay(self):
        self.across.wait_recv()
        self.relayed = self.links.send(self.slot(2), self.slot(3), self.links.mate(1))

    def wait(self):
        self.own.wait()
        self.beside.wait_recv()
        self.relayed.wait_recv()


class Quarter:
    def __init__(self, links, piece_of, target, columns=None):
        rows = target.shape[0] // 4
        columns = pl.ds(0, target.shape[1]) if columns is None else columns
        slot = lambda r: target.at[pl.ds(r * rows, rows), columns]
        self.own = links.keep(piece_of(links.utt), slot(0))
        self.copies = [
            links.send(piece_of(links.utt_of(r)), slot(r), links.mate(r)) for r in (2, 3, 1)
        ]

    def wait(self):
        self.own.wait()
        for copy in self.copies:
            copy.wait_recv()


class Share:
    def __init__(self, links, y_first, left, right, columns, tile, got_a, got_b, got_z2, result):
        self.links, self.y_first = links, y_first
        self.left, self.right, self.columns = left, right, columns
        self.tile, self.got_a, self.got_b, self.got_z2 = tile, got_a, got_b, got_z2
        self.result = result
        seq = links.seq
        self.y, self.zl, self.zh = seq % 2, (seq // 2) % 2, seq // 4
        if y_first:
            self.a, self.b, self.peers = self.y, self.zl, (1, 2)
        else:
            self.a, self.b, self.peers = self.zl, self.y, (2, 1)

    def place(self, zh, a, b):
        return (zh, b, a) if self.y_first else (zh, a, b)

    def product(self, a):
        rows = self.tile.shape[3]

        def block(step, _):
            zh, b = step // 2, step % 2
            here = self.place(zh, a, b)
            base = pl.multiple_of((4 * zh + 2 * here[1] + here[2]) * rows, rows)
            self.tile[here] = lax.dot_general(
                self.left[:, pl.ds(base, rows)],
                self.right[:, self.columns],
                (((0,), (0,)), ((), ())),
                preferred_element_type=jnp.float32,
            ).astype(jnp.bfloat16)
            return 0

        lax.fori_loop(0, 4, block, 0)

    def start(self):
        self.product(1 - self.a)
        given = (
            self.tile.at[:, :, 1 - self.a] if self.y_first else self.tile.at[:, 1 - self.a]
        )
        self.sent_a = self.links.send(given, self.got_a, self.links.peer(self.peers[0]))
        self.product(self.a)

    def add(self, index, got):
        tile = self.tile
        tile[index] = (tile[index].astype(jnp.float32) + got.astype(jnp.float32)).astype(
            jnp.bfloat16
        )

    def after_a(self):
        self.sent_a.wait_recv()

        def block(zh, _):
            self.add(self.place(zh, self.a, 1 - self.b), self.got_a[zh, 1 - self.b])
            return 0

        lax.fori_loop(0, 2, block, 0)
        _, low, y = self.place(0, self.a, 1 - self.b)
        self.sent_b = self.links.send(
            self.tile.at[:, low, y], self.got_b, self.links.peer(self.peers[1])
        )

        def rest(zh, _):
            self.add(self.place(zh, self.a, self.b), self.got_a[zh, self.b])
            return 0

        lax.fori_loop(0, 2, rest, 0)

    def after_b(self):
        self.sent_b.wait_recv()
        self.add((1 - self.zh, self.zl, self.y), self.got_b[1 - self.zh])
        self.sent_z2 = self.links.send(
            self.tile.at[1 - self.zh, self.zl, self.y], self.got_z2, self.links.peer(4)
        )
        self.add((self.zh, self.zl, self.y), self.got_b[self.zh])

    def after_z2(self):
        self.sent_z2.wait_recv()
        links = self.links
        mine = self.result(links.utt)
        mine[...] = (
            self.tile[self.zh, self.zl, self.y].astype(jnp.float32)
            + self.got_z2[...].astype(jnp.float32)
        ).astype(jnp.bfloat16)
        self.across = links.send(mine, mine, links.mate(2))
        self.beside = links.send(mine, mine, links.mate(1))

    def relay(self):
        self.across.wait_recv()
        links = self.links
        theirs = self.result(links.utt_of(2))
        self.relayed = links.send(theirs, theirs, links.mate(1))

    def wait(self):
        self.beside.wait_recv()
        self.relayed.wait_recv()


def share_scratch(rows, columns):
    return [
        pltpu.VMEM((2, 2, 2, rows, columns), jnp.bfloat16),
        pltpu.VMEM((2, 2, rows, columns), jnp.bfloat16),
        pltpu.VMEM((2, rows, columns), jnp.bfloat16),
        pltpu.VMEM((rows, columns), jnp.bfloat16),
    ]


def run_shares(shares, hooks):
    stages = ("after_a", "after_b", "after_z2", "relay", "wait")
    for turn in range(len(shares) + len(stages) - 1):
        for hook in hooks.get(turn, ()):
            hook()
        for place, stage in enumerate(stages):
            if 0 <= turn - place < len(shares):
                getattr(shares[turn - place], stage)()


def semaphores(count):
    return [pltpu.SemaphoreType.DMA((count,))] * 2 + [pltpu.SemaphoreType.DMA((32,))]


def comm_params(collective_id):
    return pltpu.CompilerParams(
        collective_id=collective_id, has_side_effects=True, vmem_limit_bytes=VMEM_LIMIT
    )


class Frames:
    def __init__(self, utts, lengths_ref):
        self.starts, self.ends, end = [], [], 0
        for u in range(utts):
            self.starts.append(end)
            end = end + lengths_ref[0, u]
            self.ends.append(end)

    def segment(self, frame):
        return sum((frame >= end).astype(jnp.int32) for end in self.ends)

    def of(self, segment, values):
        total = jnp.zeros_like(segment)
        for u, value in enumerate(values):
            total = jnp.where(segment == u, value, total)
        return total


def frame_column(first, count):
    return first + lax.broadcasted_iota(jnp.int32, (count, 1), 0)


def per_frame(mod_ref, segment, utts, piece, model):
    columns = slice(piece * model, (piece + 1) * model)
    value = jnp.broadcast_to(mod_ref[0:1, columns], (segment.shape[0], model))
    for u in range(1, utts):
        value = jnp.where(segment == u, mod_ref[u : u + 1, columns], value)
    return value


FAR_FIRST = (6, 7, 4, 5, 2, 3, 1)


def attend_kernel(
    utts, lengths_ref, chars_ref, drop_ref, flow_ref, act_ref, table_ref, frames_ref, skip_ref,
    b_skip_ref, b_mod_ref, b_qkv_ref, w_skip_ref, w_mod_ref, w_qkv_ref,
    attn_ref, heads_ref, exact_ref, total_ref, loss_ref, flows_ref, norm_all, joined_all,
    resid_ref, mod_ref, cos_ref, sin_ref,
    attn_heads, counts_got, sums_ref, flow_own, packed, norm_ref, w_skip, w_mod, w_qkv,
    send_sems, recv_sems, local_sems,
):
    links = Links(send_sems, recv_sems, local_sems)
    rows, model = frames_ref.shape
    total_rows = heads_ref.shape[0]
    early, late = pl.ds(0, 2 * model), pl.ds(2 * model, 4 * model)
    load_skip = links.keep(w_skip_ref, w_skip)
    load_early = links.keep(w_mod_ref.at[:, early], w_mod.at[:, early])
    load_qkv = links.keep(w_qkv_ref, w_qkv)
    load_late = links.keep(w_mod_ref.at[:, late], w_mod.at[:, late])
    links.enter((1, 2, 3), range(1, 8))
    gathers = [
        Gathered(links, frames_ref, joined_all, pl.ds(0, model)),
        Gathered(links, skip_ref, joined_all, pl.ds(model, model)),
    ]
    flow_own[...] = jnp.zeros_like(flow_own)
    flow_own[0:1, 0:utts] = flow_ref[...]
    flows_ref[links.utt] = flow_own[...]
    flow_copies = [
        links.send(flow_own, flows_ref.at[links.utt], links.mate(r)) for r in (1, 2, 3)
    ]
    tables = Frames(utts, lengths_ref)
    first_row = pl.multiple_of(links.seq * rows, rows)
    own_rows = pl.ds(first_row, rows)
    frame = frame_column(links.seq * rows, rows)
    segment = tables.segment(frame)
    position = frame - tables.of(segment, tables.starts)
    prompt = tables.of(segment, [chars_ref[0, u] for u in range(utts)])
    in_loss = jnp.where(position >= prompt, 1.0, 0.0)
    across = lax.broadcasted_iota(jnp.int32, (rows, rows), 1)
    down = lax.broadcasted_iota(jnp.int32, (rows, rows), 0)
    dropped = jnp.sum(
        jnp.where(across == down, drop_ref[...].astype(jnp.float32), 0.0), axis=1, keepdims=True
    )
    lane = lax.broadcasted_iota(jnp.int32, sums_ref.shape, 1)
    n_drop = jnp.sum(in_loss * dropped, axis=0, keepdims=True)
    n_keep = jnp.sum(in_loss * (1.0 - dropped), axis=0, keepdims=True)
    sums_ref[...] = jnp.where(lane == 0, n_drop, jnp.where(lane == 1, n_keep, 0.0))
    targets = [links.mate(1), links.mate(2), links.peer(1), links.peer(2), links.peer(4)]
    turn = []

    def count_turn():
        place = len(turn)
        if place > 0:
            turn[-1].wait_recv()
            sums_ref[...] = sums_ref[...] + counts_got[place - 1]
        if place < 5:
            counts_got[5 + place] = sums_ref[...]
            turn.append(
                links.send(counts_got.at[5 + place], counts_got.at[place], targets[place])
            )

    count_turn()
    quarter = total_rows // 4
    for out, kind in ((cos_ref, 0), (sin_ref, 1)):
        for j in range(4):
            block = table_ref[kind, :, 32 * j : 32 * (j + 1)]
            if kind == 0:
                wide = jnp.concatenate([block] * 4, axis=1)
            else:
                wide = jnp.concatenate([-block, block] * 2, axis=1)
            out[j * quarter : (j + 1) * quarter, :] = wide
    load_skip.wait()
    residual = (
        jnp.dot(frames_ref[...], w_skip[0:model, :], preferred_element_type=jnp.float32)
        + jnp.dot(skip_ref[...], w_skip[model:, :], preferred_element_type=jnp.float32)
        + b_skip_ref[...]
    )
    resid_ref[...] = residual
    count_turn()

    def modulate_columns(columns):
        mod_ref[:, columns] = (
            jnp.dot(act_ref[...], w_mod[:, columns], preferred_element_type=jnp.float32)
            + b_mod_ref[:, columns]
        )

    load_early.wait()
    modulate_columns(slice(0, 2 * model))
    unit, _ = normal_parts(residual)
    norm_ref[...] = (
        unit * (1.0 + per_frame(mod_ref, segment, utts, 1, model))
        + per_frame(mod_ref, segment, utts, 0, model)
    ).astype(jnp.bfloat16)
    gathers.append(Gathered(links, norm_ref, norm_all))
    count_turn()
    load_qkv.wait()
    cos, sin = cos_ref[own_rows, :], sin_ref[own_rows, :]
    lower = lower_half((rows, 128))

    def project(place, base):
        columns = pl.ds(pl.multiple_of(base + place * 128, 128), 128)
        return (
            jnp.dot(norm_ref[...], w_qkv[:, columns], preferred_element_type=jnp.float32)
            + b_qkv_ref[:, columns]
        )

    def pack(place):
        q, k = project(place, 0), project(place, model)
        packed[place, :, 0:128] = (q * cos + swap_halves(q, lower) * sin).astype(jnp.bfloat16)
        packed[place, :, 128:256] = (k * cos + swap_halves(k, lower) * sin).astype(jnp.bfloat16)
        packed[place, :, 256:384] = project(place, 2 * model).astype(jnp.bfloat16)

    incoming = []
    for r in FAR_FIRST:
        place = links.seq_of(r)
        pack(place)
        incoming.append(
            links.send(packed.at[place], heads_ref.at[own_rows, :], links.peer(r))
        )
    pack(links.seq)
    own = links.keep(packed.at[links.seq], heads_ref.at[own_rows, :])
    count_turn()
    load_late.wait()
    modulate_columns(slice(2 * model, 6 * model))
    count_turn()
    gathers[0].relay()
    gathers[1].relay()
    count_turn()
    n_drop, n_keep = sums_ref[0:1, 0:1], sums_ref[0:1, 1:2]
    loss_weight = (
        in_loss
        * (n_drop + n_keep)
        * 0.5
        * (dropped / (n_drop + 1.0) + (1.0 - dropped) / (n_keep + 1.0))
    )
    loss_ref[...] = jnp.broadcast_to(loss_weight, loss_ref.shape)
    own.wait()
    for copy in incoming:
        copy.wait_recv()
    first = lax.broadcasted_iota(jnp.int32, (256, 128), 1) < HEAD_DIM
    zero = jnp.zeros((256, 128), jnp.bfloat16)
    k, v = heads_ref[:, 128:256], heads_ref[:, 256:384]
    seg_k = tables.segment(lax.broadcasted_iota(jnp.int32, (1, total_rows), 1))

    def block(step, _):
        here = pl.ds(pl.multiple_of(step * 256, 256), 256)
        q, seg_q = heads_ref[here, 0:128], tables.segment(frame_column(step * 256, 256))
        results = []
        for mine in (first, jnp.logical_not(first)):
            weights = head_scores(jnp.where(mine, q, zero), k, seg_q, seg_k)
            total = jnp.sum(weights, axis=1, keepdims=True)
            summed = jnp.dot(weights.astype(jnp.bfloat16), v, preferred_element_type=jnp.float32)
            results.append((summed, total))
        total = jnp.where(first, results[0][1], results[1][1])
        attended = jnp.where(first, results[0][0], results[1][0]) / total
        attn_heads[here, :] = attended.astype(jnp.bfloat16)
        exact_ref[here, :] = attended
        total_ref[here, :] = total
        return 0

    lax.fori_loop(0, total_rows // 256, block, 0)
    column = attn_ref.at[:, pl.ds(pl.multiple_of(links.seq * 128, 128), 128)]
    part = lambda place: attn_heads.at[pl.ds(pl.multiple_of(place * rows, rows), rows), :]
    own = links.keep(part(links.seq), column)
    incoming = [
        links.send(part(links.seq_of(r)), column, links.peer(r)) for r in FAR_FIRST
    ]
    gathers[2].relay()
    for copy in flow_copies:
        copy.wait_recv()
    own.wait()
    for copy in incoming:
        copy.wait_recv()
    for gather in gathers:
        gather.wait()
    links.leave()


def attend(
    lengths, chars, drop, flow, act, table, frames, skip, b_skip, b_mod, b_qkv, w_skip, w_mod,
    w_qkv, shards,
):
    rows, width = frames.shape
    total_rows = shards * rows
    utts = flow.shape[1]
    vmem, there, scalar = everywhere(pltpu.VMEM), everywhere(pl.ANY), everywhere(pltpu.SMEM)
    shape = jax.ShapeDtypeStruct
    bf16 = lambda *dims: pltpu.VMEM(dims, jnp.bfloat16)
    return pl.pallas_call(
        partial(attend_kernel, utts),
        in_specs=[scalar] * 2 + [vmem] * 9 + [there] * 3,
        out_specs=[vmem] * 12,
        out_shape=[
            shape((rows, width), jnp.bfloat16),
            shape((total_rows, 384), jnp.bfloat16),
            shape((total_rows, 128), jnp.float32),
            shape((total_rows, 128), jnp.float32),
            shape((rows, 128), jnp.float32),
            shape((4, 8, 128), jnp.float32),
            shape((4 * rows, width), jnp.bfloat16),
            shape((4 * rows, 2 * width), jnp.bfloat16),
            shape((rows, width), jnp.float32),
            shape((8, 6 * width), jnp.float32),
            shape((total_rows, 128), jnp.float32),
            shape((total_rows, 128), jnp.float32),
        ],
        scratch_shapes=[
            bf16(total_rows, 128),
            pltpu.VMEM((10, 8, 128), jnp.float32),
            pltpu.VMEM((8, 128), jnp.float32),
            pltpu.VMEM((8, 128), jnp.float32),
            bf16(shards, rows, 384),
            bf16(rows, width),
            bf16(*w_skip.shape),
            bf16(*w_mod.shape),
            bf16(*w_qkv.shape),
        ]
        + semaphores(40),
        compiler_params=comm_params(1),
    )(
        lengths, chars, drop, flow, act, table, frames, skip,
        b_skip[None, :], b_mod[None, :], b_qkv[None, :], w_skip, w_mod, w_qkv,
    )


ALONG = (((1,), (1,)), ((), ()))
DOWN = (((0,), (0,)), ((), ()))


def normal_parts(values):
    centred = values - jnp.mean(values, axis=1, keepdims=True)
    scale = lax.rsqrt(jnp.mean(centred * centred, axis=1, keepdims=True) + EPSILON)
    return centred * scale, scale


def normal_back(inward, unit, scale):
    return scale * (
        inward
        - jnp.mean(inward, axis=1, keepdims=True)
        - unit * jnp.mean(inward * unit, axis=1, keepdims=True)
    )


def column_sum(values):
    return jnp.sum(values.astype(jnp.float32), axis=0, keepdims=True)


def backward_kernel(
    utts, lengths_ref, attn_ref, resid_ref, mod_ref, loss_ref, out_grad_ref,
    b_out_ref, b_up_ref, b_down_ref,
    heads_ref, exact_ref, total_ref, cos_ref, sin_ref,
    norm_a_ref, joined_ref, w_out_ref, w_up_ref, w_down_ref, w_qkv_ref, w_skip_ref,
    mixed, g_down, g_up, g_out, g_qkv, g_skip, smalls, g_frames, g_skip_in,
    d_ff, norm_f, act, d_inner, d_branch, d_attn, pieces, d_mid, ff_sum, d_norm,
    grad_heads, d_heads, dk_ref, dv_ref,
    d_ff_all, act_all, norm_all, d_inner_all, attn_all, d_branch_all,
    norm_a_all, joined_all, d_qkv, d_qkv_all, d_resid, d_resid_all,
    up_ring, down_ring, w_out, w_qkv, w_skip, small_own, small_got, small_sum,
    *rest,
):
    tiles, (send_sems, recv_sems, local_sems, ring_sems) = rest[:-4], rest[-4:]
    links = Links(send_sems, recv_sems, local_sems)
    rows, model = resid_ref.shape
    block_width = up_ring.shape[2]
    steps = w_up_ref.shape[1] // block_width

    def ring(c):
        slot = c % 2
        columns = pl.ds(pl.multiple_of(c * block_width, block_width), block_width)
        return (
            pltpu.make_async_copy(w_up_ref.at[:, columns], up_ring.at[slot], ring_sems.at[slot]),
            pltpu.make_async_copy(
                w_down_ref.at[columns, :], down_ring.at[slot], ring_sems.at[2 + slot]
            ),
        )

    load_out = links.keep(w_out_ref, w_out)
    for c in (0, 1):
        for copy in ring(c):
            copy.start()
    loads = [
        links.keep(w_qkv_ref, w_qkv),
        links.keep(w_skip_ref, w_skip),
        links.keep(norm_a_ref, norm_a_all),
        links.keep(joined_ref, joined_all),
    ]
    links.enter((1, 2, 3), range(1, 8))

    tables = Frames(utts, lengths_ref)
    segment = tables.segment(frame_column(links.seq * rows, rows))

    def modulation(piece):
        return per_frame(mod_ref, segment, utts, piece, model)

    def d_out():
        return out_grad_ref[...].astype(jnp.float32) * loss_ref[:, 0:1]

    d_ff[...] = (modulation(5) * d_out()).astype(jnp.bfloat16)
    gather_d = Gathered(links, d_ff, d_ff_all)
    load_out.wait()
    branch = (
        jnp.dot(attn_ref[...], w_out[...], preferred_element_type=jnp.float32) + b_out_ref[...]
    )
    pieces[0] = branch
    mid = resid_ref[...] + modulation(2) * branch
    d_mid[...] = mid
    unit, _ = normal_parts(mid)
    norm_f[...] = (unit * (1.0 + modulation(4)) + modulation(3)).astype(jnp.bfloat16)
    ff_sum[...] = jnp.zeros_like(ff_sum)
    d_norm[...] = jnp.zeros_like(d_norm)
    const = math.sqrt(2.0 / math.pi)
    width = d_inner_all.shape[1]

    def feed(c, _):
        slot = c % 2
        columns = pl.ds(pl.multiple_of(c * block_width, block_width), block_width)
        for copy in ring(c):
            copy.wait()
        inner = (
            jnp.dot(norm_f[...], up_ring[slot], preferred_element_type=jnp.float32)
            + b_up_ref[:, columns]
        )
        square = inner * inner
        slope = jnp.tanh(const * inner * (1.0 + 0.044715 * square))
        gate = 0.5 * (1.0 + slope)
        act_b = (inner * gate).astype(jnp.bfloat16)
        turn = gate + 0.5 * inner * (1.0 - slope * slope) * (
            const * (1.0 + 3.0 * 0.044715 * square)
        )
        here = pl.ds(pl.multiple_of(c * 128, 128), 128)
        d_act = lax.dot_general(
            d_ff[...], down_ring[slot], ALONG, preferred_element_type=jnp.float32
        )
        d_inner_b = (turn * d_act).astype(jnp.bfloat16)
        for u in range(4):
            act[u, :, here] = act_b[:, u * 128 : (u + 1) * 128]
            d_inner[u, :, here] = d_inner_b[:, u * 128 : (u + 1) * 128]
        ff_sum[...] += jnp.dot(act_b, down_ring[slot], preferred_element_type=jnp.float32)
        d_norm[...] += lax.dot_general(
            d_inner_b, up_ring[slot], ALONG, preferred_element_type=jnp.float32
        )

        @pl.when(c + 2 < steps)
        def _():
            for copy in ring(c + 2):
                copy.start()

        return 0

    middle = width // 2
    left_half, right_half = pl.ds(0, middle), pl.ds(middle, middle)
    lax.fori_loop(0, steps // 2, feed, 0)
    quarters_a = [Quarter(links, lambda u: act.at[u, :, left_half], act_all, left_half)]
    lax.fori_loop(steps // 2, steps, feed, 0)
    gather_d.relay()
    quarters_a.append(Quarter(links, lambda u: act.at[u, :, right_half], act_all, right_half))
    gather_n = Gathered(links, norm_f, norm_all)
    own_rows = pl.ds(pl.multiple_of(links.seq * rows, rows), rows)
    strip = lambda ref, place, size: ref.at[
        :, pl.ds(pl.multiple_of(place * size, size), size)
    ]
    narrow = d_branch_all.shape[1]
    quarter_i = Quarter(links, lambda u: d_inner.at[u], d_inner_all)
    mid = d_mid[...]
    unit, scale = normal_parts(mid)
    d_norm_f = d_norm[...]
    pieces[2] = d_norm_f * unit
    d_mid_f = d_out() + normal_back(d_norm_f * (1.0 + modulation(4)), unit, scale)
    gate_a = modulation(2)
    d_branch[...] = (gate_a * d_mid_f).astype(jnp.bfloat16)
    pieces[0] = pieces[0] * d_mid_f
    d_mid[...] = d_mid_f
    d_attn[...] = lax.dot_general(
        d_branch[...], w_out[...], ALONG, preferred_element_type=jnp.float32
    ).astype(jnp.bfloat16)
    own = links.keep(strip(d_attn, links.seq, 128), grad_heads.at[own_rows, :])
    incoming_d = [
        links.send(
            strip(d_attn, links.seq_of(r), 128), grad_heads.at[own_rows, :], links.peer(r)
        )
        for r in FAR_FIRST
    ]
    quarter_b = Quarter(links, lambda u: strip(d_branch, u, narrow), d_branch_all)
    gather_b = Gathered(links, attn_ref, attn_all)
    ff_out = ff_sum[...] + b_down_ref[...]
    mixed[...] = (mid + modulation(5) * ff_out).astype(jnp.bfloat16)
    pieces[1] = d_out() * ff_out
    small_own[...] = jnp.zeros_like(small_own)
    small_own[4:5, :] = column_sum(d_branch[...])
    for c in range(4):
        small_own[5 + c : 6 + c, :] = column_sum(d_inner[c])
    small_own[9:10, :] = column_sum(d_ff[...])

    def utterance_sums(piece, values):
        for u in range(utts):
            row = 10 + utts * piece + u
            small_own[row : row + 1, :] = jnp.sum(
                jnp.where(segment == u, values, 0.0), axis=0, keepdims=True
            )

    utterance_sums(2, pieces[0])
    utterance_sums(3, d_norm[...])
    utterance_sums(4, pieces[2])
    utterance_sums(5, pieces[1])
    half = width // 2
    down_at = lambda h: lambda u: g_down.at[
        pl.ds(pl.multiple_of(u * 128, 128), 128), pl.ds(h * half, half)
    ]
    column_at = lambda ref, step, offset, size: lambda u: ref.at[
        :, pl.ds(pl.multiple_of(u * step + offset, 128), size)
    ]
    wide, thin = d_qkv_all.shape[1], d_resid_all.shape[1]
    third, slim = wide // 2, thin // 2
    plans = [
        (act_all, d_ff_all, pl.ds(0, half), down_at(0)),
        (act_all, d_ff_all, pl.ds(half, half), down_at(1)),
        (norm_all, d_inner_all, pl.ds(0, half), column_at(g_up, width, 0, half)),
        (norm_all, d_inner_all, pl.ds(half, half), column_at(g_up, width, half, half)),
        (attn_all, d_branch_all, pl.ds(0, narrow), column_at(g_out, narrow, 0, narrow)),
        (norm_a_all, d_qkv_all, pl.ds(0, third), column_at(g_qkv, wide, 0, third)),
        (norm_a_all, d_qkv_all, pl.ds(third, third), column_at(g_qkv, wide, third, third)),
        (joined_all, d_resid_all, pl.ds(0, slim), column_at(g_skip, thin, 0, slim)),
        (joined_all, d_resid_all, pl.ds(slim, slim), column_at(g_skip, thin, slim, slim)),
    ]
    y_first = (True, False, True, True, True, False, True, True, True)
    shares = [
        Share(links, y_first[i], left, right, columns, *tiles[4 * i : 4 * i + 4], result)
        for i, (left, right, columns, result) in enumerate(plans)
    ]
    gather_n.relay()
    gather_d.wait()
    for quarter in quarters_a:
        quarter.wait()
    shares[0].start()
    shares[1].start()
    own.wait()
    for copy in incoming_d:
        copy.wait_recv()
    dk_ref[...] = jnp.zeros_like(dk_ref)
    dv_ref[...] = jnp.zeros_like(dv_ref)
    first = lax.broadcasted_iota(jnp.int32, (256, 128), 1) < HEAD_DIM
    zero = jnp.zeros((256, 128), jnp.bfloat16)
    lower = lower_half((256, 128))
    k, v = heads_ref[:, 128:256], heads_ref[:, 256:384]
    seg_k = tables.segment(lax.broadcasted_iota(jnp.int32, (1, heads_ref.shape[0]), 1))

    def turned(values, here):
        return (
            values * cos_ref[here, :] - swap_halves(values, lower) * sin_ref[here, :]
        ).astype(jnp.bfloat16)

    def block(step, _):
        here = pl.ds(pl.multiple_of(step * 256, 256), 256)
        q, seg_q = heads_ref[here, 0:128], tables.segment(frame_column(step * 256, 256))
        scaled = grad_heads[here, :].astype(jnp.float32) / total_ref[here, :]
        grad_acc = scaled.astype(jnp.bfloat16)
        product = scaled * exact_ref[here, :]
        d_query = []
        for mine in (first, jnp.logical_not(first)):
            q_own = jnp.where(mine, q, zero)
            g_own = jnp.where(mine, grad_acc, zero)
            delta = jnp.sum(jnp.where(mine, product, 0.0), axis=1, keepdims=True)
            weights = head_scores(q_own, k, seg_q, seg_k)
            dots = lax.dot_general(g_own, v, ALONG, preferred_element_type=jnp.float32)
            d_scores = (weights * (dots - delta)).astype(jnp.bfloat16)
            d_query.append(jnp.dot(d_scores, k, preferred_element_type=jnp.float32))
            dk_ref[...] += lax.dot_general(
                d_scores, q_own, DOWN, preferred_element_type=jnp.float32
            )
            dv_ref[...] += lax.dot_general(
                weights.astype(jnp.bfloat16), g_own, DOWN, preferred_element_type=jnp.float32
            )
        d_heads[here, 0:128] = turned(jnp.where(first, d_query[0], d_query[1]) * 0.125, here)
        return 0

    blocks = heads_ref.shape[0] // 256
    lax.fori_loop(0, blocks, block, 0)

    def finish(step, _):
        here = pl.ds(pl.multiple_of(step * 256, 256), 256)
        d_heads[here, 128:256] = turned(dk_ref[here, :] * 0.125, here)
        d_heads[here, 256:384] = dv_ref[here, :].astype(jnp.bfloat16)
        return 0

    lax.fori_loop(0, blocks, finish, 0)
    part = lambda place, c: d_heads.at[
        pl.ds(pl.multiple_of(place * rows, rows), rows), pl.ds(c * 128, 128)
    ]
    home = lambda c: d_qkv.at[
        :, pl.ds(pl.multiple_of(c * model + links.seq * 128, 128), 128)
    ]
    owns = [links.keep(part(links.seq, c), home(c)) for c in range(3)]
    incoming = [
        links.send(part(links.seq_of(r), c), home(c), links.peer(r))
        for r in FAR_FIRST
        for c in range(3)
    ]
    gather_n.wait()
    quarter_i.wait()
    shares[2].start()
    shares[3].start()
    gather_b.relay()
    gather_b.wait()
    quarter_b.wait()
    shares[4].start()
    state = {}

    def projections():
        for copy in owns:
            copy.wait()
        for copy in incoming:
            copy.wait_recv()
        for copy in loads:
            copy.wait()
        state["qkv"] = Quarter(links, lambda u: strip(d_qkv, u, wide), d_qkv_all)
        d_norm_a = lax.dot_general(
            d_qkv[...], w_qkv[...], ALONG, preferred_element_type=jnp.float32
        )
        unit, scale = normal_parts(resid_ref[...])
        d_resid_f = d_mid[...] + normal_back(d_norm_a * (1.0 + modulation(1)), unit, scale)
        rounded = d_resid_f.astype(jnp.bfloat16)
        d_resid[...] = rounded
        state["resid"] = Quarter(links, lambda u: strip(d_resid, u, thin), d_resid_all)
        small_own[0:1, :] = column_sum(rounded)
        for c in range(3):
            small_own[1 + c : 2 + c, :] = column_sum(d_qkv[:, c * model : (c + 1) * model])
        utterance_sums(0, d_norm_a)
        utterance_sums(1, d_norm_a * unit)
        state["small"] = links.send(small_own, small_got.at[0], links.peer(1))

    def last_shares():
        state["qkv"].wait()
        shares[5].start()
        shares[6].start()
        state["resid"].wait()
        shares[7].start()
        shares[8].start()

    def inputs():
        for index, out in enumerate((g_frames, g_skip_in)):
            out[...] = lax.dot_general(
                d_resid[...],
                w_skip[pl.ds(index * model, model), :],
                ALONG,
                preferred_element_type=jnp.float32,
            ).astype(jnp.bfloat16)

    def small_y():
        state["small"].wait_recv()
        small_sum[0] = small_own[...] + small_got[0]
        state["small"] = links.send(small_sum.at[0], small_got.at[1], links.peer(2))

    def small_z1():
        state["small"].wait_recv()
        small_sum[1] = small_sum[0] + small_got[1]
        state["small"] = links.send(small_sum.at[1], small_got.at[2], links.peer(4))

    def small_z2():
        state["small"].wait_recv()
        mine = smalls.at[links.utt]
        mine[...] = small_sum[1] + small_got[2]
        state["spread"] = [links.send(mine, mine, links.mate(r)) for r in (2, 3, 1)]

    run_shares(
        shares,
        {
            1: (projections,),
            2: (last_shares,),
            3: (inputs, small_y),
            4: (small_z1,),
            5: (small_z2,),
        },
    )
    for copy in state["spread"]:
        copy.wait_recv()
    links.leave()


def backward(
    lengths, attn_b, resid, mod, loss, out_grad, b_out, b_up, b_down,
    heads, exact, total, cos, sin,
    norm_a_all, joined_all, w_out, w_up, w_down, w_qkv, w_skip,
):
    rows, model = resid.shape
    frames, inner = heads.shape[0], w_up.shape[1]
    utts = lengths.shape[1]
    small = (-(-(10 + 6 * utts) // 8) * 8, model)
    vmem, there = everywhere(pltpu.VMEM), everywhere(pl.ANY)
    shape = jax.ShapeDtypeStruct
    bf16 = lambda *dims: pltpu.VMEM(dims, jnp.bfloat16)
    f32 = lambda *dims: pltpu.VMEM(dims, jnp.float32)
    part, step = model // 8, inner // 8
    return pl.pallas_call(
        partial(backward_kernel, utts),
        in_specs=[everywhere(pltpu.SMEM)] + [vmem] * 13 + [there] * 7,
        out_specs=[vmem] * 9,
        out_shape=[
            shape((rows, model), jnp.bfloat16),
            shape((inner // 8, model), jnp.bfloat16),
            shape((part, inner), jnp.bfloat16),
            shape((part, model), jnp.bfloat16),
            shape((part, 3 * model), jnp.bfloat16),
            shape((2 * part, model), jnp.bfloat16),
            shape((4,) + small, jnp.float32),
            shape((rows, model), jnp.bfloat16),
            shape((rows, model), jnp.bfloat16),
        ],
        scratch_shapes=[
            bf16(rows, model),
            bf16(rows, model),
            bf16(4, rows, inner // 4),
            bf16(4, rows, inner // 4),
            bf16(rows, model),
            bf16(rows, model),
            f32(3, rows, model),
            f32(rows, model),
            f32(rows, model),
            f32(rows, model),
            bf16(frames, 128),
            bf16(frames, 384),
            f32(frames, 128),
            f32(frames, 128),
            bf16(4 * rows, model),
            bf16(4 * rows, inner // 4),
            bf16(4 * rows, model),
            bf16(4 * rows, inner // 4),
            bf16(4 * rows, model),
            bf16(4 * rows, model // 4),
            bf16(4 * rows, model),
            bf16(4 * rows, 2 * model),
            bf16(rows, 3 * model),
            bf16(4 * rows, 3 * model // 4),
            bf16(rows, model),
            bf16(4 * rows, model // 4),
            bf16(2, model, step),
            bf16(2, step, model),
            bf16(*w_out.shape),
            bf16(*w_qkv.shape),
            bf16(*w_skip.shape),
            f32(*small),
            f32(3, *small),
            f32(2, *small),
        ]
        + share_scratch(part, inner // 8) * 4
        + share_scratch(part, model // 4)
        + share_scratch(part, 3 * model // 8) * 2
        + share_scratch(2 * part, model // 8) * 2
        + semaphores(128)
        + [pltpu.SemaphoreType.DMA((4,))],
        compiler_params=comm_params(2),
    )(
        lengths, attn_b, resid, mod, loss, out_grad,
        b_out[None, :], b_up[None, :], b_down[None, :],
        heads, exact, total, cos, sin,
        norm_a_all, joined_all, w_out, w_up, w_down, w_qkv, w_skip,
    )


UP = 3


def finish_kernel(utts, shards, act_ref, *rest):
    kept_in, wide_in, smalls_in = rest[:3], rest[3:8], rest[8]
    kept_out, wide_out, mod_out, bias_out = rest[9:12], rest[12:17], rest[17], rest[18:24]
    kept, wide, staged = rest[24:27], rest[27:32], rest[32:37]
    smalls_ref, mod_stage, bias_stage, d_mod, totals, sems, load_sems = rest[37:]
    seq = lax.axis_index("seq")
    loads, copies = [], []
    for source, target in zip((*wide_in, smalls_in, *kept_in), (*wide, smalls_ref, *kept)):
        copy = pltpu.make_async_copy(source, target, load_sems.at[len(loads)])
        copy.start()
        loads.append(copy)

    def put(source, target):
        copy = pltpu.make_async_copy(source, target, sems.at[len(copies)])
        copy.start()
        copies.append(copy)

    model = smalls_ref.shape[2]
    lanes = 128
    for place, (source, stage, target) in enumerate(zip(wide, staged, wide_out)):
        loads[place].wait()
        if place == UP:
            for u in range(4):
                for c in range(shards):
                    stage[:, (4 * c + u) * lanes : (4 * c + u + 1) * lanes] = source[
                        :, u * model + c * lanes : u * model + (c + 1) * lanes
                    ].astype(jnp.float32)
        else:
            stage[...] = source[...].astype(jnp.float32)
        put(stage, target)
    groups = smalls_ref.shape[0]
    loads[5].wait()
    bias_sum = (
        smalls_ref[0, 0:10] + smalls_ref[1, 0:10] + smalls_ref[2, 0:10] + smalls_ref[3, 0:10]
    )
    for row in range(10):
        totals[row, 0:1] = bias_sum[row : row + 1]
    d_mod[...] = jnp.zeros_like(d_mod)
    for piece in range(6):
        first = 10 + utts * piece
        for g in range(groups):
            d_mod[piece, g * utts : (g + 1) * utts, :] = smalls_ref[g, first : first + utts, :]
        rows = d_mod[piece]
        totals[10 + piece, 0:1] = jnp.sum(rows, axis=0, keepdims=True)
        columns = slice(piece * model, (piece + 1) * model)
        mod_stage[:, columns] = jnp.dot(
            act_ref[...], rows, precision=HIGHEST_PRECISION, preferred_element_type=jnp.float32
        )
    put(mod_stage, mod_out)
    for load, source, target in zip(loads[6:], kept, kept_out):
        load.wait()
        put(source, target)
    line = model // lanes
    first = 0
    for place, target in enumerate(bias_out):
        count = target.shape[1] // lanes
        for i in range(count):
            unit = i * line + seq if place == UP else seq * count + i
            column = pl.multiple_of((unit % line) * lanes, lanes)
            bias_stage[place, 0:1, i * lanes : (i + 1) * lanes] = totals[
                first + unit // line, 0:1, pl.ds(column, lanes)
            ]
        first += count * shards // line
        put(bias_stage.at[place, pl.ds(0, 1), pl.ds(0, count * lanes)], target)
    for copy in copies:
        copy.wait()


def finish(shards, utts, act_own, smalls, mixed, frames, skip, grads):
    vmem, there = everywhere(pltpu.VMEM), everywhere(pl.ANY)
    shape = jax.ShapeDtypeStruct
    model = smalls.shape[2]
    own = model // shards
    depth = act_own.shape[1]
    mod_shape = (own, 6 * model)
    widths = [own, 3 * own, own, 4 * own, own, 6 * own]
    kept = (mixed, frames, skip)
    outs = pl.pallas_call(
        partial(finish_kernel, utts, shards),
        in_specs=[vmem] + [there] * 9,
        out_specs=[there] * 15,
        out_shape=[shape(v.shape, v.dtype) for v in kept]
        + [shape(g.shape, jnp.float32) for g in grads]
        + [shape(mod_shape, jnp.float32)]
        + [shape((1, w), jnp.float32) for w in widths],
        scratch_shapes=[pltpu.VMEM(v.shape, v.dtype) for v in (*kept, *grads)]
        + [pltpu.VMEM(g.shape, jnp.float32) for g in grads]
        + [
            pltpu.VMEM(smalls.shape, jnp.float32),
            pltpu.VMEM(mod_shape, jnp.float32),
            pltpu.VMEM((6, 8, max(widths)), jnp.float32),
            pltpu.VMEM((6, depth, model), jnp.float32),
            pltpu.VMEM((16, 8, model), jnp.float32),
            pltpu.SemaphoreType.DMA((15,)),
            pltpu.SemaphoreType.DMA((9,)),
        ],
        compiler_params=pltpu.CompilerParams(vmem_limit_bytes=VMEM_LIMIT),
    )(act_own, *kept, *grads, smalls)
    return outs[:9], [v.reshape(-1) for v in outs[9:]]


def own_time_act(flows, seq_place, shards, model):
    half_dim, own = model // 2, model // shards
    column = seq_place * own + jnp.arange(own, dtype=jnp.int32)
    inverse = jnp.exp(
        -math.log(10000.0) * (column % half_dim).astype(jnp.float32) / half_dim
    )
    angles = 1000.0 * flows[None, :] * inverse[:, None]
    wave = jnp.where((column < half_dim)[:, None], jnp.sin(angles), jnp.cos(angles))
    return jax.nn.silu(wave).astype(jnp.bfloat16).astype(jnp.float32)


def compact_tables(lengths, total_rows):
    half_dim = HEAD_DIM // 2
    shape = (total_rows // 4, 128)
    lane = lax.broadcasted_iota(jnp.int32, shape, 1)
    frame = lax.broadcasted_iota(jnp.int32, shape, 0) + (lane // half_dim) * shape[0]
    start, end = jnp.zeros(shape, jnp.int32), jnp.int32(0)
    for u in range(lengths.shape[0]):
        end = end + lengths[u]
        start = jnp.where(frame >= end, end, start)
    inverse = jnp.exp(
        -math.log(10000.0) * 2.0 * (lane % half_dim).astype(jnp.float32) / HEAD_DIM
    )
    angles = (frame - start).astype(jnp.float32) * inverse
    return jnp.stack([jnp.cos(angles), jnp.sin(angles)])


def padded_time_act(flow_vals, model):
    half_dim = model // 2
    column = jnp.arange(model, dtype=jnp.int32)
    inverse = jnp.exp(-math.log(10000.0) * (column % half_dim).astype(jnp.float32) / half_dim)
    flow_vals = jnp.pad(flow_vals, (0, 8 - flow_vals.shape[0]))
    angles = 1000.0 * flow_vals[:, None] * inverse[None, :]
    wave = jnp.where((column < half_dim)[None, :], jnp.sin(angles), jnp.cos(angles))
    return jax.nn.silu(wave).astype(jnp.bfloat16)


def local(
    frames_in,
    skip_in,
    flow_times,
    frame_lengths,
    char_lengths,
    drop_mask,
    out_grad,
    w_skip,
    b_skip,
    w_mod,
    b_mod,
    w_qkv,
    b_qkv,
    w_out,
    b_out,
    w_up,
    b_up,
    w_down,
    b_down,
):
    local_rows = frames_in.shape[1]
    model_width = frames_in.shape[2]
    shards = lax.axis_size("seq")
    seq_place = lax.axis_index("seq")
    lengths = frame_lengths[0]
    whole = model_width * 4
    fused = (
        lax.axis_size("utt") == 4
        and shards == 8
        and HEADS * HEAD_DIM == 1024
        and model_width == 1024
        and w_up.shape[1] == whole
        and local_rows == 128
        and flow_times.shape[1] <= 8
    )
    if not fused:
        utt_ends = jnp.cumsum(lengths)
        segment, position, in_loss, member = frame_tables(
            lengths, char_lengths[0], seq_place * local_rows, local_rows
        )
        member_f = member.astype(jnp.float32)
        loss_mask = in_loss.astype(jnp.float32)
        dropped = drop_mask[0].astype(jnp.float32)
        counts = jnp.stack([jnp.sum(loss_mask * dropped), jnp.sum(loss_mask * (1.0 - dropped))])
        counts = jnp.pad(counts[None, :], ((0, 7), (0, 126)))
        counts = xor_sum(xor_sum(counts, "utt"), "seq")
        time_act = jax.nn.silu(time_embed(flow_times[0], model_width)).astype(jnp.bfloat16)
        mod_u = jnp.dot(time_act, w_mod, preferred_element_type=jnp.float32) + b_mod
        mod_f = jnp.dot(member_f, mod_u, precision=HIGHEST_PRECISION)
        shift_a, scale_a, gate_a, shift_f, scale_f, gate_f = jnp.split(mod_f, 6, axis=1)
        joined = jnp.concatenate([frames_in[0], skip_in[0]], axis=1)
        residual = jnp.dot(joined, w_skip, preferred_element_type=jnp.float32) + b_skip
        norm_a = modulate(residual, scale_a, shift_a).astype(jnp.bfloat16)
        qkv_full = jnp.dot(norm_a, w_qkv, preferred_element_type=jnp.float32) + b_qkv
    if fused:
        (
            attn_b, qkv_heads, exact, total, loss, flows, norm_all, joined_all,
            residual, mod_u, cos_all, sin_all,
        ) = attend(
            frame_lengths,
            char_lengths,
            drop_mask,
            flow_times,
            padded_time_act(flow_times[0], model_width),
            compact_tables(lengths, local_rows * shards),
            frames_in[0],
            skip_in[0],
            b_skip,
            b_mod,
            b_qkv,
            w_skip,
            w_mod,
            w_qkv,
            shards,
        )
    else:
        angle_cos, angle_sin = rotary_tables(position, HEAD_DIM)
        queries = rotate(
            qkv_full[:, :model_width].reshape(local_rows, HEADS, HEAD_DIM), angle_cos, angle_sin
        ).astype(jnp.bfloat16)
        key_rot = rotate(
            qkv_full[:, model_width : 2 * model_width].reshape(local_rows, HEADS, HEAD_DIM),
            angle_cos,
            angle_sin,
        ).astype(jnp.bfloat16)
        key_value = jnp.stack(
            [
                key_rot.reshape(local_rows, model_width),
                qkv_full[:, 2 * model_width :].astype(jnp.bfloat16),
            ],
            axis=0,
        )
        start_state = (
            jnp.zeros((local_rows, HEADS, HEAD_DIM), jnp.float32),
            jnp.zeros((HEADS, local_rows), jnp.float32),
        )
        fwd_piece = partial(forward_piece, queries=queries, query_segment=segment, utt_ends=utt_ends)
        weighted, totals = over_blocks(
            partial(fwd_piece, usable=True),
            start_state,
            lax.all_gather(key_value, "seq", axis=1, tiled=True),
            jnp.int32(0),
            local_rows,
        )
        totals_rows = jnp.transpose(totals)
        attended = weighted / totals_rows[:, :, None]
        attn_b = attended.reshape(local_rows, model_width).astype(jnp.bfloat16)
    if fused:
        mixed, g_w_down, g_w_up, g_w_out, g_w_qkv, g_w_skip, smalls, g_frames, g_skip_in = backward(
            frame_lengths,
            attn_b,
            residual,
            mod_u,
            loss,
            out_grad[0],
            b_out,
            b_up,
            b_down,
            qkv_heads,
            exact,
            total,
            cos_all,
            sin_all,
            norm_all,
            joined_all,
            w_out,
            w_up,
            w_down,
            w_qkv,
            w_skip,
        )
        utts = flow_times.shape[1]
        act_own = own_time_act(flows[:, 0, :utts].reshape(-1), seq_place, shards, model_width)
        act_own = jnp.pad(act_own, ((0, 0), (0, -act_own.shape[1] % 8)))
        wide, biases = finish(
            shards,
            utts,
            act_own,
            smalls,
            mixed,
            g_frames,
            g_skip_in,
            (g_w_skip, g_w_qkv, g_w_out, g_w_up, g_w_down),
        )
        mixed, g_frames, g_skip_in, g_w_skip, g_w_qkv, g_w_out, g_w_up, g_w_down, g_w_mod = wide
        own_biases, g_b_mod = biases[:5], biases[5]
    else:
        n_drop, n_keep = counts[0, 0], counts[0, 1]
        loss_weight = (
            loss_mask
            * (n_drop + n_keep)
            * 0.5
            * (dropped / (n_drop + 1.0) + (1.0 - dropped) / (n_keep + 1.0))
        )
        branch = jnp.dot(attn_b, w_out, preferred_element_type=jnp.float32) + b_out
        mid_state = residual + gate_a * branch
        norm_f = modulate(mid_state, scale_f, shift_f).astype(jnp.bfloat16)
        ff_inner = jnp.dot(norm_f, w_up, preferred_element_type=jnp.float32) + b_up
        ff_act, gelu_pull = jax.vjp(partial(jax.nn.gelu, approximate=True), ff_inner)
        act_b = ff_act.astype(jnp.bfloat16)
        ff_out = jnp.dot(act_b, w_down, preferred_element_type=jnp.float32) + b_down
        out_state = mid_state + gate_f * ff_out
        d_out = out_grad[0].astype(jnp.float32) * loss_weight[:, None]
        d_ff = (gate_f * d_out).astype(jnp.bfloat16)
        d_gate_f = d_out * ff_out
        g_b_down = jnp.sum(d_ff.astype(jnp.float32), axis=0)
        (d_inner,) = gelu_pull(back_product(d_ff, w_down))
        d_inner_b = d_inner.astype(jnp.bfloat16)
        g_b_up = jnp.sum(d_inner_b.astype(jnp.float32), axis=0)
        d_norm_f = back_product(d_inner_b, w_up)
        _, norm_f_pull = jax.vjp(modulate, mid_state, scale_f, shift_f)
        d_mid_norm, d_scale_f, d_shift_f = norm_f_pull(d_norm_f)
        d_mid = d_out + d_mid_norm
        d_branch = (gate_a * d_mid).astype(jnp.bfloat16)
        d_gate_a = d_mid * branch
        g_b_out = jnp.sum(d_branch.astype(jnp.float32), axis=0)
        d_attn = back_product(d_branch, w_out)
        mixed = out_state.astype(jnp.bfloat16)
        g_w_down = weight_grad(gather_left(act_b), d_ff)
        g_w_up = weight_grad(gather_left(norm_f), d_inner_b)
        g_w_out = weight_grad(gather_left(attn_b), d_branch)
        d_attn = d_attn.reshape(local_rows, HEADS, HEAD_DIM)
        grad_acc = (d_attn / totals_rows[:, :, None]).astype(jnp.bfloat16)
        delta = jnp.transpose(jnp.sum(d_attn * attended, axis=2) / totals_rows)
        bwd_piece = partial(
            backward_piece,
            queries=queries,
            query_segment=segment,
            utt_ends=utt_ends,
            grad_acc=grad_acc,
            delta=delta,
        )
        zero_query = jnp.zeros((local_rows, HEADS, HEAD_DIM), jnp.float32)
        zero_all = jnp.zeros((2, local_rows * shards, model_width), jnp.float32)

        def block_fn(inner_state, portion, block_start):
            d_query_sum, d_all = inner_state
            d_query_add, d_block = bwd_piece(portion, block_start, True)
            return (
                d_query_sum + d_query_add,
                lax.dynamic_update_slice_in_dim(d_all, d_block, block_start, 1),
            )

        d_query, d_all = over_blocks(
            block_fn,
            (zero_query, zero_all),
            lax.all_gather(key_value, "seq", axis=1, tiled=True),
            jnp.int32(0),
            local_rows,
        )
        d_key_value = lax.psum_scatter(d_all, "seq", scatter_dimension=1, tiled=True)
        d_query_pre = unrotate(d_query, angle_cos, angle_sin).reshape(local_rows, model_width)
        d_key_pre = unrotate(
            d_key_value[0].reshape(local_rows, HEADS, HEAD_DIM), angle_cos, angle_sin
        ).reshape(local_rows, model_width)
        d_qkv = jnp.concatenate([d_query_pre, d_key_pre, d_key_value[1]], axis=1).astype(jnp.bfloat16)
        g_b_qkv = jnp.sum(d_qkv.astype(jnp.float32), axis=0)
        d_norm_a = back_product(d_qkv, w_qkv)
        _, norm_a_pull = jax.vjp(modulate, residual, scale_a, shift_a)
        d_resid_norm, d_scale_a, d_shift_a = norm_a_pull(d_norm_a)
        d_resid = (d_mid + d_resid_norm).astype(jnp.bfloat16)
        g_b_skip = jnp.sum(d_resid.astype(jnp.float32), axis=0)
        d_joined = back_product(d_resid, w_skip)
        d_mod_f = jnp.concatenate(
            [d_shift_a, d_scale_a, d_gate_a, d_shift_f, d_scale_f, d_gate_f], axis=1
        )
        d_mod_u = jnp.dot(jnp.transpose(member_f), d_mod_f, precision=HIGHEST_PRECISION)
        small = jnp.concatenate(
            [g_b_skip, g_b_qkv, g_b_out, g_b_up, g_b_down, d_mod_u.reshape(-1)]
        )
        biases = small.shape[0] - d_mod_u.size
        g_w_qkv = weight_grad(gather_left(norm_a), d_qkv)
        g_w_skip = weight_grad(gather_left(joined), d_resid)
        small = xor_sum(small.reshape(-1, 128), "seq").reshape(-1)
        bias_sum = xor_sum(small[:biases].reshape(-1, 128), "utt").reshape(-1)
        d_mod_all = gather_ordered(small[biases:].reshape(d_mod_u.shape), 0)
        act_all = gather_ordered(time_act, 0)
        g_frames = d_joined[:, :model_width].astype(jnp.bfloat16)
        g_skip_in = d_joined[:, model_width:].astype(jnp.bfloat16)
        act_all = act_all.astype(jnp.float32)
        own_width = model_width // shards
        act_own = lax.dynamic_slice_in_dim(act_all, seq_place * own_width, own_width, 1)
        g_w_mod = jnp.dot(jnp.transpose(act_own), d_mod_all, precision=HIGHEST_PRECISION)
        mod_width = d_mod_all.shape[1] // shards
        g_b_mod = jnp.sum(
            lax.dynamic_slice_in_dim(d_mod_all, seq_place * mod_width, mod_width, 1), axis=0
        )
        own_biases, offset = [], 0
        for size in (b_skip.shape[0], b_qkv.shape[0], b_out.shape[0], b_up.shape[0], b_down.shape[0]):
            width = size // shards
            own_biases.append(
                lax.dynamic_slice_in_dim(bias_sum, offset + seq_place * width, width, 0)
            )
            offset += size
    return (
        mixed[None],
        g_frames[None],
        g_skip_in[None],
        g_w_skip,
        own_biases[0],
        g_w_mod,
        g_b_mod,
        g_w_qkv,
        own_biases[1],
        g_w_out,
        own_biases[2],
        g_w_up,
        own_biases[3],
        g_w_down,
        own_biases[4],
    )


def solution(mesh):
    return jax.shard_map(
        local,
        mesh=mesh,
        in_specs=(
            P("utt", "seq", None),
            P("utt", "seq", None),
            P("utt", None),
            P("utt", None),
            P("utt", None),
            P("utt", "seq"),
            P("utt", "seq", None),
            P(),
            P(),
            P(),
            P(),
            P(),
            P(),
            P(),
            P(),
            P(),
            P(),
            P(),
            P(),
        ),
        out_specs=(
            P("utt", "seq", None),
            P("utt", "seq", None),
            P("utt", "seq", None),
            P("seq", None),
            P("seq"),
            P("seq", None),
            P("seq"),
            P("seq", None),
            P("seq"),
            P("seq", None),
            P("seq"),
            P("seq", None),
            P("seq"),
            P("seq", None),
            P("seq"),
        ),
        check_vma=False,
    )
```

```python
from functools import partial
import math

import jax
import jax.numpy as jnp
from jax import lax
from jax.experimental import pallas as pl
from jax.experimental.pallas import tpu as pltpu
from jax.sharding import PartitionSpec as P

HEADS = 16
HEAD_DIM = 64


HIGHEST_PRECISION = lax.Precision.HIGHEST
EPSILON = 1e-06


def layer_norm(values):
    average = jnp.mean(values, axis=-1, keepdims=True)
    centred = values - average
    spread = jnp.mean(centred * centred, axis=-1, keepdims=True)
    return centred * lax.rsqrt(spread + EPSILON)


def modulate(values, scale_part, shift_part):
    return layer_norm(values) * (1.0 + scale_part) + shift_part


def time_embed(flow_vals, model_width):
    half_dim = model_width // 2
    inverse = jnp.exp(-math.log(10000.0) * jnp.arange(half_dim, dtype=jnp.float32) / half_dim)
    angles = 1000.0 * flow_vals[:, None] * inverse[None, :]
    return jnp.concatenate([jnp.sin(angles), jnp.cos(angles)], axis=1)


def rotary_tables(position, head_size):
    half_dim = head_size // 2
    inverse = jnp.exp(
        -math.log(10000.0) * 2.0 * jnp.arange(half_dim, dtype=jnp.float32) / head_size
    )
    angles = position.astype(jnp.float32)[:, None] * inverse[None, :]
    return (jnp.cos(angles)[:, None, :], jnp.sin(angles)[:, None, :])


def rotate(tensor, angle_cos, angle_sin):
    half_dim = tensor.shape[-1] // 2
    leading = tensor[..., :half_dim]
    trailing = tensor[..., half_dim:]
    return jnp.concatenate(
        [leading * angle_cos - trailing * angle_sin, trailing * angle_cos + leading * angle_sin],
        axis=-1,
    )


def unrotate(gradient, angle_cos, angle_sin):
    half_dim = gradient.shape[-1] // 2
    leading = gradient[..., :half_dim]
    trailing = gradient[..., half_dim:]
    return jnp.concatenate(
        [leading * angle_cos + trailing * angle_sin, trailing * angle_cos - leading * angle_sin],
        axis=-1,
    )


def frame_tables(lengths, char_counts, first_frame, frame_count):
    utt_ends = jnp.cumsum(lengths)
    utt_starts = utt_ends - lengths
    frame_index = first_frame + jnp.arange(frame_count, dtype=jnp.int32)
    segment = jnp.sum((frame_index[:, None] >= utt_ends[None, :]).astype(jnp.int32), axis=1)
    member = segment[:, None] == jnp.arange(lengths.shape[0], dtype=jnp.int32)[None, :]
    position = frame_index - jnp.sum(jnp.where(member, utt_starts[None, :], 0), axis=1)
    prompt = jnp.sum(jnp.where(member, char_counts[None, :], 0), axis=1)
    return (segment, position, position >= prompt, member)


def key_segments(key_start, key_count, utt_ends):
    frame_index = key_start + jnp.arange(key_count, dtype=jnp.int32)
    return jnp.sum((frame_index[:, None] >= utt_ends[None, :]).astype(jnp.int32), axis=1)


def block_scores(queries, key_piece, query_segment, key_segment, usable):
    key_rows = key_piece.reshape(key_piece.shape[0], queries.shape[1], queries.shape[2])
    scores = (
        jnp.einsum("qhd,khd->hqk", queries, key_rows, preferred_element_type=jnp.float32) * 0.125
    )
    allowed = jnp.logical_and(query_segment[:, None] == key_segment[None, :], usable)
    return (jnp.where(allowed[None], jnp.exp(scores), 0.0), key_rows)


def over_blocks(block_fn, running, piece, key_start, shard_rows):
    key_count = piece.shape[1]
    shard_total = key_count // shard_rows
    group_size = max(1, min(shard_total, 1024 // shard_rows))
    while shard_total % group_size != 0:
        group_size = group_size - 1
    block_rows = group_size * shard_rows
    if block_rows == key_count:
        return block_fn(running, piece, key_start)

    def one_block(block_index, inner_state):
        portion = lax.dynamic_slice_in_dim(piece, block_index * block_rows, block_rows, 1)
        return block_fn(inner_state, portion, key_start + block_index * block_rows)

    return lax.fori_loop(0, key_count // block_rows, one_block, running)


def forward_piece(running, piece, key_start, usable, queries, query_segment, utt_ends):
    weighted, totals = running
    key_segment = key_segments(key_start, piece.shape[1], utt_ends)
    weights, key_rows = block_scores(queries, piece[0], query_segment, key_segment, usable)
    value_rows = piece[1].reshape(key_rows.shape)
    totals = totals + jnp.sum(weights, axis=2)
    weighted = weighted + jnp.einsum(
        "hqk,khd->qhd", weights.astype(jnp.bfloat16), value_rows, preferred_element_type=jnp.float32
    )
    return (weighted, totals)


def backward_piece(piece, key_start, usable, queries, query_segment, utt_ends, grad_acc, delta):
    key_count = piece.shape[1]
    key_segment = key_segments(key_start, key_count, utt_ends)
    weights, key_rows = block_scores(queries, piece[0], query_segment, key_segment, usable)
    value_rows = piece[1].reshape(key_rows.shape)
    value_dots = jnp.einsum(
        "qhd,khd->hqk", grad_acc, value_rows, preferred_element_type=jnp.float32
    )
    d_scores = (weights * (value_dots - delta[:, :, None])).astype(jnp.bfloat16)
    d_query = (
        jnp.einsum("hqk,khd->qhd", d_scores, key_rows, preferred_element_type=jnp.float32) * 0.125
    )
    d_key = (
        jnp.einsum("hqk,qhd->khd", d_scores, queries, preferred_element_type=jnp.float32) * 0.125
    )
    d_value = jnp.einsum(
        "hqk,qhd->khd", weights.astype(jnp.bfloat16), grad_acc, preferred_element_type=jnp.float32
    )
    return (
        d_query,
        jnp.stack([d_key.reshape(key_count, -1), d_value.reshape(key_count, -1)], axis=0),
    )


def back_product(gradient_rows, matrix):
    return jnp.einsum("fo,io->fi", gradient_rows, matrix, preferred_element_type=jnp.float32)


def xor_permute(value, axis_name, bit):
    size = lax.axis_size(axis_name)
    return lax.ppermute(value, axis_name, [(i, i ^ bit) for i in range(size)])


def bits_of(axis_name):
    size, bits, bit = lax.axis_size(axis_name), [], 1
    while bit < size:
        bits.append(bit)
        bit *= 2
    return bits


def xor_sum(value, axis_name):
    for bit in bits_of(axis_name):
        value = value + xor_permute(value, axis_name, bit)
    return value


def gather_left(rows):
    for bit in reversed(bits_of("utt")):
        rows = jnp.concatenate([rows, xor_permute(rows, "utt", bit)], axis=0)
    return rows


def gather_right(rows):
    place = lax.axis_index("utt")
    for bit in reversed(bits_of("utt")):
        mine = (place & bit) // bit
        width = rows.shape[1] // 2
        kept = lax.dynamic_slice_in_dim(rows, mine * width, width, 1)
        given = lax.dynamic_slice_in_dim(rows, (1 - mine) * width, width, 1)
        rows = jnp.concatenate([kept, xor_permute(given, "utt", bit)], axis=0)
    return rows


def gather_ordered(value, axis):
    place = lax.axis_index("utt")
    for bit in bits_of("utt"):
        other = xor_permute(value, "utt", bit)
        low = (place & bit) == 0
        value = jnp.concatenate(
            [jnp.where(low, value, other), jnp.where(low, other, value)], axis=axis
        )
    return value


def scatter_rows(tile):
    place = lax.axis_index("seq")
    for bit in bits_of("seq"):
        mine = (place & bit) // bit
        rest = lax.axis_size("seq") // (2 * bit)
        pieces = tile.reshape(rest, 2, -1, tile.shape[-1])
        kept = lax.dynamic_index_in_dim(pieces, mine, 1, keepdims=False)
        given = lax.dynamic_index_in_dim(pieces, 1 - mine, 1, keepdims=False)
        given = xor_permute(given, "seq", bit)
        tile = (kept.astype(jnp.float32) + given.astype(jnp.float32)).astype(jnp.bfloat16)
    return tile.reshape(-1, tile.shape[-1])


def weight_grad(left_all, right_rows):
    right_all = gather_right(right_rows)
    tile = jnp.einsum(
        "fi,fo->io", left_all, right_all, preferred_element_type=jnp.float32
    ).astype(jnp.bfloat16)
    tile = tile.reshape(-1, tile.shape[-1])
    piece = scatter_rows(tile)
    return gather_ordered(piece, 1).astype(jnp.float32)


def swap_halves(values, lower):
    return jnp.where(lower, pltpu.roll(values, 96, 1), pltpu.roll(values, 32, 1))


def lower_half(shape):
    return lax.broadcasted_iota(jnp.int32, shape, 1) % HEAD_DIM < HEAD_DIM // 2


def head_scores(q, k, seg_q, seg_k):
    scores = lax.dot_general(q, k, (((1,), (1,)), ((), ())), preferred_element_type=jnp.float32)
    return jnp.where(seg_q == seg_k, jnp.exp(scores * 0.125), 0.0)


MESH = pl.DeviceIdType.MESH
VMEM_LIMIT = 62 * 1024 * 1024


def flip(index, bit):
    return index + bit - 2 * bit * ((index // bit) % 2)


def everywhere(memory):
    return pl.BlockSpec(memory_space=memory)


class Links:
    def __init__(self, send_sems, recv_sems, local_sems):
        self.send_sems, self.recv_sems, self.local_sems = send_sems, recv_sems, local_sems
        self.sent, self.held = [], 0
        self.utt, self.seq = lax.axis_index("utt"), lax.axis_index("seq")

    def enter(self, utt_peers, seq_peers):
        barrier = pltpu.get_barrier_semaphore()
        targets = [self.mate(r) for r in utt_peers] + [self.peer(r) for r in seq_peers]
        for target in targets:
            pl.semaphore_signal(barrier, inc=1, device_id=target, device_id_type=MESH)
        pl.semaphore_wait(barrier, len(targets))

    def mate(self, offset):
        return (self.utt_of(offset), self.seq)

    def utt_of(self, offset):
        place = self.utt
        for bit in (1, 2):
            if offset & bit:
                place = flip(place, bit)
        return place

    def seq_of(self, offset):
        place = self.seq
        for bit in (1, 2, 4):
            if offset & bit:
                place = flip(place, bit)
        return place

    def peer(self, offset):
        return (self.utt, self.seq_of(offset))

    def send(self, source, target, device):
        index = len(self.sent)
        copy = pltpu.make_async_remote_copy(
            src_ref=source,
            dst_ref=target,
            send_sem=self.send_sems.at[index],
            recv_sem=self.recv_sems.at[index],
            device_id=device,
            device_id_type=MESH,
        )
        copy.start()
        self.sent.append(copy)
        return copy

    def keep(self, source, target):
        copy = pltpu.make_async_copy(source, target, self.local_sems.at[self.held])
        self.held += 1
        copy.start()
        return copy

    def leave(self):
        assert len(self.sent) <= self.send_sems.shape[0]
        assert self.held <= self.local_sems.shape[0]
        for copy in self.sent:
            copy.wait_send()


class Gathered:
    def __init__(self, links, source, target, columns=None):
        self.links, self.target = links, target
        self.rows = source.shape[0]
        self.columns = columns
        self.own = links.keep(source, self.slot(0))
        self.across = links.send(source, self.slot(2), links.mate(2))
        self.beside = links.send(source, self.slot(1), links.mate(1))

    def slot(self, offset):
        rows = pl.ds(offset * self.rows, self.rows)
        if self.columns is None:
            return self.target.at[rows, :]
        return self.target.at[rows, self.columns]

    def relay(self):
        self.across.wait_recv()
        self.relayed = self.links.send(self.slot(2), self.slot(3), self.links.mate(1))

    def wait(self):
        self.own.wait()
        self.beside.wait_recv()
        self.relayed.wait_recv()


class Quarter:
    def __init__(self, links, piece_of, target, columns=None):
        rows = target.shape[0] // 4
        columns = pl.ds(0, target.shape[1]) if columns is None else columns
        slot = lambda r: target.at[pl.ds(r * rows, rows), columns]
        self.own = links.keep(piece_of(links.utt), slot(0))
        self.copies = [
            links.send(piece_of(links.utt_of(r)), slot(r), links.mate(r)) for r in (2, 3, 1)
        ]

    def wait(self):
        self.own.wait()
        for copy in self.copies:
            copy.wait_recv()


class Share:
    def __init__(self, links, y_first, left, right, columns, tile, got_a, got_b, got_z2, result):
        self.links, self.y_first = links, y_first
        self.left, self.right, self.columns = left, right, columns
        self.tile, self.got_a, self.got_b, self.got_z2 = tile, got_a, got_b, got_z2
        self.result = result
        seq = links.seq
        self.y, self.zl, self.zh = seq % 2, (seq // 2) % 2, seq // 4
        if y_first:
            self.a, self.b, self.peers = self.y, self.zl, (1, 2)
        else:
            self.a, self.b, self.peers = self.zl, self.y, (2, 1)

    def place(self, zh, a, b):
        return (zh, b, a) if self.y_first else (zh, a, b)

    def product(self, a):
        rows = self.tile.shape[3]

        def block(step, _):
            zh, b = step // 2, step % 2
            here = self.place(zh, a, b)
            base = pl.multiple_of((4 * zh + 2 * here[1] + here[2]) * rows, rows)
            self.tile[here] = lax.dot_general(
                self.left[:, pl.ds(base, rows)],
                self.right[:, self.columns],
                (((0,), (0,)), ((), ())),
                preferred_element_type=jnp.float32,
            ).astype(jnp.bfloat16)
            return 0

        lax.fori_loop(0, 4, block, 0)

    def start(self):
        self.product(1 - self.a)
        given = (
            self.tile.at[:, :, 1 - self.a] if self.y_first else self.tile.at[:, 1 - self.a]
        )
        self.sent_a = self.links.send(given, self.got_a, self.links.peer(self.peers[0]))
        self.product(self.a)

    def add(self, index, got):
        tile = self.tile
        tile[index] = (tile[index].astype(jnp.float32) + got.astype(jnp.float32)).astype(
            jnp.bfloat16
        )

    def after_a(self):
        self.sent_a.wait_recv()

        def block(zh, _):
            self.add(self.place(zh, self.a, 1 - self.b), self.got_a[zh, 1 - self.b])
            return 0

        lax.fori_loop(0, 2, block, 0)
        _, low, y = self.place(0, self.a, 1 - self.b)
        self.sent_b = self.links.send(
            self.tile.at[:, low, y], self.got_b, self.links.peer(self.peers[1])
        )

        def rest(zh, _):
            self.add(self.place(zh, self.a, self.b), self.got_a[zh, self.b])
            return 0

        lax.fori_loop(0, 2, rest, 0)

    def after_b(self):
        self.sent_b.wait_recv()
        self.add((1 - self.zh, self.zl, self.y), self.got_b[1 - self.zh])
        self.sent_z2 = self.links.send(
            self.tile.at[1 - self.zh, self.zl, self.y], self.got_z2, self.links.peer(4)
        )
        self.add((self.zh, self.zl, self.y), self.got_b[self.zh])

    def after_z2(self):
        self.sent_z2.wait_recv()
        links = self.links
        mine = self.result(links.utt)
        mine[...] = (
            self.tile[self.zh, self.zl, self.y].astype(jnp.float32)
            + self.got_z2[...].astype(jnp.float32)
        ).astype(jnp.bfloat16)
        self.across = links.send(mine, mine, links.mate(2))
        self.beside = links.send(mine, mine, links.mate(1))

    def relay(self):
        self.across.wait_recv()
        links = self.links
        theirs = self.result(links.utt_of(2))
        self.relayed = links.send(theirs, theirs, links.mate(1))

    def wait(self):
        self.beside.wait_recv()
        self.relayed.wait_recv()


def share_scratch(rows, columns):
    return [
        pltpu.VMEM((2, 2, 2, rows, columns), jnp.bfloat16),
        pltpu.VMEM((2, 2, rows, columns), jnp.bfloat16),
        pltpu.VMEM((2, rows, columns), jnp.bfloat16),
        pltpu.VMEM((rows, columns), jnp.bfloat16),
    ]


def semaphores(count):
    return [pltpu.SemaphoreType.DMA((count,))] * 2 + [pltpu.SemaphoreType.DMA((32,))]


def comm_params(collective_id):
    return pltpu.CompilerParams(
        collective_id=collective_id, has_side_effects=True, vmem_limit_bytes=VMEM_LIMIT
    )


class Frames:
    def __init__(self, utts, lengths_ref):
        self.starts, self.ends, end = [], [], 0
        for u in range(utts):
            self.starts.append(end)
            end = end + lengths_ref[0, u]
            self.ends.append(end)

    def segment(self, frame):
        return sum((frame >= end).astype(jnp.int32) for end in self.ends)

    def of(self, segment, values):
        total = jnp.zeros_like(segment)
        for u, value in enumerate(values):
            total = jnp.where(segment == u, value, total)
        return total


def frame_column(first, count):
    return first + lax.broadcasted_iota(jnp.int32, (count, 1), 0)


def per_frame(mod_ref, segment, utts, piece, model):
    columns = slice(piece * model, (piece + 1) * model)
    value = jnp.broadcast_to(mod_ref[0:1, columns], (segment.shape[0], model))
    for u in range(1, utts):
        value = jnp.where(segment == u, mod_ref[u : u + 1, columns], value)
    return value


FAR_FIRST = (6, 7, 4, 5, 2, 3, 1)


def attend_kernel(
    utts, lengths_ref, chars_ref, drop_ref, flow_ref, act_ref, table_ref, frames_ref, skip_ref,
    out_grad_ref,
    b_skip_ref, b_mod_ref, b_qkv_ref, w_skip_ref, w_mod_ref, w_qkv_ref,
    attn_ref, heads_ref, exact_ref, total_ref, loss_ref, flows_ref, norm_all, joined_all,
    resid_ref, mod_ref, cos_ref, sin_ref, d_ff_ref, d_ff_all,
    attn_heads, counts_got, sums_ref, flow_own, packed, norm_ref, w_skip, w_mod, w_qkv,
    send_sems, recv_sems, local_sems,
):
    links = Links(send_sems, recv_sems, local_sems)
    rows, model = frames_ref.shape
    total_rows = heads_ref.shape[0]
    early, late = pl.ds(0, 2 * model), pl.ds(2 * model, 4 * model)
    load_skip = links.keep(w_skip_ref, w_skip)
    load_early = links.keep(w_mod_ref.at[:, early], w_mod.at[:, early])
    load_qkv = links.keep(w_qkv_ref, w_qkv)
    load_late = links.keep(w_mod_ref.at[:, late], w_mod.at[:, late])
    links.enter((1, 2, 3), range(1, 8))
    gathers = [
        Gathered(links, frames_ref, joined_all, pl.ds(0, model)),
        Gathered(links, skip_ref, joined_all, pl.ds(model, model)),
    ]
    flow_own[...] = jnp.zeros_like(flow_own)
    flow_own[0:1, 0:utts] = flow_ref[...]
    flows_ref[links.utt] = flow_own[...]
    flow_copies = [
        links.send(flow_own, flows_ref.at[links.utt], links.mate(r)) for r in (1, 2, 3)
    ]
    tables = Frames(utts, lengths_ref)
    first_row = pl.multiple_of(links.seq * rows, rows)
    own_rows = pl.ds(first_row, rows)
    frame = frame_column(links.seq * rows, rows)
    segment = tables.segment(frame)
    position = frame - tables.of(segment, tables.starts)
    prompt = tables.of(segment, [chars_ref[0, u] for u in range(utts)])
    in_loss = jnp.where(position >= prompt, 1.0, 0.0)
    across = lax.broadcasted_iota(jnp.int32, (rows, rows), 1)
    down = lax.broadcasted_iota(jnp.int32, (rows, rows), 0)
    dropped = jnp.sum(
        jnp.where(across == down, drop_ref[...].astype(jnp.float32), 0.0), axis=1, keepdims=True
    )
    lane = lax.broadcasted_iota(jnp.int32, sums_ref.shape, 1)
    n_drop = jnp.sum(in_loss * dropped, axis=0, keepdims=True)
    n_keep = jnp.sum(in_loss * (1.0 - dropped), axis=0, keepdims=True)
    sums_ref[...] = jnp.where(lane == 0, n_drop, jnp.where(lane == 1, n_keep, 0.0))
    targets = [links.mate(1), links.mate(2), links.peer(1), links.peer(2), links.peer(4)]
    turn = []

    def count_turn():
        place = len(turn)
        if place > 0:
            turn[-1].wait_recv()
            sums_ref[...] = sums_ref[...] + counts_got[place - 1]
        if place < 5:
            counts_got[5 + place] = sums_ref[...]
            turn.append(
                links.send(counts_got.at[5 + place], counts_got.at[place], targets[place])
            )

    count_turn()
    quarter = total_rows // 4
    for out, kind in ((cos_ref, 0), (sin_ref, 1)):
        for j in range(4):
            block = table_ref[kind, :, 32 * j : 32 * (j + 1)]
            if kind == 0:
                wide = jnp.concatenate([block] * 4, axis=1)
            else:
                wide = jnp.concatenate([-block, block] * 2, axis=1)
            out[j * quarter : (j + 1) * quarter, :] = wide
    load_skip.wait()
    residual = (
        jnp.dot(frames_ref[...], w_skip[0:model, :], preferred_element_type=jnp.float32)
        + jnp.dot(skip_ref[...], w_skip[model:, :], preferred_element_type=jnp.float32)
        + b_skip_ref[...]
    )
    resid_ref[...] = residual
    count_turn()

    def modulate_columns(columns):
        mod_ref[:, columns] = (
            jnp.dot(act_ref[...], w_mod[:, columns], preferred_element_type=jnp.float32)
            + b_mod_ref[:, columns]
        )

    load_early.wait()
    modulate_columns(slice(0, 2 * model))
    unit, _ = normal_parts(residual)
    norm_ref[...] = (
        unit * (1.0 + per_frame(mod_ref, segment, utts, 1, model))
        + per_frame(mod_ref, segment, utts, 0, model)
    ).astype(jnp.bfloat16)
    gathers.append(Gathered(links, norm_ref, norm_all))
    count_turn()
    load_qkv.wait()
    cos, sin = cos_ref[own_rows, :], sin_ref[own_rows, :]
    lower = lower_half((rows, 128))

    def project(place, base):
        columns = pl.ds(pl.multiple_of(base + place * 128, 128), 128)
        return (
            jnp.dot(norm_ref[...], w_qkv[:, columns], preferred_element_type=jnp.float32)
            + b_qkv_ref[:, columns]
        )

    def pack(place):
        q, k = project(place, 0), project(place, model)
        packed[place, :, 0:128] = (q * cos + swap_halves(q, lower) * sin).astype(jnp.bfloat16)
        packed[place, :, 128:256] = (k * cos + swap_halves(k, lower) * sin).astype(jnp.bfloat16)
        packed[place, :, 256:384] = project(place, 2 * model).astype(jnp.bfloat16)

    incoming = []
    for r in FAR_FIRST:
        place = links.seq_of(r)
        pack(place)
        incoming.append(
            links.send(packed.at[place], heads_ref.at[own_rows, :], links.peer(r))
        )
    pack(links.seq)
    own = links.keep(packed.at[links.seq], heads_ref.at[own_rows, :])
    count_turn()
    load_late.wait()
    modulate_columns(slice(2 * model, 6 * model))
    count_turn()
    gathers[0].relay()
    gathers[1].relay()
    count_turn()
    n_drop, n_keep = sums_ref[0:1, 0:1], sums_ref[0:1, 1:2]
    loss_weight = (
        in_loss
        * (n_drop + n_keep)
        * 0.5
        * (dropped / (n_drop + 1.0) + (1.0 - dropped) / (n_keep + 1.0))
    )
    loss_ref[...] = jnp.broadcast_to(loss_weight, loss_ref.shape)
    d_out = out_grad_ref[...].astype(jnp.float32) * loss_weight
    d_ff_ref[...] = (per_frame(mod_ref, segment, utts, 5, model) * d_out).astype(jnp.bfloat16)
    gathers.append(Gathered(links, d_ff_ref, d_ff_all))
    own.wait()
    for copy in incoming:
        copy.wait_recv()
    first = lax.broadcasted_iota(jnp.int32, (rows, 128), 1) < HEAD_DIM
    zero = jnp.zeros((rows, 128), jnp.bfloat16)
    k, v = heads_ref[:, 128:256], heads_ref[:, 256:384]
    seg_k = tables.segment(lax.broadcasted_iota(jnp.int32, (1, total_rows), 1))
    part = lambda place: pl.ds(pl.multiple_of(place * rows, rows), rows)
    column = attn_ref.at[:, pl.ds(pl.multiple_of(links.seq * 128, 128), 128)]

    def attend_rows(place):
        here = part(place)
        q, seg_q = heads_ref[here, 0:128], tables.segment(frame_column(place * rows, rows))
        results = []
        for mine in (first, jnp.logical_not(first)):
            weights = head_scores(jnp.where(mine, q, zero), k, seg_q, seg_k)
            total = jnp.sum(weights, axis=1, keepdims=True)
            summed = jnp.dot(weights.astype(jnp.bfloat16), v, preferred_element_type=jnp.float32)
            results.append((summed, total))
        total = jnp.where(first, results[0][1], results[1][1])
        attended = jnp.where(first, results[0][0], results[1][0]) / total
        attn_heads[here, :] = attended.astype(jnp.bfloat16)
        exact_ref[here, :] = attended
        total_ref[here, :] = total

    incoming = []
    for r in FAR_FIRST:
        place = links.seq_of(r)
        attend_rows(place)
        incoming.append(links.send(attn_heads.at[part(place), :], column, links.peer(r)))
    attend_rows(links.seq)
    own = links.keep(attn_heads.at[part(links.seq), :], column)
    gathers[2].relay()
    gathers[3].relay()
    for copy in flow_copies:
        copy.wait_recv()
    own.wait()
    for copy in incoming:
        copy.wait_recv()
    for gather in gathers:
        gather.wait()
    links.leave()


def attend(
    lengths, chars, drop, flow, act, table, frames, skip, out_grad, b_skip, b_mod, b_qkv, w_skip,
    w_mod, w_qkv, shards,
):
    rows, width = frames.shape
    total_rows = shards * rows
    utts = flow.shape[1]
    vmem, there, scalar = everywhere(pltpu.VMEM), everywhere(pl.ANY), everywhere(pltpu.SMEM)
    shape = jax.ShapeDtypeStruct
    bf16 = lambda *dims: pltpu.VMEM(dims, jnp.bfloat16)
    return pl.pallas_call(
        partial(attend_kernel, utts),
        in_specs=[scalar] * 2 + [vmem] * 10 + [there] * 3,
        out_specs=[vmem] * 14,
        out_shape=[
            shape((rows, width), jnp.bfloat16),
            shape((total_rows, 384), jnp.bfloat16),
            shape((total_rows, 128), jnp.float32),
            shape((total_rows, 128), jnp.float32),
            shape((rows, 128), jnp.float32),
            shape((4, 8, 128), jnp.float32),
            shape((4 * rows, width), jnp.bfloat16),
            shape((4 * rows, 2 * width), jnp.bfloat16),
            shape((rows, width), jnp.float32),
            shape((8, 6 * width), jnp.float32),
            shape((total_rows, 128), jnp.float32),
            shape((total_rows, 128), jnp.float32),
            shape((rows, width), jnp.bfloat16),
            shape((4 * rows, width), jnp.bfloat16),
        ],
        scratch_shapes=[
            bf16(total_rows, 128),
            pltpu.VMEM((10, 8, 128), jnp.float32),
            pltpu.VMEM((8, 128), jnp.float32),
            pltpu.VMEM((8, 128), jnp.float32),
            bf16(shards, rows, 384),
            bf16(rows, width),
            bf16(*w_skip.shape),
            bf16(*w_mod.shape),
            bf16(*w_qkv.shape),
        ]
        + semaphores(40),
        compiler_params=comm_params(1),
    )(
        lengths, chars, drop, flow, act, table, frames, skip, out_grad,
        b_skip[None, :], b_mod[None, :], b_qkv[None, :], w_skip, w_mod, w_qkv,
    )


ALONG = (((1,), (1,)), ((), ()))
DOWN = (((0,), (0,)), ((), ()))


def normal_parts(values):
    centred = values - jnp.mean(values, axis=1, keepdims=True)
    scale = lax.rsqrt(jnp.mean(centred * centred, axis=1, keepdims=True) + EPSILON)
    return centred * scale, scale


def normal_back(inward, unit, scale):
    return scale * (
        inward
        - jnp.mean(inward, axis=1, keepdims=True)
        - unit * jnp.mean(inward * unit, axis=1, keepdims=True)
    )


def column_sum(values):
    return jnp.sum(values.astype(jnp.float32), axis=0, keepdims=True)


def backward_kernel(
    utts, lengths_ref, attn_ref, resid_ref, mod_ref, loss_ref, out_grad_ref, d_ff,
    b_out_ref, b_up_ref, b_down_ref,
    heads_ref, exact_ref, total_ref, cos_ref, sin_ref,
    norm_a_ref, joined_ref, d_ff_ref, w_out_ref, w_up_ref, w_down_ref, w_qkv_ref, w_skip_ref,
    mixed, g_down, g_up, g_out, g_qkv, g_skip, smalls, g_frames, g_skip_in,
    norm_f, act, d_inner, d_branch, d_attn, pieces, d_mid, ff_sum, d_norm,
    grad_heads, d_heads, dk_ref, dv_ref,
    d_ff_all, act_all, norm_all, d_inner_all, attn_all, d_branch_all,
    norm_a_all, joined_all, d_qkv, d_qkv_all, d_resid, d_resid_all,
    up_ring, down_ring, w_out, w_qkv, w_skip, small_own, small_got, small_sum,
    *rest,
):
    tiles, (send_sems, recv_sems, local_sems, ring_sems) = rest[:-4], rest[-4:]
    links = Links(send_sems, recv_sems, local_sems)
    rows, model = resid_ref.shape
    block_width = up_ring.shape[2]
    steps = w_up_ref.shape[1] // block_width

    def ring(c):
        slot = c % 2
        columns = pl.ds(pl.multiple_of(c * block_width, block_width), block_width)
        return (
            pltpu.make_async_copy(w_up_ref.at[:, columns], up_ring.at[slot], ring_sems.at[slot]),
            pltpu.make_async_copy(
                w_down_ref.at[columns, :], down_ring.at[slot], ring_sems.at[2 + slot]
            ),
        )

    load_out = links.keep(w_out_ref, w_out)
    load_d = links.keep(d_ff_ref, d_ff_all)
    for c in (0, 1):
        for copy in ring(c):
            copy.start()
    loads = [
        links.keep(w_qkv_ref, w_qkv),
        links.keep(w_skip_ref, w_skip),
        links.keep(norm_a_ref, norm_a_all),
        links.keep(joined_ref, joined_all),
    ]
    links.enter((1, 2, 3), range(1, 8))

    tables = Frames(utts, lengths_ref)
    segment = tables.segment(frame_column(links.seq * rows, rows))

    def modulation(piece):
        return per_frame(mod_ref, segment, utts, piece, model)

    def d_out():
        return out_grad_ref[...].astype(jnp.float32) * loss_ref[:, 0:1]

    load_out.wait()
    branch = (
        jnp.dot(attn_ref[...], w_out[...], preferred_element_type=jnp.float32) + b_out_ref[...]
    )
    pieces[0] = branch
    mid = resid_ref[...] + modulation(2) * branch
    d_mid[...] = mid
    unit, _ = normal_parts(mid)
    norm_f[...] = (unit * (1.0 + modulation(4)) + modulation(3)).astype(jnp.bfloat16)
    ff_sum[...] = jnp.zeros_like(ff_sum)
    d_norm[...] = jnp.zeros_like(d_norm)
    const = math.sqrt(2.0 / math.pi)
    width = d_inner_all.shape[1]

    def feed(c, _):
        slot = c % 2
        columns = pl.ds(pl.multiple_of(c * block_width, block_width), block_width)
        for copy in ring(c):
            copy.wait()
        inner = (
            jnp.dot(norm_f[...], up_ring[slot], preferred_element_type=jnp.float32)
            + b_up_ref[:, columns]
        )
        square = inner * inner
        slope = jnp.tanh(const * inner * (1.0 + 0.044715 * square))
        gate = 0.5 * (1.0 + slope)
        act_b = (inner * gate).astype(jnp.bfloat16)
        turn = gate + 0.5 * inner * (1.0 - slope * slope) * (
            const * (1.0 + 3.0 * 0.044715 * square)
        )
        here = pl.ds(pl.multiple_of(c * 128, 128), 128)
        d_act = lax.dot_general(
            d_ff[...], down_ring[slot], ALONG, preferred_element_type=jnp.float32
        )
        d_inner_b = (turn * d_act).astype(jnp.bfloat16)
        for u in range(4):
            act[u, :, here] = act_b[:, u * 128 : (u + 1) * 128]
            d_inner[u, :, here] = d_inner_b[:, u * 128 : (u + 1) * 128]
        ff_sum[...] += jnp.dot(act_b, down_ring[slot], preferred_element_type=jnp.float32)
        d_norm[...] += lax.dot_general(
            d_inner_b, up_ring[slot], ALONG, preferred_element_type=jnp.float32
        )

        @pl.when(c + 2 < steps)
        def _():
            for copy in ring(c + 2):
                copy.start()

        return 0

    middle = width // 2
    left_half, right_half = pl.ds(0, middle), pl.ds(middle, middle)
    lax.fori_loop(0, steps // 2, feed, 0)
    quarters_a = [Quarter(links, lambda u: act.at[u, :, left_half], act_all, left_half)]
    lax.fori_loop(steps // 2, steps, feed, 0)
    quarters_a.append(Quarter(links, lambda u: act.at[u, :, right_half], act_all, right_half))
    gather_n = Gathered(links, norm_f, norm_all)
    own_rows = pl.ds(pl.multiple_of(links.seq * rows, rows), rows)
    strip = lambda ref, place, size: ref.at[
        :, pl.ds(pl.multiple_of(place * size, size), size)
    ]
    narrow = d_branch_all.shape[1]
    quarter_i = Quarter(links, lambda u: d_inner.at[u], d_inner_all)
    mid = d_mid[...]
    unit, scale = normal_parts(mid)
    d_norm_f = d_norm[...]
    pieces[2] = d_norm_f * unit
    d_mid_f = d_out() + normal_back(d_norm_f * (1.0 + modulation(4)), unit, scale)
    gate_a = modulation(2)
    d_branch[...] = (gate_a * d_mid_f).astype(jnp.bfloat16)
    pieces[0] = pieces[0] * d_mid_f
    d_mid[...] = d_mid_f
    d_attn[...] = lax.dot_general(
        d_branch[...], w_out[...], ALONG, preferred_element_type=jnp.float32
    ).astype(jnp.bfloat16)
    own = links.keep(strip(d_attn, links.seq, 128), grad_heads.at[own_rows, :])
    incoming_d = [
        links.send(
            strip(d_attn, links.seq_of(r), 128), grad_heads.at[own_rows, :], links.peer(r)
        )
        for r in FAR_FIRST
    ]
    quarter_b = Quarter(links, lambda u: strip(d_branch, u, narrow), d_branch_all)
    gather_b = Gathered(links, attn_ref, attn_all)
    ff_out = ff_sum[...] + b_down_ref[...]
    mixed[...] = (mid + modulation(5) * ff_out).astype(jnp.bfloat16)
    pieces[1] = d_out() * ff_out
    small_own[...] = jnp.zeros_like(small_own)
    small_own[4:5, :] = column_sum(d_branch[...])
    for c in range(4):
        small_own[5 + c : 6 + c, :] = column_sum(d_inner[c])
    small_own[9:10, :] = column_sum(d_ff[...])

    def utterance_sums(piece, values):
        for u in range(utts):
            row = 10 + utts * piece + u
            small_own[row : row + 1, :] = jnp.sum(
                jnp.where(segment == u, values, 0.0), axis=0, keepdims=True
            )

    utterance_sums(2, pieces[0])
    utterance_sums(3, d_norm[...])
    utterance_sums(4, pieces[2])
    utterance_sums(5, pieces[1])
    half = width // 2
    down_at = lambda h: lambda u: g_down.at[
        pl.ds(pl.multiple_of(u * 128, 128), 128), pl.ds(h * half, half)
    ]
    column_at = lambda ref, step, offset, size: lambda u: ref.at[
        :, pl.ds(pl.multiple_of(u * step + offset, 128), size)
    ]
    wide, thin = d_qkv_all.shape[1], d_resid_all.shape[1]
    third, slim = wide // 2, thin // 2
    plans = [
        (act_all, d_ff_all, pl.ds(0, half), down_at(0)),
        (act_all, d_ff_all, pl.ds(half, half), down_at(1)),
        (norm_all, d_inner_all, pl.ds(0, half), column_at(g_up, width, 0, half)),
        (norm_all, d_inner_all, pl.ds(half, half), column_at(g_up, width, half, half)),
        (attn_all, d_branch_all, pl.ds(0, narrow), column_at(g_out, narrow, 0, narrow)),
        (norm_a_all, d_qkv_all, pl.ds(0, third), column_at(g_qkv, wide, 0, third)),
        (norm_a_all, d_qkv_all, pl.ds(third, third), column_at(g_qkv, wide, third, third)),
        (joined_all, d_resid_all, pl.ds(0, slim), column_at(g_skip, thin, 0, slim)),
        (joined_all, d_resid_all, pl.ds(slim, slim), column_at(g_skip, thin, slim, slim)),
    ]
    y_first = (True, False, True, False, True, True, True, True, True)
    shares = [
        Share(links, y_first[i], left, right, columns, *tiles[4 * i : 4 * i + 4], result)
        for i, (left, right, columns, result) in enumerate(plans)
    ]
    gather_n.relay()
    load_d.wait()
    for quarter in quarters_a:
        quarter.wait()
    shares[0].start()
    shares[1].start()
    own.wait()
    for copy in incoming_d:
        copy.wait_recv()
    dk_ref[...] = jnp.zeros_like(dk_ref)
    dv_ref[...] = jnp.zeros_like(dv_ref)
    first = lax.broadcasted_iota(jnp.int32, (256, 128), 1) < HEAD_DIM
    zero = jnp.zeros((256, 128), jnp.bfloat16)
    lower = lower_half((256, 128))
    k, v = heads_ref[:, 128:256], heads_ref[:, 256:384]
    seg_k = tables.segment(lax.broadcasted_iota(jnp.int32, (1, heads_ref.shape[0]), 1))

    def turned(values, here):
        return (
            values * cos_ref[here, :] - swap_halves(values, lower) * sin_ref[here, :]
        ).astype(jnp.bfloat16)

    def block(step, _):
        here = pl.ds(pl.multiple_of(step * 256, 256), 256)
        q, seg_q = heads_ref[here, 0:128], tables.segment(frame_column(step * 256, 256))
        scaled = grad_heads[here, :].astype(jnp.float32) / total_ref[here, :]
        grad_acc = scaled.astype(jnp.bfloat16)
        product = scaled * exact_ref[here, :]
        d_query = []
        for mine in (first, jnp.logical_not(first)):
            q_own = jnp.where(mine, q, zero)
            g_own = jnp.where(mine, grad_acc, zero)
            delta = jnp.sum(jnp.where(mine, product, 0.0), axis=1, keepdims=True)
            weights = head_scores(q_own, k, seg_q, seg_k)
            dots = lax.dot_general(g_own, v, ALONG, preferred_element_type=jnp.float32)
            d_scores = (weights * (dots - delta)).astype(jnp.bfloat16)
            d_query.append(jnp.dot(d_scores, k, preferred_element_type=jnp.float32))
            dk_ref[...] += lax.dot_general(
                d_scores, q_own, DOWN, preferred_element_type=jnp.float32
            )
            dv_ref[...] += lax.dot_general(
                weights.astype(jnp.bfloat16), g_own, DOWN, preferred_element_type=jnp.float32
            )
        d_heads[here, 0:128] = turned(jnp.where(first, d_query[0], d_query[1]) * 0.125, here)
        return 0

    blocks = heads_ref.shape[0] // 256
    lax.fori_loop(0, blocks, block, 0)

    def finish(step, _):
        here = pl.ds(pl.multiple_of(step * 256, 256), 256)
        d_heads[here, 128:256] = turned(dk_ref[here, :] * 0.125, here)
        d_heads[here, 256:384] = dv_ref[here, :].astype(jnp.bfloat16)
        return 0

    lax.fori_loop(0, blocks, finish, 0)
    part = lambda place, c: d_heads.at[
        pl.ds(pl.multiple_of(place * rows, rows), rows), pl.ds(c * 128, 128)
    ]
    home = lambda c: d_qkv.at[
        :, pl.ds(pl.multiple_of(c * model + links.seq * 128, 128), 128)
    ]
    owns = [links.keep(part(links.seq, c), home(c)) for c in range(3)]
    incoming = [
        links.send(part(links.seq_of(r), c), home(c), links.peer(r))
        for r in FAR_FIRST
        for c in range(3)
    ]
    gather_n.wait()
    quarter_i.wait()
    state = {}

    def output_share():
        gather_b.relay()
        gather_b.wait()
        quarter_b.wait()
        shares[4].start()

    def projections():
        for copy in owns:
            copy.wait()
        for copy in incoming:
            copy.wait_recv()
        for copy in loads:
            copy.wait()
        state["qkv"] = Quarter(links, lambda u: strip(d_qkv, u, wide), d_qkv_all)
        d_norm_a = lax.dot_general(
            d_qkv[...], w_qkv[...], ALONG, preferred_element_type=jnp.float32
        )
        unit, scale = normal_parts(resid_ref[...])
        d_resid_f = d_mid[...] + normal_back(d_norm_a * (1.0 + modulation(1)), unit, scale)
        rounded = d_resid_f.astype(jnp.bfloat16)
        d_resid[...] = rounded
        state["resid"] = Quarter(links, lambda u: strip(d_resid, u, thin), d_resid_all)
        small_own[0:1, :] = column_sum(rounded)
        for c in range(3):
            small_own[1 + c : 2 + c, :] = column_sum(d_qkv[:, c * model : (c + 1) * model])
        utterance_sums(0, d_norm_a)
        utterance_sums(1, d_norm_a * unit)
        state["small"] = links.send(small_own, small_got.at[0], links.peer(1))

    def qkv_shares():
        state["qkv"].wait()
        shares[5].start()
        shares[6].start()

    def skip_shares():
        state["resid"].wait()
        shares[7].start()
        shares[8].start()

    def inputs():
        for index, out in enumerate((g_frames, g_skip_in)):
            out[...] = lax.dot_general(
                d_resid[...],
                w_skip[pl.ds(index * model, model), :],
                ALONG,
                preferred_element_type=jnp.float32,
            ).astype(jnp.bfloat16)

    def small_y():
        state["small"].wait_recv()
        small_sum[0] = small_own[...] + small_got[0]
        state["small"] = links.send(small_sum.at[0], small_got.at[1], links.peer(2))

    def small_z1():
        state["small"].wait_recv()
        small_sum[1] = small_sum[0] + small_got[1]
        state["small"] = links.send(small_sum.at[1], small_got.at[2], links.peer(4))

    def small_z2():
        state["small"].wait_recv()
        mine = smalls.at[links.utt]
        mine[...] = small_sum[1] + small_got[2]
        state["spread"] = [links.send(mine, mine, links.mate(r)) for r in (2, 3, 1)]

    stages = ("start", "after_a", "after_b", "after_z2", "relay", "wait")
    s, a, b, z, r, w = ([getattr(share, stage) for share in shares] for stage in stages)
    for step in (
        s[2], a[0], s[3], a[1],
        output_share, projections,
        a[2], b[0],
        qkv_shares,
        b[1], z[0],
        small_y, inputs,
        z[1], a[4], a[3],
        skip_shares, small_z1,
        b[2], a[5], r[0], r[1], b[4], z[2],
        small_z2,
        z[4], w[0], w[1], a[6], b[5], r[2], r[4], b[3], z[5], b[6], a[7], z[3], r[5], z[6],
        a[8], b[7], r[3], r[6], w[2], w[4], w[5], z[7], b[8], w[3], w[6], r[7], z[8], w[7],
        r[8], w[8],
    ):
        step()
    for copy in state["spread"]:
        copy.wait_recv()
    links.leave()


def backward(
    lengths, attn_b, resid, mod, loss, out_grad, d_ff, b_out, b_up, b_down,
    heads, exact, total, cos, sin,
    norm_a_all, joined_all, d_ff_all, w_out, w_up, w_down, w_qkv, w_skip,
):
    rows, model = resid.shape
    frames, inner = heads.shape[0], w_up.shape[1]
    utts = lengths.shape[1]
    small = (-(-(10 + 6 * utts) // 8) * 8, model)
    vmem, there = everywhere(pltpu.VMEM), everywhere(pl.ANY)
    shape = jax.ShapeDtypeStruct
    bf16 = lambda *dims: pltpu.VMEM(dims, jnp.bfloat16)
    f32 = lambda *dims: pltpu.VMEM(dims, jnp.float32)
    part, step = model // 8, inner // 8
    return pl.pallas_call(
        partial(backward_kernel, utts),
        in_specs=[everywhere(pltpu.SMEM)] + [vmem] * 14 + [there] * 8,
        out_specs=[vmem] * 9,
        out_shape=[
            shape((rows, model), jnp.bfloat16),
            shape((inner // 8, model), jnp.bfloat16),
            shape((part, inner), jnp.bfloat16),
            shape((part, model), jnp.bfloat16),
            shape((part, 3 * model), jnp.bfloat16),
            shape((2 * part, model), jnp.bfloat16),
            shape((4,) + small, jnp.float32),
            shape((rows, model), jnp.bfloat16),
            shape((rows, model), jnp.bfloat16),
        ],
        scratch_shapes=[
            bf16(rows, model),
            bf16(4, rows, inner // 4),
            bf16(4, rows, inner // 4),
            bf16(rows, model),
            bf16(rows, model),
            f32(3, rows, model),
            f32(rows, model),
            f32(rows, model),
            f32(rows, model),
            bf16(frames, 128),
            bf16(frames, 384),
            f32(frames, 128),
            f32(frames, 128),
            bf16(4 * rows, model),
            bf16(4 * rows, inner // 4),
            bf16(4 * rows, model),
            bf16(4 * rows, inner // 4),
            bf16(4 * rows, model),
            bf16(4 * rows, model // 4),
            bf16(4 * rows, model),
            bf16(4 * rows, 2 * model),
            bf16(rows, 3 * model),
            bf16(4 * rows, 3 * model // 4),
            bf16(rows, model),
            bf16(4 * rows, model // 4),
            bf16(2, model, step),
            bf16(2, step, model),
            bf16(*w_out.shape),
            bf16(*w_qkv.shape),
            bf16(*w_skip.shape),
            f32(*small),
            f32(3, *small),
            f32(2, *small),
        ]
        + share_scratch(part, inner // 8) * 4
        + share_scratch(part, model // 4)
        + share_scratch(part, 3 * model // 8) * 2
        + share_scratch(2 * part, model // 8) * 2
        + semaphores(128)
        + [pltpu.SemaphoreType.DMA((4,))],
        compiler_params=comm_params(2),
    )(
        lengths, attn_b, resid, mod, loss, out_grad, d_ff,
        b_out[None, :], b_up[None, :], b_down[None, :],
        heads, exact, total, cos, sin,
        norm_a_all, joined_all, d_ff_all, w_out, w_up, w_down, w_qkv, w_skip,
    )


UP = 3


def finish_kernel(utts, shards, act_ref, *rest):
    kept_in, wide_in, smalls_in = rest[:3], rest[3:8], rest[8]
    kept_out, wide_out, mod_out, bias_out = rest[9:12], rest[12:17], rest[17], rest[18:24]
    kept, wide, staged = rest[24:27], rest[27:32], rest[32:37]
    smalls_ref, mod_stage, bias_stage, d_mod, totals, sems, load_sems = rest[37:]
    seq = lax.axis_index("seq")
    loads, copies = [], []
    for source, target in zip((*wide_in, smalls_in, *kept_in), (*wide, smalls_ref, *kept)):
        copy = pltpu.make_async_copy(source, target, load_sems.at[len(loads)])
        copy.start()
        loads.append(copy)

    def put(source, target):
        copy = pltpu.make_async_copy(source, target, sems.at[len(copies)])
        copy.start()
        copies.append(copy)

    model = smalls_ref.shape[2]
    lanes = 128
    for place, (source, stage, target) in enumerate(zip(wide, staged, wide_out)):
        loads[place].wait()
        if place == UP:
            for u in range(4):
                for c in range(shards):
                    stage[:, (4 * c + u) * lanes : (4 * c + u + 1) * lanes] = source[
                        :, u * model + c * lanes : u * model + (c + 1) * lanes
                    ].astype(jnp.float32)
        else:
            stage[...] = source[...].astype(jnp.float32)
        put(stage, target)
    groups = smalls_ref.shape[0]
    loads[5].wait()
    bias_sum = (
        smalls_ref[0, 0:10] + smalls_ref[1, 0:10] + smalls_ref[2, 0:10] + smalls_ref[3, 0:10]
    )
    for row in range(10):
        totals[row, 0:1] = bias_sum[row : row + 1]
    d_mod[...] = jnp.zeros_like(d_mod)
    for piece in range(6):
        first = 10 + utts * piece
        for g in range(groups):
            d_mod[piece, g * utts : (g + 1) * utts, :] = smalls_ref[g, first : first + utts, :]
        rows = d_mod[piece]
        totals[10 + piece, 0:1] = jnp.sum(rows, axis=0, keepdims=True)
        columns = slice(piece * model, (piece + 1) * model)
        mod_stage[:, columns] = jnp.dot(
            act_ref[...], rows, precision=HIGHEST_PRECISION, preferred_element_type=jnp.float32
        )
    put(mod_stage, mod_out)
    for load, source, target in zip(loads[6:], kept, kept_out):
        load.wait()
        put(source, target)
    line = model // lanes
    first = 0
    for place, target in enumerate(bias_out):
        count = target.shape[1] // lanes
        for i in range(count):
            unit = i * line + seq if place == UP else seq * count + i
            column = pl.multiple_of((unit % line) * lanes, lanes)
            bias_stage[place, 0:1, i * lanes : (i + 1) * lanes] = totals[
                first + unit // line, 0:1, pl.ds(column, lanes)
            ]
        first += count * shards // line
        put(bias_stage.at[place, pl.ds(0, 1), pl.ds(0, count * lanes)], target)
    for copy in copies:
        copy.wait()


def finish(shards, utts, act_own, smalls, mixed, frames, skip, grads):
    vmem, there = everywhere(pltpu.VMEM), everywhere(pl.ANY)
    shape = jax.ShapeDtypeStruct
    model = smalls.shape[2]
    own = model // shards
    depth = act_own.shape[1]
    mod_shape = (own, 6 * model)
    widths = [own, 3 * own, own, 4 * own, own, 6 * own]
    kept = (mixed, frames, skip)
    outs = pl.pallas_call(
        partial(finish_kernel, utts, shards),
        in_specs=[vmem] + [there] * 9,
        out_specs=[there] * 15,
        out_shape=[shape(v.shape, v.dtype) for v in kept]
        + [shape(g.shape, jnp.float32) for g in grads]
        + [shape(mod_shape, jnp.float32)]
        + [shape((1, w), jnp.float32) for w in widths],
        scratch_shapes=[pltpu.VMEM(v.shape, v.dtype) for v in (*kept, *grads)]
        + [pltpu.VMEM(g.shape, jnp.float32) for g in grads]
        + [
            pltpu.VMEM(smalls.shape, jnp.float32),
            pltpu.VMEM(mod_shape, jnp.float32),
            pltpu.VMEM((6, 8, max(widths)), jnp.float32),
            pltpu.VMEM((6, depth, model), jnp.float32),
            pltpu.VMEM((16, 8, model), jnp.float32),
            pltpu.SemaphoreType.DMA((15,)),
            pltpu.SemaphoreType.DMA((9,)),
        ],
        compiler_params=pltpu.CompilerParams(vmem_limit_bytes=VMEM_LIMIT),
    )(act_own, *kept, *grads, smalls)
    return outs[:9], [v.reshape(-1) for v in outs[9:]]


def own_time_act(flows, seq_place, shards, model):
    half_dim, own = model // 2, model // shards
    column = seq_place * own + jnp.arange(own, dtype=jnp.int32)
    inverse = jnp.exp(
        -math.log(10000.0) * (column % half_dim).astype(jnp.float32) / half_dim
    )
    angles = 1000.0 * flows[None, :] * inverse[:, None]
    wave = jnp.where((column < half_dim)[:, None], jnp.sin(angles), jnp.cos(angles))
    return jax.nn.silu(wave).astype(jnp.bfloat16).astype(jnp.float32)


def compact_tables(lengths, total_rows):
    half_dim = HEAD_DIM // 2
    shape = (total_rows // 4, 128)
    lane = lax.broadcasted_iota(jnp.int32, shape, 1)
    frame = lax.broadcasted_iota(jnp.int32, shape, 0) + (lane // half_dim) * shape[0]
    start, end = jnp.zeros(shape, jnp.int32), jnp.int32(0)
    for u in range(lengths.shape[0]):
        end = end + lengths[u]
        start = jnp.where(frame >= end, end, start)
    inverse = jnp.exp(
        -math.log(10000.0) * 2.0 * (lane % half_dim).astype(jnp.float32) / HEAD_DIM
    )
    angles = (frame - start).astype(jnp.float32) * inverse
    return jnp.stack([jnp.cos(angles), jnp.sin(angles)])


def padded_time_act(flow_vals, model):
    half_dim = model // 2
    column = jnp.arange(model, dtype=jnp.int32)
    inverse = jnp.exp(-math.log(10000.0) * (column % half_dim).astype(jnp.float32) / half_dim)
    flow_vals = jnp.pad(flow_vals, (0, 8 - flow_vals.shape[0]))
    angles = 1000.0 * flow_vals[:, None] * inverse[None, :]
    wave = jnp.where((column < half_dim)[None, :], jnp.sin(angles), jnp.cos(angles))
    return jax.nn.silu(wave).astype(jnp.bfloat16)


def local(
    frames_in,
    skip_in,
    flow_times,
    frame_lengths,
    char_lengths,
    drop_mask,
    out_grad,
    w_skip,
    b_skip,
    w_mod,
    b_mod,
    w_qkv,
    b_qkv,
    w_out,
    b_out,
    w_up,
    b_up,
    w_down,
    b_down,
):
    local_rows = frames_in.shape[1]
    model_width = frames_in.shape[2]
    shards = lax.axis_size("seq")
    seq_place = lax.axis_index("seq")
    lengths = frame_lengths[0]
    whole = model_width * 4
    fused = (
        lax.axis_size("utt") == 4
        and shards == 8
        and HEADS * HEAD_DIM == 1024
        and model_width == 1024
        and w_up.shape[1] == whole
        and local_rows == 128
        and flow_times.shape[1] <= 8
    )
    if not fused:
        utt_ends = jnp.cumsum(lengths)
        segment, position, in_loss, member = frame_tables(
            lengths, char_lengths[0], seq_place * local_rows, local_rows
        )
        member_f = member.astype(jnp.float32)
        loss_mask = in_loss.astype(jnp.float32)
        dropped = drop_mask[0].astype(jnp.float32)
        counts = jnp.stack([jnp.sum(loss_mask * dropped), jnp.sum(loss_mask * (1.0 - dropped))])
        counts = jnp.pad(counts[None, :], ((0, 7), (0, 126)))
        counts = xor_sum(xor_sum(counts, "utt"), "seq")
        time_act = jax.nn.silu(time_embed(flow_times[0], model_width)).astype(jnp.bfloat16)
        mod_u = jnp.dot(time_act, w_mod, preferred_element_type=jnp.float32) + b_mod
        mod_f = jnp.dot(member_f, mod_u, precision=HIGHEST_PRECISION)
        shift_a, scale_a, gate_a, shift_f, scale_f, gate_f = jnp.split(mod_f, 6, axis=1)
        joined = jnp.concatenate([frames_in[0], skip_in[0]], axis=1)
        residual = jnp.dot(joined, w_skip, preferred_element_type=jnp.float32) + b_skip
        norm_a = modulate(residual, scale_a, shift_a).astype(jnp.bfloat16)
        qkv_full = jnp.dot(norm_a, w_qkv, preferred_element_type=jnp.float32) + b_qkv
    if fused:
        (
            attn_b, qkv_heads, exact, total, loss, flows, norm_all, joined_all,
            residual, mod_u, cos_all, sin_all, d_ff, d_ff_all,
        ) = attend(
            frame_lengths,
            char_lengths,
            drop_mask,
            flow_times,
            padded_time_act(flow_times[0], model_width),
            compact_tables(lengths, local_rows * shards),
            frames_in[0],
            skip_in[0],
            out_grad[0],
            b_skip,
            b_mod,
            b_qkv,
            w_skip,
            w_mod,
            w_qkv,
            shards,
        )
    else:
        angle_cos, angle_sin = rotary_tables(position, HEAD_DIM)
        queries = rotate(
            qkv_full[:, :model_width].reshape(local_rows, HEADS, HEAD_DIM), angle_cos, angle_sin
        ).astype(jnp.bfloat16)
        key_rot = rotate(
            qkv_full[:, model_width : 2 * model_width].reshape(local_rows, HEADS, HEAD_DIM),
            angle_cos,
            angle_sin,
        ).astype(jnp.bfloat16)
        key_value = jnp.stack(
            [
                key_rot.reshape(local_rows, model_width),
                qkv_full[:, 2 * model_width :].astype(jnp.bfloat16),
            ],
            axis=0,
        )
        start_state = (
            jnp.zeros((local_rows, HEADS, HEAD_DIM), jnp.float32),
            jnp.zeros((HEADS, local_rows), jnp.float32),
        )
        fwd_piece = partial(forward_piece, queries=queries, query_segment=segment, utt_ends=utt_ends)
        weighted, totals = over_blocks(
            partial(fwd_piece, usable=True),
            start_state,
            lax.all_gather(key_value, "seq", axis=1, tiled=True),
            jnp.int32(0),
            local_rows,
        )
        totals_rows = jnp.transpose(totals)
        attended = weighted / totals_rows[:, :, None]
        attn_b = attended.reshape(local_rows, model_width).astype(jnp.bfloat16)
    if fused:
        mixed, g_w_down, g_w_up, g_w_out, g_w_qkv, g_w_skip, smalls, g_frames, g_skip_in = backward(
            frame_lengths,
            attn_b,
            residual,
            mod_u,
            loss,
            out_grad[0],
            d_ff,
            b_out,
            b_up,
            b_down,
            qkv_heads,
            exact,
            total,
            cos_all,
            sin_all,
            norm_all,
            joined_all,
            d_ff_all,
            w_out,
            w_up,
            w_down,
            w_qkv,
            w_skip,
        )
        utts = flow_times.shape[1]
        act_own = own_time_act(flows[:, 0, :utts].reshape(-1), seq_place, shards, model_width)
        act_own = jnp.pad(act_own, ((0, 0), (0, -act_own.shape[1] % 8)))
        wide, biases = finish(
            shards,
            utts,
            act_own,
            smalls,
            mixed,
            g_frames,
            g_skip_in,
            (g_w_skip, g_w_qkv, g_w_out, g_w_up, g_w_down),
        )
        mixed, g_frames, g_skip_in, g_w_skip, g_w_qkv, g_w_out, g_w_up, g_w_down, g_w_mod = wide
        own_biases, g_b_mod = biases[:5], biases[5]
    else:
        n_drop, n_keep = counts[0, 0], counts[0, 1]
        loss_weight = (
            loss_mask
            * (n_drop + n_keep)
            * 0.5
            * (dropped / (n_drop + 1.0) + (1.0 - dropped) / (n_keep + 1.0))
        )
        branch = jnp.dot(attn_b, w_out, preferred_element_type=jnp.float32) + b_out
        mid_state = residual + gate_a * branch
        norm_f = modulate(mid_state, scale_f, shift_f).astype(jnp.bfloat16)
        ff_inner = jnp.dot(norm_f, w_up, preferred_element_type=jnp.float32) + b_up
        ff_act, gelu_pull = jax.vjp(partial(jax.nn.gelu, approximate=True), ff_inner)
        act_b = ff_act.astype(jnp.bfloat16)
        ff_out = jnp.dot(act_b, w_down, preferred_element_type=jnp.float32) + b_down
        out_state = mid_state + gate_f * ff_out
        d_out = out_grad[0].astype(jnp.float32) * loss_weight[:, None]
        d_ff = (gate_f * d_out).astype(jnp.bfloat16)
        d_gate_f = d_out * ff_out
        g_b_down = jnp.sum(d_ff.astype(jnp.float32), axis=0)
        (d_inner,) = gelu_pull(back_product(d_ff, w_down))
        d_inner_b = d_inner.astype(jnp.bfloat16)
        g_b_up = jnp.sum(d_inner_b.astype(jnp.float32), axis=0)
        d_norm_f = back_product(d_inner_b, w_up)
        _, norm_f_pull = jax.vjp(modulate, mid_state, scale_f, shift_f)
        d_mid_norm, d_scale_f, d_shift_f = norm_f_pull(d_norm_f)
        d_mid = d_out + d_mid_norm
        d_branch = (gate_a * d_mid).astype(jnp.bfloat16)
        d_gate_a = d_mid * branch
        g_b_out = jnp.sum(d_branch.astype(jnp.float32), axis=0)
        d_attn = back_product(d_branch, w_out)
        mixed = out_state.astype(jnp.bfloat16)
        g_w_down = weight_grad(gather_left(act_b), d_ff)
        g_w_up = weight_grad(gather_left(norm_f), d_inner_b)
        g_w_out = weight_grad(gather_left(attn_b), d_branch)
        d_attn = d_attn.reshape(local_rows, HEADS, HEAD_DIM)
        grad_acc = (d_attn / totals_rows[:, :, None]).astype(jnp.bfloat16)
        delta = jnp.transpose(jnp.sum(d_attn * attended, axis=2) / totals_rows)
        bwd_piece = partial(
            backward_piece,
            queries=queries,
            query_segment=segment,
            utt_ends=utt_ends,
            grad_acc=grad_acc,
            delta=delta,
        )
        zero_query = jnp.zeros((local_rows, HEADS, HEAD_DIM), jnp.float32)
        zero_all = jnp.zeros((2, local_rows * shards, model_width), jnp.float32)

        def block_fn(inner_state, portion, block_start):
            d_query_sum, d_all = inner_state
            d_query_add, d_block = bwd_piece(portion, block_start, True)
            return (
                d_query_sum + d_query_add,
                lax.dynamic_update_slice_in_dim(d_all, d_block, block_start, 1),
            )

        d_query, d_all = over_blocks(
            block_fn,
            (zero_query, zero_all),
            lax.all_gather(key_value, "seq", axis=1, tiled=True),
            jnp.int32(0),
            local_rows,
        )
        d_key_value = lax.psum_scatter(d_all, "seq", scatter_dimension=1, tiled=True)
        d_query_pre = unrotate(d_query, angle_cos, angle_sin).reshape(local_rows, model_width)
        d_key_pre = unrotate(
            d_key_value[0].reshape(local_rows, HEADS, HEAD_DIM), angle_cos, angle_sin
        ).reshape(local_rows, model_width)
        d_qkv = jnp.concatenate([d_query_pre, d_key_pre, d_key_value[1]], axis=1).astype(jnp.bfloat16)
        g_b_qkv = jnp.sum(d_qkv.astype(jnp.float32), axis=0)
        d_norm_a = back_product(d_qkv, w_qkv)
        _, norm_a_pull = jax.vjp(modulate, residual, scale_a, shift_a)
        d_resid_norm, d_scale_a, d_shift_a = norm_a_pull(d_norm_a)
        d_resid = (d_mid + d_resid_norm).astype(jnp.bfloat16)
        g_b_skip = jnp.sum(d_resid.astype(jnp.float32), axis=0)
        d_joined = back_product(d_resid, w_skip)
        d_mod_f = jnp.concatenate(
            [d_shift_a, d_scale_a, d_gate_a, d_shift_f, d_scale_f, d_gate_f], axis=1
        )
        d_mod_u = jnp.dot(jnp.transpose(member_f), d_mod_f, precision=HIGHEST_PRECISION)
        small = jnp.concatenate(
            [g_b_skip, g_b_qkv, g_b_out, g_b_up, g_b_down, d_mod_u.reshape(-1)]
        )
        biases = small.shape[0] - d_mod_u.size
        g_w_qkv = weight_grad(gather_left(norm_a), d_qkv)
        g_w_skip = weight_grad(gather_left(joined), d_resid)
        small = xor_sum(small.reshape(-1, 128), "seq").reshape(-1)
        bias_sum = xor_sum(small[:biases].reshape(-1, 128), "utt").reshape(-1)
        d_mod_all = gather_ordered(small[biases:].reshape(d_mod_u.shape), 0)
        act_all = gather_ordered(time_act, 0)
        g_frames = d_joined[:, :model_width].astype(jnp.bfloat16)
        g_skip_in = d_joined[:, model_width:].astype(jnp.bfloat16)
        act_all = act_all.astype(jnp.float32)
        own_width = model_width // shards
        act_own = lax.dynamic_slice_in_dim(act_all, seq_place * own_width, own_width, 1)
        g_w_mod = jnp.dot(jnp.transpose(act_own), d_mod_all, precision=HIGHEST_PRECISION)
        mod_width = d_mod_all.shape[1] // shards
        g_b_mod = jnp.sum(
            lax.dynamic_slice_in_dim(d_mod_all, seq_place * mod_width, mod_width, 1), axis=0
        )
        own_biases, offset = [], 0
        for size in (b_skip.shape[0], b_qkv.shape[0], b_out.shape[0], b_up.shape[0], b_down.shape[0]):
            width = size // shards
            own_biases.append(
                lax.dynamic_slice_in_dim(bias_sum, offset + seq_place * width, width, 0)
            )
            offset += size
    return (
        mixed[None],
        g_frames[None],
        g_skip_in[None],
        g_w_skip,
        own_biases[0],
        g_w_mod,
        g_b_mod,
        g_w_qkv,
        own_biases[1],
        g_w_out,
        own_biases[2],
        g_w_up,
        own_biases[3],
        g_w_down,
        own_biases[4],
    )


def solution(mesh):
    return jax.shard_map(
        local,
        mesh=mesh,
        in_specs=(
            P("utt", "seq", None),
            P("utt", "seq", None),
            P("utt", None),
            P("utt", None),
            P("utt", None),
            P("utt", "seq"),
            P("utt", "seq", None),
            P(),
            P(),
            P(),
            P(),
            P(),
            P(),
            P(),
            P(),
            P(),
            P(),
            P(),
            P(),
        ),
        out_specs=(
            P("utt", "seq", None),
            P("utt", "seq", None),
            P("utt", "seq", None),
            P("seq", None),
            P("seq"),
            P("seq", None),
            P("seq"),
            P("seq", None),
            P("seq"),
            P("seq", None),
            P("seq"),
            P("seq", None),
            P("seq"),
            P("seq", None),
            P("seq"),
        ),
        check_vma=False,
    )
```

```python
from functools import partial
import math

import jax
import jax.numpy as jnp
from jax import lax
from jax.experimental import pallas as pl
from jax.experimental.pallas import tpu as pltpu
from jax.sharding import PartitionSpec as P

HEADS = 16
HEAD_DIM = 64


HIGHEST_PRECISION = lax.Precision.HIGHEST
EPSILON = 1e-06


def layer_norm(values):
    average = jnp.mean(values, axis=-1, keepdims=True)
    centred = values - average
    spread = jnp.mean(centred * centred, axis=-1, keepdims=True)
    return centred * lax.rsqrt(spread + EPSILON)


def modulate(values, scale_part, shift_part):
    return layer_norm(values) * (1.0 + scale_part) + shift_part


def time_embed(flow_vals, model_width):
    half_dim = model_width // 2
    inverse = jnp.exp(-math.log(10000.0) * jnp.arange(half_dim, dtype=jnp.float32) / half_dim)
    angles = 1000.0 * flow_vals[:, None] * inverse[None, :]
    return jnp.concatenate([jnp.sin(angles), jnp.cos(angles)], axis=1)


def rotary_tables(position, head_size):
    half_dim = head_size // 2
    inverse = jnp.exp(
        -math.log(10000.0) * 2.0 * jnp.arange(half_dim, dtype=jnp.float32) / head_size
    )
    angles = position.astype(jnp.float32)[:, None] * inverse[None, :]
    return (jnp.cos(angles)[:, None, :], jnp.sin(angles)[:, None, :])


def rotate(tensor, angle_cos, angle_sin):
    half_dim = tensor.shape[-1] // 2
    leading = tensor[..., :half_dim]
    trailing = tensor[..., half_dim:]
    return jnp.concatenate(
        [leading * angle_cos - trailing * angle_sin, trailing * angle_cos + leading * angle_sin],
        axis=-1,
    )


def unrotate(gradient, angle_cos, angle_sin):
    half_dim = gradient.shape[-1] // 2
    leading = gradient[..., :half_dim]
    trailing = gradient[..., half_dim:]
    return jnp.concatenate(
        [leading * angle_cos + trailing * angle_sin, trailing * angle_cos - leading * angle_sin],
        axis=-1,
    )


def frame_tables(lengths, char_counts, first_frame, frame_count):
    utt_ends = jnp.cumsum(lengths)
    utt_starts = utt_ends - lengths
    frame_index = first_frame + jnp.arange(frame_count, dtype=jnp.int32)
    segment = jnp.sum((frame_index[:, None] >= utt_ends[None, :]).astype(jnp.int32), axis=1)
    member = segment[:, None] == jnp.arange(lengths.shape[0], dtype=jnp.int32)[None, :]
    position = frame_index - jnp.sum(jnp.where(member, utt_starts[None, :], 0), axis=1)
    prompt = jnp.sum(jnp.where(member, char_counts[None, :], 0), axis=1)
    return (segment, position, position >= prompt, member)


def key_segments(key_start, key_count, utt_ends):
    frame_index = key_start + jnp.arange(key_count, dtype=jnp.int32)
    return jnp.sum((frame_index[:, None] >= utt_ends[None, :]).astype(jnp.int32), axis=1)


def block_scores(queries, key_piece, query_segment, key_segment, usable):
    key_rows = key_piece.reshape(key_piece.shape[0], queries.shape[1], queries.shape[2])
    scores = (
        jnp.einsum("qhd,khd->hqk", queries, key_rows, preferred_element_type=jnp.float32) * 0.125
    )
    allowed = jnp.logical_and(query_segment[:, None] == key_segment[None, :], usable)
    return (jnp.where(allowed[None], jnp.exp(scores), 0.0), key_rows)


def over_blocks(block_fn, running, piece, key_start, shard_rows):
    key_count = piece.shape[1]
    shard_total = key_count // shard_rows
    group_size = max(1, min(shard_total, 1024 // shard_rows))
    while shard_total % group_size != 0:
        group_size = group_size - 1
    block_rows = group_size * shard_rows
    if block_rows == key_count:
        return block_fn(running, piece, key_start)

    def one_block(block_index, inner_state):
        portion = lax.dynamic_slice_in_dim(piece, block_index * block_rows, block_rows, 1)
        return block_fn(inner_state, portion, key_start + block_index * block_rows)

    return lax.fori_loop(0, key_count // block_rows, one_block, running)


def forward_piece(running, piece, key_start, usable, queries, query_segment, utt_ends):
    weighted, totals = running
    key_segment = key_segments(key_start, piece.shape[1], utt_ends)
    weights, key_rows = block_scores(queries, piece[0], query_segment, key_segment, usable)
    value_rows = piece[1].reshape(key_rows.shape)
    totals = totals + jnp.sum(weights, axis=2)
    weighted = weighted + jnp.einsum(
        "hqk,khd->qhd", weights.astype(jnp.bfloat16), value_rows, preferred_element_type=jnp.float32
    )
    return (weighted, totals)


def backward_piece(piece, key_start, usable, queries, query_segment, utt_ends, grad_acc, delta):
    key_count = piece.shape[1]
    key_segment = key_segments(key_start, key_count, utt_ends)
    weights, key_rows = block_scores(queries, piece[0], query_segment, key_segment, usable)
    value_rows = piece[1].reshape(key_rows.shape)
    value_dots = jnp.einsum(
        "qhd,khd->hqk", grad_acc, value_rows, preferred_element_type=jnp.float32
    )
    d_scores = (weights * (value_dots - delta[:, :, None])).astype(jnp.bfloat16)
    d_query = (
        jnp.einsum("hqk,khd->qhd", d_scores, key_rows, preferred_element_type=jnp.float32) * 0.125
    )
    d_key = (
        jnp.einsum("hqk,qhd->khd", d_scores, queries, preferred_element_type=jnp.float32) * 0.125
    )
    d_value = jnp.einsum(
        "hqk,qhd->khd", weights.astype(jnp.bfloat16), grad_acc, preferred_element_type=jnp.float32
    )
    return (
        d_query,
        jnp.stack([d_key.reshape(key_count, -1), d_value.reshape(key_count, -1)], axis=0),
    )


def back_product(gradient_rows, matrix):
    return jnp.einsum("fo,io->fi", gradient_rows, matrix, preferred_element_type=jnp.float32)


def xor_permute(value, axis_name, bit):
    size = lax.axis_size(axis_name)
    return lax.ppermute(value, axis_name, [(i, i ^ bit) for i in range(size)])


def bits_of(axis_name):
    size, bits, bit = lax.axis_size(axis_name), [], 1
    while bit < size:
        bits.append(bit)
        bit *= 2
    return bits


def xor_sum(value, axis_name):
    for bit in bits_of(axis_name):
        value = value + xor_permute(value, axis_name, bit)
    return value


def gather_left(rows):
    for bit in reversed(bits_of("utt")):
        rows = jnp.concatenate([rows, xor_permute(rows, "utt", bit)], axis=0)
    return rows


def gather_right(rows):
    place = lax.axis_index("utt")
    for bit in reversed(bits_of("utt")):
        mine = (place & bit) // bit
        width = rows.shape[1] // 2
        kept = lax.dynamic_slice_in_dim(rows, mine * width, width, 1)
        given = lax.dynamic_slice_in_dim(rows, (1 - mine) * width, width, 1)
        rows = jnp.concatenate([kept, xor_permute(given, "utt", bit)], axis=0)
    return rows


def gather_ordered(value, axis):
    place = lax.axis_index("utt")
    for bit in bits_of("utt"):
        other = xor_permute(value, "utt", bit)
        low = (place & bit) == 0
        value = jnp.concatenate(
            [jnp.where(low, value, other), jnp.where(low, other, value)], axis=axis
        )
    return value


def scatter_rows(tile):
    place = lax.axis_index("seq")
    for bit in bits_of("seq"):
        mine = (place & bit) // bit
        rest = lax.axis_size("seq") // (2 * bit)
        pieces = tile.reshape(rest, 2, -1, tile.shape[-1])
        kept = lax.dynamic_index_in_dim(pieces, mine, 1, keepdims=False)
        given = lax.dynamic_index_in_dim(pieces, 1 - mine, 1, keepdims=False)
        given = xor_permute(given, "seq", bit)
        tile = (kept.astype(jnp.float32) + given.astype(jnp.float32)).astype(jnp.bfloat16)
    return tile.reshape(-1, tile.shape[-1])


def weight_grad(left_all, right_rows):
    right_all = gather_right(right_rows)
    tile = jnp.einsum(
        "fi,fo->io", left_all, right_all, preferred_element_type=jnp.float32
    ).astype(jnp.bfloat16)
    tile = tile.reshape(-1, tile.shape[-1])
    piece = scatter_rows(tile)
    return gather_ordered(piece, 1).astype(jnp.float32)


def swap_halves(values, lower):
    return jnp.where(lower, pltpu.roll(values, 96, 1), pltpu.roll(values, 32, 1))


def lower_half(shape):
    return lax.broadcasted_iota(jnp.int32, shape, 1) % HEAD_DIM < HEAD_DIM // 2


def head_scores(q, k, seg_q, seg_k):
    scores = lax.dot_general(q, k, (((1,), (1,)), ((), ())), preferred_element_type=jnp.float32)
    return jnp.where(seg_q == seg_k, jnp.exp(scores * 0.125), 0.0)


MESH = pl.DeviceIdType.MESH
VMEM_LIMIT = 62 * 1024 * 1024


def flip(index, bit):
    return index + bit - 2 * bit * ((index // bit) % 2)


def everywhere(memory):
    return pl.BlockSpec(memory_space=memory)


class Links:
    def __init__(self, send_sems, recv_sems, local_sems):
        self.send_sems, self.recv_sems, self.local_sems = send_sems, recv_sems, local_sems
        self.sent, self.held = [], 0
        self.utt, self.seq = lax.axis_index("utt"), lax.axis_index("seq")

    def enter(self, utt_peers, seq_peers):
        barrier = pltpu.get_barrier_semaphore()
        targets = [self.mate(r) for r in utt_peers] + [self.peer(r) for r in seq_peers]
        for target in targets:
            pl.semaphore_signal(barrier, inc=1, device_id=target, device_id_type=MESH)
        pl.semaphore_wait(barrier, len(targets))

    def mate(self, offset):
        return (self.utt_of(offset), self.seq)

    def utt_of(self, offset):
        place = self.utt
        for bit in (1, 2):
            if offset & bit:
                place = flip(place, bit)
        return place

    def seq_of(self, offset):
        place = self.seq
        for bit in (1, 2, 4):
            if offset & bit:
                place = flip(place, bit)
        return place

    def peer(self, offset):
        return (self.utt, self.seq_of(offset))

    def send(self, source, target, device):
        index = len(self.sent)
        copy = pltpu.make_async_remote_copy(
            src_ref=source,
            dst_ref=target,
            send_sem=self.send_sems.at[index],
            recv_sem=self.recv_sems.at[index],
            device_id=device,
            device_id_type=MESH,
        )
        copy.start()
        self.sent.append(copy)
        return copy

    def keep(self, source, target):
        copy = pltpu.make_async_copy(source, target, self.local_sems.at[self.held])
        self.held += 1
        copy.start()
        return copy

    def leave(self):
        assert len(self.sent) <= self.send_sems.shape[0]
        assert self.held <= self.local_sems.shape[0]
        for copy in self.sent:
            copy.wait_send()


class Gathered:
    def __init__(self, links, source, target, columns=None):
        self.links, self.target = links, target
        self.rows = source.shape[0]
        self.columns = columns
        self.own = links.keep(source, self.slot(0))
        self.across = links.send(source, self.slot(2), links.mate(2))
        self.beside = links.send(source, self.slot(1), links.mate(1))

    def slot(self, offset):
        rows = pl.ds(offset * self.rows, self.rows)
        if self.columns is None:
            return self.target.at[rows, :]
        return self.target.at[rows, self.columns]

    def relay(self):
        self.across.wait_recv()
        self.relayed = self.links.send(self.slot(2), self.slot(3), self.links.mate(1))

    def wait(self):
        self.own.wait()
        self.beside.wait_recv()
        self.relayed.wait_recv()


class Quarter:
    def __init__(self, links, piece_of, target, columns=None):
        rows = target.shape[0] // 4
        columns = pl.ds(0, target.shape[1]) if columns is None else columns
        slot = lambda r: target.at[pl.ds(r * rows, rows), columns]
        self.own = links.keep(piece_of(links.utt), slot(0))
        self.copies = [
            links.send(piece_of(links.utt_of(r)), slot(r), links.mate(r)) for r in (2, 3, 1)
        ]

    def wait(self):
        self.own.wait()
        for copy in self.copies:
            copy.wait_recv()


class Share:
    def __init__(self, links, y_first, left, right, columns, tile, got_a, got_b, got_z2, result):
        self.links, self.y_first = links, y_first
        self.left, self.right, self.columns = left, right, columns
        self.tile, self.got_a, self.got_b, self.got_z2 = tile, got_a, got_b, got_z2
        self.result = result
        seq = links.seq
        self.y, self.zl, self.zh = seq % 2, (seq // 2) % 2, seq // 4
        if y_first:
            self.a, self.b, self.peers = self.y, self.zl, (1, 2)
        else:
            self.a, self.b, self.peers = self.zl, self.y, (2, 1)

    def place(self, zh, a, b):
        return (zh, b, a) if self.y_first else (zh, a, b)

    def product(self, zh, a):
        rows = self.tile.shape[3]

        def block(b, _):
            here = self.place(zh, a, b)
            base = pl.multiple_of((4 * zh + 2 * here[1] + here[2]) * rows, rows)
            self.tile[here] = lax.dot_general(
                self.left[:, pl.ds(base, rows)],
                self.right[:, self.columns],
                (((0,), (0,)), ((), ())),
                preferred_element_type=jnp.float32,
            ).astype(jnp.bfloat16)
            return 0

        lax.fori_loop(0, 2, block, 0)

    def give(self, zh):
        self.product(zh, 1 - self.a)
        given = self.tile.at[zh, :, 1 - self.a] if self.y_first else self.tile.at[zh, 1 - self.a]
        self.sent_a.append(
            self.links.send(given, self.got_a.at[zh], self.links.peer(self.peers[0]))
        )

    def start_far(self):
        self.sent_a, self.sent_b = [], []
        self.give(1 - self.zh)
        self.product(1 - self.zh, self.a)

    def start_near(self):
        self.give(self.zh)
        self.product(self.zh, self.a)

    def start(self):
        self.sent_a, self.sent_b = [], []
        self.give(1 - self.zh)
        self.give(self.zh)
        self.product(1 - self.zh, self.a)
        self.product(self.zh, self.a)

    def add(self, index, got):
        tile = self.tile
        tile[index] = (tile[index].astype(jnp.float32) + got.astype(jnp.float32)).astype(
            jnp.bfloat16
        )

    def after_a(self):
        halves = (1 - self.zh, self.zh)
        for sent, zh in zip(self.sent_a, halves):
            sent.wait_recv()
            here = self.place(zh, self.a, 1 - self.b)
            self.add(here, self.got_a[zh, 1 - self.b])
            self.sent_b.append(
                self.links.send(
                    self.tile.at[here], self.got_b.at[zh], self.links.peer(self.peers[1])
                )
            )
        for zh in halves:
            self.add(self.place(zh, self.a, self.b), self.got_a[zh, self.b])

    def after_b(self):
        self.sent_b[0].wait_recv()
        self.add((1 - self.zh, self.zl, self.y), self.got_b[1 - self.zh])
        self.sent_z2 = self.links.send(
            self.tile.at[1 - self.zh, self.zl, self.y], self.got_z2, self.links.peer(4)
        )
        self.sent_b[1].wait_recv()
        self.add((self.zh, self.zl, self.y), self.got_b[self.zh])

    def after_z2(self):
        self.sent_z2.wait_recv()
        links = self.links
        mine = self.result(links.utt)
        mine[...] = (
            self.tile[self.zh, self.zl, self.y].astype(jnp.float32)
            + self.got_z2[...].astype(jnp.float32)
        ).astype(jnp.bfloat16)
        self.across = links.send(mine, mine, links.mate(2))
        self.beside = links.send(mine, mine, links.mate(1))

    def relay(self):
        self.across.wait_recv()
        links = self.links
        theirs = self.result(links.utt_of(2))
        self.relayed = links.send(theirs, theirs, links.mate(1))

    def wait(self):
        self.beside.wait_recv()
        self.relayed.wait_recv()


def share_scratch(rows, columns):
    return [
        pltpu.VMEM((2, 2, 2, rows, columns), jnp.bfloat16),
        pltpu.VMEM((2, 2, rows, columns), jnp.bfloat16),
        pltpu.VMEM((2, rows, columns), jnp.bfloat16),
        pltpu.VMEM((rows, columns), jnp.bfloat16),
    ]


def semaphores(count):
    return [pltpu.SemaphoreType.DMA((count,))] * 2 + [pltpu.SemaphoreType.DMA((32,))]


def comm_params(collective_id):
    return pltpu.CompilerParams(
        collective_id=collective_id, has_side_effects=True, vmem_limit_bytes=VMEM_LIMIT
    )


class Frames:
    def __init__(self, utts, lengths_ref):
        self.starts, self.ends, end = [], [], 0
        for u in range(utts):
            self.starts.append(end)
            end = end + lengths_ref[0, u]
            self.ends.append(end)

    def segment(self, frame):
        return sum((frame >= end).astype(jnp.int32) for end in self.ends)

    def of(self, segment, values):
        total = jnp.zeros_like(segment)
        for u, value in enumerate(values):
            total = jnp.where(segment == u, value, total)
        return total


def frame_column(first, count):
    return first + lax.broadcasted_iota(jnp.int32, (count, 1), 0)


def per_frame(mod_ref, segment, utts, piece, model):
    columns = slice(piece * model, (piece + 1) * model)
    value = jnp.broadcast_to(mod_ref[0:1, columns], (segment.shape[0], model))
    for u in range(1, utts):
        value = jnp.where(segment == u, mod_ref[u : u + 1, columns], value)
    return value


FAR_FIRST = (6, 7, 4, 5, 2, 3, 1)


def attend_kernel(
    utts, lengths_ref, chars_ref, drop_ref, flow_ref, act_ref, table_ref, frames_ref, skip_ref,
    out_grad_ref,
    b_skip_ref, b_mod_ref, b_qkv_ref, w_skip_ref, w_mod_ref, w_qkv_ref,
    attn_ref, heads_ref, exact_ref, total_ref, loss_ref, flows_ref, norm_all, joined_all,
    resid_ref, mod_ref, cos_ref, sin_ref, d_ff_ref, d_ff_all,
    attn_heads, counts_got, sums_ref, flow_own, packed, norm_ref, w_skip, w_mod, w_qkv,
    send_sems, recv_sems, local_sems,
):
    links = Links(send_sems, recv_sems, local_sems)
    rows, model = frames_ref.shape
    total_rows = heads_ref.shape[0]
    early, late = pl.ds(0, 2 * model), pl.ds(2 * model, 4 * model)
    load_skip = links.keep(w_skip_ref, w_skip)
    load_early = links.keep(w_mod_ref.at[:, early], w_mod.at[:, early])
    load_qkv = links.keep(w_qkv_ref, w_qkv)
    load_late = links.keep(w_mod_ref.at[:, late], w_mod.at[:, late])
    links.enter((1, 2, 3), range(1, 8))
    gathers = [
        Gathered(links, frames_ref, joined_all, pl.ds(0, model)),
        Gathered(links, skip_ref, joined_all, pl.ds(model, model)),
    ]
    flow_own[...] = jnp.zeros_like(flow_own)
    flow_own[0:1, 0:utts] = flow_ref[...]
    flows_ref[links.utt] = flow_own[...]
    flow_copies = [
        links.send(flow_own, flows_ref.at[links.utt], links.mate(r)) for r in (1, 2, 3)
    ]
    tables = Frames(utts, lengths_ref)
    first_row = pl.multiple_of(links.seq * rows, rows)
    own_rows = pl.ds(first_row, rows)
    frame = frame_column(links.seq * rows, rows)
    segment = tables.segment(frame)
    position = frame - tables.of(segment, tables.starts)
    prompt = tables.of(segment, [chars_ref[0, u] for u in range(utts)])
    in_loss = jnp.where(position >= prompt, 1.0, 0.0)
    across = lax.broadcasted_iota(jnp.int32, (rows, rows), 1)
    down = lax.broadcasted_iota(jnp.int32, (rows, rows), 0)
    dropped = jnp.sum(
        jnp.where(across == down, drop_ref[...].astype(jnp.float32), 0.0), axis=1, keepdims=True
    )
    lane = lax.broadcasted_iota(jnp.int32, sums_ref.shape, 1)
    n_drop = jnp.sum(in_loss * dropped, axis=0, keepdims=True)
    n_keep = jnp.sum(in_loss * (1.0 - dropped), axis=0, keepdims=True)
    sums_ref[...] = jnp.where(lane == 0, n_drop, jnp.where(lane == 1, n_keep, 0.0))
    targets = [links.mate(1), links.mate(2), links.peer(1), links.peer(2), links.peer(4)]
    turn = []

    def count_turn():
        place = len(turn)
        if place > 0:
            turn[-1].wait_recv()
            sums_ref[...] = sums_ref[...] + counts_got[place - 1]
        if place < 5:
            counts_got[5 + place] = sums_ref[...]
            turn.append(
                links.send(counts_got.at[5 + place], counts_got.at[place], targets[place])
            )

    count_turn()
    quarter = total_rows // 4
    for out, kind in ((cos_ref, 0), (sin_ref, 1)):
        for j in range(4):
            block = table_ref[kind, :, 32 * j : 32 * (j + 1)]
            if kind == 0:
                wide = jnp.concatenate([block] * 4, axis=1)
            else:
                wide = jnp.concatenate([-block, block] * 2, axis=1)
            out[j * quarter : (j + 1) * quarter, :] = wide
    load_skip.wait()
    residual = (
        jnp.dot(frames_ref[...], w_skip[0:model, :], preferred_element_type=jnp.float32)
        + jnp.dot(skip_ref[...], w_skip[model:, :], preferred_element_type=jnp.float32)
        + b_skip_ref[...]
    )
    resid_ref[...] = residual
    count_turn()

    def modulate_columns(columns):
        mod_ref[:, columns] = (
            jnp.dot(act_ref[...], w_mod[:, columns], preferred_element_type=jnp.float32)
            + b_mod_ref[:, columns]
        )

    load_early.wait()
    modulate_columns(slice(0, 2 * model))
    unit, _ = normal_parts(residual)
    norm_ref[...] = (
        unit * (1.0 + per_frame(mod_ref, segment, utts, 1, model))
        + per_frame(mod_ref, segment, utts, 0, model)
    ).astype(jnp.bfloat16)
    gathers.append(Gathered(links, norm_ref, norm_all))
    count_turn()
    load_qkv.wait()
    cos, sin = cos_ref[own_rows, :], sin_ref[own_rows, :]
    lower = lower_half((rows, 128))

    def project(place, base):
        columns = pl.ds(pl.multiple_of(base + place * 128, 128), 128)
        return (
            jnp.dot(norm_ref[...], w_qkv[:, columns], preferred_element_type=jnp.float32)
            + b_qkv_ref[:, columns]
        )

    def pack(place):
        q, k = project(place, 0), project(place, model)
        packed[place, :, 0:128] = (q * cos + swap_halves(q, lower) * sin).astype(jnp.bfloat16)
        packed[place, :, 128:256] = (k * cos + swap_halves(k, lower) * sin).astype(jnp.bfloat16)
        packed[place, :, 256:384] = project(place, 2 * model).astype(jnp.bfloat16)

    incoming = []
    for r in FAR_FIRST:
        place = links.seq_of(r)
        pack(place)
        incoming.append(
            links.send(packed.at[place], heads_ref.at[own_rows, :], links.peer(r))
        )
    pack(links.seq)
    own = links.keep(packed.at[links.seq], heads_ref.at[own_rows, :])
    count_turn()
    load_late.wait()
    modulate_columns(slice(2 * model, 6 * model))
    count_turn()
    gathers[0].relay()
    gathers[1].relay()
    count_turn()
    n_drop, n_keep = sums_ref[0:1, 0:1], sums_ref[0:1, 1:2]
    loss_weight = (
        in_loss
        * (n_drop + n_keep)
        * 0.5
        * (dropped / (n_drop + 1.0) + (1.0 - dropped) / (n_keep + 1.0))
    )
    loss_ref[...] = jnp.broadcast_to(loss_weight, loss_ref.shape)
    d_out = out_grad_ref[...].astype(jnp.float32) * loss_weight
    d_ff_ref[...] = (per_frame(mod_ref, segment, utts, 5, model) * d_out).astype(jnp.bfloat16)
    gathers.append(Gathered(links, d_ff_ref, d_ff_all))
    own.wait()
    for copy in incoming:
        copy.wait_recv()
    first = lax.broadcasted_iota(jnp.int32, (rows, 128), 1) < HEAD_DIM
    zero = jnp.zeros((rows, 128), jnp.bfloat16)
    k, v = heads_ref[:, 128:256], heads_ref[:, 256:384]
    seg_k = tables.segment(lax.broadcasted_iota(jnp.int32, (1, total_rows), 1))
    part = lambda place: pl.ds(pl.multiple_of(place * rows, rows), rows)
    column = attn_ref.at[:, pl.ds(pl.multiple_of(links.seq * 128, 128), 128)]

    def attend_rows(place):
        here = part(place)
        q, seg_q = heads_ref[here, 0:128], tables.segment(frame_column(place * rows, rows))
        results = []
        for mine in (first, jnp.logical_not(first)):
            weights = head_scores(jnp.where(mine, q, zero), k, seg_q, seg_k)
            total = jnp.sum(weights, axis=1, keepdims=True)
            summed = jnp.dot(weights.astype(jnp.bfloat16), v, preferred_element_type=jnp.float32)
            results.append((summed, total))
        total = jnp.where(first, results[0][1], results[1][1])
        attended = jnp.where(first, results[0][0], results[1][0]) / total
        attn_heads[here, :] = attended.astype(jnp.bfloat16)
        exact_ref[here, :] = attended
        total_ref[here, :] = total

    incoming = []
    for r in FAR_FIRST:
        place = links.seq_of(r)
        attend_rows(place)
        incoming.append(links.send(attn_heads.at[part(place), :], column, links.peer(r)))
    attend_rows(links.seq)
    own = links.keep(attn_heads.at[part(links.seq), :], column)
    gathers[2].relay()
    gathers[3].relay()
    for copy in flow_copies:
        copy.wait_recv()
    own.wait()
    for copy in incoming:
        copy.wait_recv()
    for gather in gathers:
        gather.wait()
    links.leave()


def attend(
    lengths, chars, drop, flow, act, table, frames, skip, out_grad, b_skip, b_mod, b_qkv, w_skip,
    w_mod, w_qkv, shards,
):
    rows, width = frames.shape
    total_rows = shards * rows
    utts = flow.shape[1]
    vmem, there, scalar = everywhere(pltpu.VMEM), everywhere(pl.ANY), everywhere(pltpu.SMEM)
    shape = jax.ShapeDtypeStruct
    bf16 = lambda *dims: pltpu.VMEM(dims, jnp.bfloat16)
    return pl.pallas_call(
        partial(attend_kernel, utts),
        in_specs=[scalar] * 2 + [vmem] * 10 + [there] * 3,
        out_specs=[vmem] * 14,
        out_shape=[
            shape((rows, width), jnp.bfloat16),
            shape((total_rows, 384), jnp.bfloat16),
            shape((total_rows, 128), jnp.float32),
            shape((total_rows, 128), jnp.float32),
            shape((rows, 128), jnp.float32),
            shape((4, 8, 128), jnp.float32),
            shape((4 * rows, width), jnp.bfloat16),
            shape((4 * rows, 2 * width), jnp.bfloat16),
            shape((rows, width), jnp.float32),
            shape((8, 6 * width), jnp.float32),
            shape((total_rows, 128), jnp.float32),
            shape((total_rows, 128), jnp.float32),
            shape((rows, width), jnp.bfloat16),
            shape((4 * rows, width), jnp.bfloat16),
        ],
        scratch_shapes=[
            bf16(total_rows, 128),
            pltpu.VMEM((10, 8, 128), jnp.float32),
            pltpu.VMEM((8, 128), jnp.float32),
            pltpu.VMEM((8, 128), jnp.float32),
            bf16(shards, rows, 384),
            bf16(rows, width),
            bf16(*w_skip.shape),
            bf16(*w_mod.shape),
            bf16(*w_qkv.shape),
        ]
        + semaphores(40),
        compiler_params=comm_params(1),
    )(
        lengths, chars, drop, flow, act, table, frames, skip, out_grad,
        b_skip[None, :], b_mod[None, :], b_qkv[None, :], w_skip, w_mod, w_qkv,
    )


ALONG = (((1,), (1,)), ((), ()))
DOWN = (((0,), (0,)), ((), ()))


def normal_parts(values):
    centred = values - jnp.mean(values, axis=1, keepdims=True)
    scale = lax.rsqrt(jnp.mean(centred * centred, axis=1, keepdims=True) + EPSILON)
    return centred * scale, scale


def normal_back(inward, unit, scale):
    return scale * (
        inward
        - jnp.mean(inward, axis=1, keepdims=True)
        - unit * jnp.mean(inward * unit, axis=1, keepdims=True)
    )


def column_sum(values):
    return jnp.sum(values.astype(jnp.float32), axis=0, keepdims=True)


def backward_kernel(
    utts, lengths_ref, attn_ref, resid_ref, mod_ref, loss_ref, out_grad_ref, d_ff,
    b_out_ref, b_up_ref, b_down_ref,
    heads_ref, exact_ref, total_ref, cos_ref, sin_ref,
    norm_a_ref, joined_ref, d_ff_ref, w_out_ref, w_up_ref, w_down_ref, w_qkv_ref, w_skip_ref,
    mixed, g_down, g_up, g_out, g_qkv, g_skip, smalls, g_frames, g_skip_in,
    norm_f, act, d_inner, d_branch, d_attn, pieces, d_mid, ff_sum, d_norm,
    grad_heads, d_heads, dk_ref, dv_ref,
    d_ff_all, act_all, norm_all, d_inner_all, attn_all, d_branch_all,
    norm_a_all, joined_all, d_qkv, d_qkv_all, d_resid, d_resid_all,
    up_ring, down_ring, w_out, w_qkv, w_skip, small_own, small_got, small_out,
    *rest,
):
    tiles, (send_sems, recv_sems, local_sems, ring_sems) = rest[:-4], rest[-4:]
    links = Links(send_sems, recv_sems, local_sems)
    rows, model = resid_ref.shape
    block_width = up_ring.shape[2]
    steps = w_up_ref.shape[1] // block_width

    zh = links.seq // 4

    def chunk(c):
        return (c + (1 - zh) * (steps // 2)) % steps

    def ring(c):
        slot = c % 2
        columns = pl.ds(pl.multiple_of(chunk(c) * block_width, block_width), block_width)
        return (
            pltpu.make_async_copy(w_up_ref.at[:, columns], up_ring.at[slot], ring_sems.at[slot]),
            pltpu.make_async_copy(
                w_down_ref.at[columns, :], down_ring.at[slot], ring_sems.at[2 + slot]
            ),
        )

    load_out = links.keep(w_out_ref, w_out)
    load_d = links.keep(d_ff_ref, d_ff_all)
    for c in (0, 1):
        for copy in ring(c):
            copy.start()
    loads = [
        links.keep(w_qkv_ref, w_qkv),
        links.keep(w_skip_ref, w_skip),
        links.keep(norm_a_ref, norm_a_all),
        links.keep(joined_ref, joined_all),
    ]
    links.enter((1, 2, 3), range(1, 8))

    tables = Frames(utts, lengths_ref)
    segment = tables.segment(frame_column(links.seq * rows, rows))

    def modulation(piece):
        return per_frame(mod_ref, segment, utts, piece, model)

    def d_out():
        return out_grad_ref[...].astype(jnp.float32) * loss_ref[:, 0:1]

    load_out.wait()
    branch = (
        jnp.dot(attn_ref[...], w_out[...], preferred_element_type=jnp.float32) + b_out_ref[...]
    )
    pieces[0] = branch
    mid = resid_ref[...] + modulation(2) * branch
    d_mid[...] = mid
    unit, _ = normal_parts(mid)
    norm_f[...] = (unit * (1.0 + modulation(4)) + modulation(3)).astype(jnp.bfloat16)
    ff_sum[...] = jnp.zeros_like(ff_sum)
    d_norm[...] = jnp.zeros_like(d_norm)
    const = math.sqrt(2.0 / math.pi)
    width = d_inner_all.shape[1]

    def feed(c, _):
        slot = c % 2
        columns = pl.ds(pl.multiple_of(chunk(c) * block_width, block_width), block_width)
        for copy in ring(c):
            copy.wait()
        inner = (
            jnp.dot(norm_f[...], up_ring[slot], preferred_element_type=jnp.float32)
            + b_up_ref[:, columns]
        )
        square = inner * inner
        slope = jnp.tanh(const * inner * (1.0 + 0.044715 * square))
        gate = 0.5 * (1.0 + slope)
        act_b = (inner * gate).astype(jnp.bfloat16)
        turn = gate + 0.5 * inner * (1.0 - slope * slope) * (
            const * (1.0 + 3.0 * 0.044715 * square)
        )
        here = pl.ds(pl.multiple_of(chunk(c) * 128, 128), 128)
        d_act = lax.dot_general(
            d_ff[...], down_ring[slot], ALONG, preferred_element_type=jnp.float32
        )
        d_inner_b = (turn * d_act).astype(jnp.bfloat16)
        for u in range(4):
            act[u, :, here] = act_b[:, u * 128 : (u + 1) * 128]
            d_inner[u, :, here] = d_inner_b[:, u * 128 : (u + 1) * 128]
        ff_sum[...] += jnp.dot(act_b, down_ring[slot], preferred_element_type=jnp.float32)
        d_norm[...] += lax.dot_general(
            d_inner_b, up_ring[slot], ALONG, preferred_element_type=jnp.float32
        )

        @pl.when(c + 2 < steps)
        def _():
            for copy in ring(c + 2):
                copy.start()

        return 0

    middle = width // 2
    half_at = lambda place: pl.ds(pl.multiple_of(place * middle, middle), middle)
    far_half, near_half = half_at(1 - zh), half_at(zh)
    lax.fori_loop(0, steps // 2, feed, 0)
    quarters_a = [Quarter(links, lambda u: act.at[u, :, far_half], act_all, far_half)]
    lax.fori_loop(steps // 2, steps, feed, 0)
    quarters_a.append(Quarter(links, lambda u: act.at[u, :, near_half], act_all, near_half))
    gather_n = Gathered(links, norm_f, norm_all)
    own_rows = pl.ds(pl.multiple_of(links.seq * rows, rows), rows)
    strip = lambda ref, place, size: ref.at[
        :, pl.ds(pl.multiple_of(place * size, size), size)
    ]
    narrow = d_branch_all.shape[1]
    quarter_i = Quarter(links, lambda u: d_inner.at[u], d_inner_all)
    mid = d_mid[...]
    unit, scale = normal_parts(mid)
    d_norm_f = d_norm[...]
    pieces[2] = d_norm_f * unit
    d_mid_f = d_out() + normal_back(d_norm_f * (1.0 + modulation(4)), unit, scale)
    gate_a = modulation(2)
    d_branch[...] = (gate_a * d_mid_f).astype(jnp.bfloat16)
    pieces[0] = pieces[0] * d_mid_f
    d_mid[...] = d_mid_f
    d_attn[...] = lax.dot_general(
        d_branch[...], w_out[...], ALONG, preferred_element_type=jnp.float32
    ).astype(jnp.bfloat16)
    own = links.keep(strip(d_attn, links.seq, 128), grad_heads.at[own_rows, :])
    incoming_d = [
        links.send(
            strip(d_attn, links.seq_of(r), 128), grad_heads.at[own_rows, :], links.peer(r)
        )
        for r in FAR_FIRST
    ]
    quarter_b = Quarter(links, lambda u: strip(d_branch, u, narrow), d_branch_all)
    gather_b = Gathered(links, attn_ref, attn_all)
    half = width // 2
    down_at = lambda h: lambda u: g_down.at[
        pl.ds(pl.multiple_of(u * 128, 128), 128), pl.ds(h * half, half)
    ]
    column_at = lambda ref, step, offset, size: lambda u: ref.at[
        :, pl.ds(pl.multiple_of(u * step + offset, 128), size)
    ]
    wide, thin = d_qkv_all.shape[1], d_resid_all.shape[1]
    third, slim = wide // 2, thin // 2
    plans = [
        (act_all, d_ff_all, pl.ds(0, half), down_at(0)),
        (act_all, d_ff_all, pl.ds(half, half), down_at(1)),
        (norm_all, d_inner_all, pl.ds(0, half), column_at(g_up, width, 0, half)),
        (norm_all, d_inner_all, pl.ds(half, half), column_at(g_up, width, half, half)),
        (attn_all, d_branch_all, pl.ds(0, narrow), column_at(g_out, narrow, 0, narrow)),
        (norm_a_all, d_qkv_all, pl.ds(0, third), column_at(g_qkv, wide, 0, third)),
        (norm_a_all, d_qkv_all, pl.ds(third, third), column_at(g_qkv, wide, third, third)),
        (joined_all, d_resid_all, pl.ds(0, slim), column_at(g_skip, thin, 0, slim)),
        (joined_all, d_resid_all, pl.ds(slim, slim), column_at(g_skip, thin, slim, slim)),
    ]
    y_first = (True, False, True, True, True, True, True, True, True)
    shares = [
        Share(links, y_first[i], left, right, columns, *tiles[4 * i : 4 * i + 4], result)
        for i, (left, right, columns, result) in enumerate(plans)
    ]
    load_d.wait()
    quarters_a[0].wait()
    shares[0].start_far()
    shares[1].start_far()
    ff_out = ff_sum[...] + b_down_ref[...]
    mixed[...] = (mid + modulation(5) * ff_out).astype(jnp.bfloat16)
    pieces[1] = d_out() * ff_out
    small_own[...] = jnp.zeros_like(small_own)
    small_own[4:5, :] = column_sum(d_branch[...])
    for c in range(4):
        small_own[5 + c : 6 + c, :] = column_sum(d_inner[c])
    small_own[9:10, :] = column_sum(d_ff[...])

    def utterance_sums(piece, values):
        for u in range(utts):
            row = 10 + utts * piece + u
            small_own[row : row + 1, :] = jnp.sum(
                jnp.where(segment == u, values, 0.0), axis=0, keepdims=True
            )

    utterance_sums(2, pieces[0])
    utterance_sums(3, d_norm[...])
    utterance_sums(4, pieces[2])
    utterance_sums(5, pieces[1])
    gather_n.relay()
    quarters_a[1].wait()
    shares[0].start_near()
    shares[1].start_near()
    own.wait()
    for copy in incoming_d:
        copy.wait_recv()
    dk_ref[...] = jnp.zeros_like(dk_ref)
    dv_ref[...] = jnp.zeros_like(dv_ref)
    first = lax.broadcasted_iota(jnp.int32, (256, 128), 1) < HEAD_DIM
    zero = jnp.zeros((256, 128), jnp.bfloat16)
    lower = lower_half((256, 128))
    k, v = heads_ref[:, 128:256], heads_ref[:, 256:384]
    seg_k = tables.segment(lax.broadcasted_iota(jnp.int32, (1, heads_ref.shape[0]), 1))

    def turned(values, here):
        return (
            values * cos_ref[here, :] - swap_halves(values, lower) * sin_ref[here, :]
        ).astype(jnp.bfloat16)

    def block(step, _):
        here = pl.ds(pl.multiple_of(step * 256, 256), 256)
        q, seg_q = heads_ref[here, 0:128], tables.segment(frame_column(step * 256, 256))
        scaled = grad_heads[here, :].astype(jnp.float32) / total_ref[here, :]
        grad_acc = scaled.astype(jnp.bfloat16)
        product = scaled * exact_ref[here, :]
        d_query = []
        for mine in (first, jnp.logical_not(first)):
            q_own = jnp.where(mine, q, zero)
            g_own = jnp.where(mine, grad_acc, zero)
            delta = jnp.sum(jnp.where(mine, product, 0.0), axis=1, keepdims=True)
            weights = head_scores(q_own, k, seg_q, seg_k)
            dots = lax.dot_general(g_own, v, ALONG, preferred_element_type=jnp.float32)
            d_scores = (weights * (dots - delta)).astype(jnp.bfloat16)
            d_query.append(jnp.dot(d_scores, k, preferred_element_type=jnp.float32))
            dk_ref[...] += lax.dot_general(
                d_scores, q_own, DOWN, preferred_element_type=jnp.float32
            )
            dv_ref[...] += lax.dot_general(
                weights.astype(jnp.bfloat16), g_own, DOWN, preferred_element_type=jnp.float32
            )
        d_heads[here, 0:128] = turned(jnp.where(first, d_query[0], d_query[1]) * 0.125, here)
        return 0

    blocks = heads_ref.shape[0] // 256
    lax.fori_loop(0, blocks, block, 0)

    def finish(step, _):
        here = pl.ds(pl.multiple_of(step * 256, 256), 256)
        d_heads[here, 128:256] = turned(dk_ref[here, :] * 0.125, here)
        d_heads[here, 256:384] = dv_ref[here, :].astype(jnp.bfloat16)
        return 0

    lax.fori_loop(0, blocks, finish, 0)
    part = lambda place, c: d_heads.at[
        pl.ds(pl.multiple_of(place * rows, rows), rows), pl.ds(c * 128, 128)
    ]
    home = lambda c: d_qkv.at[
        :, pl.ds(pl.multiple_of(c * model + links.seq * 128, 128), 128)
    ]
    owns = [links.keep(part(links.seq, c), home(c)) for c in range(3)]
    incoming = [
        links.send(part(links.seq_of(r), c), home(c), links.peer(r))
        for r in FAR_FIRST
        for c in range(3)
    ]
    gather_n.wait()
    quarter_i.wait()
    state = {}

    def output_share():
        gather_b.relay()
        gather_b.wait()
        quarter_b.wait()
        shares[4].start()

    def projections():
        for copy in owns:
            copy.wait()
        for copy in incoming:
            copy.wait_recv()
        for copy in loads:
            copy.wait()
        state["qkv"] = Quarter(links, lambda u: strip(d_qkv, u, wide), d_qkv_all)
        d_norm_a = lax.dot_general(
            d_qkv[...], w_qkv[...], ALONG, preferred_element_type=jnp.float32
        )
        unit, scale = normal_parts(resid_ref[...])
        d_resid_f = d_mid[...] + normal_back(d_norm_a * (1.0 + modulation(1)), unit, scale)
        rounded = d_resid_f.astype(jnp.bfloat16)
        d_resid[...] = rounded
        state["resid"] = Quarter(links, lambda u: strip(d_resid, u, thin), d_resid_all)
        small_own[0:1, :] = column_sum(rounded)
        for c in range(3):
            small_own[1 + c : 2 + c, :] = column_sum(d_qkv[:, c * model : (c + 1) * model])
        utterance_sums(0, d_norm_a)
        utterance_sums(1, d_norm_a * unit)
        small_out[0] = small_own[...].astype(jnp.bfloat16)
        state["small"] = links.send(small_out.at[0], small_got.at[0], links.peer(1))

    def qkv_shares():
        state["qkv"].wait()
        shares[5].start()
        shares[6].start()

    def skip_shares():
        state["resid"].wait()
        shares[7].start()
        shares[8].start()

    def inputs():
        for index, out in enumerate((g_frames, g_skip_in)):
            out[...] = lax.dot_general(
                d_resid[...],
                w_skip[pl.ds(index * model, model), :],
                ALONG,
                preferred_element_type=jnp.float32,
            ).astype(jnp.bfloat16)

    def small_y():
        state["small"].wait_recv()
        small_own[...] += small_got[0].astype(jnp.float32)
        small_out[1] = small_own[...].astype(jnp.bfloat16)
        state["small"] = links.send(small_out.at[1], small_got.at[1], links.peer(2))

    def small_z1():
        state["small"].wait_recv()
        small_own[...] += small_got[1].astype(jnp.float32)
        small_out[2] = small_own[...].astype(jnp.bfloat16)
        state["small"] = links.send(small_out.at[2], small_got.at[2], links.peer(4))

    def small_z2():
        state["small"].wait_recv()
        mine = smalls.at[links.utt]
        mine[...] = (small_own[...] + small_got[2].astype(jnp.float32)).astype(jnp.bfloat16)
        state["spread"] = [links.send(mine, mine, links.mate(r)) for r in (2, 3, 1)]

    stages = ("start", "after_a", "after_b", "after_z2", "relay", "wait")
    s, a, b, z, r, w = ([getattr(share, stage) for share in shares] for stage in stages)
    for step in (
        s[2], a[0], a[1], s[3],
        output_share, projections,
        a[2], b[0], b[1],
        qkv_shares,
        z[0], b[2],
        small_y, inputs,
        z[1], z[2],
        skip_shares,
        a[3], r[0], r[1],
        small_z1,
        a[4], b[3], r[2], z[3], b[4],
        small_z2,
        w[0], w[1], a[5], z[4], r[3], b[5], w[2], a[6], r[4], z[5], b[6], w[3], a[7], r[5],
        z[6], b[7], w[4], a[8], b[8], z[7], r[6], w[5], z[8], r[7], w[6], r[8], w[7], w[8],
    ):
        step()
    for copy in state["spread"]:
        copy.wait_recv()
    links.leave()


def backward(
    lengths, attn_b, resid, mod, loss, out_grad, d_ff, b_out, b_up, b_down,
    heads, exact, total, cos, sin,
    norm_a_all, joined_all, d_ff_all, w_out, w_up, w_down, w_qkv, w_skip,
):
    rows, model = resid.shape
    frames, inner = heads.shape[0], w_up.shape[1]
    utts = lengths.shape[1]
    small = (-(-(10 + 6 * utts) // 16) * 16, model)
    vmem, there = everywhere(pltpu.VMEM), everywhere(pl.ANY)
    shape = jax.ShapeDtypeStruct
    bf16 = lambda *dims: pltpu.VMEM(dims, jnp.bfloat16)
    f32 = lambda *dims: pltpu.VMEM(dims, jnp.float32)
    part, step = model // 8, inner // 8
    return pl.pallas_call(
        partial(backward_kernel, utts),
        in_specs=[everywhere(pltpu.SMEM)] + [vmem] * 14 + [there] * 8,
        out_specs=[vmem] * 9,
        out_shape=[
            shape((rows, model), jnp.bfloat16),
            shape((inner // 8, model), jnp.bfloat16),
            shape((part, inner), jnp.bfloat16),
            shape((part, model), jnp.bfloat16),
            shape((part, 3 * model), jnp.bfloat16),
            shape((2 * part, model), jnp.bfloat16),
            shape((4,) + small, jnp.bfloat16),
            shape((rows, model), jnp.bfloat16),
            shape((rows, model), jnp.bfloat16),
        ],
        scratch_shapes=[
            bf16(rows, model),
            bf16(4, rows, inner // 4),
            bf16(4, rows, inner // 4),
            bf16(rows, model),
            bf16(rows, model),
            f32(3, rows, model),
            f32(rows, model),
            f32(rows, model),
            f32(rows, model),
            bf16(frames, 128),
            bf16(frames, 384),
            f32(frames, 128),
            f32(frames, 128),
            bf16(4 * rows, model),
            bf16(4 * rows, inner // 4),
            bf16(4 * rows, model),
            bf16(4 * rows, inner // 4),
            bf16(4 * rows, model),
            bf16(4 * rows, model // 4),
            bf16(4 * rows, model),
            bf16(4 * rows, 2 * model),
            bf16(rows, 3 * model),
            bf16(4 * rows, 3 * model // 4),
            bf16(rows, model),
            bf16(4 * rows, model // 4),
            bf16(2, model, step),
            bf16(2, step, model),
            bf16(*w_out.shape),
            bf16(*w_qkv.shape),
            bf16(*w_skip.shape),
            f32(*small),
            bf16(3, *small),
            bf16(3, *small),
        ]
        + share_scratch(part, inner // 8) * 4
        + share_scratch(part, model // 4)
        + share_scratch(part, 3 * model // 8) * 2
        + share_scratch(2 * part, model // 8) * 2
        + semaphores(160)
        + [pltpu.SemaphoreType.DMA((4,))],
        compiler_params=comm_params(2),
    )(
        lengths, attn_b, resid, mod, loss, out_grad, d_ff,
        b_out[None, :], b_up[None, :], b_down[None, :],
        heads, exact, total, cos, sin,
        norm_a_all, joined_all, d_ff_all, w_out, w_up, w_down, w_qkv, w_skip,
    )


UP = 3


def finish_kernel(utts, shards, act_ref, *rest):
    kept_in, wide_in, smalls_in = rest[:3], rest[3:8], rest[8]
    kept_out, wide_out, mod_out, bias_out = rest[9:12], rest[12:17], rest[17], rest[18:24]
    kept, wide, staged = rest[24:27], rest[27:32], rest[32:37]
    smalls_got, smalls_ref, mod_stage, bias_stage, d_mod, totals, sems, load_sems = rest[37:]
    seq = lax.axis_index("seq")
    loads, copies = [], []
    for source, target in zip((*wide_in, smalls_in, *kept_in), (*wide, smalls_got, *kept)):
        copy = pltpu.make_async_copy(source, target, load_sems.at[len(loads)])
        copy.start()
        loads.append(copy)

    def put(source, target):
        copy = pltpu.make_async_copy(source, target, sems.at[len(copies)])
        copy.start()
        copies.append(copy)

    model = smalls_ref.shape[2]
    lanes = 128
    for place, (source, stage, target) in enumerate(zip(wide, staged, wide_out)):
        loads[place].wait()
        if place == UP:
            for u in range(4):
                for c in range(shards):
                    stage[:, (4 * c + u) * lanes : (4 * c + u + 1) * lanes] = source[
                        :, u * model + c * lanes : u * model + (c + 1) * lanes
                    ].astype(jnp.float32)
        else:
            stage[...] = source[...].astype(jnp.float32)
        put(stage, target)
    groups = smalls_ref.shape[0]
    loads[5].wait()
    smalls_ref[...] = smalls_got[...].astype(jnp.float32)
    bias_sum = (
        smalls_ref[0, 0:10] + smalls_ref[1, 0:10] + smalls_ref[2, 0:10] + smalls_ref[3, 0:10]
    )
    for row in range(10):
        totals[row, 0:1] = bias_sum[row : row + 1]
    d_mod[...] = jnp.zeros_like(d_mod)
    for piece in range(6):
        first = 10 + utts * piece
        for g in range(groups):
            d_mod[piece, g * utts : (g + 1) * utts, :] = smalls_ref[g, first : first + utts, :]
        rows = d_mod[piece]
        totals[10 + piece, 0:1] = jnp.sum(rows, axis=0, keepdims=True)
        columns = slice(piece * model, (piece + 1) * model)
        mod_stage[:, columns] = jnp.dot(
            act_ref[...], rows, precision=HIGHEST_PRECISION, preferred_element_type=jnp.float32
        )
    put(mod_stage, mod_out)
    for load, source, target in zip(loads[6:], kept, kept_out):
        load.wait()
        put(source, target)
    line = model // lanes
    first = 0
    for place, target in enumerate(bias_out):
        count = target.shape[1] // lanes
        for i in range(count):
            unit = i * line + seq if place == UP else seq * count + i
            column = pl.multiple_of((unit % line) * lanes, lanes)
            bias_stage[place, 0:1, i * lanes : (i + 1) * lanes] = totals[
                first + unit // line, 0:1, pl.ds(column, lanes)
            ]
        first += count * shards // line
        put(bias_stage.at[place, pl.ds(0, 1), pl.ds(0, count * lanes)], target)
    for copy in copies:
        copy.wait()


def finish(shards, utts, act_own, smalls, mixed, frames, skip, grads):
    vmem, there = everywhere(pltpu.VMEM), everywhere(pl.ANY)
    shape = jax.ShapeDtypeStruct
    model = smalls.shape[2]
    own = model // shards
    depth = act_own.shape[1]
    mod_shape = (own, 6 * model)
    widths = [own, 3 * own, own, 4 * own, own, 6 * own]
    kept = (mixed, frames, skip)
    outs = pl.pallas_call(
        partial(finish_kernel, utts, shards),
        in_specs=[vmem] + [there] * 9,
        out_specs=[there] * 15,
        out_shape=[shape(v.shape, v.dtype) for v in kept]
        + [shape(g.shape, jnp.float32) for g in grads]
        + [shape(mod_shape, jnp.float32)]
        + [shape((1, w), jnp.float32) for w in widths],
        scratch_shapes=[pltpu.VMEM(v.shape, v.dtype) for v in (*kept, *grads)]
        + [pltpu.VMEM(g.shape, jnp.float32) for g in grads]
        + [
            pltpu.VMEM(smalls.shape, smalls.dtype),
            pltpu.VMEM(smalls.shape, jnp.float32),
            pltpu.VMEM(mod_shape, jnp.float32),
            pltpu.VMEM((6, 8, max(widths)), jnp.float32),
            pltpu.VMEM((6, depth, model), jnp.float32),
            pltpu.VMEM((16, 8, model), jnp.float32),
            pltpu.SemaphoreType.DMA((15,)),
            pltpu.SemaphoreType.DMA((9,)),
        ],
        compiler_params=pltpu.CompilerParams(vmem_limit_bytes=VMEM_LIMIT),
    )(act_own, *kept, *grads, smalls)
    return outs[:9], [v.reshape(-1) for v in outs[9:]]


def own_time_act(flows, seq_place, shards, model):
    half_dim, own = model // 2, model // shards
    column = seq_place * own + jnp.arange(own, dtype=jnp.int32)
    inverse = jnp.exp(
        -math.log(10000.0) * (column % half_dim).astype(jnp.float32) / half_dim
    )
    angles = 1000.0 * flows[None, :] * inverse[:, None]
    wave = jnp.where((column < half_dim)[:, None], jnp.sin(angles), jnp.cos(angles))
    return jax.nn.silu(wave).astype(jnp.bfloat16).astype(jnp.float32)


def compact_tables(lengths, total_rows):
    half_dim = HEAD_DIM // 2
    shape = (total_rows // 4, 128)
    lane = lax.broadcasted_iota(jnp.int32, shape, 1)
    frame = lax.broadcasted_iota(jnp.int32, shape, 0) + (lane // half_dim) * shape[0]
    start, end = jnp.zeros(shape, jnp.int32), jnp.int32(0)
    for u in range(lengths.shape[0]):
        end = end + lengths[u]
        start = jnp.where(frame >= end, end, start)
    inverse = jnp.exp(
        -math.log(10000.0) * 2.0 * (lane % half_dim).astype(jnp.float32) / HEAD_DIM
    )
    angles = (frame - start).astype(jnp.float32) * inverse
    return jnp.stack([jnp.cos(angles), jnp.sin(angles)])


def padded_time_act(flow_vals, model):
    half_dim = model // 2
    column = jnp.arange(model, dtype=jnp.int32)
    inverse = jnp.exp(-math.log(10000.0) * (column % half_dim).astype(jnp.float32) / half_dim)
    flow_vals = jnp.pad(flow_vals, (0, 8 - flow_vals.shape[0]))
    angles = 1000.0 * flow_vals[:, None] * inverse[None, :]
    wave = jnp.where((column < half_dim)[None, :], jnp.sin(angles), jnp.cos(angles))
    return jax.nn.silu(wave).astype(jnp.bfloat16)


def local(
    frames_in,
    skip_in,
    flow_times,
    frame_lengths,
    char_lengths,
    drop_mask,
    out_grad,
    w_skip,
    b_skip,
    w_mod,
    b_mod,
    w_qkv,
    b_qkv,
    w_out,
    b_out,
    w_up,
    b_up,
    w_down,
    b_down,
):
    local_rows = frames_in.shape[1]
    model_width = frames_in.shape[2]
    shards = lax.axis_size("seq")
    seq_place = lax.axis_index("seq")
    lengths = frame_lengths[0]
    whole = model_width * 4
    fused = (
        lax.axis_size("utt") == 4
        and shards == 8
        and HEADS * HEAD_DIM == 1024
        and model_width == 1024
        and w_up.shape[1] == whole
        and local_rows == 128
        and flow_times.shape[1] <= 8
    )
    if not fused:
        utt_ends = jnp.cumsum(lengths)
        segment, position, in_loss, member = frame_tables(
            lengths, char_lengths[0], seq_place * local_rows, local_rows
        )
        member_f = member.astype(jnp.float32)
        loss_mask = in_loss.astype(jnp.float32)
        dropped = drop_mask[0].astype(jnp.float32)
        counts = jnp.stack([jnp.sum(loss_mask * dropped), jnp.sum(loss_mask * (1.0 - dropped))])
        counts = jnp.pad(counts[None, :], ((0, 7), (0, 126)))
        counts = xor_sum(xor_sum(counts, "utt"), "seq")
        time_act = jax.nn.silu(time_embed(flow_times[0], model_width)).astype(jnp.bfloat16)
        mod_u = jnp.dot(time_act, w_mod, preferred_element_type=jnp.float32) + b_mod
        mod_f = jnp.dot(member_f, mod_u, precision=HIGHEST_PRECISION)
        shift_a, scale_a, gate_a, shift_f, scale_f, gate_f = jnp.split(mod_f, 6, axis=1)
        joined = jnp.concatenate([frames_in[0], skip_in[0]], axis=1)
        residual = jnp.dot(joined, w_skip, preferred_element_type=jnp.float32) + b_skip
        norm_a = modulate(residual, scale_a, shift_a).astype(jnp.bfloat16)
        qkv_full = jnp.dot(norm_a, w_qkv, preferred_element_type=jnp.float32) + b_qkv
    if fused:
        (
            attn_b, qkv_heads, exact, total, loss, flows, norm_all, joined_all,
            residual, mod_u, cos_all, sin_all, d_ff, d_ff_all,
        ) = attend(
            frame_lengths,
            char_lengths,
            drop_mask,
            flow_times,
            padded_time_act(flow_times[0], model_width),
            compact_tables(lengths, local_rows * shards),
            frames_in[0],
            skip_in[0],
            out_grad[0],
            b_skip,
            b_mod,
            b_qkv,
            w_skip,
            w_mod,
            w_qkv,
            shards,
        )
    else:
        angle_cos, angle_sin = rotary_tables(position, HEAD_DIM)
        queries = rotate(
            qkv_full[:, :model_width].reshape(local_rows, HEADS, HEAD_DIM), angle_cos, angle_sin
        ).astype(jnp.bfloat16)
        key_rot = rotate(
            qkv_full[:, model_width : 2 * model_width].reshape(local_rows, HEADS, HEAD_DIM),
            angle_cos,
            angle_sin,
        ).astype(jnp.bfloat16)
        key_value = jnp.stack(
            [
                key_rot.reshape(local_rows, model_width),
                qkv_full[:, 2 * model_width :].astype(jnp.bfloat16),
            ],
            axis=0,
        )
        start_state = (
            jnp.zeros((local_rows, HEADS, HEAD_DIM), jnp.float32),
            jnp.zeros((HEADS, local_rows), jnp.float32),
        )
        fwd_piece = partial(forward_piece, queries=queries, query_segment=segment, utt_ends=utt_ends)
        weighted, totals = over_blocks(
            partial(fwd_piece, usable=True),
            start_state,
            lax.all_gather(key_value, "seq", axis=1, tiled=True),
            jnp.int32(0),
            local_rows,
        )
        totals_rows = jnp.transpose(totals)
        attended = weighted / totals_rows[:, :, None]
        attn_b = attended.reshape(local_rows, model_width).astype(jnp.bfloat16)
    if fused:
        mixed, g_w_down, g_w_up, g_w_out, g_w_qkv, g_w_skip, smalls, g_frames, g_skip_in = backward(
            frame_lengths,
            attn_b,
            residual,
            mod_u,
            loss,
            out_grad[0],
            d_ff,
            b_out,
            b_up,
            b_down,
            qkv_heads,
            exact,
            total,
            cos_all,
            sin_all,
            norm_all,
            joined_all,
            d_ff_all,
            w_out,
            w_up,
            w_down,
            w_qkv,
            w_skip,
        )
        utts = flow_times.shape[1]
        act_own = own_time_act(flows[:, 0, :utts].reshape(-1), seq_place, shards, model_width)
        act_own = jnp.pad(act_own, ((0, 0), (0, -act_own.shape[1] % 8)))
        wide, biases = finish(
            shards,
            utts,
            act_own,
            smalls,
            mixed,
            g_frames,
            g_skip_in,
            (g_w_skip, g_w_qkv, g_w_out, g_w_up, g_w_down),
        )
        mixed, g_frames, g_skip_in, g_w_skip, g_w_qkv, g_w_out, g_w_up, g_w_down, g_w_mod = wide
        own_biases, g_b_mod = biases[:5], biases[5]
    else:
        n_drop, n_keep = counts[0, 0], counts[0, 1]
        loss_weight = (
            loss_mask
            * (n_drop + n_keep)
            * 0.5
            * (dropped / (n_drop + 1.0) + (1.0 - dropped) / (n_keep + 1.0))
        )
        branch = jnp.dot(attn_b, w_out, preferred_element_type=jnp.float32) + b_out
        mid_state = residual + gate_a * branch
        norm_f = modulate(mid_state, scale_f, shift_f).astype(jnp.bfloat16)
        ff_inner = jnp.dot(norm_f, w_up, preferred_element_type=jnp.float32) + b_up
        ff_act, gelu_pull = jax.vjp(partial(jax.nn.gelu, approximate=True), ff_inner)
        act_b = ff_act.astype(jnp.bfloat16)
        ff_out = jnp.dot(act_b, w_down, preferred_element_type=jnp.float32) + b_down
        out_state = mid_state + gate_f * ff_out
        d_out = out_grad[0].astype(jnp.float32) * loss_weight[:, None]
        d_ff = (gate_f * d_out).astype(jnp.bfloat16)
        d_gate_f = d_out * ff_out
        g_b_down = jnp.sum(d_ff.astype(jnp.float32), axis=0)
        (d_inner,) = gelu_pull(back_product(d_ff, w_down))
        d_inner_b = d_inner.astype(jnp.bfloat16)
        g_b_up = jnp.sum(d_inner_b.astype(jnp.float32), axis=0)
        d_norm_f = back_product(d_inner_b, w_up)
        _, norm_f_pull = jax.vjp(modulate, mid_state, scale_f, shift_f)
        d_mid_norm, d_scale_f, d_shift_f = norm_f_pull(d_norm_f)
        d_mid = d_out + d_mid_norm
        d_branch = (gate_a * d_mid).astype(jnp.bfloat16)
        d_gate_a = d_mid * branch
        g_b_out = jnp.sum(d_branch.astype(jnp.float32), axis=0)
        d_attn = back_product(d_branch, w_out)
        mixed = out_state.astype(jnp.bfloat16)
        g_w_down = weight_grad(gather_left(act_b), d_ff)
        g_w_up = weight_grad(gather_left(norm_f), d_inner_b)
        g_w_out = weight_grad(gather_left(attn_b), d_branch)
        d_attn = d_attn.reshape(local_rows, HEADS, HEAD_DIM)
        grad_acc = (d_attn / totals_rows[:, :, None]).astype(jnp.bfloat16)
        delta = jnp.transpose(jnp.sum(d_attn * attended, axis=2) / totals_rows)
        bwd_piece = partial(
            backward_piece,
            queries=queries,
            query_segment=segment,
            utt_ends=utt_ends,
            grad_acc=grad_acc,
            delta=delta,
        )
        zero_query = jnp.zeros((local_rows, HEADS, HEAD_DIM), jnp.float32)
        zero_all = jnp.zeros((2, local_rows * shards, model_width), jnp.float32)

        def block_fn(inner_state, portion, block_start):
            d_query_sum, d_all = inner_state
            d_query_add, d_block = bwd_piece(portion, block_start, True)
            return (
                d_query_sum + d_query_add,
                lax.dynamic_update_slice_in_dim(d_all, d_block, block_start, 1),
            )

        d_query, d_all = over_blocks(
            block_fn,
            (zero_query, zero_all),
            lax.all_gather(key_value, "seq", axis=1, tiled=True),
            jnp.int32(0),
            local_rows,
        )
        d_key_value = lax.psum_scatter(d_all, "seq", scatter_dimension=1, tiled=True)
        d_query_pre = unrotate(d_query, angle_cos, angle_sin).reshape(local_rows, model_width)
        d_key_pre = unrotate(
            d_key_value[0].reshape(local_rows, HEADS, HEAD_DIM), angle_cos, angle_sin
        ).reshape(local_rows, model_width)
        d_qkv = jnp.concatenate([d_query_pre, d_key_pre, d_key_value[1]], axis=1).astype(jnp.bfloat16)
        g_b_qkv = jnp.sum(d_qkv.astype(jnp.float32), axis=0)
        d_norm_a = back_product(d_qkv, w_qkv)
        _, norm_a_pull = jax.vjp(modulate, residual, scale_a, shift_a)
        d_resid_norm, d_scale_a, d_shift_a = norm_a_pull(d_norm_a)
        d_resid = (d_mid + d_resid_norm).astype(jnp.bfloat16)
        g_b_skip = jnp.sum(d_resid.astype(jnp.float32), axis=0)
        d_joined = back_product(d_resid, w_skip)
        d_mod_f = jnp.concatenate(
            [d_shift_a, d_scale_a, d_gate_a, d_shift_f, d_scale_f, d_gate_f], axis=1
        )
        d_mod_u = jnp.dot(jnp.transpose(member_f), d_mod_f, precision=HIGHEST_PRECISION)
        small = jnp.concatenate(
            [g_b_skip, g_b_qkv, g_b_out, g_b_up, g_b_down, d_mod_u.reshape(-1)]
        )
        biases = small.shape[0] - d_mod_u.size
        g_w_qkv = weight_grad(gather_left(norm_a), d_qkv)
        g_w_skip = weight_grad(gather_left(joined), d_resid)
        small = xor_sum(small.reshape(-1, 128), "seq").reshape(-1)
        bias_sum = xor_sum(small[:biases].reshape(-1, 128), "utt").reshape(-1)
        d_mod_all = gather_ordered(small[biases:].reshape(d_mod_u.shape), 0)
        act_all = gather_ordered(time_act, 0)
        g_frames = d_joined[:, :model_width].astype(jnp.bfloat16)
        g_skip_in = d_joined[:, model_width:].astype(jnp.bfloat16)
        act_all = act_all.astype(jnp.float32)
        own_width = model_width // shards
        act_own = lax.dynamic_slice_in_dim(act_all, seq_place * own_width, own_width, 1)
        g_w_mod = jnp.dot(jnp.transpose(act_own), d_mod_all, precision=HIGHEST_PRECISION)
        mod_width = d_mod_all.shape[1] // shards
        g_b_mod = jnp.sum(
            lax.dynamic_slice_in_dim(d_mod_all, seq_place * mod_width, mod_width, 1), axis=0
        )
        own_biases, offset = [], 0
        for size in (b_skip.shape[0], b_qkv.shape[0], b_out.shape[0], b_up.shape[0], b_down.shape[0]):
            width = size // shards
            own_biases.append(
                lax.dynamic_slice_in_dim(bias_sum, offset + seq_place * width, width, 0)
            )
            offset += size
    return (
        mixed[None],
        g_frames[None],
        g_skip_in[None],
        g_w_skip,
        own_biases[0],
        g_w_mod,
        g_b_mod,
        g_w_qkv,
        own_biases[1],
        g_w_out,
        own_biases[2],
        g_w_up,
        own_biases[3],
        g_w_down,
        own_biases[4],
    )


def solution(mesh):
    return jax.shard_map(
        local,
        mesh=mesh,
        in_specs=(
            P("utt", "seq", None),
            P("utt", "seq", None),
            P("utt", None),
            P("utt", None),
            P("utt", None),
            P("utt", "seq"),
            P("utt", "seq", None),
            P(),
            P(),
            P(),
            P(),
            P(),
            P(),
            P(),
            P(),
            P(),
            P(),
            P(),
            P(),
        ),
        out_specs=(
            P("utt", "seq", None),
            P("utt", "seq", None),
            P("utt", "seq", None),
            P("seq", None),
            P("seq"),
            P("seq", None),
            P("seq"),
            P("seq", None),
            P("seq"),
            P("seq", None),
            P("seq"),
            P("seq", None),
            P("seq"),
            P("seq", None),
            P("seq"),
        ),
        check_vma=False,
    )
```

```python
from functools import partial
import math

import jax
import jax.numpy as jnp
from jax import lax
from jax.experimental import pallas as pl
from jax.experimental.pallas import tpu as pltpu
from jax.sharding import PartitionSpec as P

HEADS = 16
HEAD_DIM = 64


HIGHEST_PRECISION = lax.Precision.HIGHEST
EPSILON = 1e-06


def layer_norm(values):
    average = jnp.mean(values, axis=-1, keepdims=True)
    centred = values - average
    spread = jnp.mean(centred * centred, axis=-1, keepdims=True)
    return centred * lax.rsqrt(spread + EPSILON)


def modulate(values, scale_part, shift_part):
    return layer_norm(values) * (1.0 + scale_part) + shift_part


def time_embed(flow_vals, model_width):
    half_dim = model_width // 2
    inverse = jnp.exp(-math.log(10000.0) * jnp.arange(half_dim, dtype=jnp.float32) / half_dim)
    angles = 1000.0 * flow_vals[:, None] * inverse[None, :]
    return jnp.concatenate([jnp.sin(angles), jnp.cos(angles)], axis=1)


def rotary_tables(position, head_size):
    half_dim = head_size // 2
    inverse = jnp.exp(
        -math.log(10000.0) * 2.0 * jnp.arange(half_dim, dtype=jnp.float32) / head_size
    )
    angles = position.astype(jnp.float32)[:, None] * inverse[None, :]
    return (jnp.cos(angles)[:, None, :], jnp.sin(angles)[:, None, :])


def rotate(tensor, angle_cos, angle_sin):
    half_dim = tensor.shape[-1] // 2
    leading = tensor[..., :half_dim]
    trailing = tensor[..., half_dim:]
    return jnp.concatenate(
        [leading * angle_cos - trailing * angle_sin, trailing * angle_cos + leading * angle_sin],
        axis=-1,
    )


def unrotate(gradient, angle_cos, angle_sin):
    half_dim = gradient.shape[-1] // 2
    leading = gradient[..., :half_dim]
    trailing = gradient[..., half_dim:]
    return jnp.concatenate(
        [leading * angle_cos + trailing * angle_sin, trailing * angle_cos - leading * angle_sin],
        axis=-1,
    )


def frame_tables(lengths, char_counts, first_frame, frame_count):
    utt_ends = jnp.cumsum(lengths)
    utt_starts = utt_ends - lengths
    frame_index = first_frame + jnp.arange(frame_count, dtype=jnp.int32)
    segment = jnp.sum((frame_index[:, None] >= utt_ends[None, :]).astype(jnp.int32), axis=1)
    member = segment[:, None] == jnp.arange(lengths.shape[0], dtype=jnp.int32)[None, :]
    position = frame_index - jnp.sum(jnp.where(member, utt_starts[None, :], 0), axis=1)
    prompt = jnp.sum(jnp.where(member, char_counts[None, :], 0), axis=1)
    return (segment, position, position >= prompt, member)


def key_segments(key_start, key_count, utt_ends):
    frame_index = key_start + jnp.arange(key_count, dtype=jnp.int32)
    return jnp.sum((frame_index[:, None] >= utt_ends[None, :]).astype(jnp.int32), axis=1)


def block_scores(queries, key_piece, query_segment, key_segment, usable):
    key_rows = key_piece.reshape(key_piece.shape[0], queries.shape[1], queries.shape[2])
    scores = (
        jnp.einsum("qhd,khd->hqk", queries, key_rows, preferred_element_type=jnp.float32) * 0.125
    )
    allowed = jnp.logical_and(query_segment[:, None] == key_segment[None, :], usable)
    return (jnp.where(allowed[None], jnp.exp(scores), 0.0), key_rows)


def over_blocks(block_fn, running, piece, key_start, shard_rows):
    key_count = piece.shape[1]
    shard_total = key_count // shard_rows
    group_size = max(1, min(shard_total, 1024 // shard_rows))
    while shard_total % group_size != 0:
        group_size = group_size - 1
    block_rows = group_size * shard_rows
    if block_rows == key_count:
        return block_fn(running, piece, key_start)

    def one_block(block_index, inner_state):
        portion = lax.dynamic_slice_in_dim(piece, block_index * block_rows, block_rows, 1)
        return block_fn(inner_state, portion, key_start + block_index * block_rows)

    return lax.fori_loop(0, key_count // block_rows, one_block, running)


def forward_piece(running, piece, key_start, usable, queries, query_segment, utt_ends):
    weighted, totals = running
    key_segment = key_segments(key_start, piece.shape[1], utt_ends)
    weights, key_rows = block_scores(queries, piece[0], query_segment, key_segment, usable)
    value_rows = piece[1].reshape(key_rows.shape)
    totals = totals + jnp.sum(weights, axis=2)
    weighted = weighted + jnp.einsum(
        "hqk,khd->qhd", weights.astype(jnp.bfloat16), value_rows, preferred_element_type=jnp.float32
    )
    return (weighted, totals)


def backward_piece(piece, key_start, usable, queries, query_segment, utt_ends, grad_acc, delta):
    key_count = piece.shape[1]
    key_segment = key_segments(key_start, key_count, utt_ends)
    weights, key_rows = block_scores(queries, piece[0], query_segment, key_segment, usable)
    value_rows = piece[1].reshape(key_rows.shape)
    value_dots = jnp.einsum(
        "qhd,khd->hqk", grad_acc, value_rows, preferred_element_type=jnp.float32
    )
    d_scores = (weights * (value_dots - delta[:, :, None])).astype(jnp.bfloat16)
    d_query = (
        jnp.einsum("hqk,khd->qhd", d_scores, key_rows, preferred_element_type=jnp.float32) * 0.125
    )
    d_key = (
        jnp.einsum("hqk,qhd->khd", d_scores, queries, preferred_element_type=jnp.float32) * 0.125
    )
    d_value = jnp.einsum(
        "hqk,qhd->khd", weights.astype(jnp.bfloat16), grad_acc, preferred_element_type=jnp.float32
    )
    return (
        d_query,
        jnp.stack([d_key.reshape(key_count, -1), d_value.reshape(key_count, -1)], axis=0),
    )


def back_product(gradient_rows, matrix):
    return jnp.einsum("fo,io->fi", gradient_rows, matrix, preferred_element_type=jnp.float32)


def xor_permute(value, axis_name, bit):
    size = lax.axis_size(axis_name)
    return lax.ppermute(value, axis_name, [(i, i ^ bit) for i in range(size)])


def bits_of(axis_name):
    size, bits, bit = lax.axis_size(axis_name), [], 1
    while bit < size:
        bits.append(bit)
        bit *= 2
    return bits


def xor_sum(value, axis_name):
    for bit in bits_of(axis_name):
        value = value + xor_permute(value, axis_name, bit)
    return value


def gather_left(rows):
    for bit in reversed(bits_of("utt")):
        rows = jnp.concatenate([rows, xor_permute(rows, "utt", bit)], axis=0)
    return rows


def gather_right(rows):
    place = lax.axis_index("utt")
    for bit in reversed(bits_of("utt")):
        mine = (place & bit) // bit
        width = rows.shape[1] // 2
        kept = lax.dynamic_slice_in_dim(rows, mine * width, width, 1)
        given = lax.dynamic_slice_in_dim(rows, (1 - mine) * width, width, 1)
        rows = jnp.concatenate([kept, xor_permute(given, "utt", bit)], axis=0)
    return rows


def gather_ordered(value, axis):
    place = lax.axis_index("utt")
    for bit in bits_of("utt"):
        other = xor_permute(value, "utt", bit)
        low = (place & bit) == 0
        value = jnp.concatenate(
            [jnp.where(low, value, other), jnp.where(low, other, value)], axis=axis
        )
    return value


def scatter_rows(tile):
    place = lax.axis_index("seq")
    for bit in bits_of("seq"):
        mine = (place & bit) // bit
        rest = lax.axis_size("seq") // (2 * bit)
        pieces = tile.reshape(rest, 2, -1, tile.shape[-1])
        kept = lax.dynamic_index_in_dim(pieces, mine, 1, keepdims=False)
        given = lax.dynamic_index_in_dim(pieces, 1 - mine, 1, keepdims=False)
        given = xor_permute(given, "seq", bit)
        tile = (kept.astype(jnp.float32) + given.astype(jnp.float32)).astype(jnp.bfloat16)
    return tile.reshape(-1, tile.shape[-1])


def weight_grad(left_all, right_rows):
    right_all = gather_right(right_rows)
    tile = jnp.einsum(
        "fi,fo->io", left_all, right_all, preferred_element_type=jnp.float32
    ).astype(jnp.bfloat16)
    tile = tile.reshape(-1, tile.shape[-1])
    piece = scatter_rows(tile)
    return gather_ordered(piece, 1).astype(jnp.float32)


def swap_halves(values, lower):
    return jnp.where(lower, pltpu.roll(values, 96, 1), pltpu.roll(values, 32, 1))


def lower_half(shape):
    return lax.broadcasted_iota(jnp.int32, shape, 1) % HEAD_DIM < HEAD_DIM // 2


def head_scores(q, k, seg_q, seg_k):
    scores = lax.dot_general(q, k, (((1,), (1,)), ((), ())), preferred_element_type=jnp.float32)
    return jnp.where(seg_q == seg_k, jnp.exp(scores * 0.125), 0.0)


MESH = pl.DeviceIdType.MESH
VMEM_LIMIT = 62 * 1024 * 1024


def flip(index, bit):
    return index + bit - 2 * bit * ((index // bit) % 2)


def everywhere(memory):
    return pl.BlockSpec(memory_space=memory)


class Links:
    def __init__(self, send_sems, recv_sems, local_sems):
        self.send_sems, self.recv_sems, self.local_sems = send_sems, recv_sems, local_sems
        self.sent, self.held = [], 0
        self.utt, self.seq = lax.axis_index("utt"), lax.axis_index("seq")

    def enter(self, utt_peers, seq_peers):
        barrier = pltpu.get_barrier_semaphore()
        targets = [self.mate(r) for r in utt_peers] + [self.peer(r) for r in seq_peers]
        for target in targets:
            pl.semaphore_signal(barrier, inc=1, device_id=target, device_id_type=MESH)
        pl.semaphore_wait(barrier, len(targets))

    def mate(self, offset):
        return (self.utt_of(offset), self.seq)

    def utt_of(self, offset):
        place = self.utt
        for bit in (1, 2):
            if offset & bit:
                place = flip(place, bit)
        return place

    def seq_of(self, offset):
        place = self.seq
        for bit in (1, 2, 4):
            if offset & bit:
                place = flip(place, bit)
        return place

    def peer(self, offset):
        return (self.utt, self.seq_of(offset))

    def send(self, source, target, device):
        index = len(self.sent)
        copy = pltpu.make_async_remote_copy(
            src_ref=source,
            dst_ref=target,
            send_sem=self.send_sems.at[index],
            recv_sem=self.recv_sems.at[index],
            device_id=device,
            device_id_type=MESH,
        )
        copy.start()
        self.sent.append(copy)
        return copy

    def keep(self, source, target):
        copy = pltpu.make_async_copy(source, target, self.local_sems.at[self.held])
        self.held += 1
        copy.start()
        return copy

    def leave(self):
        assert len(self.sent) <= self.send_sems.shape[0]
        assert self.held <= self.local_sems.shape[0]
        for copy in self.sent:
            copy.wait_send()


class Gathered:
    def __init__(self, links, source, target, columns=None):
        self.links, self.target = links, target
        self.rows = source.shape[0]
        self.columns = columns
        self.own = links.keep(source, self.slot(0))
        self.across = links.send(source, self.slot(2), links.mate(2))
        self.beside = links.send(source, self.slot(1), links.mate(1))

    def slot(self, offset):
        rows = pl.ds(offset * self.rows, self.rows)
        if self.columns is None:
            return self.target.at[rows, :]
        return self.target.at[rows, self.columns]

    def relay(self):
        self.across.wait_recv()
        self.relayed = self.links.send(self.slot(2), self.slot(3), self.links.mate(1))

    def wait(self):
        self.own.wait()
        self.beside.wait_recv()
        self.relayed.wait_recv()


class Quarter:
    def __init__(self, links, piece_of, target, columns=None):
        rows = target.shape[0] // 4
        columns = pl.ds(0, target.shape[1]) if columns is None else columns
        slot = lambda r: target.at[pl.ds(r * rows, rows), columns]
        self.own = links.keep(piece_of(links.utt), slot(0))
        self.copies = [
            links.send(piece_of(links.utt_of(r)), slot(r), links.mate(r)) for r in (2, 3, 1)
        ]

    def wait(self):
        self.own.wait()
        for copy in self.copies:
            copy.wait_recv()


class Share:
    def __init__(self, links, y_first, left, right, columns, tile, got_a, got_b, got_z2, result):
        self.links, self.y_first = links, y_first
        self.left, self.right, self.columns = left, right, columns
        self.tile, self.got_a, self.got_b, self.got_z2 = tile, got_a, got_b, got_z2
        self.result = result
        seq = links.seq
        self.y, self.zl, self.zh = seq % 2, (seq // 2) % 2, seq // 4
        if y_first:
            self.a, self.b, self.peers = self.y, self.zl, (1, 2)
        else:
            self.a, self.b, self.peers = self.zl, self.y, (2, 1)

    def place(self, zh, a, b):
        return (zh, b, a) if self.y_first else (zh, a, b)

    def product(self, zh, a):
        rows = self.tile.shape[3]

        def block(b, _):
            here = self.place(zh, a, b)
            base = pl.multiple_of((4 * zh + 2 * here[1] + here[2]) * rows, rows)
            self.tile[here] = lax.dot_general(
                self.left[:, pl.ds(base, rows)],
                self.right[:, self.columns],
                (((0,), (0,)), ((), ())),
                preferred_element_type=jnp.float32,
            ).astype(jnp.bfloat16)
            return 0

        lax.fori_loop(0, 2, block, 0)

    def give(self, zh):
        self.product(zh, 1 - self.a)
        given = self.tile.at[zh, :, 1 - self.a] if self.y_first else self.tile.at[zh, 1 - self.a]
        self.sent_a.append(
            self.links.send(given, self.got_a.at[zh], self.links.peer(self.peers[0]))
        )

    def start_far(self):
        self.sent_a, self.sent_b = [], []
        self.give(1 - self.zh)
        self.product(1 - self.zh, self.a)

    def start_near(self):
        self.give(self.zh)
        self.product(self.zh, self.a)

    def start(self):
        self.sent_a, self.sent_b = [], []
        self.give(1 - self.zh)
        self.give(self.zh)
        self.product(1 - self.zh, self.a)
        self.product(self.zh, self.a)

    def add(self, index, got):
        tile = self.tile
        tile[index] = (tile[index].astype(jnp.float32) + got.astype(jnp.float32)).astype(
            jnp.bfloat16
        )

    def after_a(self):
        halves = (1 - self.zh, self.zh)
        for sent, zh in zip(self.sent_a, halves):
            sent.wait_recv()
            here = self.place(zh, self.a, 1 - self.b)
            self.add(here, self.got_a[zh, 1 - self.b])
            self.sent_b.append(
                self.links.send(
                    self.tile.at[here], self.got_b.at[zh], self.links.peer(self.peers[1])
                )
            )
        for zh in halves:
            self.add(self.place(zh, self.a, self.b), self.got_a[zh, self.b])

    def after_b(self):
        self.sent_b[0].wait_recv()
        self.add((1 - self.zh, self.zl, self.y), self.got_b[1 - self.zh])
        self.sent_z2 = self.links.send(
            self.tile.at[1 - self.zh, self.zl, self.y], self.got_z2, self.links.peer(4)
        )
        self.sent_b[1].wait_recv()
        self.add((self.zh, self.zl, self.y), self.got_b[self.zh])

    def after_z2(self):
        self.sent_z2.wait_recv()
        links = self.links
        mine = self.result(links.utt)
        mine[...] = (
            self.tile[self.zh, self.zl, self.y].astype(jnp.float32)
            + self.got_z2[...].astype(jnp.float32)
        ).astype(jnp.bfloat16)
        self.across = links.send(mine, mine, links.mate(2))
        self.beside = links.send(mine, mine, links.mate(1))

    def relay(self):
        self.across.wait_recv()
        links = self.links
        theirs = self.result(links.utt_of(2))
        self.relayed = links.send(theirs, theirs, links.mate(1))

    def wait(self):
        self.beside.wait_recv()
        self.relayed.wait_recv()


def share_scratch(rows, columns):
    return [
        pltpu.VMEM((2, 2, 2, rows, columns), jnp.bfloat16),
        pltpu.VMEM((2, 2, rows, columns), jnp.bfloat16),
        pltpu.VMEM((2, rows, columns), jnp.bfloat16),
        pltpu.VMEM((rows, columns), jnp.bfloat16),
    ]


def semaphores(count):
    return [pltpu.SemaphoreType.DMA((count,))] * 2 + [pltpu.SemaphoreType.DMA((40,))]


def comm_params(collective_id):
    return pltpu.CompilerParams(
        collective_id=collective_id, has_side_effects=True, vmem_limit_bytes=VMEM_LIMIT
    )


class Frames:
    def __init__(self, utts, lengths_ref):
        self.starts, self.ends, end = [], [], 0
        for u in range(utts):
            self.starts.append(end)
            end = end + lengths_ref[0, u]
            self.ends.append(end)

    def segment(self, frame):
        return sum((frame >= end).astype(jnp.int32) for end in self.ends)

    def of(self, segment, values):
        total = jnp.zeros_like(segment)
        for u, value in enumerate(values):
            total = jnp.where(segment == u, value, total)
        return total


def frame_column(first, count):
    return first + lax.broadcasted_iota(jnp.int32, (count, 1), 0)


def per_frame(mod_ref, segment, utts, piece, model):
    columns = slice(piece * model, (piece + 1) * model)
    value = jnp.broadcast_to(mod_ref[0:1, columns], (segment.shape[0], model))
    for u in range(1, utts):
        value = jnp.where(segment == u, mod_ref[u : u + 1, columns], value)
    return value


FAR_FIRST = (6, 7, 4, 5, 2, 3, 1)


def attend_kernel(
    utts, lengths_ref, chars_ref, drop_ref, act_ref, cos_in, sin_in, frames_ref, skip_ref,
    out_grad_ref,
    b_skip_ref, b_mod_ref, b_qkv_ref, w_skip_ref, w_mod_ref, w_qkv_ref,
    attn_ref, heads_ref, exact_ref, total_ref, loss_ref, acts_ref, norm_all, joined_all,
    resid_ref, mod_ref, cos_ref, sin_ref, d_ff_ref, d_ff_all,
    attn_heads, counts_got, sums_ref, packed, norm_ref, w_skip, w_mod, w_qkv,
    send_sems, recv_sems, local_sems,
):
    links = Links(send_sems, recv_sems, local_sems)
    rows, model = frames_ref.shape
    total_rows = heads_ref.shape[0]
    early, late = pl.ds(0, 2 * model), pl.ds(2 * model, 4 * model)
    load_skip = links.keep(w_skip_ref, w_skip)
    load_early = links.keep(w_mod_ref.at[:, early], w_mod.at[:, early])
    load_qkv = links.keep(w_qkv_ref, w_qkv)
    load_late = links.keep(w_mod_ref.at[:, late], w_mod.at[:, late])
    links.enter((1, 2, 3), range(1, 8))
    gathers = [
        Gathered(links, frames_ref, joined_all, pl.ds(0, model)),
        Gathered(links, skip_ref, joined_all, pl.ds(model, model)),
    ]
    act_own = links.keep(act_ref, acts_ref.at[links.utt])
    act_copies = [
        links.send(act_ref, acts_ref.at[links.utt], links.mate(r)) for r in (1, 2, 3)
    ]
    tables = Frames(utts, lengths_ref)
    first_row = pl.multiple_of(links.seq * rows, rows)
    own_rows = pl.ds(first_row, rows)
    frame = frame_column(links.seq * rows, rows)
    segment = tables.segment(frame)
    position = frame - tables.of(segment, tables.starts)
    prompt = tables.of(segment, [chars_ref[0, u] for u in range(utts)])
    in_loss = jnp.where(position >= prompt, 1.0, 0.0)
    across = lax.broadcasted_iota(jnp.int32, (rows, rows), 1)
    down = lax.broadcasted_iota(jnp.int32, (rows, rows), 0)
    dropped = jnp.sum(
        jnp.where(across == down, drop_ref[...].astype(jnp.float32), 0.0), axis=1, keepdims=True
    )
    lane = lax.broadcasted_iota(jnp.int32, sums_ref.shape, 1)
    n_drop = jnp.sum(in_loss * dropped, axis=0, keepdims=True)
    n_keep = jnp.sum(in_loss * (1.0 - dropped), axis=0, keepdims=True)
    sums_ref[...] = jnp.where(lane == 0, n_drop, jnp.where(lane == 1, n_keep, 0.0))
    targets = [links.mate(1), links.mate(2), links.peer(1), links.peer(2), links.peer(4)]
    turn = []

    def count_turn():
        place = len(turn)
        if place > 0:
            turn[-1].wait_recv()
            sums_ref[...] = sums_ref[...] + counts_got[place - 1]
        if place < 5:
            counts_got[5 + place] = sums_ref[...]
            turn.append(
                links.send(counts_got.at[5 + place], counts_got.at[place], targets[place])
            )

    count_turn()
    quarter = total_rows // 4
    for j in range(4):
        here, lanes = slice(j * quarter, (j + 1) * quarter), slice(32 * j, 32 * (j + 1))
        cosines, sines = cos_in[:, lanes], sin_in[:, lanes]
        cos_ref[here, :] = jnp.concatenate([cosines] * 4, axis=1)
        sin_ref[here, :] = jnp.concatenate([-sines, sines] * 2, axis=1)
    load_skip.wait()
    residual = (
        jnp.dot(frames_ref[...], w_skip[0:model, :], preferred_element_type=jnp.float32)
        + jnp.dot(skip_ref[...], w_skip[model:, :], preferred_element_type=jnp.float32)
        + b_skip_ref[...]
    )
    resid_ref[...] = residual
    count_turn()

    def modulate_columns(columns):
        mod_ref[:, columns] = (
            jnp.dot(act_ref[...], w_mod[:, columns], preferred_element_type=jnp.float32)
            + b_mod_ref[:, columns]
        )

    load_early.wait()
    modulate_columns(slice(0, 2 * model))
    unit, _ = normal_parts(residual)
    norm_ref[...] = (
        unit * (1.0 + per_frame(mod_ref, segment, utts, 1, model))
        + per_frame(mod_ref, segment, utts, 0, model)
    ).astype(jnp.bfloat16)
    gathers.append(Gathered(links, norm_ref, norm_all))
    count_turn()
    load_qkv.wait()
    cos, sin = cos_ref[own_rows, :], sin_ref[own_rows, :]
    lower = lower_half((rows, 128))

    def project(place, base):
        columns = pl.ds(pl.multiple_of(base + place * 128, 128), 128)
        return (
            jnp.dot(norm_ref[...], w_qkv[:, columns], preferred_element_type=jnp.float32)
            + b_qkv_ref[:, columns]
        )

    def pack(place):
        q, k = project(place, 0), project(place, model)
        packed[place, :, 0:128] = (q * cos + swap_halves(q, lower) * sin).astype(jnp.bfloat16)
        packed[place, :, 128:256] = (k * cos + swap_halves(k, lower) * sin).astype(jnp.bfloat16)
        packed[place, :, 256:384] = project(place, 2 * model).astype(jnp.bfloat16)

    incoming = []
    for r in FAR_FIRST:
        place = links.seq_of(r)
        pack(place)
        incoming.append(
            links.send(packed.at[place], heads_ref.at[own_rows, :], links.peer(r))
        )
    pack(links.seq)
    own = links.keep(packed.at[links.seq], heads_ref.at[own_rows, :])
    count_turn()
    load_late.wait()
    modulate_columns(slice(2 * model, 6 * model))
    count_turn()
    gathers[0].relay()
    gathers[1].relay()
    count_turn()
    n_drop, n_keep = sums_ref[0:1, 0:1], sums_ref[0:1, 1:2]
    loss_weight = (
        in_loss
        * (n_drop + n_keep)
        * 0.5
        * (dropped / (n_drop + 1.0) + (1.0 - dropped) / (n_keep + 1.0))
    )
    loss_ref[...] = jnp.broadcast_to(loss_weight, loss_ref.shape)
    d_out = out_grad_ref[...].astype(jnp.float32) * loss_weight
    d_ff_ref[...] = (per_frame(mod_ref, segment, utts, 5, model) * d_out).astype(jnp.bfloat16)
    gathers.append(Gathered(links, d_ff_ref, d_ff_all))
    own.wait()
    for copy in incoming:
        copy.wait_recv()
    first = lax.broadcasted_iota(jnp.int32, (rows, 128), 1) < HEAD_DIM
    zero = jnp.zeros((rows, 128), jnp.bfloat16)
    k, v = heads_ref[:, 128:256], heads_ref[:, 256:384]
    seg_k = tables.segment(lax.broadcasted_iota(jnp.int32, (1, total_rows), 1))
    part = lambda place: pl.ds(pl.multiple_of(place * rows, rows), rows)
    column = attn_ref.at[:, pl.ds(pl.multiple_of(links.seq * 128, 128), 128)]

    def attend_rows(place):
        here = part(place)
        q, seg_q = heads_ref[here, 0:128], tables.segment(frame_column(place * rows, rows))
        results = []
        for mine in (first, jnp.logical_not(first)):
            weights = head_scores(jnp.where(mine, q, zero), k, seg_q, seg_k)
            total = jnp.sum(weights, axis=1, keepdims=True)
            summed = jnp.dot(weights.astype(jnp.bfloat16), v, preferred_element_type=jnp.float32)
            results.append((summed, total))
        total = jnp.where(first, results[0][1], results[1][1])
        attended = jnp.where(first, results[0][0], results[1][0]) / total
        attn_heads[here, :] = attended.astype(jnp.bfloat16)
        exact_ref[here, :] = attended
        total_ref[here, :] = total

    incoming = []
    for r in FAR_FIRST:
        place = links.seq_of(r)
        attend_rows(place)
        incoming.append(links.send(attn_heads.at[part(place), :], column, links.peer(r)))
    attend_rows(links.seq)
    own = links.keep(attn_heads.at[part(links.seq), :], column)
    gathers[2].relay()
    gathers[3].relay()
    act_own.wait()
    for copy in act_copies:
        copy.wait_recv()
    own.wait()
    for copy in incoming:
        copy.wait_recv()
    for gather in gathers:
        gather.wait()
    links.leave()


def attend(
    lengths, chars, drop, act, cos, sin, frames, skip, out_grad, b_skip, b_mod, b_qkv, w_skip,
    w_mod, w_qkv, shards,
):
    rows, width = frames.shape
    total_rows = shards * rows
    utts = lengths.shape[1]
    vmem, there, scalar = everywhere(pltpu.VMEM), everywhere(pl.ANY), everywhere(pltpu.SMEM)
    shape = jax.ShapeDtypeStruct
    bf16 = lambda *dims: pltpu.VMEM(dims, jnp.bfloat16)
    return pl.pallas_call(
        partial(attend_kernel, utts),
        in_specs=[scalar] * 2 + [vmem] * 10 + [there] * 3,
        out_specs=[vmem] * 5 + [there] * 3 + [vmem] * 5 + [there],
        out_shape=[
            shape((rows, width), jnp.bfloat16),
            shape((total_rows, 384), jnp.bfloat16),
            shape((total_rows, 128), jnp.float32),
            shape((total_rows, 128), jnp.float32),
            shape((rows, 128), jnp.float32),
            shape((4,) + act.shape, act.dtype),
            shape((4 * rows, width), jnp.bfloat16),
            shape((4 * rows, 2 * width), jnp.bfloat16),
            shape((rows, width), jnp.float32),
            shape((8, 6 * width), jnp.float32),
            shape((total_rows, 128), jnp.float32),
            shape((total_rows, 128), jnp.float32),
            shape((rows, width), jnp.bfloat16),
            shape((4 * rows, width), jnp.bfloat16),
        ],
        scratch_shapes=[
            bf16(total_rows, 128),
            pltpu.VMEM((10, 8, 128), jnp.float32),
            pltpu.VMEM((8, 128), jnp.float32),
            bf16(shards, rows, 384),
            bf16(rows, width),
            bf16(*w_skip.shape),
            bf16(*w_mod.shape),
            bf16(*w_qkv.shape),
        ]
        + semaphores(40),
        compiler_params=comm_params(1),
    )(
        lengths, chars, drop, act, cos, sin, frames, skip, out_grad,
        b_skip[None, :], b_mod[None, :], b_qkv[None, :], w_skip, w_mod, w_qkv,
    )


ALONG = (((1,), (1,)), ((), ()))
DOWN = (((0,), (0,)), ((), ()))


def normal_parts(values):
    centred = values - jnp.mean(values, axis=1, keepdims=True)
    scale = lax.rsqrt(jnp.mean(centred * centred, axis=1, keepdims=True) + EPSILON)
    return centred * scale, scale


def normal_back(inward, unit, scale):
    return scale * (
        inward
        - jnp.mean(inward, axis=1, keepdims=True)
        - unit * jnp.mean(inward * unit, axis=1, keepdims=True)
    )


def column_sum(values):
    return jnp.sum(values.astype(jnp.float32), axis=0, keepdims=True)


def backward_kernel(
    utts, lengths_ref, attn_ref, resid_ref, mod_ref, loss_ref, out_grad_ref, d_ff,
    b_out_ref, b_up_ref, b_down_ref,
    heads_in, exact_in, total_in, cos_in, sin_in,
    norm_a_ref, joined_ref, d_ff_ref, w_out_ref, w_up_ref, w_down_ref, w_qkv_ref, w_skip_ref,
    mixed_out, down_out, up_out, out_out, qkv_out, skip_out, smalls_out, frames_out, skip_in_out,
    mixed, g_down, g_up, g_out, g_qkv, g_skip, smalls, g_frames, g_skip_in,
    norm_f, act, d_inner, d_branch, d_attn, pieces, d_mid, ff_sum, d_norm,
    grad_heads, d_heads, dk_ref, dv_ref,
    d_ff_all, act_all, norm_all, d_inner_all, attn_all, d_branch_all,
    norm_a_all, joined_all, d_qkv, d_qkv_all, d_resid, d_resid_all,
    heads_ref, exact_ref, total_ref, cos_ref, sin_ref,
    up_ring, down_ring, w_out, w_qkv, w_skip, small_own, small_got, small_out,
    *rest,
):
    tiles, (send_sems, recv_sems, local_sems, ring_sems) = rest[:-4], rest[-4:]
    links = Links(send_sems, recv_sems, local_sems)
    rows, model = resid_ref.shape
    block_width = up_ring.shape[2]
    steps = w_up_ref.shape[1] // block_width

    zh = links.seq // 4

    def chunk(c):
        return (c + (1 - zh) * (steps // 2)) % steps

    def ring(c):
        slot = c % 2
        columns = pl.ds(pl.multiple_of(chunk(c) * block_width, block_width), block_width)
        return (
            pltpu.make_async_copy(w_up_ref.at[:, columns], up_ring.at[slot], ring_sems.at[slot]),
            pltpu.make_async_copy(
                w_down_ref.at[columns, :], down_ring.at[slot], ring_sems.at[2 + slot]
            ),
        )

    load_out = links.keep(w_out_ref, w_out)
    load_d = links.keep(d_ff_ref, d_ff_all)
    for c in (0, 1):
        for copy in ring(c):
            copy.start()
    head_loads = [
        links.keep(source, target)
        for source, target in (
            (heads_in, heads_ref), (exact_in, exact_ref), (total_in, total_ref),
            (cos_in, cos_ref), (sin_in, sin_ref),
        )
    ]
    loads = [
        links.keep(w_qkv_ref, w_qkv),
        links.keep(w_skip_ref, w_skip),
        links.keep(norm_a_ref, norm_a_all),
        links.keep(joined_ref, joined_all),
    ]
    links.enter((1, 2, 3), range(1, 8))

    tables = Frames(utts, lengths_ref)
    segment = tables.segment(frame_column(links.seq * rows, rows))

    def modulation(piece):
        return per_frame(mod_ref, segment, utts, piece, model)

    def d_out():
        return out_grad_ref[...].astype(jnp.float32) * loss_ref[:, 0:1]

    load_out.wait()
    branch = (
        jnp.dot(attn_ref[...], w_out[...], preferred_element_type=jnp.float32) + b_out_ref[...]
    )
    pieces[0] = branch
    mid = resid_ref[...] + modulation(2) * branch
    d_mid[...] = mid
    unit, _ = normal_parts(mid)
    norm_f[...] = (unit * (1.0 + modulation(4)) + modulation(3)).astype(jnp.bfloat16)
    ff_sum[...] = jnp.zeros_like(ff_sum)
    d_norm[...] = jnp.zeros_like(d_norm)
    const = math.sqrt(2.0 / math.pi)
    width = d_inner_all.shape[1]

    def feed(c, _):
        slot = c % 2
        columns = pl.ds(pl.multiple_of(chunk(c) * block_width, block_width), block_width)
        for copy in ring(c):
            copy.wait()
        inner = (
            jnp.dot(norm_f[...], up_ring[slot], preferred_element_type=jnp.float32)
            + b_up_ref[:, columns]
        )
        square = inner * inner
        slope = jnp.tanh(const * inner * (1.0 + 0.044715 * square))
        gate = 0.5 * (1.0 + slope)
        act_b = (inner * gate).astype(jnp.bfloat16)
        turn = gate + 0.5 * inner * (1.0 - slope * slope) * (
            const * (1.0 + 3.0 * 0.044715 * square)
        )
        here = pl.ds(pl.multiple_of(chunk(c) * 128, 128), 128)
        d_act = lax.dot_general(
            d_ff[...], down_ring[slot], ALONG, preferred_element_type=jnp.float32
        )
        d_inner_b = (turn * d_act).astype(jnp.bfloat16)
        for u in range(4):
            act[u, :, here] = act_b[:, u * 128 : (u + 1) * 128]
            d_inner[u, :, here] = d_inner_b[:, u * 128 : (u + 1) * 128]
        ff_sum[...] += jnp.dot(act_b, down_ring[slot], preferred_element_type=jnp.float32)
        d_norm[...] += lax.dot_general(
            d_inner_b, up_ring[slot], ALONG, preferred_element_type=jnp.float32
        )

        @pl.when(c + 2 < steps)
        def _():
            for copy in ring(c + 2):
                copy.start()

        return 0

    middle = width // 2
    half_at = lambda place: pl.ds(pl.multiple_of(place * middle, middle), middle)
    far_half, near_half = half_at(1 - zh), half_at(zh)
    lax.fori_loop(0, steps // 2, feed, 0)
    quarters_a = [Quarter(links, lambda u: act.at[u, :, far_half], act_all, far_half)]
    lax.fori_loop(steps // 2, steps, feed, 0)
    quarters_a.append(Quarter(links, lambda u: act.at[u, :, near_half], act_all, near_half))
    gather_n = Gathered(links, norm_f, norm_all)
    own_rows = pl.ds(pl.multiple_of(links.seq * rows, rows), rows)
    strip = lambda ref, place, size: ref.at[
        :, pl.ds(pl.multiple_of(place * size, size), size)
    ]
    narrow = d_branch_all.shape[1]
    quarter_i = Quarter(links, lambda u: d_inner.at[u], d_inner_all)
    mid = d_mid[...]
    unit, scale = normal_parts(mid)
    d_norm_f = d_norm[...]
    pieces[2] = d_norm_f * unit
    d_mid_f = d_out() + normal_back(d_norm_f * (1.0 + modulation(4)), unit, scale)
    gate_a = modulation(2)
    d_branch[...] = (gate_a * d_mid_f).astype(jnp.bfloat16)
    pieces[0] = pieces[0] * d_mid_f
    d_mid[...] = d_mid_f
    d_attn[...] = lax.dot_general(
        d_branch[...], w_out[...], ALONG, preferred_element_type=jnp.float32
    ).astype(jnp.bfloat16)
    own = links.keep(strip(d_attn, links.seq, 128), grad_heads.at[own_rows, :])
    incoming_d = [
        links.send(
            strip(d_attn, links.seq_of(r), 128), grad_heads.at[own_rows, :], links.peer(r)
        )
        for r in FAR_FIRST
    ]
    quarter_b = Quarter(links, lambda u: strip(d_branch, u, narrow), d_branch_all)
    gather_b = Gathered(links, attn_ref, attn_all)
    half = width // 2
    down_at = lambda h: lambda u: g_down.at[
        pl.ds(pl.multiple_of(u * 128, 128), 128), pl.ds(h * half, half)
    ]
    column_at = lambda ref, step, offset, size: lambda u: ref.at[
        :, pl.ds(pl.multiple_of(u * step + offset, 128), size)
    ]
    wide, thin = d_qkv_all.shape[1], d_resid_all.shape[1]
    third, slim = wide // 2, thin // 2
    plans = [
        (act_all, d_ff_all, pl.ds(0, half), down_at(0)),
        (act_all, d_ff_all, pl.ds(half, half), down_at(1)),
        (norm_all, d_inner_all, pl.ds(0, half), column_at(g_up, width, 0, half)),
        (norm_all, d_inner_all, pl.ds(half, half), column_at(g_up, width, half, half)),
        (attn_all, d_branch_all, pl.ds(0, narrow), column_at(g_out, narrow, 0, narrow)),
        (norm_a_all, d_qkv_all, pl.ds(0, third), column_at(g_qkv, wide, 0, third)),
        (norm_a_all, d_qkv_all, pl.ds(third, third), column_at(g_qkv, wide, third, third)),
        (joined_all, d_resid_all, pl.ds(0, slim), column_at(g_skip, thin, 0, slim)),
        (joined_all, d_resid_all, pl.ds(slim, slim), column_at(g_skip, thin, slim, slim)),
    ]
    y_first = (True, False, True, True, True, True, True, True, True)
    shares = [
        Share(links, y_first[i], left, right, columns, *tiles[4 * i : 4 * i + 4], result)
        for i, (left, right, columns, result) in enumerate(plans)
    ]
    load_d.wait()
    quarters_a[0].wait()
    shares[0].start_far()
    shares[1].start_far()
    ff_out = ff_sum[...] + b_down_ref[...]
    mixed[...] = (mid + modulation(5) * ff_out).astype(jnp.bfloat16)
    saved = [links.keep(mixed, mixed_out)]
    pieces[1] = d_out() * ff_out
    small_own[...] = jnp.zeros_like(small_own)
    small_own[4:5, :] = column_sum(d_branch[...])
    for c in range(4):
        small_own[5 + c : 6 + c, :] = column_sum(d_inner[c])
    small_own[9:10, :] = column_sum(d_ff[...])

    def utterance_sums(piece, values):
        for u in range(utts):
            row = 10 + utts * piece + u
            small_own[row : row + 1, :] = jnp.sum(
                jnp.where(segment == u, values, 0.0), axis=0, keepdims=True
            )

    utterance_sums(2, pieces[0])
    utterance_sums(3, d_norm[...])
    utterance_sums(4, pieces[2])
    utterance_sums(5, pieces[1])
    gather_n.relay()
    quarters_a[1].wait()
    shares[0].start_near()
    shares[1].start_near()
    own.wait()
    for copy in incoming_d:
        copy.wait_recv()
    for copy in head_loads:
        copy.wait()
    dk_ref[...] = jnp.zeros_like(dk_ref)
    dv_ref[...] = jnp.zeros_like(dv_ref)
    first = lax.broadcasted_iota(jnp.int32, (256, 128), 1) < HEAD_DIM
    zero = jnp.zeros((256, 128), jnp.bfloat16)
    lower = lower_half((256, 128))
    k, v = heads_ref[:, 128:256], heads_ref[:, 256:384]
    seg_k = tables.segment(lax.broadcasted_iota(jnp.int32, (1, heads_ref.shape[0]), 1))

    def turned(values, here):
        return (
            values * cos_ref[here, :] - swap_halves(values, lower) * sin_ref[here, :]
        ).astype(jnp.bfloat16)

    def block(step, _):
        here = pl.ds(pl.multiple_of(step * 256, 256), 256)
        q, seg_q = heads_ref[here, 0:128], tables.segment(frame_column(step * 256, 256))
        scaled = grad_heads[here, :].astype(jnp.float32) / total_ref[here, :]
        grad_acc = scaled.astype(jnp.bfloat16)
        product = scaled * exact_ref[here, :]
        d_query = []
        for mine in (first, jnp.logical_not(first)):
            q_own = jnp.where(mine, q, zero)
            g_own = jnp.where(mine, grad_acc, zero)
            delta = jnp.sum(jnp.where(mine, product, 0.0), axis=1, keepdims=True)
            weights = head_scores(q_own, k, seg_q, seg_k)
            dots = lax.dot_general(g_own, v, ALONG, preferred_element_type=jnp.float32)
            d_scores = (weights * (dots - delta)).astype(jnp.bfloat16)
            d_query.append(jnp.dot(d_scores, k, preferred_element_type=jnp.float32))
            dk_ref[...] += lax.dot_general(
                d_scores, q_own, DOWN, preferred_element_type=jnp.float32
            )
            dv_ref[...] += lax.dot_general(
                weights.astype(jnp.bfloat16), g_own, DOWN, preferred_element_type=jnp.float32
            )
        d_heads[here, 0:128] = turned(jnp.where(first, d_query[0], d_query[1]) * 0.125, here)
        return 0

    blocks = heads_ref.shape[0] // 256
    lax.fori_loop(0, blocks, block, 0)

    def finish(step, _):
        here = pl.ds(pl.multiple_of(step * 256, 256), 256)
        d_heads[here, 128:256] = turned(dk_ref[here, :] * 0.125, here)
        d_heads[here, 256:384] = dv_ref[here, :].astype(jnp.bfloat16)
        return 0

    lax.fori_loop(0, blocks, finish, 0)
    part = lambda place, c: d_heads.at[
        pl.ds(pl.multiple_of(place * rows, rows), rows), pl.ds(c * 128, 128)
    ]
    home = lambda c: d_qkv.at[
        :, pl.ds(pl.multiple_of(c * model + links.seq * 128, 128), 128)
    ]
    owns = [links.keep(part(links.seq, c), home(c)) for c in range(3)]
    incoming = [
        links.send(part(links.seq_of(r), c), home(c), links.peer(r))
        for r in FAR_FIRST
        for c in range(3)
    ]
    gather_n.wait()
    quarter_i.wait()
    state = {}

    def output_share():
        gather_b.relay()
        gather_b.wait()
        quarter_b.wait()
        shares[4].start()

    def projections():
        for copy in owns:
            copy.wait()
        for copy in incoming:
            copy.wait_recv()
        for copy in loads:
            copy.wait()
        state["qkv"] = Quarter(links, lambda u: strip(d_qkv, u, wide), d_qkv_all)
        d_norm_a = lax.dot_general(
            d_qkv[...], w_qkv[...], ALONG, preferred_element_type=jnp.float32
        )
        unit, scale = normal_parts(resid_ref[...])
        d_resid_f = d_mid[...] + normal_back(d_norm_a * (1.0 + modulation(1)), unit, scale)
        rounded = d_resid_f.astype(jnp.bfloat16)
        d_resid[...] = rounded
        state["resid"] = Quarter(links, lambda u: strip(d_resid, u, thin), d_resid_all)
        small_own[0:1, :] = column_sum(rounded)
        for c in range(3):
            small_own[1 + c : 2 + c, :] = column_sum(d_qkv[:, c * model : (c + 1) * model])
        utterance_sums(0, d_norm_a)
        utterance_sums(1, d_norm_a * unit)
        small_out[0] = small_own[...].astype(jnp.bfloat16)
        state["small"] = links.send(small_out.at[0], small_got.at[0], links.peer(1))

    def qkv_shares():
        state["qkv"].wait()
        shares[5].start()
        shares[6].start()

    def skip_shares():
        state["resid"].wait()
        shares[7].start()
        shares[8].start()

    def inputs():
        for index, out in enumerate((g_frames, g_skip_in)):
            out[...] = lax.dot_general(
                d_resid[...],
                w_skip[pl.ds(index * model, model), :],
                ALONG,
                preferred_element_type=jnp.float32,
            ).astype(jnp.bfloat16)

    def small_y():
        state["small"].wait_recv()
        small_own[...] += small_got[0].astype(jnp.float32)
        small_out[1] = small_own[...].astype(jnp.bfloat16)
        state["small"] = links.send(small_out.at[1], small_got.at[1], links.peer(2))

    def small_z1():
        state["small"].wait_recv()
        small_own[...] += small_got[1].astype(jnp.float32)
        small_out[2] = small_own[...].astype(jnp.bfloat16)
        state["small"] = links.send(small_out.at[2], small_got.at[2], links.peer(4))

    def small_z2():
        state["small"].wait_recv()
        mine = smalls.at[links.utt]
        mine[...] = (small_own[...] + small_got[2].astype(jnp.float32)).astype(jnp.bfloat16)
        state["spread"] = [links.send(mine, mine, links.mate(r)) for r in (2, 3, 1)]

    def save(*pairs):
        return lambda: saved.extend(links.keep(source, target) for source, target in pairs)

    stages = ("start", "after_a", "after_b", "after_z2", "relay", "wait")
    s, a, b, z, r, w = ([getattr(share, stage) for share in shares] for stage in stages)
    for step in (
        s[2], a[0], a[1], s[3],
        output_share, projections,
        a[2], b[0], b[1],
        qkv_shares,
        z[0], b[2],
        small_y, inputs, save((g_frames, frames_out), (g_skip_in, skip_in_out)),
        z[1], z[2],
        skip_shares,
        a[3], r[0], r[1],
        small_z1,
        a[4], b[3], r[2], z[3], b[4],
        small_z2,
        w[0], w[1], save((g_down, down_out)), a[5], z[4], r[3], b[5], w[2], a[6], r[4], z[5], b[6], w[3], save((g_up, up_out)), a[7], r[5],
        z[6], b[7], w[4], save((g_out, out_out)), a[8], b[8], z[7], r[6], w[5], z[8], r[7], w[6], save((g_qkv, qkv_out)), r[8], w[7], w[8], save((g_skip, skip_out)),
    ):
        step()
    for copy in state["spread"]:
        copy.wait_recv()
    save((smalls, smalls_out))()
    for copy in saved:
        copy.wait()
    links.leave()


def backward(
    lengths, attn_b, resid, mod, loss, out_grad, d_ff, b_out, b_up, b_down,
    heads, exact, total, cos, sin,
    norm_a_all, joined_all, d_ff_all, w_out, w_up, w_down, w_qkv, w_skip,
):
    rows, model = resid.shape
    frames, inner = heads.shape[0], w_up.shape[1]
    utts = lengths.shape[1]
    small = (-(-(10 + 6 * utts) // 16) * 16, model)
    vmem, there = everywhere(pltpu.VMEM), everywhere(pl.ANY)
    shape = jax.ShapeDtypeStruct
    bf16 = lambda *dims: pltpu.VMEM(dims, jnp.bfloat16)
    f32 = lambda *dims: pltpu.VMEM(dims, jnp.float32)
    part, step = model // 8, inner // 8
    outs = [
        shape((rows, model), jnp.bfloat16),
        shape((inner // 8, model), jnp.bfloat16),
        shape((part, inner), jnp.bfloat16),
        shape((part, model), jnp.bfloat16),
        shape((part, 3 * model), jnp.bfloat16),
        shape((2 * part, model), jnp.bfloat16),
        shape((4,) + small, jnp.bfloat16),
        shape((rows, model), jnp.bfloat16),
        shape((rows, model), jnp.bfloat16),
    ]
    return pl.pallas_call(
        partial(backward_kernel, utts),
        in_specs=[everywhere(pltpu.SMEM)] + [vmem] * 9 + [there] * 13,
        out_specs=[there] * 9,
        out_shape=outs,
        scratch_shapes=[pltpu.VMEM(out.shape, out.dtype) for out in outs]
        + [
            bf16(rows, model),
            bf16(4, rows, inner // 4),
            bf16(4, rows, inner // 4),
            bf16(rows, model),
            bf16(rows, model),
            f32(3, rows, model),
            f32(rows, model),
            f32(rows, model),
            f32(rows, model),
            bf16(frames, 128),
            bf16(frames, 384),
            f32(frames, 128),
            f32(frames, 128),
            bf16(4 * rows, model),
            bf16(4 * rows, inner // 4),
            bf16(4 * rows, model),
            bf16(4 * rows, inner // 4),
            bf16(4 * rows, model),
            bf16(4 * rows, model // 4),
            bf16(4 * rows, model),
            bf16(4 * rows, 2 * model),
            bf16(rows, 3 * model),
            bf16(4 * rows, 3 * model // 4),
            bf16(rows, model),
            bf16(4 * rows, model // 4),
            bf16(frames, 384),
            f32(frames, 128),
            f32(frames, 128),
            f32(frames, 128),
            f32(frames, 128),
            bf16(2, model, step),
            bf16(2, step, model),
            bf16(*w_out.shape),
            bf16(*w_qkv.shape),
            bf16(*w_skip.shape),
            f32(*small),
            bf16(3, *small),
            bf16(3, *small),
        ]
        + share_scratch(part, inner // 8) * 4
        + share_scratch(part, model // 4)
        + share_scratch(part, 3 * model // 8) * 2
        + share_scratch(2 * part, model // 8) * 2
        + semaphores(160)
        + [pltpu.SemaphoreType.DMA((4,))],
        compiler_params=comm_params(2),
    )(
        lengths, attn_b, resid, mod, loss, out_grad, d_ff,
        b_out[None, :], b_up[None, :], b_down[None, :],
        heads, exact, total, cos, sin,
        norm_a_all, joined_all, d_ff_all, w_out, w_up, w_down, w_qkv, w_skip,
    )


UP = 3


def finish_kernel(utts, shards, *rest):
    kept_in, wide_in, smalls_in, act_in = rest[:3], rest[3:8], rest[8], rest[9]
    rest = rest[1:]
    kept_out, wide_out, mod_out, bias_out = rest[9:12], rest[12:17], rest[17], rest[18:24]
    kept, wide, staged = rest[24:27], rest[27:32], rest[32:37]
    smalls_got, act_got, bias_stage = rest[37], rest[38], rest[39:45]
    smalls_ref, act_rows, mod_stage, d_mod, totals, sems, load_sems = rest[45:]
    seq = lax.axis_index("seq")
    loads, copies = [], []
    for source, target in zip(
        (*wide_in, smalls_in, act_in, *kept_in), (*wide, smalls_got, act_got, *kept)
    ):
        copy = pltpu.make_async_copy(source, target, load_sems.at[len(loads)])
        copy.start()
        loads.append(copy)

    def put(source, target):
        copy = pltpu.make_async_copy(source, target, sems.at[len(copies)])
        copy.start()
        copies.append(copy)

    model = smalls_ref.shape[2]
    lanes = 128
    for place, (source, stage, target) in enumerate(zip(wide, staged, wide_out)):
        loads[place].wait()
        if place == UP:
            for u in range(4):
                for c in range(shards):
                    stage[:, (4 * c + u) * lanes : (4 * c + u + 1) * lanes] = source[
                        :, u * model + c * lanes : u * model + (c + 1) * lanes
                    ].astype(jnp.float32)
        else:
            stage[...] = source[...].astype(jnp.float32)
        put(stage, target)
    groups = smalls_ref.shape[0]
    loads[5].wait()
    smalls_ref[...] = smalls_got[...].astype(jnp.float32)
    loads[6].wait()
    act_rows[...] = jnp.zeros_like(act_rows)
    own = act_rows.shape[1]
    own_columns = pl.ds(pl.multiple_of(seq * own, own), own)
    for g in range(groups):
        act_rows[g * utts : (g + 1) * utts, :] = act_got[g, :, own_columns].astype(jnp.float32)[
            0:utts
        ]
    bias_sum = (
        smalls_ref[0, 0:10] + smalls_ref[1, 0:10] + smalls_ref[2, 0:10] + smalls_ref[3, 0:10]
    )
    for row in range(10):
        totals[row, 0:1] = bias_sum[row : row + 1]
    d_mod[...] = jnp.zeros_like(d_mod)
    for piece in range(6):
        first = 10 + utts * piece
        for g in range(groups):
            d_mod[piece, g * utts : (g + 1) * utts, :] = smalls_ref[g, first : first + utts, :]
        rows = d_mod[piece]
        totals[10 + piece, 0:1] = jnp.sum(rows, axis=0, keepdims=True)
        columns = slice(piece * model, (piece + 1) * model)
        mod_stage[:, columns] = lax.dot_general(
            act_rows[...],
            rows,
            DOWN,
            precision=HIGHEST_PRECISION,
            preferred_element_type=jnp.float32,
        )
    put(mod_stage, mod_out)
    for load, source, target in zip(loads[7:], kept, kept_out):
        load.wait()
        put(source, target)
    line = model // lanes
    first = 0
    for place, target in enumerate(bias_out):
        count = target.shape[0] // lanes
        for i in range(count):
            unit = i * line + seq if place == UP else seq * count + i
            column = pl.multiple_of((unit % line) * lanes, lanes)
            bias_stage[place][i * lanes : (i + 1) * lanes] = totals[
                first + unit // line, 0, pl.ds(column, lanes)
            ]
        first += count * shards // line
        put(bias_stage[place], target)
    for copy in copies:
        copy.wait()


def finish(shards, utts, acts, smalls, mixed, frames, skip, grads):
    there = everywhere(pl.ANY)
    shape = jax.ShapeDtypeStruct
    model = smalls.shape[2]
    own = model // shards
    depth = -(-acts.shape[0] * utts // 8) * 8
    mod_shape = (own, 6 * model)
    widths = [own, 3 * own, own, 4 * own, own, 6 * own]
    kept = (mixed, frames, skip)
    outs = pl.pallas_call(
        partial(finish_kernel, utts, shards),
        in_specs=[there] * 10,
        out_specs=[there] * 15,
        out_shape=[shape(v.shape, v.dtype) for v in kept]
        + [shape(g.shape, jnp.float32) for g in grads]
        + [shape(mod_shape, jnp.float32)]
        + [shape((w,), jnp.float32) for w in widths],
        scratch_shapes=[pltpu.VMEM(v.shape, v.dtype) for v in (*kept, *grads)]
        + [pltpu.VMEM(g.shape, jnp.float32) for g in grads]
        + [
            pltpu.VMEM(smalls.shape, smalls.dtype),
            pltpu.VMEM(acts.shape, acts.dtype),
        ]
        + [pltpu.VMEM((w,), jnp.float32) for w in widths]
        + [
            pltpu.VMEM(smalls.shape, jnp.float32),
            pltpu.VMEM((depth, own), jnp.float32),
            pltpu.VMEM(mod_shape, jnp.float32),
            pltpu.VMEM((6, depth, model), jnp.float32),
            pltpu.VMEM((16, 8, model), jnp.float32),
            pltpu.SemaphoreType.DMA((15,)),
            pltpu.SemaphoreType.DMA((10,)),
        ],
        compiler_params=pltpu.CompilerParams(vmem_limit_bytes=VMEM_LIMIT),
    )(*kept, *grads, smalls, acts)
    return outs[:9], outs[9:]


def compact_tables(lengths, total_rows):
    half_dim = HEAD_DIM // 2
    shape = (total_rows // 4, 128)
    lane = lax.broadcasted_iota(jnp.int32, shape, 1)
    frame = lax.broadcasted_iota(jnp.int32, shape, 0) + (lane // half_dim) * shape[0]
    start, end = jnp.zeros(shape, jnp.int32), jnp.int32(0)
    for u in range(lengths.shape[0]):
        end = end + lengths[u]
        start = jnp.where(frame >= end, end, start)
    inverse = jnp.exp(
        -math.log(10000.0) * 2.0 * (lane % half_dim).astype(jnp.float32) / HEAD_DIM
    )
    angles = (frame - start).astype(jnp.float32) * inverse
    return jnp.cos(angles), jnp.sin(angles)


def padded_time_act(flow_vals, model):
    half_dim = model // 2
    column = jnp.arange(model, dtype=jnp.int32)
    inverse = jnp.exp(-math.log(10000.0) * (column % half_dim).astype(jnp.float32) / half_dim)
    flow_vals = jnp.pad(flow_vals, (0, 8 - flow_vals.shape[0]))
    angles = 1000.0 * flow_vals[:, None] * inverse[None, :]
    wave = jnp.where((column < half_dim)[None, :], jnp.sin(angles), jnp.cos(angles))
    return jax.nn.silu(wave).astype(jnp.bfloat16)


def local(
    frames_in,
    skip_in,
    flow_times,
    frame_lengths,
    char_lengths,
    drop_mask,
    out_grad,
    w_skip,
    b_skip,
    w_mod,
    b_mod,
    w_qkv,
    b_qkv,
    w_out,
    b_out,
    w_up,
    b_up,
    w_down,
    b_down,
):
    local_rows = frames_in.shape[1]
    model_width = frames_in.shape[2]
    shards = lax.axis_size("seq")
    seq_place = lax.axis_index("seq")
    lengths = frame_lengths[0]
    whole = model_width * 4
    fused = (
        lax.axis_size("utt") == 4
        and shards == 8
        and HEADS * HEAD_DIM == 1024
        and model_width == 1024
        and w_up.shape[1] == whole
        and local_rows == 128
        and flow_times.shape[1] <= 8
    )
    if not fused:
        utt_ends = jnp.cumsum(lengths)
        segment, position, in_loss, member = frame_tables(
            lengths, char_lengths[0], seq_place * local_rows, local_rows
        )
        member_f = member.astype(jnp.float32)
        loss_mask = in_loss.astype(jnp.float32)
        dropped = drop_mask[0].astype(jnp.float32)
        counts = jnp.stack([jnp.sum(loss_mask * dropped), jnp.sum(loss_mask * (1.0 - dropped))])
        counts = jnp.pad(counts[None, :], ((0, 7), (0, 126)))
        counts = xor_sum(xor_sum(counts, "utt"), "seq")
        time_act = jax.nn.silu(time_embed(flow_times[0], model_width)).astype(jnp.bfloat16)
        mod_u = jnp.dot(time_act, w_mod, preferred_element_type=jnp.float32) + b_mod
        mod_f = jnp.dot(member_f, mod_u, precision=HIGHEST_PRECISION)
        shift_a, scale_a, gate_a, shift_f, scale_f, gate_f = jnp.split(mod_f, 6, axis=1)
        joined = jnp.concatenate([frames_in[0], skip_in[0]], axis=1)
        residual = jnp.dot(joined, w_skip, preferred_element_type=jnp.float32) + b_skip
        norm_a = modulate(residual, scale_a, shift_a).astype(jnp.bfloat16)
        qkv_full = jnp.dot(norm_a, w_qkv, preferred_element_type=jnp.float32) + b_qkv
    if fused:
        (
            attn_b, qkv_heads, exact, total, loss, acts, norm_all, joined_all,
            residual, mod_u, cos_all, sin_all, d_ff, d_ff_all,
        ) = attend(
            frame_lengths,
            char_lengths,
            drop_mask,
            padded_time_act(flow_times[0], model_width),
            *compact_tables(lengths, local_rows * shards),
            frames_in[0],
            skip_in[0],
            out_grad[0],
            b_skip,
            b_mod,
            b_qkv,
            w_skip,
            w_mod,
            w_qkv,
            shards,
        )
    else:
        angle_cos, angle_sin = rotary_tables(position, HEAD_DIM)
        queries = rotate(
            qkv_full[:, :model_width].reshape(local_rows, HEADS, HEAD_DIM), angle_cos, angle_sin
        ).astype(jnp.bfloat16)
        key_rot = rotate(
            qkv_full[:, model_width : 2 * model_width].reshape(local_rows, HEADS, HEAD_DIM),
            angle_cos,
            angle_sin,
        ).astype(jnp.bfloat16)
        key_value = jnp.stack(
            [
                key_rot.reshape(local_rows, model_width),
                qkv_full[:, 2 * model_width :].astype(jnp.bfloat16),
            ],
            axis=0,
        )
        start_state = (
            jnp.zeros((local_rows, HEADS, HEAD_DIM), jnp.float32),
            jnp.zeros((HEADS, local_rows), jnp.float32),
        )
        fwd_piece = partial(forward_piece, queries=queries, query_segment=segment, utt_ends=utt_ends)
        weighted, totals = over_blocks(
            partial(fwd_piece, usable=True),
            start_state,
            lax.all_gather(key_value, "seq", axis=1, tiled=True),
            jnp.int32(0),
            local_rows,
        )
        totals_rows = jnp.transpose(totals)
        attended = weighted / totals_rows[:, :, None]
        attn_b = attended.reshape(local_rows, model_width).astype(jnp.bfloat16)
    if fused:
        mixed, g_w_down, g_w_up, g_w_out, g_w_qkv, g_w_skip, smalls, g_frames, g_skip_in = backward(
            frame_lengths,
            attn_b,
            residual,
            mod_u,
            loss,
            out_grad[0],
            d_ff,
            b_out,
            b_up,
            b_down,
            qkv_heads,
            exact,
            total,
            cos_all,
            sin_all,
            norm_all,
            joined_all,
            d_ff_all,
            w_out,
            w_up,
            w_down,
            w_qkv,
            w_skip,
        )
        utts = flow_times.shape[1]
        wide, biases = finish(
            shards,
            utts,
            acts,
            smalls,
            mixed,
            g_frames,
            g_skip_in,
            (g_w_skip, g_w_qkv, g_w_out, g_w_up, g_w_down),
        )
        mixed, g_frames, g_skip_in, g_w_skip, g_w_qkv, g_w_out, g_w_up, g_w_down, g_w_mod = wide
        own_biases, g_b_mod = biases[:5], biases[5]
    else:
        n_drop, n_keep = counts[0, 0], counts[0, 1]
        loss_weight = (
            loss_mask
            * (n_drop + n_keep)
            * 0.5
            * (dropped / (n_drop + 1.0) + (1.0 - dropped) / (n_keep + 1.0))
        )
        branch = jnp.dot(attn_b, w_out, preferred_element_type=jnp.float32) + b_out
        mid_state = residual + gate_a * branch
        norm_f = modulate(mid_state, scale_f, shift_f).astype(jnp.bfloat16)
        ff_inner = jnp.dot(norm_f, w_up, preferred_element_type=jnp.float32) + b_up
        ff_act, gelu_pull = jax.vjp(partial(jax.nn.gelu, approximate=True), ff_inner)
        act_b = ff_act.astype(jnp.bfloat16)
        ff_out = jnp.dot(act_b, w_down, preferred_element_type=jnp.float32) + b_down
        out_state = mid_state + gate_f * ff_out
        d_out = out_grad[0].astype(jnp.float32) * loss_weight[:, None]
        d_ff = (gate_f * d_out).astype(jnp.bfloat16)
        d_gate_f = d_out * ff_out
        g_b_down = jnp.sum(d_ff.astype(jnp.float32), axis=0)
        (d_inner,) = gelu_pull(back_product(d_ff, w_down))
        d_inner_b = d_inner.astype(jnp.bfloat16)
        g_b_up = jnp.sum(d_inner_b.astype(jnp.float32), axis=0)
        d_norm_f = back_product(d_inner_b, w_up)
        _, norm_f_pull = jax.vjp(modulate, mid_state, scale_f, shift_f)
        d_mid_norm, d_scale_f, d_shift_f = norm_f_pull(d_norm_f)
        d_mid = d_out + d_mid_norm
        d_branch = (gate_a * d_mid).astype(jnp.bfloat16)
        d_gate_a = d_mid * branch
        g_b_out = jnp.sum(d_branch.astype(jnp.float32), axis=0)
        d_attn = back_product(d_branch, w_out)
        mixed = out_state.astype(jnp.bfloat16)
        g_w_down = weight_grad(gather_left(act_b), d_ff)
        g_w_up = weight_grad(gather_left(norm_f), d_inner_b)
        g_w_out = weight_grad(gather_left(attn_b), d_branch)
        d_attn = d_attn.reshape(local_rows, HEADS, HEAD_DIM)
        grad_acc = (d_attn / totals_rows[:, :, None]).astype(jnp.bfloat16)
        delta = jnp.transpose(jnp.sum(d_attn * attended, axis=2) / totals_rows)
        bwd_piece = partial(
            backward_piece,
            queries=queries,
            query_segment=segment,
            utt_ends=utt_ends,
            grad_acc=grad_acc,
            delta=delta,
        )
        zero_query = jnp.zeros((local_rows, HEADS, HEAD_DIM), jnp.float32)
        zero_all = jnp.zeros((2, local_rows * shards, model_width), jnp.float32)

        def block_fn(inner_state, portion, block_start):
            d_query_sum, d_all = inner_state
            d_query_add, d_block = bwd_piece(portion, block_start, True)
            return (
                d_query_sum + d_query_add,
                lax.dynamic_update_slice_in_dim(d_all, d_block, block_start, 1),
            )

        d_query, d_all = over_blocks(
            block_fn,
            (zero_query, zero_all),
            lax.all_gather(key_value, "seq", axis=1, tiled=True),
            jnp.int32(0),
            local_rows,
        )
        d_key_value = lax.psum_scatter(d_all, "seq", scatter_dimension=1, tiled=True)
        d_query_pre = unrotate(d_query, angle_cos, angle_sin).reshape(local_rows, model_width)
        d_key_pre = unrotate(
            d_key_value[0].reshape(local_rows, HEADS, HEAD_DIM), angle_cos, angle_sin
        ).reshape(local_rows, model_width)
        d_qkv = jnp.concatenate([d_query_pre, d_key_pre, d_key_value[1]], axis=1).astype(jnp.bfloat16)
        g_b_qkv = jnp.sum(d_qkv.astype(jnp.float32), axis=0)
        d_norm_a = back_product(d_qkv, w_qkv)
        _, norm_a_pull = jax.vjp(modulate, residual, scale_a, shift_a)
        d_resid_norm, d_scale_a, d_shift_a = norm_a_pull(d_norm_a)
        d_resid = (d_mid + d_resid_norm).astype(jnp.bfloat16)
        g_b_skip = jnp.sum(d_resid.astype(jnp.float32), axis=0)
        d_joined = back_product(d_resid, w_skip)
        d_mod_f = jnp.concatenate(
            [d_shift_a, d_scale_a, d_gate_a, d_shift_f, d_scale_f, d_gate_f], axis=1
        )
        d_mod_u = jnp.dot(jnp.transpose(member_f), d_mod_f, precision=HIGHEST_PRECISION)
        small = jnp.concatenate(
            [g_b_skip, g_b_qkv, g_b_out, g_b_up, g_b_down, d_mod_u.reshape(-1)]
        )
        biases = small.shape[0] - d_mod_u.size
        g_w_qkv = weight_grad(gather_left(norm_a), d_qkv)
        g_w_skip = weight_grad(gather_left(joined), d_resid)
        small = xor_sum(small.reshape(-1, 128), "seq").reshape(-1)
        bias_sum = xor_sum(small[:biases].reshape(-1, 128), "utt").reshape(-1)
        d_mod_all = gather_ordered(small[biases:].reshape(d_mod_u.shape), 0)
        act_all = gather_ordered(time_act, 0)
        g_frames = d_joined[:, :model_width].astype(jnp.bfloat16)
        g_skip_in = d_joined[:, model_width:].astype(jnp.bfloat16)
        act_all = act_all.astype(jnp.float32)
        own_width = model_width // shards
        act_own = lax.dynamic_slice_in_dim(act_all, seq_place * own_width, own_width, 1)
        g_w_mod = jnp.dot(jnp.transpose(act_own), d_mod_all, precision=HIGHEST_PRECISION)
        mod_width = d_mod_all.shape[1] // shards
        g_b_mod = jnp.sum(
            lax.dynamic_slice_in_dim(d_mod_all, seq_place * mod_width, mod_width, 1), axis=0
        )
        own_biases, offset = [], 0
        for size in (b_skip.shape[0], b_qkv.shape[0], b_out.shape[0], b_up.shape[0], b_down.shape[0]):
            width = size // shards
            own_biases.append(
                lax.dynamic_slice_in_dim(bias_sum, offset + seq_place * width, width, 0)
            )
            offset += size
    return (
        mixed[None],
        g_frames[None],
        g_skip_in[None],
        g_w_skip,
        own_biases[0],
        g_w_mod,
        g_b_mod,
        g_w_qkv,
        own_biases[1],
        g_w_out,
        own_biases[2],
        g_w_up,
        own_biases[3],
        g_w_down,
        own_biases[4],
    )


def solution(mesh):
    return jax.shard_map(
        local,
        mesh=mesh,
        in_specs=(
            P("utt", "seq", None),
            P("utt", "seq", None),
            P("utt", None),
            P("utt", None),
            P("utt", None),
            P("utt", "seq"),
            P("utt", "seq", None),
            P(),
            P(),
            P(),
            P(),
            P(),
            P(),
            P(),
            P(),
            P(),
            P(),
            P(),
            P(),
        ),
        out_specs=(
            P("utt", "seq", None),
            P("utt", "seq", None),
            P("utt", "seq", None),
            P("seq", None),
            P("seq"),
            P("seq", None),
            P("seq"),
            P("seq", None),
            P("seq"),
            P("seq", None),
            P("seq"),
            P("seq", None),
            P("seq"),
            P("seq", None),
            P("seq"),
        ),
        check_vma=False,
    )
```

```python
from functools import partial
import math

import jax
import jax.numpy as jnp
from jax import lax
from jax.experimental import pallas as pl
from jax.experimental.pallas import tpu as pltpu
from jax.sharding import PartitionSpec as P

HEADS = 16
HEAD_DIM = 64


HIGHEST_PRECISION = lax.Precision.HIGHEST
EPSILON = 1e-06


def layer_norm(values):
    average = jnp.mean(values, axis=-1, keepdims=True)
    centred = values - average
    spread = jnp.mean(centred * centred, axis=-1, keepdims=True)
    return centred * lax.rsqrt(spread + EPSILON)


def modulate(values, scale_part, shift_part):
    return layer_norm(values) * (1.0 + scale_part) + shift_part


def time_embed(flow_vals, model_width):
    half_dim = model_width // 2
    inverse = jnp.exp(-math.log(10000.0) * jnp.arange(half_dim, dtype=jnp.float32) / half_dim)
    angles = 1000.0 * flow_vals[:, None] * inverse[None, :]
    return jnp.concatenate([jnp.sin(angles), jnp.cos(angles)], axis=1)


def rotary_tables(position, head_size):
    half_dim = head_size // 2
    inverse = jnp.exp(
        -math.log(10000.0) * 2.0 * jnp.arange(half_dim, dtype=jnp.float32) / head_size
    )
    angles = position.astype(jnp.float32)[:, None] * inverse[None, :]
    return (jnp.cos(angles)[:, None, :], jnp.sin(angles)[:, None, :])


def rotate(tensor, angle_cos, angle_sin):
    half_dim = tensor.shape[-1] // 2
    leading = tensor[..., :half_dim]
    trailing = tensor[..., half_dim:]
    return jnp.concatenate(
        [leading * angle_cos - trailing * angle_sin, trailing * angle_cos + leading * angle_sin],
        axis=-1,
    )


def unrotate(gradient, angle_cos, angle_sin):
    half_dim = gradient.shape[-1] // 2
    leading = gradient[..., :half_dim]
    trailing = gradient[..., half_dim:]
    return jnp.concatenate(
        [leading * angle_cos + trailing * angle_sin, trailing * angle_cos - leading * angle_sin],
        axis=-1,
    )


def frame_tables(lengths, char_counts, first_frame, frame_count):
    utt_ends = jnp.cumsum(lengths)
    utt_starts = utt_ends - lengths
    frame_index = first_frame + jnp.arange(frame_count, dtype=jnp.int32)
    segment = jnp.sum((frame_index[:, None] >= utt_ends[None, :]).astype(jnp.int32), axis=1)
    member = segment[:, None] == jnp.arange(lengths.shape[0], dtype=jnp.int32)[None, :]
    position = frame_index - jnp.sum(jnp.where(member, utt_starts[None, :], 0), axis=1)
    prompt = jnp.sum(jnp.where(member, char_counts[None, :], 0), axis=1)
    return (segment, position, position >= prompt, member)


def key_segments(key_start, key_count, utt_ends):
    frame_index = key_start + jnp.arange(key_count, dtype=jnp.int32)
    return jnp.sum((frame_index[:, None] >= utt_ends[None, :]).astype(jnp.int32), axis=1)


def block_scores(queries, key_piece, query_segment, key_segment, usable):
    key_rows = key_piece.reshape(key_piece.shape[0], queries.shape[1], queries.shape[2])
    scores = (
        jnp.einsum("qhd,khd->hqk", queries, key_rows, preferred_element_type=jnp.float32) * 0.125
    )
    allowed = jnp.logical_and(query_segment[:, None] == key_segment[None, :], usable)
    return (jnp.where(allowed[None], jnp.exp(scores), 0.0), key_rows)


def over_blocks(block_fn, running, piece, key_start, shard_rows):
    key_count = piece.shape[1]
    shard_total = key_count // shard_rows
    group_size = max(1, min(shard_total, 1024 // shard_rows))
    while shard_total % group_size != 0:
        group_size = group_size - 1
    block_rows = group_size * shard_rows
    if block_rows == key_count:
        return block_fn(running, piece, key_start)

    def one_block(block_index, inner_state):
        portion = lax.dynamic_slice_in_dim(piece, block_index * block_rows, block_rows, 1)
        return block_fn(inner_state, portion, key_start + block_index * block_rows)

    return lax.fori_loop(0, key_count // block_rows, one_block, running)


def forward_piece(running, piece, key_start, usable, queries, query_segment, utt_ends):
    weighted, totals = running
    key_segment = key_segments(key_start, piece.shape[1], utt_ends)
    weights, key_rows = block_scores(queries, piece[0], query_segment, key_segment, usable)
    value_rows = piece[1].reshape(key_rows.shape)
    totals = totals + jnp.sum(weights, axis=2)
    weighted = weighted + jnp.einsum(
        "hqk,khd->qhd", weights.astype(jnp.bfloat16), value_rows, preferred_element_type=jnp.float32
    )
    return (weighted, totals)


def backward_piece(piece, key_start, usable, queries, query_segment, utt_ends, grad_acc, delta):
    key_count = piece.shape[1]
    key_segment = key_segments(key_start, key_count, utt_ends)
    weights, key_rows = block_scores(queries, piece[0], query_segment, key_segment, usable)
    value_rows = piece[1].reshape(key_rows.shape)
    value_dots = jnp.einsum(
        "qhd,khd->hqk", grad_acc, value_rows, preferred_element_type=jnp.float32
    )
    d_scores = (weights * (value_dots - delta[:, :, None])).astype(jnp.bfloat16)
    d_query = (
        jnp.einsum("hqk,khd->qhd", d_scores, key_rows, preferred_element_type=jnp.float32) * 0.125
    )
    d_key = (
        jnp.einsum("hqk,qhd->khd", d_scores, queries, preferred_element_type=jnp.float32) * 0.125
    )
    d_value = jnp.einsum(
        "hqk,qhd->khd", weights.astype(jnp.bfloat16), grad_acc, preferred_element_type=jnp.float32
    )
    return (
        d_query,
        jnp.stack([d_key.reshape(key_count, -1), d_value.reshape(key_count, -1)], axis=0),
    )


def back_product(gradient_rows, matrix):
    return jnp.einsum("fo,io->fi", gradient_rows, matrix, preferred_element_type=jnp.float32)


def xor_permute(value, axis_name, bit):
    size = lax.axis_size(axis_name)
    return lax.ppermute(value, axis_name, [(i, i ^ bit) for i in range(size)])


def bits_of(axis_name):
    size, bits, bit = lax.axis_size(axis_name), [], 1
    while bit < size:
        bits.append(bit)
        bit *= 2
    return bits


def xor_sum(value, axis_name):
    for bit in bits_of(axis_name):
        value = value + xor_permute(value, axis_name, bit)
    return value


def gather_left(rows):
    for bit in reversed(bits_of("utt")):
        rows = jnp.concatenate([rows, xor_permute(rows, "utt", bit)], axis=0)
    return rows


def gather_right(rows):
    place = lax.axis_index("utt")
    for bit in reversed(bits_of("utt")):
        mine = (place & bit) // bit
        width = rows.shape[1] // 2
        kept = lax.dynamic_slice_in_dim(rows, mine * width, width, 1)
        given = lax.dynamic_slice_in_dim(rows, (1 - mine) * width, width, 1)
        rows = jnp.concatenate([kept, xor_permute(given, "utt", bit)], axis=0)
    return rows


def gather_ordered(value, axis):
    place = lax.axis_index("utt")
    for bit in bits_of("utt"):
        other = xor_permute(value, "utt", bit)
        low = (place & bit) == 0
        value = jnp.concatenate(
            [jnp.where(low, value, other), jnp.where(low, other, value)], axis=axis
        )
    return value


def scatter_rows(tile):
    place = lax.axis_index("seq")
    for bit in bits_of("seq"):
        mine = (place & bit) // bit
        rest = lax.axis_size("seq") // (2 * bit)
        pieces = tile.reshape(rest, 2, -1, tile.shape[-1])
        kept = lax.dynamic_index_in_dim(pieces, mine, 1, keepdims=False)
        given = lax.dynamic_index_in_dim(pieces, 1 - mine, 1, keepdims=False)
        given = xor_permute(given, "seq", bit)
        tile = (kept.astype(jnp.float32) + given.astype(jnp.float32)).astype(jnp.bfloat16)
    return tile.reshape(-1, tile.shape[-1])


def weight_grad(left_all, right_rows):
    right_all = gather_right(right_rows)
    tile = jnp.einsum(
        "fi,fo->io", left_all, right_all, preferred_element_type=jnp.float32
    ).astype(jnp.bfloat16)
    tile = tile.reshape(-1, tile.shape[-1])
    piece = scatter_rows(tile)
    return gather_ordered(piece, 1).astype(jnp.float32)


def swap_halves(values, lower):
    return jnp.where(lower, pltpu.roll(values, 96, 1), pltpu.roll(values, 32, 1))


def lower_half(shape):
    return lax.broadcasted_iota(jnp.int32, shape, 1) % HEAD_DIM < HEAD_DIM // 2


def head_scores(q, k, seg_q, seg_k):
    scores = lax.dot_general(q, k, (((1,), (1,)), ((), ())), preferred_element_type=jnp.float32)
    return jnp.where(seg_q == seg_k, jnp.exp(scores * 0.125), 0.0)


MESH = pl.DeviceIdType.MESH
VMEM_LIMIT = 62 * 1024 * 1024


def flip(index, bit):
    return index + bit - 2 * bit * ((index // bit) % 2)


def everywhere(memory):
    return pl.BlockSpec(memory_space=memory)


class Links:
    def __init__(self, send_sems, recv_sems, local_sems):
        self.send_sems, self.recv_sems, self.local_sems = send_sems, recv_sems, local_sems
        self.sent, self.held = [], 0
        self.utt, self.seq = lax.axis_index("utt"), lax.axis_index("seq")

    def enter(self, utt_peers, seq_peers):
        barrier = pltpu.get_barrier_semaphore()
        targets = [self.mate(r) for r in utt_peers] + [self.peer(r) for r in seq_peers]
        for target in targets:
            pl.semaphore_signal(barrier, inc=1, device_id=target, device_id_type=MESH)
        pl.semaphore_wait(barrier, len(targets))

    def mate(self, offset):
        return (self.utt_of(offset), self.seq)

    def utt_of(self, offset):
        place = self.utt
        for bit in (1, 2):
            if offset & bit:
                place = flip(place, bit)
        return place

    def seq_of(self, offset):
        place = self.seq
        for bit in (1, 2, 4):
            if offset & bit:
                place = flip(place, bit)
        return place

    def peer(self, offset):
        return (self.utt, self.seq_of(offset))

    def send(self, source, target, device):
        index = len(self.sent)
        copy = pltpu.make_async_remote_copy(
            src_ref=source,
            dst_ref=target,
            send_sem=self.send_sems.at[index],
            recv_sem=self.recv_sems.at[index],
            device_id=device,
            device_id_type=MESH,
        )
        copy.start()
        self.sent.append(copy)
        return copy

    def keep(self, source, target):
        copy = pltpu.make_async_copy(source, target, self.local_sems.at[self.held])
        self.held += 1
        copy.start()
        return copy

    def leave(self):
        assert len(self.sent) <= self.send_sems.shape[0]
        assert self.held <= self.local_sems.shape[0]
        for copy in self.sent:
            copy.wait_send()


class Gathered:
    def __init__(self, links, source, target, columns=None):
        self.links, self.target = links, target
        self.rows = source.shape[0]
        self.columns = columns
        self.own = links.keep(source, self.slot(0))
        self.across = links.send(source, self.slot(2), links.mate(2))
        self.beside = links.send(source, self.slot(1), links.mate(1))

    def slot(self, offset):
        rows = pl.ds(offset * self.rows, self.rows)
        if self.columns is None:
            return self.target.at[rows, :]
        return self.target.at[rows, self.columns]

    def relay(self):
        self.across.wait_recv()
        self.relayed = self.links.send(self.slot(2), self.slot(3), self.links.mate(1))

    def wait(self):
        self.own.wait()
        self.beside.wait_recv()
        self.relayed.wait_recv()


class Quarter:
    def __init__(self, links, piece_of, target, columns=None):
        rows = target.shape[0] // 4
        columns = pl.ds(0, target.shape[1]) if columns is None else columns
        slot = lambda r: target.at[pl.ds(r * rows, rows), columns]
        self.own = links.keep(piece_of(links.utt), slot(0))
        self.copies = [
            links.send(piece_of(links.utt_of(r)), slot(r), links.mate(r)) for r in (2, 3, 1)
        ]

    def wait(self):
        self.own.wait()
        for copy in self.copies:
            copy.wait_recv()


class Share:
    def __init__(self, links, y_first, left, right, columns, tile, got_a, got_b, got_z2, result):
        self.links, self.y_first = links, y_first
        self.left, self.right, self.columns = left, right, columns
        self.tile, self.got_a, self.got_b, self.got_z2 = tile, got_a, got_b, got_z2
        self.result = result
        seq = links.seq
        self.y, self.zl, self.zh = seq % 2, (seq // 2) % 2, seq // 4
        if y_first:
            self.a, self.b, self.peers = self.y, self.zl, (1, 2)
        else:
            self.a, self.b, self.peers = self.zl, self.y, (2, 1)

    def place(self, zh, a, b):
        return (zh, b, a) if self.y_first else (zh, a, b)

    def product(self, zh, a):
        rows = self.tile.shape[3]

        def block(b, _):
            here = self.place(zh, a, b)
            base = pl.multiple_of((4 * zh + 2 * here[1] + here[2]) * rows, rows)
            self.tile[here] = lax.dot_general(
                self.left[:, pl.ds(base, rows)],
                self.right[:, self.columns],
                (((0,), (0,)), ((), ())),
                preferred_element_type=jnp.float32,
            ).astype(jnp.bfloat16)
            return 0

        lax.fori_loop(0, 2, block, 0)

    def give(self, zh):
        self.product(zh, 1 - self.a)
        given = self.tile.at[zh, :, 1 - self.a] if self.y_first else self.tile.at[zh, 1 - self.a]
        self.sent_a.append(
            self.links.send(given, self.got_a.at[zh], self.links.peer(self.peers[0]))
        )

    def start_far(self):
        self.sent_a, self.sent_b = [], []
        self.give(1 - self.zh)
        self.product(1 - self.zh, self.a)

    def start_near(self):
        self.give(self.zh)
        self.product(self.zh, self.a)

    def start(self):
        self.sent_a, self.sent_b = [], []
        self.give(1 - self.zh)
        self.give(self.zh)
        self.product(1 - self.zh, self.a)
        self.product(self.zh, self.a)

    def add(self, index, got):
        tile = self.tile
        tile[index] = (tile[index].astype(jnp.float32) + got.astype(jnp.float32)).astype(
            jnp.bfloat16
        )

    def after_a(self):
        halves = (1 - self.zh, self.zh)
        for sent, zh in zip(self.sent_a, halves):
            sent.wait_recv()
            here = self.place(zh, self.a, 1 - self.b)
            self.add(here, self.got_a[zh, 1 - self.b])
            self.sent_b.append(
                self.links.send(
                    self.tile.at[here], self.got_b.at[zh], self.links.peer(self.peers[1])
                )
            )
        for zh in halves:
            self.add(self.place(zh, self.a, self.b), self.got_a[zh, self.b])

    def after_b(self):
        self.sent_b[0].wait_recv()
        self.add((1 - self.zh, self.zl, self.y), self.got_b[1 - self.zh])
        self.sent_z2 = self.links.send(
            self.tile.at[1 - self.zh, self.zl, self.y], self.got_z2, self.links.peer(4)
        )
        self.sent_b[1].wait_recv()
        self.add((self.zh, self.zl, self.y), self.got_b[self.zh])

    def after_z2(self):
        self.sent_z2.wait_recv()
        links = self.links
        mine = self.result(links.utt)
        mine[...] = (
            self.tile[self.zh, self.zl, self.y].astype(jnp.float32)
            + self.got_z2[...].astype(jnp.float32)
        ).astype(jnp.bfloat16)
        self.across = links.send(mine, mine, links.mate(2))
        self.beside = links.send(mine, mine, links.mate(1))

    def relay(self):
        self.across.wait_recv()
        links = self.links
        theirs = self.result(links.utt_of(2))
        self.relayed = links.send(theirs, theirs, links.mate(1))

    def wait(self):
        self.beside.wait_recv()
        self.relayed.wait_recv()


def share_scratch(rows, columns):
    return [
        pltpu.VMEM((2, 2, 2, rows, columns), jnp.bfloat16),
        pltpu.VMEM((2, 2, rows, columns), jnp.bfloat16),
        pltpu.VMEM((2, rows, columns), jnp.bfloat16),
        pltpu.VMEM((rows, columns), jnp.bfloat16),
    ]


def semaphores(count):
    return [pltpu.SemaphoreType.DMA((count,))] * 2 + [pltpu.SemaphoreType.DMA((40,))]


def comm_params(collective_id):
    return pltpu.CompilerParams(
        collective_id=collective_id, has_side_effects=True, vmem_limit_bytes=VMEM_LIMIT
    )


class Frames:
    def __init__(self, utts, lengths_ref):
        self.starts, self.ends, end = [], [], 0
        for u in range(utts):
            self.starts.append(end)
            end = end + lengths_ref[0, u]
            self.ends.append(end)

    def segment(self, frame):
        return sum((frame >= end).astype(jnp.int32) for end in self.ends)

    def of(self, segment, values):
        total = jnp.zeros_like(segment)
        for u, value in enumerate(values):
            total = jnp.where(segment == u, value, total)
        return total


def frame_column(first, count):
    return first + lax.broadcasted_iota(jnp.int32, (count, 1), 0)


def per_frame(mod_ref, segment, utts, piece, model):
    columns = slice(piece * model, (piece + 1) * model)
    value = jnp.broadcast_to(mod_ref[0:1, columns], (segment.shape[0], model))
    for u in range(1, utts):
        value = jnp.where(segment == u, mod_ref[u : u + 1, columns], value)
    return value


FAR_FIRST = (6, 7, 4, 5, 2, 3, 1)


def attend_kernel(
    utts, lengths_ref, chars_ref, drop_ref, act_ref, cos_in, sin_in, frames_ref, skip_ref,
    out_grad_ref,
    b_skip_ref, b_mod_ref, b_qkv_ref, w_skip_ref, w_mod_ref, w_qkv_ref,
    attn_ref, heads_ref, exact_ref, total_ref, loss_ref, acts_ref, norm_all, joined_all,
    resid_ref, mod_ref, cos_ref, sin_ref, d_ff_ref, d_ff_all,
    attn_heads, counts_got, sums_ref, packed, norm_ref, w_skip, w_mod, w_qkv,
    send_sems, recv_sems, local_sems,
):
    links = Links(send_sems, recv_sems, local_sems)
    rows, model = frames_ref.shape
    total_rows = heads_ref.shape[0]
    early, late = pl.ds(0, 2 * model), pl.ds(2 * model, 4 * model)
    load_skip = links.keep(w_skip_ref, w_skip)
    load_early = links.keep(w_mod_ref.at[:, early], w_mod.at[:, early])
    load_qkv = links.keep(w_qkv_ref, w_qkv)
    load_late = links.keep(w_mod_ref.at[:, late], w_mod.at[:, late])
    links.enter((1, 2, 3), range(1, 8))
    gathers = [
        Gathered(links, frames_ref, joined_all, pl.ds(0, model)),
        Gathered(links, skip_ref, joined_all, pl.ds(model, model)),
    ]
    act_own = links.keep(act_ref, acts_ref.at[links.utt])
    act_copies = [
        links.send(act_ref, acts_ref.at[links.utt], links.mate(r)) for r in (1, 2, 3)
    ]
    tables = Frames(utts, lengths_ref)
    first_row = pl.multiple_of(links.seq * rows, rows)
    own_rows = pl.ds(first_row, rows)
    frame = frame_column(links.seq * rows, rows)
    segment = tables.segment(frame)
    position = frame - tables.of(segment, tables.starts)
    prompt = tables.of(segment, [chars_ref[0, u] for u in range(utts)])
    in_loss = jnp.where(position >= prompt, 1.0, 0.0)
    across = lax.broadcasted_iota(jnp.int32, (rows, rows), 1)
    down = lax.broadcasted_iota(jnp.int32, (rows, rows), 0)
    dropped = jnp.sum(
        jnp.where(across == down, drop_ref[...].astype(jnp.float32), 0.0), axis=1, keepdims=True
    )
    lane = lax.broadcasted_iota(jnp.int32, sums_ref.shape, 1)
    n_drop = jnp.sum(in_loss * dropped, axis=0, keepdims=True)
    n_keep = jnp.sum(in_loss * (1.0 - dropped), axis=0, keepdims=True)
    sums_ref[...] = jnp.where(lane == 0, n_drop, jnp.where(lane == 1, n_keep, 0.0))
    targets = [links.mate(1), links.mate(2), links.peer(1), links.peer(2), links.peer(4)]
    turn = []

    def count_turn():
        place = len(turn)
        if place > 0:
            turn[-1].wait_recv()
            sums_ref[...] = sums_ref[...] + counts_got[place - 1]
        if place < 5:
            counts_got[5 + place] = sums_ref[...]
            turn.append(
                links.send(counts_got.at[5 + place], counts_got.at[place], targets[place])
            )

    count_turn()
    quarter = total_rows // 4
    for j in range(4):
        here, lanes = slice(j * quarter, (j + 1) * quarter), slice(32 * j, 32 * (j + 1))
        cosines, sines = cos_in[:, lanes], sin_in[:, lanes]
        cos_ref[here, :] = jnp.concatenate([cosines] * 4, axis=1)
        sin_ref[here, :] = jnp.concatenate([-sines, sines] * 2, axis=1)
    load_skip.wait()
    residual = (
        jnp.dot(frames_ref[...], w_skip[0:model, :], preferred_element_type=jnp.float32)
        + jnp.dot(skip_ref[...], w_skip[model:, :], preferred_element_type=jnp.float32)
        + b_skip_ref[...]
    )
    resid_ref[...] = residual
    count_turn()

    def modulate_columns(columns):
        mod_ref[:, columns] = (
            jnp.dot(act_ref[...], w_mod[:, columns], preferred_element_type=jnp.float32)
            + b_mod_ref[:, columns]
        )

    load_early.wait()
    modulate_columns(slice(0, 2 * model))
    unit, _ = normal_parts(residual)
    norm_ref[...] = (
        unit * (1.0 + per_frame(mod_ref, segment, utts, 1, model))
        + per_frame(mod_ref, segment, utts, 0, model)
    ).astype(jnp.bfloat16)
    gathers.append(Gathered(links, norm_ref, norm_all))
    count_turn()
    load_qkv.wait()
    cos, sin = cos_ref[own_rows, :], sin_ref[own_rows, :]
    lower = lower_half((rows, 128))

    def project(place, base):
        columns = pl.ds(pl.multiple_of(base + place * 128, 128), 128)
        return (
            jnp.dot(norm_ref[...], w_qkv[:, columns], preferred_element_type=jnp.float32)
            + b_qkv_ref[:, columns]
        )

    def pack(place):
        q, k = project(place, 0), project(place, model)
        packed[place, :, 0:128] = (q * cos + swap_halves(q, lower) * sin).astype(jnp.bfloat16)
        packed[place, :, 128:256] = (k * cos + swap_halves(k, lower) * sin).astype(jnp.bfloat16)
        packed[place, :, 256:384] = project(place, 2 * model).astype(jnp.bfloat16)

    incoming = []
    for r in FAR_FIRST:
        place = links.seq_of(r)
        pack(place)
        incoming.append(
            links.send(packed.at[place], heads_ref.at[own_rows, :], links.peer(r))
        )
    pack(links.seq)
    own = links.keep(packed.at[links.seq], heads_ref.at[own_rows, :])
    count_turn()
    load_late.wait()
    modulate_columns(slice(2 * model, 6 * model))
    count_turn()
    gathers[0].relay()
    gathers[1].relay()
    count_turn()
    n_drop, n_keep = sums_ref[0:1, 0:1], sums_ref[0:1, 1:2]
    loss_weight = (
        in_loss
        * (n_drop + n_keep)
        * 0.5
        * (dropped / (n_drop + 1.0) + (1.0 - dropped) / (n_keep + 1.0))
    )
    loss_ref[...] = jnp.broadcast_to(loss_weight, loss_ref.shape)
    d_out = out_grad_ref[...].astype(jnp.float32) * loss_weight
    d_ff_ref[...] = (per_frame(mod_ref, segment, utts, 5, model) * d_out).astype(jnp.bfloat16)
    gathers.append(Gathered(links, d_ff_ref, d_ff_all))
    own.wait()
    for copy in incoming:
        copy.wait_recv()
    first = lax.broadcasted_iota(jnp.int32, (rows, 128), 1) < HEAD_DIM
    zero = jnp.zeros((rows, 128), jnp.bfloat16)
    k, v = heads_ref[:, 128:256], heads_ref[:, 256:384]
    seg_k = tables.segment(lax.broadcasted_iota(jnp.int32, (1, total_rows), 1))
    part = lambda place: pl.ds(pl.multiple_of(place * rows, rows), rows)
    column = attn_ref.at[:, pl.ds(pl.multiple_of(links.seq * 128, 128), 128)]

    def attend_rows(place):
        here = part(place)
        q, seg_q = heads_ref[here, 0:128], tables.segment(frame_column(place * rows, rows))
        results = []
        for mine in (first, jnp.logical_not(first)):
            weights = head_scores(jnp.where(mine, q, zero), k, seg_q, seg_k)
            total = jnp.sum(weights, axis=1, keepdims=True)
            summed = jnp.dot(weights.astype(jnp.bfloat16), v, preferred_element_type=jnp.float32)
            results.append((summed, total))
        total = jnp.where(first, results[0][1], results[1][1])
        attended = jnp.where(first, results[0][0], results[1][0]) / total
        attn_heads[here, :] = attended.astype(jnp.bfloat16)
        exact_ref[here, :] = attended
        total_ref[here, :] = total

    incoming = []
    for r in FAR_FIRST:
        place = links.seq_of(r)
        attend_rows(place)
        incoming.append(links.send(attn_heads.at[part(place), :], column, links.peer(r)))
    attend_rows(links.seq)
    own = links.keep(attn_heads.at[part(links.seq), :], column)
    gathers[2].relay()
    gathers[3].relay()
    act_own.wait()
    for copy in act_copies:
        copy.wait_recv()
    own.wait()
    for copy in incoming:
        copy.wait_recv()
    for gather in gathers:
        gather.wait()
    links.leave()


def attend(
    lengths, chars, drop, act, cos, sin, frames, skip, out_grad, b_skip, b_mod, b_qkv, w_skip,
    w_mod, w_qkv, shards,
):
    rows, width = frames.shape
    total_rows = shards * rows
    utts = lengths.shape[1]
    vmem, there, scalar = everywhere(pltpu.VMEM), everywhere(pl.ANY), everywhere(pltpu.SMEM)
    shape = jax.ShapeDtypeStruct
    bf16 = lambda *dims: pltpu.VMEM(dims, jnp.bfloat16)
    return pl.pallas_call(
        partial(attend_kernel, utts),
        in_specs=[scalar] * 2 + [vmem] * 10 + [there] * 3,
        out_specs=[vmem] * 5 + [there] * 3 + [vmem] * 5 + [there],
        out_shape=[
            shape((rows, width), jnp.bfloat16),
            shape((total_rows, 384), jnp.bfloat16),
            shape((total_rows, 128), jnp.float32),
            shape((total_rows, 128), jnp.float32),
            shape((rows, 128), jnp.float32),
            shape((4,) + act.shape, act.dtype),
            shape((4 * rows, width), jnp.bfloat16),
            shape((4 * rows, 2 * width), jnp.bfloat16),
            shape((rows, width), jnp.float32),
            shape((8, 6 * width), jnp.float32),
            shape((total_rows, 128), jnp.float32),
            shape((total_rows, 128), jnp.float32),
            shape((rows, width), jnp.bfloat16),
            shape((4 * rows, width), jnp.bfloat16),
        ],
        scratch_shapes=[
            bf16(total_rows, 128),
            pltpu.VMEM((10, 8, 128), jnp.float32),
            pltpu.VMEM((8, 128), jnp.float32),
            bf16(shards, rows, 384),
            bf16(rows, width),
            bf16(*w_skip.shape),
            bf16(*w_mod.shape),
            bf16(*w_qkv.shape),
        ]
        + semaphores(40),
        compiler_params=comm_params(1),
    )(
        lengths, chars, drop, act, cos, sin, frames, skip, out_grad,
        b_skip[None, :], b_mod[None, :], b_qkv[None, :], w_skip, w_mod, w_qkv,
    )


ALONG = (((1,), (1,)), ((), ()))
DOWN = (((0,), (0,)), ((), ()))


def normal_parts(values):
    centred = values - jnp.mean(values, axis=1, keepdims=True)
    scale = lax.rsqrt(jnp.mean(centred * centred, axis=1, keepdims=True) + EPSILON)
    return centred * scale, scale


def normal_back(inward, unit, scale):
    return scale * (
        inward
        - jnp.mean(inward, axis=1, keepdims=True)
        - unit * jnp.mean(inward * unit, axis=1, keepdims=True)
    )


def column_sum(values):
    return jnp.sum(values.astype(jnp.float32), axis=0, keepdims=True)


def backward_kernel(
    utts, lengths_ref, attn_ref, resid_ref, mod_ref, loss_ref, out_grad_ref, d_ff,
    b_out_ref, b_up_ref, b_down_ref,
    heads_in, exact_in, total_in, cos_in, sin_in,
    norm_a_ref, joined_ref, d_ff_ref, w_out_ref, w_up_ref, w_down_ref, w_qkv_ref, w_skip_ref,
    mixed_out, down_out, up_out, out_out, qkv_out, skip_out, smalls_out, frames_out, skip_in_out,
    mixed, g_down, g_up, g_out, g_qkv, g_skip, smalls, g_frames, g_skip_in,
    norm_f, act, d_inner, d_branch, d_attn, pieces, d_mid, ff_sum, d_norm,
    grad_heads, d_heads, dk_ref, dv_ref,
    d_ff_all, act_all, norm_all, d_inner_all, attn_all, d_branch_all,
    norm_a_all, joined_all, d_qkv, d_qkv_all, d_resid, d_resid_all,
    heads_ref, exact_ref, total_ref, cos_ref, sin_ref,
    up_ring, down_ring, w_out, w_qkv, w_skip, small_own, small_got, small_out,
    *rest,
):
    tiles, (send_sems, recv_sems, local_sems, ring_sems) = rest[:-4], rest[-4:]
    links = Links(send_sems, recv_sems, local_sems)
    rows, model = resid_ref.shape
    block_width = up_ring.shape[2]
    steps = w_up_ref.shape[1] // block_width

    zh = links.seq // 4

    def chunk(c):
        return (c + (1 - zh) * (steps // 2)) % steps

    def ring(c):
        slot = c % 2
        columns = pl.ds(pl.multiple_of(chunk(c) * block_width, block_width), block_width)
        return (
            pltpu.make_async_copy(w_up_ref.at[:, columns], up_ring.at[slot], ring_sems.at[slot]),
            pltpu.make_async_copy(
                w_down_ref.at[columns, :], down_ring.at[slot], ring_sems.at[2 + slot]
            ),
        )

    load_out = links.keep(w_out_ref, w_out)
    load_d = links.keep(d_ff_ref, d_ff_all)
    for c in (0, 1):
        for copy in ring(c):
            copy.start()
    head_loads = [
        links.keep(source, target)
        for source, target in (
            (heads_in, heads_ref), (exact_in, exact_ref), (total_in, total_ref),
            (cos_in, cos_ref), (sin_in, sin_ref),
        )
    ]
    loads = [
        links.keep(w_qkv_ref, w_qkv),
        links.keep(w_skip_ref, w_skip),
        links.keep(norm_a_ref, norm_a_all),
        links.keep(joined_ref, joined_all),
    ]
    links.enter((1, 2, 3), range(1, 8))

    tables = Frames(utts, lengths_ref)
    segment = tables.segment(frame_column(links.seq * rows, rows))

    def modulation(piece):
        return per_frame(mod_ref, segment, utts, piece, model)

    def d_out():
        return out_grad_ref[...].astype(jnp.float32) * loss_ref[:, 0:1]

    load_out.wait()
    branch = (
        jnp.dot(attn_ref[...], w_out[...], preferred_element_type=jnp.float32) + b_out_ref[...]
    )
    pieces[0] = branch
    mid = resid_ref[...] + modulation(2) * branch
    d_mid[...] = mid
    unit, _ = normal_parts(mid)
    norm_f[...] = (unit * (1.0 + modulation(4)) + modulation(3)).astype(jnp.bfloat16)
    ff_sum[...] = jnp.zeros_like(ff_sum)
    d_norm[...] = jnp.zeros_like(d_norm)
    const = math.sqrt(2.0 / math.pi)
    width = d_inner_all.shape[1]

    def feed(c, _):
        slot = c % 2
        columns = pl.ds(pl.multiple_of(chunk(c) * block_width, block_width), block_width)
        for copy in ring(c):
            copy.wait()
        inner = (
            jnp.dot(norm_f[...], up_ring[slot], preferred_element_type=jnp.float32)
            + b_up_ref[:, columns]
        )
        square = inner * inner
        slope = jnp.tanh(const * inner * (1.0 + 0.044715 * square))
        gate = 0.5 * (1.0 + slope)
        act_b = (inner * gate).astype(jnp.bfloat16)
        turn = gate + 0.5 * inner * (1.0 - slope * slope) * (
            const * (1.0 + 3.0 * 0.044715 * square)
        )
        here = pl.ds(pl.multiple_of(chunk(c) * 128, 128), 128)
        d_act = lax.dot_general(
            d_ff[...], down_ring[slot], ALONG, preferred_element_type=jnp.float32
        )
        d_inner_b = (turn * d_act).astype(jnp.bfloat16)
        for u in range(4):
            act[u, :, here] = act_b[:, u * 128 : (u + 1) * 128]
            d_inner[u, :, here] = d_inner_b[:, u * 128 : (u + 1) * 128]
        ff_sum[...] += jnp.dot(act_b, down_ring[slot], preferred_element_type=jnp.float32)
        d_norm[...] += lax.dot_general(
            d_inner_b, up_ring[slot], ALONG, preferred_element_type=jnp.float32
        )

        @pl.when(c + 2 < steps)
        def _():
            for copy in ring(c + 2):
                copy.start()

        return 0

    middle = width // 2
    half_at = lambda place: pl.ds(pl.multiple_of(place * middle, middle), middle)
    far_half, near_half = half_at(1 - zh), half_at(zh)
    lax.fori_loop(0, steps // 2, feed, 0)
    quarters_a = [Quarter(links, lambda u: act.at[u, :, far_half], act_all, far_half)]
    lax.fori_loop(steps // 2, steps, feed, 0)
    quarters_a.append(Quarter(links, lambda u: act.at[u, :, near_half], act_all, near_half))
    gather_n = Gathered(links, norm_f, norm_all)
    own_rows = pl.ds(pl.multiple_of(links.seq * rows, rows), rows)
    strip = lambda ref, place, size: ref.at[
        :, pl.ds(pl.multiple_of(place * size, size), size)
    ]
    narrow = d_branch_all.shape[1]
    quarter_i = Quarter(links, lambda u: d_inner.at[u], d_inner_all)
    mid = d_mid[...]
    unit, scale = normal_parts(mid)
    d_norm_f = d_norm[...]
    pieces[2] = d_norm_f * unit
    d_mid_f = d_out() + normal_back(d_norm_f * (1.0 + modulation(4)), unit, scale)
    gate_a = modulation(2)
    d_branch[...] = (gate_a * d_mid_f).astype(jnp.bfloat16)
    pieces[0] = pieces[0] * d_mid_f
    d_mid[...] = d_mid_f
    d_attn[...] = lax.dot_general(
        d_branch[...], w_out[...], ALONG, preferred_element_type=jnp.float32
    ).astype(jnp.bfloat16)
    own = links.keep(strip(d_attn, links.seq, 128), grad_heads.at[own_rows, :])
    incoming_d = [
        links.send(
            strip(d_attn, links.seq_of(r), 128), grad_heads.at[own_rows, :], links.peer(r)
        )
        for r in FAR_FIRST
    ]
    quarter_b = Quarter(links, lambda u: strip(d_branch, u, narrow), d_branch_all)
    gather_b = Gathered(links, attn_ref, attn_all)
    half = width // 2
    down_at = lambda h: lambda u: g_down.at[
        pl.ds(pl.multiple_of(u * 128, 128), 128), pl.ds(h * half, half)
    ]
    column_at = lambda ref, step, offset, size: lambda u: ref.at[
        :, pl.ds(pl.multiple_of(u * step + offset, 128), size)
    ]
    wide, thin = d_qkv_all.shape[1], d_resid_all.shape[1]
    third, slim = wide // 2, thin // 2
    plans = [
        (act_all, d_ff_all, pl.ds(0, half), down_at(0)),
        (act_all, d_ff_all, pl.ds(half, half), down_at(1)),
        (norm_all, d_inner_all, pl.ds(0, half), column_at(g_up, width, 0, half)),
        (norm_all, d_inner_all, pl.ds(half, half), column_at(g_up, width, half, half)),
        (attn_all, d_branch_all, pl.ds(0, narrow), column_at(g_out, narrow, 0, narrow)),
        (norm_a_all, d_qkv_all, pl.ds(0, third), column_at(g_qkv, wide, 0, third)),
        (norm_a_all, d_qkv_all, pl.ds(third, third), column_at(g_qkv, wide, third, third)),
        (joined_all, d_resid_all, pl.ds(0, slim), column_at(g_skip, thin, 0, slim)),
        (joined_all, d_resid_all, pl.ds(slim, slim), column_at(g_skip, thin, slim, slim)),
    ]
    y_first = (True,) * 9
    shares = [
        Share(links, y_first[i], left, right, columns, *tiles[4 * i : 4 * i + 4], result)
        for i, (left, right, columns, result) in enumerate(plans)
    ]
    load_d.wait()
    quarters_a[0].wait()
    shares[0].start_far()
    shares[1].start_far()
    ff_out = ff_sum[...] + b_down_ref[...]
    mixed[...] = (mid + modulation(5) * ff_out).astype(jnp.bfloat16)
    saved = [links.keep(mixed, mixed_out)]
    pieces[1] = d_out() * ff_out
    small_own[...] = jnp.zeros_like(small_own)
    small_own[4:5, :] = column_sum(d_branch[...])
    for c in range(4):
        small_own[5 + c : 6 + c, :] = column_sum(d_inner[c])
    small_own[9:10, :] = column_sum(d_ff[...])

    def utterance_sums(piece, values):
        for u in range(utts):
            row = 10 + utts * piece + u
            small_own[row : row + 1, :] = jnp.sum(
                jnp.where(segment == u, values, 0.0), axis=0, keepdims=True
            )

    utterance_sums(2, pieces[0])
    utterance_sums(3, d_norm[...])
    utterance_sums(4, pieces[2])
    utterance_sums(5, pieces[1])
    gather_n.relay()
    quarters_a[1].wait()
    shares[0].start_near()
    shares[1].start_near()
    own.wait()
    for copy in incoming_d:
        copy.wait_recv()
    for copy in head_loads:
        copy.wait()
    dk_ref[...] = jnp.zeros_like(dk_ref)
    dv_ref[...] = jnp.zeros_like(dv_ref)
    first = lax.broadcasted_iota(jnp.int32, (256, 128), 1) < HEAD_DIM
    zero = jnp.zeros((256, 128), jnp.bfloat16)
    lower = lower_half((256, 128))
    k, v = heads_ref[:, 128:256], heads_ref[:, 256:384]
    seg_k = tables.segment(lax.broadcasted_iota(jnp.int32, (1, heads_ref.shape[0]), 1))

    def turned(values, here):
        return (
            values * cos_ref[here, :] - swap_halves(values, lower) * sin_ref[here, :]
        ).astype(jnp.bfloat16)

    def block(step, _):
        here = pl.ds(pl.multiple_of(step * 256, 256), 256)
        q, seg_q = heads_ref[here, 0:128], tables.segment(frame_column(step * 256, 256))
        scaled = grad_heads[here, :].astype(jnp.float32) / total_ref[here, :]
        grad_acc = scaled.astype(jnp.bfloat16)
        product = scaled * exact_ref[here, :]
        d_query = []
        for mine in (first, jnp.logical_not(first)):
            q_own = jnp.where(mine, q, zero)
            g_own = jnp.where(mine, grad_acc, zero)
            delta = jnp.sum(jnp.where(mine, product, 0.0), axis=1, keepdims=True)
            weights = head_scores(q_own, k, seg_q, seg_k)
            dots = lax.dot_general(g_own, v, ALONG, preferred_element_type=jnp.float32)
            d_scores = (weights * (dots - delta)).astype(jnp.bfloat16)
            d_query.append(jnp.dot(d_scores, k, preferred_element_type=jnp.float32))
            dk_ref[...] += lax.dot_general(
                d_scores, q_own, DOWN, preferred_element_type=jnp.float32
            )
            dv_ref[...] += lax.dot_general(
                weights.astype(jnp.bfloat16), g_own, DOWN, preferred_element_type=jnp.float32
            )
        d_heads[here, 0:128] = turned(jnp.where(first, d_query[0], d_query[1]) * 0.125, here)
        return 0

    blocks = heads_ref.shape[0] // 256
    lax.fori_loop(0, blocks, block, 0)

    def finish(step, _):
        here = pl.ds(pl.multiple_of(step * 256, 256), 256)
        d_heads[here, 128:256] = turned(dk_ref[here, :] * 0.125, here)
        d_heads[here, 256:384] = dv_ref[here, :].astype(jnp.bfloat16)
        return 0

    lax.fori_loop(0, blocks, finish, 0)
    part = lambda place, c: d_heads.at[
        pl.ds(pl.multiple_of(place * rows, rows), rows), pl.ds(c * 128, 128)
    ]
    home = lambda c: d_qkv.at[
        :, pl.ds(pl.multiple_of(c * model + links.seq * 128, 128), 128)
    ]
    owns = [links.keep(part(links.seq, c), home(c)) for c in range(3)]
    incoming = [
        links.send(part(links.seq_of(r), c), home(c), links.peer(r))
        for r in FAR_FIRST
        for c in range(3)
    ]
    gather_n.wait()
    quarter_i.wait()
    state = {}

    def output_share():
        gather_b.relay()
        gather_b.wait()
        quarter_b.wait()
        shares[4].start()

    def projections():
        for copy in owns:
            copy.wait()
        for copy in incoming:
            copy.wait_recv()
        for copy in loads:
            copy.wait()
        state["qkv"] = Quarter(links, lambda u: strip(d_qkv, u, wide), d_qkv_all)
        d_norm_a = lax.dot_general(
            d_qkv[...], w_qkv[...], ALONG, preferred_element_type=jnp.float32
        )
        unit, scale = normal_parts(resid_ref[...])
        d_resid_f = d_mid[...] + normal_back(d_norm_a * (1.0 + modulation(1)), unit, scale)
        rounded = d_resid_f.astype(jnp.bfloat16)
        d_resid[...] = rounded
        state["resid"] = Quarter(links, lambda u: strip(d_resid, u, thin), d_resid_all)
        small_own[0:1, :] = column_sum(rounded)
        for c in range(3):
            small_own[1 + c : 2 + c, :] = column_sum(d_qkv[:, c * model : (c + 1) * model])
        utterance_sums(0, d_norm_a)
        utterance_sums(1, d_norm_a * unit)
        small_out[0] = small_own[...].astype(jnp.bfloat16)
        state["small"] = links.send(small_out.at[0], small_got.at[0], links.peer(1))

    def qkv_shares():
        state["qkv"].wait()
        shares[5].start()
        shares[6].start()

    def skip_shares():
        state["resid"].wait()
        shares[7].start()
        shares[8].start()

    def inputs():
        for index, out in enumerate((g_frames, g_skip_in)):
            out[...] = lax.dot_general(
                d_resid[...],
                w_skip[pl.ds(index * model, model), :],
                ALONG,
                preferred_element_type=jnp.float32,
            ).astype(jnp.bfloat16)

    def small_y():
        state["small"].wait_recv()
        small_own[...] += small_got[0].astype(jnp.float32)
        small_out[1] = small_own[...].astype(jnp.bfloat16)
        state["small"] = links.send(small_out.at[1], small_got.at[1], links.peer(2))

    def small_z1():
        state["small"].wait_recv()
        small_own[...] += small_got[1].astype(jnp.float32)
        small_out[2] = small_own[...].astype(jnp.bfloat16)
        state["small"] = links.send(small_out.at[2], small_got.at[2], links.peer(4))

    def small_z2():
        state["small"].wait_recv()
        mine = smalls.at[links.utt]
        mine[...] = (small_own[...] + small_got[2].astype(jnp.float32)).astype(jnp.bfloat16)
        state["spread"] = [links.send(mine, mine, links.mate(r)) for r in (2, 3, 1)]

    def save(*pairs):
        return lambda: saved.extend(links.keep(source, target) for source, target in pairs)

    stages = ("start", "after_a", "after_b", "after_z2", "relay", "wait")
    s, a, b, z, r, w = ([getattr(share, stage) for share in shares] for stage in stages)
    for step in (
        s[2], a[0], a[1], s[3],
        output_share, projections,
        a[2], b[0], b[1],
        qkv_shares,
        z[0], b[2],
        small_y, inputs, save((g_frames, frames_out), (g_skip_in, skip_in_out)),
        z[1], z[2],
        skip_shares,
        a[3], r[0], r[1],
        small_z1,
        a[4], b[3], r[2], z[3], b[4],
        small_z2,
        w[0], w[1], save((g_down, down_out)), a[5], z[4], r[3], b[5], w[2], a[6], r[4], z[5], b[6], w[3], save((g_up, up_out)), a[7], r[5],
        z[6], b[7], w[4], save((g_out, out_out)), a[8], b[8], z[7], r[6], w[5], z[8], r[7], w[6], save((g_qkv, qkv_out)), r[8], w[7], w[8], save((g_skip, skip_out)),
    ):
        step()
    for copy in state["spread"]:
        copy.wait_recv()
    save((smalls, smalls_out))()
    for copy in saved:
        copy.wait()
    links.leave()


def backward(
    lengths, attn_b, resid, mod, loss, out_grad, d_ff, b_out, b_up, b_down,
    heads, exact, total, cos, sin,
    norm_a_all, joined_all, d_ff_all, w_out, w_up, w_down, w_qkv, w_skip,
):
    rows, model = resid.shape
    frames, inner = heads.shape[0], w_up.shape[1]
    utts = lengths.shape[1]
    small = (-(-(10 + 6 * utts) // 16) * 16, model)
    vmem, there = everywhere(pltpu.VMEM), everywhere(pl.ANY)
    shape = jax.ShapeDtypeStruct
    bf16 = lambda *dims: pltpu.VMEM(dims, jnp.bfloat16)
    f32 = lambda *dims: pltpu.VMEM(dims, jnp.float32)
    part, step = model // 8, inner // 8
    outs = [
        shape((rows, model), jnp.bfloat16),
        shape((inner // 8, model), jnp.bfloat16),
        shape((part, inner), jnp.bfloat16),
        shape((part, model), jnp.bfloat16),
        shape((part, 3 * model), jnp.bfloat16),
        shape((2 * part, model), jnp.bfloat16),
        shape((4,) + small, jnp.bfloat16),
        shape((rows, model), jnp.bfloat16),
        shape((rows, model), jnp.bfloat16),
    ]
    return pl.pallas_call(
        partial(backward_kernel, utts),
        in_specs=[everywhere(pltpu.SMEM)] + [vmem] * 9 + [there] * 13,
        out_specs=[there] * 9,
        out_shape=outs,
        scratch_shapes=[pltpu.VMEM(out.shape, out.dtype) for out in outs]
        + [
            bf16(rows, model),
            bf16(4, rows, inner // 4),
            bf16(4, rows, inner // 4),
            bf16(rows, model),
            bf16(rows, model),
            f32(3, rows, model),
            f32(rows, model),
            f32(rows, model),
            f32(rows, model),
            bf16(frames, 128),
            bf16(frames, 384),
            f32(frames, 128),
            f32(frames, 128),
            bf16(4 * rows, model),
            bf16(4 * rows, inner // 4),
            bf16(4 * rows, model),
            bf16(4 * rows, inner // 4),
            bf16(4 * rows, model),
            bf16(4 * rows, model // 4),
            bf16(4 * rows, model),
            bf16(4 * rows, 2 * model),
            bf16(rows, 3 * model),
            bf16(4 * rows, 3 * model // 4),
            bf16(rows, model),
            bf16(4 * rows, model // 4),
            bf16(frames, 384),
            f32(frames, 128),
            f32(frames, 128),
            f32(frames, 128),
            f32(frames, 128),
            bf16(2, model, step),
            bf16(2, step, model),
            bf16(*w_out.shape),
            bf16(*w_qkv.shape),
            bf16(*w_skip.shape),
            f32(*small),
            bf16(3, *small),
            bf16(3, *small),
        ]
        + share_scratch(part, inner // 8) * 4
        + share_scratch(part, model // 4)
        + share_scratch(part, 3 * model // 8) * 2
        + share_scratch(2 * part, model // 8) * 2
        + semaphores(160)
        + [pltpu.SemaphoreType.DMA((4,))],
        compiler_params=comm_params(2),
    )(
        lengths, attn_b, resid, mod, loss, out_grad, d_ff,
        b_out[None, :], b_up[None, :], b_down[None, :],
        heads, exact, total, cos, sin,
        norm_a_all, joined_all, d_ff_all, w_out, w_up, w_down, w_qkv, w_skip,
    )


UP = 3


def finish_kernel(utts, shards, *rest):
    kept_in, wide_in, smalls_in, act_in = rest[:3], rest[3:8], rest[8], rest[9]
    rest = rest[1:]
    kept_out, wide_out, mod_out, bias_out = rest[9:12], rest[12:17], rest[17], rest[18:24]
    kept, wide, staged = rest[24:27], rest[27:32], rest[32:37]
    smalls_got, act_got, bias_stage = rest[37], rest[38], rest[39:45]
    smalls_ref, act_rows, mod_stage, d_mod, totals, sems, load_sems = rest[45:]
    seq = lax.axis_index("seq")
    loads, copies = [], []
    for source, target in zip(
        (*wide_in, smalls_in, act_in, *kept_in), (*wide, smalls_got, act_got, *kept)
    ):
        copy = pltpu.make_async_copy(source, target, load_sems.at[len(loads)])
        copy.start()
        loads.append(copy)

    def put(source, target):
        copy = pltpu.make_async_copy(source, target, sems.at[len(copies)])
        copy.start()
        copies.append(copy)

    model = smalls_ref.shape[2]
    lanes = 128
    for place, (source, stage, target) in enumerate(zip(wide, staged, wide_out)):
        loads[place].wait()
        if place == UP:
            for u in range(4):
                for c in range(shards):
                    stage[:, (4 * c + u) * lanes : (4 * c + u + 1) * lanes] = source[
                        :, u * model + c * lanes : u * model + (c + 1) * lanes
                    ].astype(jnp.float32)
        else:
            stage[...] = source[...].astype(jnp.float32)
        put(stage, target)
    groups = smalls_ref.shape[0]
    loads[5].wait()
    smalls_ref[...] = smalls_got[...].astype(jnp.float32)
    loads[6].wait()
    act_rows[...] = jnp.zeros_like(act_rows)
    own = act_rows.shape[1]
    own_columns = pl.ds(pl.multiple_of(seq * own, own), own)
    for g in range(groups):
        act_rows[g * utts : (g + 1) * utts, :] = act_got[g, :, own_columns].astype(jnp.float32)[
            0:utts
        ]
    bias_sum = (
        smalls_ref[0, 0:10] + smalls_ref[1, 0:10] + smalls_ref[2, 0:10] + smalls_ref[3, 0:10]
    )
    for row in range(10):
        totals[row, 0:1] = bias_sum[row : row + 1]
    d_mod[...] = jnp.zeros_like(d_mod)
    for piece in range(6):
        first = 10 + utts * piece
        for g in range(groups):
            d_mod[piece, g * utts : (g + 1) * utts, :] = smalls_ref[g, first : first + utts, :]
        rows = d_mod[piece]
        totals[10 + piece, 0:1] = jnp.sum(rows, axis=0, keepdims=True)
        columns = slice(piece * model, (piece + 1) * model)
        mod_stage[:, columns] = lax.dot_general(
            act_rows[...],
            rows,
            DOWN,
            precision=HIGHEST_PRECISION,
            preferred_element_type=jnp.float32,
        )
    put(mod_stage, mod_out)
    for load, source, target in zip(loads[7:], kept, kept_out):
        load.wait()
        put(source, target)
    line = model // lanes
    first = 0
    for place, target in enumerate(bias_out):
        count = target.shape[0] // lanes
        for i in range(count):
            unit = i * line + seq if place == UP else seq * count + i
            column = pl.multiple_of((unit % line) * lanes, lanes)
            bias_stage[place][i * lanes : (i + 1) * lanes] = totals[
                first + unit // line, 0, pl.ds(column, lanes)
            ]
        first += count * shards // line
        put(bias_stage[place], target)
    for copy in copies:
        copy.wait()


def finish(shards, utts, acts, smalls, mixed, frames, skip, grads):
    there = everywhere(pl.ANY)
    shape = jax.ShapeDtypeStruct
    model = smalls.shape[2]
    own = model // shards
    depth = -(-acts.shape[0] * utts // 8) * 8
    mod_shape = (own, 6 * model)
    widths = [own, 3 * own, own, 4 * own, own, 6 * own]
    kept = (mixed, frames, skip)
    outs = pl.pallas_call(
        partial(finish_kernel, utts, shards),
        in_specs=[there] * 10,
        out_specs=[there] * 15,
        out_shape=[shape(v.shape, v.dtype) for v in kept]
        + [shape(g.shape, jnp.float32) for g in grads]
        + [shape(mod_shape, jnp.float32)]
        + [shape((w,), jnp.float32) for w in widths],
        scratch_shapes=[pltpu.VMEM(v.shape, v.dtype) for v in (*kept, *grads)]
        + [pltpu.VMEM(g.shape, jnp.float32) for g in grads]
        + [
            pltpu.VMEM(smalls.shape, smalls.dtype),
            pltpu.VMEM(acts.shape, acts.dtype),
        ]
        + [pltpu.VMEM((w,), jnp.float32) for w in widths]
        + [
            pltpu.VMEM(smalls.shape, jnp.float32),
            pltpu.VMEM((depth, own), jnp.float32),
            pltpu.VMEM(mod_shape, jnp.float32),
            pltpu.VMEM((6, depth, model), jnp.float32),
            pltpu.VMEM((16, 8, model), jnp.float32),
            pltpu.SemaphoreType.DMA((15,)),
            pltpu.SemaphoreType.DMA((10,)),
        ],
        compiler_params=pltpu.CompilerParams(vmem_limit_bytes=VMEM_LIMIT),
    )(*kept, *grads, smalls, acts)
    return outs[:9], outs[9:]


def compact_tables(lengths, total_rows):
    half_dim = HEAD_DIM // 2
    shape = (total_rows // 4, 128)
    lane = lax.broadcasted_iota(jnp.int32, shape, 1)
    frame = lax.broadcasted_iota(jnp.int32, shape, 0) + (lane // half_dim) * shape[0]
    start, end = jnp.zeros(shape, jnp.int32), jnp.int32(0)
    for u in range(lengths.shape[0]):
        end = end + lengths[u]
        start = jnp.where(frame >= end, end, start)
    inverse = jnp.exp(
        -math.log(10000.0) * 2.0 * (lane % half_dim).astype(jnp.float32) / HEAD_DIM
    )
    angles = (frame - start).astype(jnp.float32) * inverse
    return jnp.cos(angles), jnp.sin(angles)


def padded_time_act(flow_vals, model):
    half_dim = model // 2
    column = jnp.arange(model, dtype=jnp.int32)
    inverse = jnp.exp(-math.log(10000.0) * (column % half_dim).astype(jnp.float32) / half_dim)
    flow_vals = jnp.pad(flow_vals, (0, 8 - flow_vals.shape[0]))
    angles = 1000.0 * flow_vals[:, None] * inverse[None, :]
    wave = jnp.where((column < half_dim)[None, :], jnp.sin(angles), jnp.cos(angles))
    return jax.nn.silu(wave).astype(jnp.bfloat16)


def local(
    frames_in,
    skip_in,
    flow_times,
    frame_lengths,
    char_lengths,
    drop_mask,
    out_grad,
    w_skip,
    b_skip,
    w_mod,
    b_mod,
    w_qkv,
    b_qkv,
    w_out,
    b_out,
    w_up,
    b_up,
    w_down,
    b_down,
):
    local_rows = frames_in.shape[1]
    model_width = frames_in.shape[2]
    shards = lax.axis_size("seq")
    seq_place = lax.axis_index("seq")
    lengths = frame_lengths[0]
    whole = model_width * 4
    fused = (
        lax.axis_size("utt") == 4
        and shards == 8
        and HEADS * HEAD_DIM == 1024
        and model_width == 1024
        and w_up.shape[1] == whole
        and local_rows == 128
        and flow_times.shape[1] <= 8
    )
    if not fused:
        utt_ends = jnp.cumsum(lengths)
        segment, position, in_loss, member = frame_tables(
            lengths, char_lengths[0], seq_place * local_rows, local_rows
        )
        member_f = member.astype(jnp.float32)
        loss_mask = in_loss.astype(jnp.float32)
        dropped = drop_mask[0].astype(jnp.float32)
        counts = jnp.stack([jnp.sum(loss_mask * dropped), jnp.sum(loss_mask * (1.0 - dropped))])
        counts = jnp.pad(counts[None, :], ((0, 7), (0, 126)))
        counts = xor_sum(xor_sum(counts, "utt"), "seq")
        time_act = jax.nn.silu(time_embed(flow_times[0], model_width)).astype(jnp.bfloat16)
        mod_u = jnp.dot(time_act, w_mod, preferred_element_type=jnp.float32) + b_mod
        mod_f = jnp.dot(member_f, mod_u, precision=HIGHEST_PRECISION)
        shift_a, scale_a, gate_a, shift_f, scale_f, gate_f = jnp.split(mod_f, 6, axis=1)
        joined = jnp.concatenate([frames_in[0], skip_in[0]], axis=1)
        residual = jnp.dot(joined, w_skip, preferred_element_type=jnp.float32) + b_skip
        norm_a = modulate(residual, scale_a, shift_a).astype(jnp.bfloat16)
        qkv_full = jnp.dot(norm_a, w_qkv, preferred_element_type=jnp.float32) + b_qkv
    if fused:
        (
            attn_b, qkv_heads, exact, total, loss, acts, norm_all, joined_all,
            residual, mod_u, cos_all, sin_all, d_ff, d_ff_all,
        ) = attend(
            frame_lengths,
            char_lengths,
            drop_mask,
            padded_time_act(flow_times[0], model_width),
            *compact_tables(lengths, local_rows * shards),
            frames_in[0],
            skip_in[0],
            out_grad[0],
            b_skip,
            b_mod,
            b_qkv,
            w_skip,
            w_mod,
            w_qkv,
            shards,
        )
    else:
        angle_cos, angle_sin = rotary_tables(position, HEAD_DIM)
        queries = rotate(
            qkv_full[:, :model_width].reshape(local_rows, HEADS, HEAD_DIM), angle_cos, angle_sin
        ).astype(jnp.bfloat16)
        key_rot = rotate(
            qkv_full[:, model_width : 2 * model_width].reshape(local_rows, HEADS, HEAD_DIM),
            angle_cos,
            angle_sin,
        ).astype(jnp.bfloat16)
        key_value = jnp.stack(
            [
                key_rot.reshape(local_rows, model_width),
                qkv_full[:, 2 * model_width :].astype(jnp.bfloat16),
            ],
            axis=0,
        )
        start_state = (
            jnp.zeros((local_rows, HEADS, HEAD_DIM), jnp.float32),
            jnp.zeros((HEADS, local_rows), jnp.float32),
        )
        fwd_piece = partial(forward_piece, queries=queries, query_segment=segment, utt_ends=utt_ends)
        weighted, totals = over_blocks(
            partial(fwd_piece, usable=True),
            start_state,
            lax.all_gather(key_value, "seq", axis=1, tiled=True),
            jnp.int32(0),
            local_rows,
        )
        totals_rows = jnp.transpose(totals)
        attended = weighted / totals_rows[:, :, None]
        attn_b = attended.reshape(local_rows, model_width).astype(jnp.bfloat16)
    if fused:
        mixed, g_w_down, g_w_up, g_w_out, g_w_qkv, g_w_skip, smalls, g_frames, g_skip_in = backward(
            frame_lengths,
            attn_b,
            residual,
            mod_u,
            loss,
            out_grad[0],
            d_ff,
            b_out,
            b_up,
            b_down,
            qkv_heads,
            exact,
            total,
            cos_all,
            sin_all,
            norm_all,
            joined_all,
            d_ff_all,
            w_out,
            w_up,
            w_down,
            w_qkv,
            w_skip,
        )
        utts = flow_times.shape[1]
        wide, biases = finish(
            shards,
            utts,
            acts,
            smalls,
            mixed,
            g_frames,
            g_skip_in,
            (g_w_skip, g_w_qkv, g_w_out, g_w_up, g_w_down),
        )
        mixed, g_frames, g_skip_in, g_w_skip, g_w_qkv, g_w_out, g_w_up, g_w_down, g_w_mod = wide
        own_biases, g_b_mod = biases[:5], biases[5]
    else:
        n_drop, n_keep = counts[0, 0], counts[0, 1]
        loss_weight = (
            loss_mask
            * (n_drop + n_keep)
            * 0.5
            * (dropped / (n_drop + 1.0) + (1.0 - dropped) / (n_keep + 1.0))
        )
        branch = jnp.dot(attn_b, w_out, preferred_element_type=jnp.float32) + b_out
        mid_state = residual + gate_a * branch
        norm_f = modulate(mid_state, scale_f, shift_f).astype(jnp.bfloat16)
        ff_inner = jnp.dot(norm_f, w_up, preferred_element_type=jnp.float32) + b_up
        ff_act, gelu_pull = jax.vjp(partial(jax.nn.gelu, approximate=True), ff_inner)
        act_b = ff_act.astype(jnp.bfloat16)
        ff_out = jnp.dot(act_b, w_down, preferred_element_type=jnp.float32) + b_down
        out_state = mid_state + gate_f * ff_out
        d_out = out_grad[0].astype(jnp.float32) * loss_weight[:, None]
        d_ff = (gate_f * d_out).astype(jnp.bfloat16)
        d_gate_f = d_out * ff_out
        g_b_down = jnp.sum(d_ff.astype(jnp.float32), axis=0)
        (d_inner,) = gelu_pull(back_product(d_ff, w_down))
        d_inner_b = d_inner.astype(jnp.bfloat16)
        g_b_up = jnp.sum(d_inner_b.astype(jnp.float32), axis=0)
        d_norm_f = back_product(d_inner_b, w_up)
        _, norm_f_pull = jax.vjp(modulate, mid_state, scale_f, shift_f)
        d_mid_norm, d_scale_f, d_shift_f = norm_f_pull(d_norm_f)
        d_mid = d_out + d_mid_norm
        d_branch = (gate_a * d_mid).astype(jnp.bfloat16)
        d_gate_a = d_mid * branch
        g_b_out = jnp.sum(d_branch.astype(jnp.float32), axis=0)
        d_attn = back_product(d_branch, w_out)
        mixed = out_state.astype(jnp.bfloat16)
        g_w_down = weight_grad(gather_left(act_b), d_ff)
        g_w_up = weight_grad(gather_left(norm_f), d_inner_b)
        g_w_out = weight_grad(gather_left(attn_b), d_branch)
        d_attn = d_attn.reshape(local_rows, HEADS, HEAD_DIM)
        grad_acc = (d_attn / totals_rows[:, :, None]).astype(jnp.bfloat16)
        delta = jnp.transpose(jnp.sum(d_attn * attended, axis=2) / totals_rows)
        bwd_piece = partial(
            backward_piece,
            queries=queries,
            query_segment=segment,
            utt_ends=utt_ends,
            grad_acc=grad_acc,
            delta=delta,
        )
        zero_query = jnp.zeros((local_rows, HEADS, HEAD_DIM), jnp.float32)
        zero_all = jnp.zeros((2, local_rows * shards, model_width), jnp.float32)

        def block_fn(inner_state, portion, block_start):
            d_query_sum, d_all = inner_state
            d_query_add, d_block = bwd_piece(portion, block_start, True)
            return (
                d_query_sum + d_query_add,
                lax.dynamic_update_slice_in_dim(d_all, d_block, block_start, 1),
            )

        d_query, d_all = over_blocks(
            block_fn,
            (zero_query, zero_all),
            lax.all_gather(key_value, "seq", axis=1, tiled=True),
            jnp.int32(0),
            local_rows,
        )
        d_key_value = lax.psum_scatter(d_all, "seq", scatter_dimension=1, tiled=True)
        d_query_pre = unrotate(d_query, angle_cos, angle_sin).reshape(local_rows, model_width)
        d_key_pre = unrotate(
            d_key_value[0].reshape(local_rows, HEADS, HEAD_DIM), angle_cos, angle_sin
        ).reshape(local_rows, model_width)
        d_qkv = jnp.concatenate([d_query_pre, d_key_pre, d_key_value[1]], axis=1).astype(jnp.bfloat16)
        g_b_qkv = jnp.sum(d_qkv.astype(jnp.float32), axis=0)
        d_norm_a = back_product(d_qkv, w_qkv)
        _, norm_a_pull = jax.vjp(modulate, residual, scale_a, shift_a)
        d_resid_norm, d_scale_a, d_shift_a = norm_a_pull(d_norm_a)
        d_resid = (d_mid + d_resid_norm).astype(jnp.bfloat16)
        g_b_skip = jnp.sum(d_resid.astype(jnp.float32), axis=0)
        d_joined = back_product(d_resid, w_skip)
        d_mod_f = jnp.concatenate(
            [d_shift_a, d_scale_a, d_gate_a, d_shift_f, d_scale_f, d_gate_f], axis=1
        )
        d_mod_u = jnp.dot(jnp.transpose(member_f), d_mod_f, precision=HIGHEST_PRECISION)
        small = jnp.concatenate(
            [g_b_skip, g_b_qkv, g_b_out, g_b_up, g_b_down, d_mod_u.reshape(-1)]
        )
        biases = small.shape[0] - d_mod_u.size
        g_w_qkv = weight_grad(gather_left(norm_a), d_qkv)
        g_w_skip = weight_grad(gather_left(joined), d_resid)
        small = xor_sum(small.reshape(-1, 128), "seq").reshape(-1)
        bias_sum = xor_sum(small[:biases].reshape(-1, 128), "utt").reshape(-1)
        d_mod_all = gather_ordered(small[biases:].reshape(d_mod_u.shape), 0)
        act_all = gather_ordered(time_act, 0)
        g_frames = d_joined[:, :model_width].astype(jnp.bfloat16)
        g_skip_in = d_joined[:, model_width:].astype(jnp.bfloat16)
        act_all = act_all.astype(jnp.float32)
        own_width = model_width // shards
        act_own = lax.dynamic_slice_in_dim(act_all, seq_place * own_width, own_width, 1)
        g_w_mod = jnp.dot(jnp.transpose(act_own), d_mod_all, precision=HIGHEST_PRECISION)
        mod_width = d_mod_all.shape[1] // shards
        g_b_mod = jnp.sum(
            lax.dynamic_slice_in_dim(d_mod_all, seq_place * mod_width, mod_width, 1), axis=0
        )
        own_biases, offset = [], 0
        for size in (b_skip.shape[0], b_qkv.shape[0], b_out.shape[0], b_up.shape[0], b_down.shape[0]):
            width = size // shards
            own_biases.append(
                lax.dynamic_slice_in_dim(bias_sum, offset + seq_place * width, width, 0)
            )
            offset += size
    return (
        mixed[None],
        g_frames[None],
        g_skip_in[None],
        g_w_skip,
        own_biases[0],
        g_w_mod,
        g_b_mod,
        g_w_qkv,
        own_biases[1],
        g_w_out,
        own_biases[2],
        g_w_up,
        own_biases[3],
        g_w_down,
        own_biases[4],
    )


def solution(mesh):
    return jax.shard_map(
        local,
        mesh=mesh,
        in_specs=(
            P("utt", "seq", None),
            P("utt", "seq", None),
            P("utt", None),
            P("utt", None),
            P("utt", None),
            P("utt", "seq"),
            P("utt", "seq", None),
            P(),
            P(),
            P(),
            P(),
            P(),
            P(),
            P(),
            P(),
            P(),
            P(),
            P(),
            P(),
        ),
        out_specs=(
            P("utt", "seq", None),
            P("utt", "seq", None),
            P("utt", "seq", None),
            P("seq", None),
            P("seq"),
            P("seq", None),
            P("seq"),
            P("seq", None),
            P("seq"),
            P("seq", None),
            P("seq"),
            P("seq", None),
            P("seq"),
            P("seq", None),
            P("seq"),
        ),
        check_vma=False,
    )
```

```python
from functools import partial
import math

import jax
import jax.numpy as jnp
from jax import lax
from jax.experimental import pallas as pl
from jax.experimental.pallas import tpu as pltpu
from jax.sharding import PartitionSpec as P

HEADS = 16
HEAD_DIM = 64


HIGHEST_PRECISION = lax.Precision.HIGHEST
EPSILON = 1e-06


def layer_norm(values):
    average = jnp.mean(values, axis=-1, keepdims=True)
    centred = values - average
    spread = jnp.mean(centred * centred, axis=-1, keepdims=True)
    return centred * lax.rsqrt(spread + EPSILON)


def modulate(values, scale_part, shift_part):
    return layer_norm(values) * (1.0 + scale_part) + shift_part


def time_embed(flow_vals, model_width):
    half_dim = model_width // 2
    inverse = jnp.exp(-math.log(10000.0) * jnp.arange(half_dim, dtype=jnp.float32) / half_dim)
    angles = 1000.0 * flow_vals[:, None] * inverse[None, :]
    return jnp.concatenate([jnp.sin(angles), jnp.cos(angles)], axis=1)


def rotary_tables(position, head_size):
    half_dim = head_size // 2
    inverse = jnp.exp(
        -math.log(10000.0) * 2.0 * jnp.arange(half_dim, dtype=jnp.float32) / head_size
    )
    angles = position.astype(jnp.float32)[:, None] * inverse[None, :]
    return (jnp.cos(angles)[:, None, :], jnp.sin(angles)[:, None, :])


def rotate(tensor, angle_cos, angle_sin):
    half_dim = tensor.shape[-1] // 2
    leading = tensor[..., :half_dim]
    trailing = tensor[..., half_dim:]
    return jnp.concatenate(
        [leading * angle_cos - trailing * angle_sin, trailing * angle_cos + leading * angle_sin],
        axis=-1,
    )


def unrotate(gradient, angle_cos, angle_sin):
    half_dim = gradient.shape[-1] // 2
    leading = gradient[..., :half_dim]
    trailing = gradient[..., half_dim:]
    return jnp.concatenate(
        [leading * angle_cos + trailing * angle_sin, trailing * angle_cos - leading * angle_sin],
        axis=-1,
    )


def frame_tables(lengths, char_counts, first_frame, frame_count):
    utt_ends = jnp.cumsum(lengths)
    utt_starts = utt_ends - lengths
    frame_index = first_frame + jnp.arange(frame_count, dtype=jnp.int32)
    segment = jnp.sum((frame_index[:, None] >= utt_ends[None, :]).astype(jnp.int32), axis=1)
    member = segment[:, None] == jnp.arange(lengths.shape[0], dtype=jnp.int32)[None, :]
    position = frame_index - jnp.sum(jnp.where(member, utt_starts[None, :], 0), axis=1)
    prompt = jnp.sum(jnp.where(member, char_counts[None, :], 0), axis=1)
    return (segment, position, position >= prompt, member)


def key_segments(key_start, key_count, utt_ends):
    frame_index = key_start + jnp.arange(key_count, dtype=jnp.int32)
    return jnp.sum((frame_index[:, None] >= utt_ends[None, :]).astype(jnp.int32), axis=1)


def block_scores(queries, key_piece, query_segment, key_segment, usable):
    key_rows = key_piece.reshape(key_piece.shape[0], queries.shape[1], queries.shape[2])
    scores = (
        jnp.einsum("qhd,khd->hqk", queries, key_rows, preferred_element_type=jnp.float32) * 0.125
    )
    allowed = jnp.logical_and(query_segment[:, None] == key_segment[None, :], usable)
    return (jnp.where(allowed[None], jnp.exp(scores), 0.0), key_rows)


def over_blocks(block_fn, running, piece, key_start, shard_rows):
    key_count = piece.shape[1]
    shard_total = key_count // shard_rows
    group_size = max(1, min(shard_total, 1024 // shard_rows))
    while shard_total % group_size != 0:
        group_size = group_size - 1
    block_rows = group_size * shard_rows
    if block_rows == key_count:
        return block_fn(running, piece, key_start)

    def one_block(block_index, inner_state):
        portion = lax.dynamic_slice_in_dim(piece, block_index * block_rows, block_rows, 1)
        return block_fn(inner_state, portion, key_start + block_index * block_rows)

    return lax.fori_loop(0, key_count // block_rows, one_block, running)


def forward_piece(running, piece, key_start, usable, queries, query_segment, utt_ends):
    weighted, totals = running
    key_segment = key_segments(key_start, piece.shape[1], utt_ends)
    weights, key_rows = block_scores(queries, piece[0], query_segment, key_segment, usable)
    value_rows = piece[1].reshape(key_rows.shape)
    totals = totals + jnp.sum(weights, axis=2)
    weighted = weighted + jnp.einsum(
        "hqk,khd->qhd", weights.astype(jnp.bfloat16), value_rows, preferred_element_type=jnp.float32
    )
    return (weighted, totals)


def backward_piece(piece, key_start, usable, queries, query_segment, utt_ends, grad_acc, delta):
    key_count = piece.shape[1]
    key_segment = key_segments(key_start, key_count, utt_ends)
    weights, key_rows = block_scores(queries, piece[0], query_segment, key_segment, usable)
    value_rows = piece[1].reshape(key_rows.shape)
    value_dots = jnp.einsum(
        "qhd,khd->hqk", grad_acc, value_rows, preferred_element_type=jnp.float32
    )
    d_scores = (weights * (value_dots - delta[:, :, None])).astype(jnp.bfloat16)
    d_query = (
        jnp.einsum("hqk,khd->qhd", d_scores, key_rows, preferred_element_type=jnp.float32) * 0.125
    )
    d_key = (
        jnp.einsum("hqk,qhd->khd", d_scores, queries, preferred_element_type=jnp.float32) * 0.125
    )
    d_value = jnp.einsum(
        "hqk,qhd->khd", weights.astype(jnp.bfloat16), grad_acc, preferred_element_type=jnp.float32
    )
    return (
        d_query,
        jnp.stack([d_key.reshape(key_count, -1), d_value.reshape(key_count, -1)], axis=0),
    )


def back_product(gradient_rows, matrix):
    return jnp.einsum("fo,io->fi", gradient_rows, matrix, preferred_element_type=jnp.float32)


def xor_permute(value, axis_name, bit):
    size = lax.axis_size(axis_name)
    return lax.ppermute(value, axis_name, [(i, i ^ bit) for i in range(size)])


def bits_of(axis_name):
    size, bits, bit = lax.axis_size(axis_name), [], 1
    while bit < size:
        bits.append(bit)
        bit *= 2
    return bits


def xor_sum(value, axis_name):
    for bit in bits_of(axis_name):
        value = value + xor_permute(value, axis_name, bit)
    return value


def gather_left(rows):
    for bit in reversed(bits_of("utt")):
        rows = jnp.concatenate([rows, xor_permute(rows, "utt", bit)], axis=0)
    return rows


def gather_right(rows):
    place = lax.axis_index("utt")
    for bit in reversed(bits_of("utt")):
        mine = (place & bit) // bit
        width = rows.shape[1] // 2
        kept = lax.dynamic_slice_in_dim(rows, mine * width, width, 1)
        given = lax.dynamic_slice_in_dim(rows, (1 - mine) * width, width, 1)
        rows = jnp.concatenate([kept, xor_permute(given, "utt", bit)], axis=0)
    return rows


def gather_ordered(value, axis):
    place = lax.axis_index("utt")
    for bit in bits_of("utt"):
        other = xor_permute(value, "utt", bit)
        low = (place & bit) == 0
        value = jnp.concatenate(
            [jnp.where(low, value, other), jnp.where(low, other, value)], axis=axis
        )
    return value


def scatter_rows(tile):
    place = lax.axis_index("seq")
    for bit in bits_of("seq"):
        mine = (place & bit) // bit
        rest = lax.axis_size("seq") // (2 * bit)
        pieces = tile.reshape(rest, 2, -1, tile.shape[-1])
        kept = lax.dynamic_index_in_dim(pieces, mine, 1, keepdims=False)
        given = lax.dynamic_index_in_dim(pieces, 1 - mine, 1, keepdims=False)
        given = xor_permute(given, "seq", bit)
        tile = (kept.astype(jnp.float32) + given.astype(jnp.float32)).astype(jnp.bfloat16)
    return tile.reshape(-1, tile.shape[-1])


def weight_grad(left_all, right_rows):
    right_all = gather_right(right_rows)
    tile = jnp.einsum(
        "fi,fo->io", left_all, right_all, preferred_element_type=jnp.float32
    ).astype(jnp.bfloat16)
    tile = tile.reshape(-1, tile.shape[-1])
    piece = scatter_rows(tile)
    return gather_ordered(piece, 1).astype(jnp.float32)


def swap_halves(values, lower):
    return jnp.where(lower, pltpu.roll(values, 96, 1), pltpu.roll(values, 32, 1))


def lower_half(shape):
    return lax.broadcasted_iota(jnp.int32, shape, 1) % HEAD_DIM < HEAD_DIM // 2


def head_scores(q, k, seg_q, seg_k):
    scores = lax.dot_general(q, k, (((1,), (1,)), ((), ())), preferred_element_type=jnp.float32)
    return jnp.where(seg_q == seg_k, jnp.exp(scores * 0.125), 0.0)


MESH = pl.DeviceIdType.MESH
VMEM_LIMIT = 62 * 1024 * 1024


def flip(index, bit):
    return index + bit - 2 * bit * ((index // bit) % 2)


def everywhere(memory):
    return pl.BlockSpec(memory_space=memory)


class Links:
    def __init__(self, send_sems, recv_sems, local_sems):
        self.send_sems, self.recv_sems, self.local_sems = send_sems, recv_sems, local_sems
        self.sent, self.held = [], 0
        self.utt, self.seq = lax.axis_index("utt"), lax.axis_index("seq")

    def enter(self, utt_peers, seq_peers):
        barrier = pltpu.get_barrier_semaphore()
        targets = [self.mate(r) for r in utt_peers] + [self.peer(r) for r in seq_peers]
        for target in targets:
            pl.semaphore_signal(barrier, inc=1, device_id=target, device_id_type=MESH)
        pl.semaphore_wait(barrier, len(targets))

    def mate(self, offset):
        return (self.utt_of(offset), self.seq)

    def utt_of(self, offset):
        place = self.utt
        for bit in (1, 2):
            if offset & bit:
                place = flip(place, bit)
        return place

    def seq_of(self, offset):
        place = self.seq
        for bit in (1, 2, 4):
            if offset & bit:
                place = flip(place, bit)
        return place

    def peer(self, offset):
        return (self.utt, self.seq_of(offset))

    def send(self, source, target, device):
        index = len(self.sent)
        copy = pltpu.make_async_remote_copy(
            src_ref=source,
            dst_ref=target,
            send_sem=self.send_sems.at[index],
            recv_sem=self.recv_sems.at[index],
            device_id=device,
            device_id_type=MESH,
        )
        copy.start()
        self.sent.append(copy)
        return copy

    def keep(self, source, target):
        copy = pltpu.make_async_copy(source, target, self.local_sems.at[self.held])
        self.held += 1
        copy.start()
        return copy

    def leave(self):
        assert len(self.sent) <= self.send_sems.shape[0]
        assert self.held <= self.local_sems.shape[0]
        for copy in self.sent:
            copy.wait_send()


class Gathered:
    def __init__(self, links, source, target, columns=None):
        self.links, self.target = links, target
        self.rows = source.shape[0]
        self.columns = columns
        self.own = links.keep(source, self.slot(0))
        self.across = links.send(source, self.slot(2), links.mate(2))
        self.beside = links.send(source, self.slot(1), links.mate(1))

    def slot(self, offset):
        rows = pl.ds(offset * self.rows, self.rows)
        if self.columns is None:
            return self.target.at[rows, :]
        return self.target.at[rows, self.columns]

    def relay(self):
        self.across.wait_recv()
        self.relayed = self.links.send(self.slot(2), self.slot(3), self.links.mate(1))

    def wait(self):
        self.own.wait()
        self.beside.wait_recv()
        self.relayed.wait_recv()


class Quarter:
    def __init__(self, links, piece_of, target, columns=None):
        rows = target.shape[0] // 4
        columns = pl.ds(0, target.shape[1]) if columns is None else columns
        slot = lambda r: target.at[pl.ds(r * rows, rows), columns]
        self.own = links.keep(piece_of(links.utt), slot(0))
        self.copies = [
            links.send(piece_of(links.utt_of(r)), slot(r), links.mate(r)) for r in (2, 3, 1)
        ]

    def wait(self):
        self.own.wait()
        for copy in self.copies:
            copy.wait_recv()


class Share:
    def __init__(self, links, y_first, left, right, columns, tile, got_a, got_b, got_z2, result):
        self.links, self.y_first = links, y_first
        self.left, self.right, self.columns = left, right, columns
        self.tile, self.got_a, self.got_b, self.got_z2 = tile, got_a, got_b, got_z2
        self.result = result
        seq = links.seq
        self.y, self.zl, self.zh = seq % 2, (seq // 2) % 2, seq // 4
        if y_first:
            self.a, self.b, self.peers = self.y, self.zl, (1, 2)
        else:
            self.a, self.b, self.peers = self.zl, self.y, (2, 1)

    def place(self, zh, a, b):
        return (zh, b, a) if self.y_first else (zh, a, b)

    def product(self, zh, a):
        rows = self.tile.shape[3]

        def block(b, _):
            here = self.place(zh, a, b)
            base = pl.multiple_of((4 * zh + 2 * here[1] + here[2]) * rows, rows)
            self.tile[here] = lax.dot_general(
                self.left[:, pl.ds(base, rows)],
                self.right[:, self.columns],
                (((0,), (0,)), ((), ())),
                preferred_element_type=jnp.float32,
            ).astype(jnp.bfloat16)
            return 0

        lax.fori_loop(0, 2, block, 0)

    def give(self, zh):
        self.product(zh, 1 - self.a)
        given = self.tile.at[zh, :, 1 - self.a] if self.y_first else self.tile.at[zh, 1 - self.a]
        self.sent_a.append(
            self.links.send(given, self.got_a.at[zh], self.links.peer(self.peers[0]))
        )

    def start_far(self):
        self.sent_a, self.sent_b = [], []
        self.give(1 - self.zh)
        self.product(1 - self.zh, self.a)

    def start_near(self):
        self.give(self.zh)
        self.product(self.zh, self.a)

    def start(self):
        self.sent_a, self.sent_b = [], []
        self.give(1 - self.zh)
        self.give(self.zh)
        self.product(1 - self.zh, self.a)
        self.product(self.zh, self.a)

    def add(self, index, got):
        tile = self.tile
        tile[index] = (tile[index].astype(jnp.float32) + got.astype(jnp.float32)).astype(
            jnp.bfloat16
        )

    def after_a(self):
        halves = (1 - self.zh, self.zh)
        for sent, zh in zip(self.sent_a, halves):
            sent.wait_recv()
            here = self.place(zh, self.a, 1 - self.b)
            self.add(here, self.got_a[zh, 1 - self.b])
            self.sent_b.append(
                self.links.send(
                    self.tile.at[here], self.got_b.at[zh], self.links.peer(self.peers[1])
                )
            )
        for zh in halves:
            self.add(self.place(zh, self.a, self.b), self.got_a[zh, self.b])

    def after_b(self):
        self.sent_b[0].wait_recv()
        self.add((1 - self.zh, self.zl, self.y), self.got_b[1 - self.zh])
        self.sent_z2 = self.links.send(
            self.tile.at[1 - self.zh, self.zl, self.y], self.got_z2, self.links.peer(4)
        )
        self.sent_b[1].wait_recv()
        self.add((self.zh, self.zl, self.y), self.got_b[self.zh])

    def after_z2(self):
        self.sent_z2.wait_recv()
        links = self.links
        mine = self.result(links.utt)
        mine[...] = (
            self.tile[self.zh, self.zl, self.y].astype(jnp.float32)
            + self.got_z2[...].astype(jnp.float32)
        ).astype(jnp.bfloat16)
        self.across = links.send(mine, mine, links.mate(2))
        self.beside = links.send(mine, mine, links.mate(1))

    def relay(self):
        self.across.wait_recv()
        links = self.links
        theirs = self.result(links.utt_of(2))
        self.relayed = links.send(theirs, theirs, links.mate(1))

    def wait(self):
        self.beside.wait_recv()
        self.relayed.wait_recv()


def share_scratch(rows, columns):
    return [
        pltpu.VMEM((2, 2, 2, rows, columns), jnp.bfloat16),
        pltpu.VMEM((2, 2, rows, columns), jnp.bfloat16),
        pltpu.VMEM((2, rows, columns), jnp.bfloat16),
        pltpu.VMEM((rows, columns), jnp.bfloat16),
    ]


def semaphores(count):
    return [pltpu.SemaphoreType.DMA((count,))] * 2 + [pltpu.SemaphoreType.DMA((40,))]


def comm_params(collective_id):
    return pltpu.CompilerParams(
        collective_id=collective_id, has_side_effects=True, vmem_limit_bytes=VMEM_LIMIT
    )


class Frames:
    def __init__(self, utts, lengths_ref):
        self.starts, self.ends, end = [], [], 0
        for u in range(utts):
            self.starts.append(end)
            end = end + lengths_ref[0, u]
            self.ends.append(end)

    def segment(self, frame):
        return sum((frame >= end).astype(jnp.int32) for end in self.ends)

    def of(self, segment, values):
        total = jnp.zeros_like(segment)
        for u, value in enumerate(values):
            total = jnp.where(segment == u, value, total)
        return total


def frame_column(first, count):
    return first + lax.broadcasted_iota(jnp.int32, (count, 1), 0)


def per_frame(mod_ref, segment, utts, piece, model):
    columns = slice(piece * model, (piece + 1) * model)
    value = jnp.broadcast_to(mod_ref[0:1, columns], (segment.shape[0], model))
    for u in range(1, utts):
        value = jnp.where(segment == u, mod_ref[u : u + 1, columns], value)
    return value


FAR_FIRST = (6, 7, 4, 5, 2, 3, 1)


def attend_kernel(
    utts, lengths_ref, chars_ref, drop_ref, act_ref, cos_in, sin_in, frames_ref, skip_ref,
    out_grad_ref,
    b_skip_ref, b_mod_ref, b_qkv_ref, w_skip_ref, w_mod_ref, w_qkv_ref,
    attn_ref, heads_ref, exact_ref, total_ref, loss_ref, acts_ref, norm_all, joined_all,
    resid_ref, mod_ref, cos_ref, sin_ref, d_ff_ref, d_ff_all,
    attn_heads, counts_got, sums_ref, packed, norm_ref, w_skip, w_mod, w_qkv,
    send_sems, recv_sems, local_sems,
):
    links = Links(send_sems, recv_sems, local_sems)
    rows, model = frames_ref.shape
    total_rows = heads_ref.shape[0]
    early, late = pl.ds(0, 2 * model), pl.ds(2 * model, 4 * model)
    load_skip = links.keep(w_skip_ref, w_skip)
    load_early = links.keep(w_mod_ref.at[:, early], w_mod.at[:, early])
    links.enter((1, 2, 3), range(1, 8))
    gathers = [
        Gathered(links, frames_ref, joined_all, pl.ds(0, model)),
        Gathered(links, skip_ref, joined_all, pl.ds(model, model)),
    ]
    act_own = links.keep(act_ref, acts_ref.at[links.utt])
    act_copies = [
        links.send(act_ref, acts_ref.at[links.utt], links.mate(r)) for r in (1, 2, 3)
    ]
    tables = Frames(utts, lengths_ref)
    first_row = pl.multiple_of(links.seq * rows, rows)
    own_rows = pl.ds(first_row, rows)
    frame = frame_column(links.seq * rows, rows)
    segment = tables.segment(frame)
    position = frame - tables.of(segment, tables.starts)
    prompt = tables.of(segment, [chars_ref[0, u] for u in range(utts)])
    in_loss = jnp.where(position >= prompt, 1.0, 0.0)
    across = lax.broadcasted_iota(jnp.int32, (rows, rows), 1)
    down = lax.broadcasted_iota(jnp.int32, (rows, rows), 0)
    dropped = jnp.sum(
        jnp.where(across == down, drop_ref[...].astype(jnp.float32), 0.0), axis=1, keepdims=True
    )
    lane = lax.broadcasted_iota(jnp.int32, sums_ref.shape, 1)
    n_drop = jnp.sum(in_loss * dropped, axis=0, keepdims=True)
    n_keep = jnp.sum(in_loss * (1.0 - dropped), axis=0, keepdims=True)
    sums_ref[...] = jnp.where(lane == 0, n_drop, jnp.where(lane == 1, n_keep, 0.0))
    targets = [links.mate(1), links.mate(2), links.peer(1), links.peer(2), links.peer(4)]
    turn = []

    def count_turn():
        place = len(turn)
        if place > 0:
            turn[-1].wait_recv()
            sums_ref[...] = sums_ref[...] + counts_got[place - 1]
        if place < 5:
            counts_got[5 + place] = sums_ref[...]
            turn.append(
                links.send(counts_got.at[5 + place], counts_got.at[place], targets[place])
            )

    count_turn()
    quarter = total_rows // 4
    for j in range(4):
        here, lanes = slice(j * quarter, (j + 1) * quarter), slice(32 * j, 32 * (j + 1))
        cosines, sines = cos_in[:, lanes], sin_in[:, lanes]
        cos_ref[here, :] = jnp.concatenate([cosines] * 4, axis=1)
        sin_ref[here, :] = jnp.concatenate([-sines, sines] * 2, axis=1)
    load_skip.wait()
    load_qkv = links.keep(w_qkv_ref, w_qkv)
    residual = (
        jnp.dot(frames_ref[...], w_skip[0:model, :], preferred_element_type=jnp.float32)
        + jnp.dot(skip_ref[...], w_skip[model:, :], preferred_element_type=jnp.float32)
        + b_skip_ref[...]
    )
    resid_ref[...] = residual
    count_turn()

    def modulate_columns(columns):
        mod_ref[:, columns] = (
            jnp.dot(act_ref[...], w_mod[:, columns], preferred_element_type=jnp.float32)
            + b_mod_ref[:, columns]
        )

    load_early.wait()
    load_late = links.keep(w_mod_ref.at[:, late], w_mod.at[:, late])
    modulate_columns(slice(0, 2 * model))
    unit, _ = normal_parts(residual)
    norm_ref[...] = (
        unit * (1.0 + per_frame(mod_ref, segment, utts, 1, model))
        + per_frame(mod_ref, segment, utts, 0, model)
    ).astype(jnp.bfloat16)
    gathers.append(Gathered(links, norm_ref, norm_all))
    count_turn()
    load_qkv.wait()
    cos, sin = cos_ref[own_rows, :], sin_ref[own_rows, :]
    lower = lower_half((rows, 128))

    def project(place, base):
        columns = pl.ds(pl.multiple_of(base + place * 128, 128), 128)
        return (
            jnp.dot(norm_ref[...], w_qkv[:, columns], preferred_element_type=jnp.float32)
            + b_qkv_ref[:, columns]
        )

    def pack(place):
        q, k = project(place, 0), project(place, model)
        packed[place, :, 0:128] = (q * cos + swap_halves(q, lower) * sin).astype(jnp.bfloat16)
        packed[place, :, 128:256] = (k * cos + swap_halves(k, lower) * sin).astype(jnp.bfloat16)
        packed[place, :, 256:384] = project(place, 2 * model).astype(jnp.bfloat16)

    incoming = []
    for r in FAR_FIRST:
        place = links.seq_of(r)
        pack(place)
        incoming.append(
            links.send(packed.at[place], heads_ref.at[own_rows, :], links.peer(r))
        )
    pack(links.seq)
    own = links.keep(packed.at[links.seq], heads_ref.at[own_rows, :])
    count_turn()
    load_late.wait()
    modulate_columns(slice(2 * model, 6 * model))
    count_turn()
    gathers[0].relay()
    gathers[1].relay()
    count_turn()
    n_drop, n_keep = sums_ref[0:1, 0:1], sums_ref[0:1, 1:2]
    loss_weight = (
        in_loss
        * (n_drop + n_keep)
        * 0.5
        * (dropped / (n_drop + 1.0) + (1.0 - dropped) / (n_keep + 1.0))
    )
    loss_ref[...] = jnp.broadcast_to(loss_weight, loss_ref.shape)
    d_out = out_grad_ref[...].astype(jnp.float32) * loss_weight
    d_ff_ref[...] = (per_frame(mod_ref, segment, utts, 5, model) * d_out).astype(jnp.bfloat16)
    gathers.append(Gathered(links, d_ff_ref, d_ff_all))
    own.wait()
    for copy in incoming:
        copy.wait_recv()
    first = lax.broadcasted_iota(jnp.int32, (rows, 128), 1) < HEAD_DIM
    zero = jnp.zeros((rows, 128), jnp.bfloat16)
    k, v = heads_ref[:, 128:256], heads_ref[:, 256:384]
    seg_k = tables.segment(lax.broadcasted_iota(jnp.int32, (1, total_rows), 1))
    part = lambda place: pl.ds(pl.multiple_of(place * rows, rows), rows)
    column = attn_ref.at[:, pl.ds(pl.multiple_of(links.seq * 128, 128), 128)]

    def attend_rows(place):
        here = part(place)
        q, seg_q = heads_ref[here, 0:128], tables.segment(frame_column(place * rows, rows))
        results = []
        for mine in (first, jnp.logical_not(first)):
            weights = head_scores(jnp.where(mine, q, zero), k, seg_q, seg_k)
            total = jnp.sum(weights, axis=1, keepdims=True)
            summed = jnp.dot(weights.astype(jnp.bfloat16), v, preferred_element_type=jnp.float32)
            results.append((summed, total))
        total = jnp.where(first, results[0][1], results[1][1])
        attended = jnp.where(first, results[0][0], results[1][0]) / total
        attn_heads[here, :] = attended.astype(jnp.bfloat16)
        exact_ref[here, :] = attended
        total_ref[here, :] = total

    incoming = []
    for r in FAR_FIRST:
        place = links.seq_of(r)
        attend_rows(place)
        incoming.append(links.send(attn_heads.at[part(place), :], column, links.peer(r)))
    attend_rows(links.seq)
    own = links.keep(attn_heads.at[part(links.seq), :], column)
    gathers[2].relay()
    gathers[3].relay()
    act_own.wait()
    for copy in act_copies:
        copy.wait_recv()
    own.wait()
    for copy in incoming:
        copy.wait_recv()
    for gather in gathers:
        gather.wait()
    links.leave()


def attend(
    lengths, chars, drop, act, cos, sin, frames, skip, out_grad, b_skip, b_mod, b_qkv, w_skip,
    w_mod, w_qkv, shards,
):
    rows, width = frames.shape
    total_rows = shards * rows
    utts = lengths.shape[1]
    vmem, there, scalar = everywhere(pltpu.VMEM), everywhere(pl.ANY), everywhere(pltpu.SMEM)
    shape = jax.ShapeDtypeStruct
    bf16 = lambda *dims: pltpu.VMEM(dims, jnp.bfloat16)
    return pl.pallas_call(
        partial(attend_kernel, utts),
        in_specs=[scalar] * 2 + [vmem] * 10 + [there] * 3,
        out_specs=[vmem] * 5 + [there] * 3 + [vmem] * 5 + [there],
        out_shape=[
            shape((rows, width), jnp.bfloat16),
            shape((total_rows, 384), jnp.bfloat16),
            shape((total_rows, 128), jnp.float32),
            shape((total_rows, 128), jnp.float32),
            shape((rows, 128), jnp.float32),
            shape((4,) + act.shape, act.dtype),
            shape((4 * rows, width), jnp.bfloat16),
            shape((4 * rows, 2 * width), jnp.bfloat16),
            shape((rows, width), jnp.float32),
            shape((8, 6 * width), jnp.float32),
            shape((total_rows, 128), jnp.float32),
            shape((total_rows, 128), jnp.float32),
            shape((rows, width), jnp.bfloat16),
            shape((4 * rows, width), jnp.bfloat16),
        ],
        scratch_shapes=[
            bf16(total_rows, 128),
            pltpu.VMEM((10, 8, 128), jnp.float32),
            pltpu.VMEM((8, 128), jnp.float32),
            bf16(shards, rows, 384),
            bf16(rows, width),
            bf16(*w_skip.shape),
            bf16(*w_mod.shape),
            bf16(*w_qkv.shape),
        ]
        + semaphores(40),
        compiler_params=comm_params(1),
    )(
        lengths, chars, drop, act, cos, sin, frames, skip, out_grad,
        b_skip[None, :], b_mod[None, :], b_qkv[None, :], w_skip, w_mod, w_qkv,
    )


ALONG = (((1,), (1,)), ((), ()))
DOWN = (((0,), (0,)), ((), ()))


def normal_parts(values):
    centred = values - jnp.mean(values, axis=1, keepdims=True)
    scale = lax.rsqrt(jnp.mean(centred * centred, axis=1, keepdims=True) + EPSILON)
    return centred * scale, scale


def normal_back(inward, unit, scale):
    return scale * (
        inward
        - jnp.mean(inward, axis=1, keepdims=True)
        - unit * jnp.mean(inward * unit, axis=1, keepdims=True)
    )


def column_sum(values):
    return jnp.sum(values.astype(jnp.float32), axis=0, keepdims=True)


def backward_kernel(
    utts, lengths_ref, attn_ref, resid_ref, mod_ref, loss_ref, out_grad_ref, d_ff,
    b_out_ref, b_up_ref, b_down_ref,
    heads_in, exact_in, total_in, cos_in, sin_in,
    norm_a_ref, joined_ref, d_ff_ref, w_out_ref, w_up_ref, w_down_ref, w_qkv_ref, w_skip_ref,
    mixed_out, down_out, up_out, out_out, qkv_out, skip_out, smalls_out, frames_out, skip_in_out,
    mixed, g_down, g_up, g_out, g_qkv, g_skip, smalls, g_frames, g_skip_in,
    norm_f, act, d_inner, d_branch, d_attn, pieces, d_mid, ff_sum, d_norm,
    grad_heads, d_heads, dk_ref, dv_ref,
    d_ff_all, act_all, norm_all, d_inner_all, attn_all, d_branch_all,
    norm_a_all, joined_all, d_qkv, d_qkv_all, d_resid, d_resid_all,
    heads_ref, exact_ref, total_ref, cos_ref, sin_ref,
    up_ring, down_ring, w_out, w_qkv, w_skip, small_own, small_got, small_out,
    *rest,
):
    tiles, (send_sems, recv_sems, local_sems, ring_sems) = rest[:-4], rest[-4:]
    links = Links(send_sems, recv_sems, local_sems)
    rows, model = resid_ref.shape
    block_width = up_ring.shape[2]
    steps = w_up_ref.shape[1] // block_width

    zh = links.seq // 4

    def chunk(c):
        return (c + (1 - zh) * (steps // 2)) % steps

    def ring(c):
        slot = c % 2
        columns = pl.ds(pl.multiple_of(chunk(c) * block_width, block_width), block_width)
        return (
            pltpu.make_async_copy(w_up_ref.at[:, columns], up_ring.at[slot], ring_sems.at[slot]),
            pltpu.make_async_copy(
                w_down_ref.at[columns, :], down_ring.at[slot], ring_sems.at[2 + slot]
            ),
        )

    load_out = links.keep(w_out_ref, w_out)
    load_d = links.keep(d_ff_ref, d_ff_all)
    for c in (0, 1):
        for copy in ring(c):
            copy.start()
    head_loads = [
        links.keep(source, target)
        for source, target in (
            (heads_in, heads_ref), (exact_in, exact_ref), (total_in, total_ref),
            (cos_in, cos_ref), (sin_in, sin_ref),
        )
    ]
    loads = [
        links.keep(w_qkv_ref, w_qkv),
        links.keep(w_skip_ref, w_skip),
        links.keep(norm_a_ref, norm_a_all),
        links.keep(joined_ref, joined_all),
    ]
    links.enter((1, 2, 3), range(1, 8))

    tables = Frames(utts, lengths_ref)
    segment = tables.segment(frame_column(links.seq * rows, rows))

    def modulation(piece):
        return per_frame(mod_ref, segment, utts, piece, model)

    def d_out():
        return out_grad_ref[...].astype(jnp.float32) * loss_ref[:, 0:1]

    load_out.wait()
    branch = (
        jnp.dot(attn_ref[...], w_out[...], preferred_element_type=jnp.float32) + b_out_ref[...]
    )
    pieces[0] = branch
    mid = resid_ref[...] + modulation(2) * branch
    d_mid[...] = mid
    unit, _ = normal_parts(mid)
    norm_f[...] = (unit * (1.0 + modulation(4)) + modulation(3)).astype(jnp.bfloat16)
    ff_sum[...] = jnp.zeros_like(ff_sum)
    d_norm[...] = jnp.zeros_like(d_norm)
    const = math.sqrt(2.0 / math.pi)
    width = d_inner_all.shape[1]

    def feed(c, _):
        slot = c % 2
        columns = pl.ds(pl.multiple_of(chunk(c) * block_width, block_width), block_width)
        for copy in ring(c):
            copy.wait()
        inner = (
            jnp.dot(norm_f[...], up_ring[slot], preferred_element_type=jnp.float32)
            + b_up_ref[:, columns]
        )
        square = inner * inner
        slope = jnp.tanh(const * inner * (1.0 + 0.044715 * square))
        gate = 0.5 * (1.0 + slope)
        act_b = (inner * gate).astype(jnp.bfloat16)
        turn = gate + 0.5 * inner * (1.0 - slope * slope) * (
            const * (1.0 + 3.0 * 0.044715 * square)
        )
        here = pl.ds(pl.multiple_of(chunk(c) * 128, 128), 128)
        d_act = lax.dot_general(
            d_ff[...], down_ring[slot], ALONG, preferred_element_type=jnp.float32
        )
        d_inner_b = (turn * d_act).astype(jnp.bfloat16)
        for u in range(4):
            act[u, :, here] = act_b[:, u * 128 : (u + 1) * 128]
            d_inner[u, :, here] = d_inner_b[:, u * 128 : (u + 1) * 128]
        ff_sum[...] += jnp.dot(act_b, down_ring[slot], preferred_element_type=jnp.float32)
        d_norm[...] += lax.dot_general(
            d_inner_b, up_ring[slot], ALONG, preferred_element_type=jnp.float32
        )

        @pl.when(c + 2 < steps)
        def _():
            for copy in ring(c + 2):
                copy.start()

        return 0

    middle = width // 2
    half_at = lambda place: pl.ds(pl.multiple_of(place * middle, middle), middle)
    far_half, near_half = half_at(1 - zh), half_at(zh)
    lax.fori_loop(0, steps // 2, feed, 0)
    quarters_a = [Quarter(links, lambda u: act.at[u, :, far_half], act_all, far_half)]
    lax.fori_loop(steps // 2, steps, feed, 0)
    quarters_a.append(Quarter(links, lambda u: act.at[u, :, near_half], act_all, near_half))
    gather_n = Gathered(links, norm_f, norm_all)
    own_rows = pl.ds(pl.multiple_of(links.seq * rows, rows), rows)
    strip = lambda ref, place, size: ref.at[
        :, pl.ds(pl.multiple_of(place * size, size), size)
    ]
    narrow = d_branch_all.shape[1]
    quarter_i = Quarter(links, lambda u: d_inner.at[u], d_inner_all)
    mid = d_mid[...]
    unit, scale = normal_parts(mid)
    d_norm_f = d_norm[...]
    pieces[2] = d_norm_f * unit
    d_mid_f = d_out() + normal_back(d_norm_f * (1.0 + modulation(4)), unit, scale)
    gate_a = modulation(2)
    d_branch[...] = (gate_a * d_mid_f).astype(jnp.bfloat16)
    pieces[0] = pieces[0] * d_mid_f
    d_mid[...] = d_mid_f
    d_attn[...] = lax.dot_general(
        d_branch[...], w_out[...], ALONG, preferred_element_type=jnp.float32
    ).astype(jnp.bfloat16)
    own = links.keep(strip(d_attn, links.seq, 128), grad_heads.at[own_rows, :])
    incoming_d = [
        links.send(
            strip(d_attn, links.seq_of(r), 128), grad_heads.at[own_rows, :], links.peer(r)
        )
        for r in FAR_FIRST
    ]
    quarter_b = Quarter(links, lambda u: strip(d_branch, u, narrow), d_branch_all)
    gather_b = Gathered(links, attn_ref, attn_all)
    half = width // 2
    down_at = lambda h: lambda u: g_down.at[
        pl.ds(pl.multiple_of(u * 128, 128), 128), pl.ds(h * half, half)
    ]
    column_at = lambda ref, step, offset, size: lambda u: ref.at[
        :, pl.ds(pl.multiple_of(u * step + offset, 128), size)
    ]
    wide, thin = d_qkv_all.shape[1], d_resid_all.shape[1]
    third, slim = wide // 2, thin // 2
    plans = [
        (act_all, d_ff_all, pl.ds(0, half), down_at(0)),
        (act_all, d_ff_all, pl.ds(half, half), down_at(1)),
        (norm_all, d_inner_all, pl.ds(0, half), column_at(g_up, width, 0, half)),
        (norm_all, d_inner_all, pl.ds(half, half), column_at(g_up, width, half, half)),
        (attn_all, d_branch_all, pl.ds(0, narrow), column_at(g_out, narrow, 0, narrow)),
        (norm_a_all, d_qkv_all, pl.ds(0, third), column_at(g_qkv, wide, 0, third)),
        (norm_a_all, d_qkv_all, pl.ds(third, third), column_at(g_qkv, wide, third, third)),
        (joined_all, d_resid_all, pl.ds(0, slim), column_at(g_skip, thin, 0, slim)),
        (joined_all, d_resid_all, pl.ds(slim, slim), column_at(g_skip, thin, slim, slim)),
    ]
    y_first = (True,) * 9
    shares = [
        Share(links, y_first[i], left, right, columns, *tiles[4 * i : 4 * i + 4], result)
        for i, (left, right, columns, result) in enumerate(plans)
    ]
    load_d.wait()
    quarters_a[0].wait()
    shares[0].start_far()
    shares[1].start_far()
    ff_out = ff_sum[...] + b_down_ref[...]
    mixed[...] = (mid + modulation(5) * ff_out).astype(jnp.bfloat16)
    saved = [links.keep(mixed, mixed_out)]
    pieces[1] = d_out() * ff_out
    small_own[...] = jnp.zeros_like(small_own)
    small_own[4:5, :] = column_sum(d_branch[...])
    for c in range(4):
        small_own[5 + c : 6 + c, :] = column_sum(d_inner[c])
    small_own[9:10, :] = column_sum(d_ff[...])

    def utterance_sums(piece, values):
        for u in range(utts):
            row = 10 + utts * piece + u
            small_own[row : row + 1, :] = jnp.sum(
                jnp.where(segment == u, values, 0.0), axis=0, keepdims=True
            )

    utterance_sums(2, pieces[0])
    utterance_sums(3, d_norm[...])
    utterance_sums(4, pieces[2])
    utterance_sums(5, pieces[1])
    gather_n.relay()
    quarters_a[1].wait()
    shares[0].start_near()
    shares[1].start_near()
    own.wait()
    for copy in incoming_d:
        copy.wait_recv()
    for copy in head_loads:
        copy.wait()
    dk_ref[...] = jnp.zeros_like(dk_ref)
    dv_ref[...] = jnp.zeros_like(dv_ref)
    first = lax.broadcasted_iota(jnp.int32, (256, 128), 1) < HEAD_DIM
    zero = jnp.zeros((256, 128), jnp.bfloat16)
    lower = lower_half((256, 128))
    k, v = heads_ref[:, 128:256], heads_ref[:, 256:384]
    seg_k = tables.segment(lax.broadcasted_iota(jnp.int32, (1, heads_ref.shape[0]), 1))

    def turned(values, here):
        return (
            values * cos_ref[here, :] - swap_halves(values, lower) * sin_ref[here, :]
        ).astype(jnp.bfloat16)

    def block(step, _):
        here = pl.ds(pl.multiple_of(step * 256, 256), 256)
        q, seg_q = heads_ref[here, 0:128], tables.segment(frame_column(step * 256, 256))
        scaled = grad_heads[here, :].astype(jnp.float32) / total_ref[here, :]
        grad_acc = scaled.astype(jnp.bfloat16)
        product = scaled * exact_ref[here, :]
        d_query = []
        for mine in (first, jnp.logical_not(first)):
            q_own = jnp.where(mine, q, zero)
            g_own = jnp.where(mine, grad_acc, zero)
            delta = jnp.sum(jnp.where(mine, product, 0.0), axis=1, keepdims=True)
            weights = head_scores(q_own, k, seg_q, seg_k)
            dots = lax.dot_general(g_own, v, ALONG, preferred_element_type=jnp.float32)
            d_scores = (weights * (dots - delta)).astype(jnp.bfloat16)
            d_query.append(jnp.dot(d_scores, k, preferred_element_type=jnp.float32))
            dk_ref[...] += lax.dot_general(
                d_scores, q_own, DOWN, preferred_element_type=jnp.float32
            )
            dv_ref[...] += lax.dot_general(
                weights.astype(jnp.bfloat16), g_own, DOWN, preferred_element_type=jnp.float32
            )
        d_heads[here, 0:128] = turned(jnp.where(first, d_query[0], d_query[1]) * 0.125, here)
        return 0

    blocks = heads_ref.shape[0] // 256
    lax.fori_loop(0, blocks, block, 0)

    def finish(step, _):
        here = pl.ds(pl.multiple_of(step * 256, 256), 256)
        d_heads[here, 128:256] = turned(dk_ref[here, :] * 0.125, here)
        d_heads[here, 256:384] = dv_ref[here, :].astype(jnp.bfloat16)
        return 0

    lax.fori_loop(0, blocks, finish, 0)
    part = lambda place, c: d_heads.at[
        pl.ds(pl.multiple_of(place * rows, rows), rows), pl.ds(c * 128, 128)
    ]
    home = lambda c: d_qkv.at[
        :, pl.ds(pl.multiple_of(c * model + links.seq * 128, 128), 128)
    ]
    owns = [links.keep(part(links.seq, c), home(c)) for c in range(3)]
    incoming = [
        links.send(part(links.seq_of(r), c), home(c), links.peer(r))
        for r in FAR_FIRST
        for c in range(3)
    ]
    gather_n.wait()
    quarter_i.wait()
    state = {}

    def output_share():
        gather_b.relay()
        gather_b.wait()
        quarter_b.wait()
        shares[4].start()

    def projections():
        for copy in owns:
            copy.wait()
        for copy in incoming:
            copy.wait_recv()
        for copy in loads:
            copy.wait()
        state["qkv"] = Quarter(links, lambda u: strip(d_qkv, u, wide), d_qkv_all)
        d_norm_a = lax.dot_general(
            d_qkv[...], w_qkv[...], ALONG, preferred_element_type=jnp.float32
        )
        unit, scale = normal_parts(resid_ref[...])
        d_resid_f = d_mid[...] + normal_back(d_norm_a * (1.0 + modulation(1)), unit, scale)
        rounded = d_resid_f.astype(jnp.bfloat16)
        d_resid[...] = rounded
        state["resid"] = Quarter(links, lambda u: strip(d_resid, u, thin), d_resid_all)
        small_own[0:1, :] = column_sum(rounded)
        for c in range(3):
            small_own[1 + c : 2 + c, :] = column_sum(d_qkv[:, c * model : (c + 1) * model])
        utterance_sums(0, d_norm_a)
        utterance_sums(1, d_norm_a * unit)
        small_out[0] = small_own[...].astype(jnp.bfloat16)
        state["small"] = links.send(small_out.at[0], small_got.at[0], links.peer(1))

    def qkv_shares():
        state["qkv"].wait()
        shares[5].start()
        shares[6].start()

    def skip_shares():
        state["resid"].wait()
        shares[7].start()
        shares[8].start()

    def inputs():
        for index, out in enumerate((g_frames, g_skip_in)):
            out[...] = lax.dot_general(
                d_resid[...],
                w_skip[pl.ds(index * model, model), :],
                ALONG,
                preferred_element_type=jnp.float32,
            ).astype(jnp.bfloat16)

    def small_y():
        state["small"].wait_recv()
        small_own[...] += small_got[0].astype(jnp.float32)
        small_out[1] = small_own[...].astype(jnp.bfloat16)
        state["small"] = links.send(small_out.at[1], small_got.at[1], links.peer(2))

    def small_z1():
        state["small"].wait_recv()
        small_own[...] += small_got[1].astype(jnp.float32)
        small_out[2] = small_own[...].astype(jnp.bfloat16)
        state["small"] = links.send(small_out.at[2], small_got.at[2], links.peer(4))

    def small_z2():
        state["small"].wait_recv()
        mine = smalls.at[links.utt]
        mine[...] = (small_own[...] + small_got[2].astype(jnp.float32)).astype(jnp.bfloat16)
        state["spread"] = [links.send(mine, mine, links.mate(r)) for r in (2, 3, 1)]

    def save(*pairs):
        return lambda: saved.extend(links.keep(source, target) for source, target in pairs)

    stages = ("start", "after_a", "after_b", "after_z2", "relay", "wait")
    s, a, b, z, r, w = ([getattr(share, stage) for share in shares] for stage in stages)
    for step in (
        s[2], a[0], a[1], s[3],
        output_share, projections,
        a[2], b[0], b[1],
        qkv_shares,
        z[0], b[2],
        small_y, inputs, save((g_frames, frames_out), (g_skip_in, skip_in_out)),
        z[1], z[2],
        skip_shares,
        a[3], r[0], r[1],
        small_z1,
        a[4], b[3], r[2], z[3], b[4],
        small_z2,
        w[0], w[1], save((g_down, down_out)), a[5], z[4], r[3], b[5], w[2], a[6], r[4], z[5], b[6], w[3], save((g_up, up_out)), a[7], r[5],
        z[6], b[7], w[4], save((g_out, out_out)), a[8], b[8], z[7], r[6], w[5], z[8], r[7], w[6], save((g_qkv, qkv_out)), r[8], w[7], w[8], save((g_skip, skip_out)),
    ):
        step()
    for copy in state["spread"]:
        copy.wait_recv()
    save((smalls, smalls_out))()
    for copy in saved:
        copy.wait()
    links.leave()


def backward(
    lengths, attn_b, resid, mod, loss, out_grad, d_ff, b_out, b_up, b_down,
    heads, exact, total, cos, sin,
    norm_a_all, joined_all, d_ff_all, w_out, w_up, w_down, w_qkv, w_skip,
):
    rows, model = resid.shape
    frames, inner = heads.shape[0], w_up.shape[1]
    utts = lengths.shape[1]
    small = (-(-(10 + 6 * utts) // 16) * 16, model)
    vmem, there = everywhere(pltpu.VMEM), everywhere(pl.ANY)
    shape = jax.ShapeDtypeStruct
    bf16 = lambda *dims: pltpu.VMEM(dims, jnp.bfloat16)
    f32 = lambda *dims: pltpu.VMEM(dims, jnp.float32)
    part, step = model // 8, inner // 8
    outs = [
        shape((rows, model), jnp.bfloat16),
        shape((inner // 8, model), jnp.bfloat16),
        shape((part, inner), jnp.bfloat16),
        shape((part, model), jnp.bfloat16),
        shape((part, 3 * model), jnp.bfloat16),
        shape((2 * part, model), jnp.bfloat16),
        shape((4,) + small, jnp.bfloat16),
        shape((rows, model), jnp.bfloat16),
        shape((rows, model), jnp.bfloat16),
    ]
    return pl.pallas_call(
        partial(backward_kernel, utts),
        in_specs=[everywhere(pltpu.SMEM)] + [vmem] * 9 + [there] * 13,
        out_specs=[there] * 9,
        out_shape=outs,
        scratch_shapes=[pltpu.VMEM(out.shape, out.dtype) for out in outs]
        + [
            bf16(rows, model),
            bf16(4, rows, inner // 4),
            bf16(4, rows, inner // 4),
            bf16(rows, model),
            bf16(rows, model),
            f32(3, rows, model),
            f32(rows, model),
            f32(rows, model),
            f32(rows, model),
            bf16(frames, 128),
            bf16(frames, 384),
            f32(frames, 128),
            f32(frames, 128),
            bf16(4 * rows, model),
            bf16(4 * rows, inner // 4),
            bf16(4 * rows, model),
            bf16(4 * rows, inner // 4),
            bf16(4 * rows, model),
            bf16(4 * rows, model // 4),
            bf16(4 * rows, model),
            bf16(4 * rows, 2 * model),
            bf16(rows, 3 * model),
            bf16(4 * rows, 3 * model // 4),
            bf16(rows, model),
            bf16(4 * rows, model // 4),
            bf16(frames, 384),
            f32(frames, 128),
            f32(frames, 128),
            f32(frames, 128),
            f32(frames, 128),
            bf16(2, model, step),
            bf16(2, step, model),
            bf16(*w_out.shape),
            bf16(*w_qkv.shape),
            bf16(*w_skip.shape),
            f32(*small),
            bf16(3, *small),
            bf16(3, *small),
        ]
        + share_scratch(part, inner // 8) * 4
        + share_scratch(part, model // 4)
        + share_scratch(part, 3 * model // 8) * 2
        + share_scratch(2 * part, model // 8) * 2
        + semaphores(160)
        + [pltpu.SemaphoreType.DMA((4,))],
        compiler_params=comm_params(2),
    )(
        lengths, attn_b, resid, mod, loss, out_grad, d_ff,
        b_out[None, :], b_up[None, :], b_down[None, :],
        heads, exact, total, cos, sin,
        norm_a_all, joined_all, d_ff_all, w_out, w_up, w_down, w_qkv, w_skip,
    )


UP = 3


def finish_kernel(utts, shards, *rest):
    kept_in, wide_in, smalls_in, act_in = rest[:3], rest[3:8], rest[8], rest[9]
    rest = rest[1:]
    kept_out, wide_out, mod_out, bias_out = rest[9:12], rest[12:17], rest[17], rest[18:24]
    kept, wide, staged = rest[24:27], rest[27:32], rest[32:37]
    smalls_got, act_got, bias_stage = rest[37], rest[38], rest[39:45]
    smalls_ref, act_rows, mod_stage, d_mod, totals, sems, load_sems = rest[45:]
    seq = lax.axis_index("seq")
    loads, copies = [], []
    for source, target in zip(
        (*wide_in, smalls_in, act_in, *kept_in), (*wide, smalls_got, act_got, *kept)
    ):
        copy = pltpu.make_async_copy(source, target, load_sems.at[len(loads)])
        copy.start()
        loads.append(copy)

    def put(source, target):
        copy = pltpu.make_async_copy(source, target, sems.at[len(copies)])
        copy.start()
        copies.append(copy)

    model = smalls_ref.shape[2]
    lanes = 128
    for place, (source, stage, target) in enumerate(zip(wide, staged, wide_out)):
        loads[place].wait()
        if place == UP:
            for u in range(4):
                for c in range(shards):
                    stage[:, (4 * c + u) * lanes : (4 * c + u + 1) * lanes] = source[
                        :, u * model + c * lanes : u * model + (c + 1) * lanes
                    ].astype(jnp.float32)
        else:
            stage[...] = source[...].astype(jnp.float32)
        put(stage, target)
    groups = smalls_ref.shape[0]
    loads[5].wait()
    smalls_ref[...] = smalls_got[...].astype(jnp.float32)
    loads[6].wait()
    act_rows[...] = jnp.zeros_like(act_rows)
    own = act_rows.shape[1]
    own_columns = pl.ds(pl.multiple_of(seq * own, own), own)
    for g in range(groups):
        act_rows[g * utts : (g + 1) * utts, :] = act_got[g, :, own_columns].astype(jnp.float32)[
            0:utts
        ]
    bias_sum = (
        smalls_ref[0, 0:10] + smalls_ref[1, 0:10] + smalls_ref[2, 0:10] + smalls_ref[3, 0:10]
    )
    for row in range(10):
        totals[row, 0:1] = bias_sum[row : row + 1]
    d_mod[...] = jnp.zeros_like(d_mod)
    for piece in range(6):
        first = 10 + utts * piece
        for g in range(groups):
            d_mod[piece, g * utts : (g + 1) * utts, :] = smalls_ref[g, first : first + utts, :]
        rows = d_mod[piece]
        totals[10 + piece, 0:1] = jnp.sum(rows, axis=0, keepdims=True)
        columns = slice(piece * model, (piece + 1) * model)
        mod_stage[:, columns] = lax.dot_general(
            act_rows[...],
            rows,
            DOWN,
            precision=HIGHEST_PRECISION,
            preferred_element_type=jnp.float32,
        )
    put(mod_stage, mod_out)
    for load, source, target in zip(loads[7:], kept, kept_out):
        load.wait()
        put(source, target)
    line = model // lanes
    first = 0
    for place, target in enumerate(bias_out):
        count = target.shape[0] // lanes
        for i in range(count):
            unit = i * line + seq if place == UP else seq * count + i
            column = pl.multiple_of((unit % line) * lanes, lanes)
            bias_stage[place][i * lanes : (i + 1) * lanes] = totals[
                first + unit // line, 0, pl.ds(column, lanes)
            ]
        first += count * shards // line
        put(bias_stage[place], target)
    for copy in copies:
        copy.wait()


def finish(shards, utts, acts, smalls, mixed, frames, skip, grads):
    there = everywhere(pl.ANY)
    shape = jax.ShapeDtypeStruct
    model = smalls.shape[2]
    own = model // shards
    depth = -(-acts.shape[0] * utts // 8) * 8
    mod_shape = (own, 6 * model)
    widths = [own, 3 * own, own, 4 * own, own, 6 * own]
    kept = (mixed, frames, skip)
    outs = pl.pallas_call(
        partial(finish_kernel, utts, shards),
        in_specs=[there] * 10,
        out_specs=[there] * 15,
        out_shape=[shape(v.shape, v.dtype) for v in kept]
        + [shape(g.shape, jnp.float32) for g in grads]
        + [shape(mod_shape, jnp.float32)]
        + [shape((w,), jnp.float32) for w in widths],
        scratch_shapes=[pltpu.VMEM(v.shape, v.dtype) for v in (*kept, *grads)]
        + [pltpu.VMEM(g.shape, jnp.float32) for g in grads]
        + [
            pltpu.VMEM(smalls.shape, smalls.dtype),
            pltpu.VMEM(acts.shape, acts.dtype),
        ]
        + [pltpu.VMEM((w,), jnp.float32) for w in widths]
        + [
            pltpu.VMEM(smalls.shape, jnp.float32),
            pltpu.VMEM((depth, own), jnp.float32),
            pltpu.VMEM(mod_shape, jnp.float32),
            pltpu.VMEM((6, depth, model), jnp.float32),
            pltpu.VMEM((16, 8, model), jnp.float32),
            pltpu.SemaphoreType.DMA((15,)),
            pltpu.SemaphoreType.DMA((10,)),
        ],
        compiler_params=pltpu.CompilerParams(vmem_limit_bytes=VMEM_LIMIT),
    )(*kept, *grads, smalls, acts)
    return outs[:9], outs[9:]


def compact_tables(lengths, total_rows):
    half_dim = HEAD_DIM // 2
    shape = (total_rows // 4, 128)
    lane = lax.broadcasted_iota(jnp.int32, shape, 1)
    frame = lax.broadcasted_iota(jnp.int32, shape, 0) + (lane // half_dim) * shape[0]
    start, end = jnp.zeros(shape, jnp.int32), jnp.int32(0)
    for u in range(lengths.shape[0]):
        end = end + lengths[u]
        start = jnp.where(frame >= end, end, start)
    inverse = jnp.exp(
        -math.log(10000.0) * 2.0 * (lane % half_dim).astype(jnp.float32) / HEAD_DIM
    )
    angles = (frame - start).astype(jnp.float32) * inverse
    return jnp.cos(angles), jnp.sin(angles)


def padded_time_act(flow_vals, model):
    half_dim = model // 2
    column = jnp.arange(model, dtype=jnp.int32)
    inverse = jnp.exp(-math.log(10000.0) * (column % half_dim).astype(jnp.float32) / half_dim)
    flow_vals = jnp.pad(flow_vals, (0, 8 - flow_vals.shape[0]))
    angles = 1000.0 * flow_vals[:, None] * inverse[None, :]
    wave = jnp.where((column < half_dim)[None, :], jnp.sin(angles), jnp.cos(angles))
    return jax.nn.silu(wave).astype(jnp.bfloat16)


def local(
    frames_in,
    skip_in,
    flow_times,
    frame_lengths,
    char_lengths,
    drop_mask,
    out_grad,
    w_skip,
    b_skip,
    w_mod,
    b_mod,
    w_qkv,
    b_qkv,
    w_out,
    b_out,
    w_up,
    b_up,
    w_down,
    b_down,
):
    local_rows = frames_in.shape[1]
    model_width = frames_in.shape[2]
    shards = lax.axis_size("seq")
    seq_place = lax.axis_index("seq")
    lengths = frame_lengths[0]
    whole = model_width * 4
    fused = (
        lax.axis_size("utt") == 4
        and shards == 8
        and HEADS * HEAD_DIM == 1024
        and model_width == 1024
        and w_up.shape[1] == whole
        and local_rows == 128
        and flow_times.shape[1] <= 8
    )
    if not fused:
        utt_ends = jnp.cumsum(lengths)
        segment, position, in_loss, member = frame_tables(
            lengths, char_lengths[0], seq_place * local_rows, local_rows
        )
        member_f = member.astype(jnp.float32)
        loss_mask = in_loss.astype(jnp.float32)
        dropped = drop_mask[0].astype(jnp.float32)
        counts = jnp.stack([jnp.sum(loss_mask * dropped), jnp.sum(loss_mask * (1.0 - dropped))])
        counts = jnp.pad(counts[None, :], ((0, 7), (0, 126)))
        counts = xor_sum(xor_sum(counts, "utt"), "seq")
        time_act = jax.nn.silu(time_embed(flow_times[0], model_width)).astype(jnp.bfloat16)
        mod_u = jnp.dot(time_act, w_mod, preferred_element_type=jnp.float32) + b_mod
        mod_f = jnp.dot(member_f, mod_u, precision=HIGHEST_PRECISION)
        shift_a, scale_a, gate_a, shift_f, scale_f, gate_f = jnp.split(mod_f, 6, axis=1)
        joined = jnp.concatenate([frames_in[0], skip_in[0]], axis=1)
        residual = jnp.dot(joined, w_skip, preferred_element_type=jnp.float32) + b_skip
        norm_a = modulate(residual, scale_a, shift_a).astype(jnp.bfloat16)
        qkv_full = jnp.dot(norm_a, w_qkv, preferred_element_type=jnp.float32) + b_qkv
    if fused:
        (
            attn_b, qkv_heads, exact, total, loss, acts, norm_all, joined_all,
            residual, mod_u, cos_all, sin_all, d_ff, d_ff_all,
        ) = attend(
            frame_lengths,
            char_lengths,
            drop_mask,
            padded_time_act(flow_times[0], model_width),
            *compact_tables(lengths, local_rows * shards),
            frames_in[0],
            skip_in[0],
            out_grad[0],
            b_skip,
            b_mod,
            b_qkv,
            w_skip,
            w_mod,
            w_qkv,
            shards,
        )
    else:
        angle_cos, angle_sin = rotary_tables(position, HEAD_DIM)
        queries = rotate(
            qkv_full[:, :model_width].reshape(local_rows, HEADS, HEAD_DIM), angle_cos, angle_sin
        ).astype(jnp.bfloat16)
        key_rot = rotate(
            qkv_full[:, model_width : 2 * model_width].reshape(local_rows, HEADS, HEAD_DIM),
            angle_cos,
            angle_sin,
        ).astype(jnp.bfloat16)
        key_value = jnp.stack(
            [
                key_rot.reshape(local_rows, model_width),
                qkv_full[:, 2 * model_width :].astype(jnp.bfloat16),
            ],
            axis=0,
        )
        start_state = (
            jnp.zeros((local_rows, HEADS, HEAD_DIM), jnp.float32),
            jnp.zeros((HEADS, local_rows), jnp.float32),
        )
        fwd_piece = partial(forward_piece, queries=queries, query_segment=segment, utt_ends=utt_ends)
        weighted, totals = over_blocks(
            partial(fwd_piece, usable=True),
            start_state,
            lax.all_gather(key_value, "seq", axis=1, tiled=True),
            jnp.int32(0),
            local_rows,
        )
        totals_rows = jnp.transpose(totals)
        attended = weighted / totals_rows[:, :, None]
        attn_b = attended.reshape(local_rows, model_width).astype(jnp.bfloat16)
    if fused:
        mixed, g_w_down, g_w_up, g_w_out, g_w_qkv, g_w_skip, smalls, g_frames, g_skip_in = backward(
            frame_lengths,
            attn_b,
            residual,
            mod_u,
            loss,
            out_grad[0],
            d_ff,
            b_out,
            b_up,
            b_down,
            qkv_heads,
            exact,
            total,
            cos_all,
            sin_all,
            norm_all,
            joined_all,
            d_ff_all,
            w_out,
            w_up,
            w_down,
            w_qkv,
            w_skip,
        )
        utts = flow_times.shape[1]
        wide, biases = finish(
            shards,
            utts,
            acts,
            smalls,
            mixed,
            g_frames,
            g_skip_in,
            (g_w_skip, g_w_qkv, g_w_out, g_w_up, g_w_down),
        )
        mixed, g_frames, g_skip_in, g_w_skip, g_w_qkv, g_w_out, g_w_up, g_w_down, g_w_mod = wide
        own_biases, g_b_mod = biases[:5], biases[5]
    else:
        n_drop, n_keep = counts[0, 0], counts[0, 1]
        loss_weight = (
            loss_mask
            * (n_drop + n_keep)
            * 0.5
            * (dropped / (n_drop + 1.0) + (1.0 - dropped) / (n_keep + 1.0))
        )
        branch = jnp.dot(attn_b, w_out, preferred_element_type=jnp.float32) + b_out
        mid_state = residual + gate_a * branch
        norm_f = modulate(mid_state, scale_f, shift_f).astype(jnp.bfloat16)
        ff_inner = jnp.dot(norm_f, w_up, preferred_element_type=jnp.float32) + b_up
        ff_act, gelu_pull = jax.vjp(partial(jax.nn.gelu, approximate=True), ff_inner)
        act_b = ff_act.astype(jnp.bfloat16)
        ff_out = jnp.dot(act_b, w_down, preferred_element_type=jnp.float32) + b_down
        out_state = mid_state + gate_f * ff_out
        d_out = out_grad[0].astype(jnp.float32) * loss_weight[:, None]
        d_ff = (gate_f * d_out).astype(jnp.bfloat16)
        d_gate_f = d_out * ff_out
        g_b_down = jnp.sum(d_ff.astype(jnp.float32), axis=0)
        (d_inner,) = gelu_pull(back_product(d_ff, w_down))
        d_inner_b = d_inner.astype(jnp.bfloat16)
        g_b_up = jnp.sum(d_inner_b.astype(jnp.float32), axis=0)
        d_norm_f = back_product(d_inner_b, w_up)
        _, norm_f_pull = jax.vjp(modulate, mid_state, scale_f, shift_f)
        d_mid_norm, d_scale_f, d_shift_f = norm_f_pull(d_norm_f)
        d_mid = d_out + d_mid_norm
        d_branch = (gate_a * d_mid).astype(jnp.bfloat16)
        d_gate_a = d_mid * branch
        g_b_out = jnp.sum(d_branch.astype(jnp.float32), axis=0)
        d_attn = back_product(d_branch, w_out)
        mixed = out_state.astype(jnp.bfloat16)
        g_w_down = weight_grad(gather_left(act_b), d_ff)
        g_w_up = weight_grad(gather_left(norm_f), d_inner_b)
        g_w_out = weight_grad(gather_left(attn_b), d_branch)
        d_attn = d_attn.reshape(local_rows, HEADS, HEAD_DIM)
        grad_acc = (d_attn / totals_rows[:, :, None]).astype(jnp.bfloat16)
        delta = jnp.transpose(jnp.sum(d_attn * attended, axis=2) / totals_rows)
        bwd_piece = partial(
            backward_piece,
            queries=queries,
            query_segment=segment,
            utt_ends=utt_ends,
            grad_acc=grad_acc,
            delta=delta,
        )
        zero_query = jnp.zeros((local_rows, HEADS, HEAD_DIM), jnp.float32)
        zero_all = jnp.zeros((2, local_rows * shards, model_width), jnp.float32)

        def block_fn(inner_state, portion, block_start):
            d_query_sum, d_all = inner_state
            d_query_add, d_block = bwd_piece(portion, block_start, True)
            return (
                d_query_sum + d_query_add,
                lax.dynamic_update_slice_in_dim(d_all, d_block, block_start, 1),
            )

        d_query, d_all = over_blocks(
            block_fn,
            (zero_query, zero_all),
            lax.all_gather(key_value, "seq", axis=1, tiled=True),
            jnp.int32(0),
            local_rows,
        )
        d_key_value = lax.psum_scatter(d_all, "seq", scatter_dimension=1, tiled=True)
        d_query_pre = unrotate(d_query, angle_cos, angle_sin).reshape(local_rows, model_width)
        d_key_pre = unrotate(
            d_key_value[0].reshape(local_rows, HEADS, HEAD_DIM), angle_cos, angle_sin
        ).reshape(local_rows, model_width)
        d_qkv = jnp.concatenate([d_query_pre, d_key_pre, d_key_value[1]], axis=1).astype(jnp.bfloat16)
        g_b_qkv = jnp.sum(d_qkv.astype(jnp.float32), axis=0)
        d_norm_a = back_product(d_qkv, w_qkv)
        _, norm_a_pull = jax.vjp(modulate, residual, scale_a, shift_a)
        d_resid_norm, d_scale_a, d_shift_a = norm_a_pull(d_norm_a)
        d_resid = (d_mid + d_resid_norm).astype(jnp.bfloat16)
        g_b_skip = jnp.sum(d_resid.astype(jnp.float32), axis=0)
        d_joined = back_product(d_resid, w_skip)
        d_mod_f = jnp.concatenate(
            [d_shift_a, d_scale_a, d_gate_a, d_shift_f, d_scale_f, d_gate_f], axis=1
        )
        d_mod_u = jnp.dot(jnp.transpose(member_f), d_mod_f, precision=HIGHEST_PRECISION)
        small = jnp.concatenate(
            [g_b_skip, g_b_qkv, g_b_out, g_b_up, g_b_down, d_mod_u.reshape(-1)]
        )
        biases = small.shape[0] - d_mod_u.size
        g_w_qkv = weight_grad(gather_left(norm_a), d_qkv)
        g_w_skip = weight_grad(gather_left(joined), d_resid)
        small = xor_sum(small.reshape(-1, 128), "seq").reshape(-1)
        bias_sum = xor_sum(small[:biases].reshape(-1, 128), "utt").reshape(-1)
        d_mod_all = gather_ordered(small[biases:].reshape(d_mod_u.shape), 0)
        act_all = gather_ordered(time_act, 0)
        g_frames = d_joined[:, :model_width].astype(jnp.bfloat16)
        g_skip_in = d_joined[:, model_width:].astype(jnp.bfloat16)
        act_all = act_all.astype(jnp.float32)
        own_width = model_width // shards
        act_own = lax.dynamic_slice_in_dim(act_all, seq_place * own_width, own_width, 1)
        g_w_mod = jnp.dot(jnp.transpose(act_own), d_mod_all, precision=HIGHEST_PRECISION)
        mod_width = d_mod_all.shape[1] // shards
        g_b_mod = jnp.sum(
            lax.dynamic_slice_in_dim(d_mod_all, seq_place * mod_width, mod_width, 1), axis=0
        )
        own_biases, offset = [], 0
        for size in (b_skip.shape[0], b_qkv.shape[0], b_out.shape[0], b_up.shape[0], b_down.shape[0]):
            width = size // shards
            own_biases.append(
                lax.dynamic_slice_in_dim(bias_sum, offset + seq_place * width, width, 0)
            )
            offset += size
    return (
        mixed[None],
        g_frames[None],
        g_skip_in[None],
        g_w_skip,
        own_biases[0],
        g_w_mod,
        g_b_mod,
        g_w_qkv,
        own_biases[1],
        g_w_out,
        own_biases[2],
        g_w_up,
        own_biases[3],
        g_w_down,
        own_biases[4],
    )


def solution(mesh):
    return jax.shard_map(
        local,
        mesh=mesh,
        in_specs=(
            P("utt", "seq", None),
            P("utt", "seq", None),
            P("utt", None),
            P("utt", None),
            P("utt", None),
            P("utt", "seq"),
            P("utt", "seq", None),
            P(),
            P(),
            P(),
            P(),
            P(),
            P(),
            P(),
            P(),
            P(),
            P(),
            P(),
            P(),
        ),
        out_specs=(
            P("utt", "seq", None),
            P("utt", "seq", None),
            P("utt", "seq", None),
            P("seq", None),
            P("seq"),
            P("seq", None),
            P("seq"),
            P("seq", None),
            P("seq"),
            P("seq", None),
            P("seq"),
            P("seq", None),
            P("seq"),
            P("seq", None),
            P("seq"),
        ),
        check_vma=False,
    )
```
